32 devices in a mesh: dp: 8 (over z, x), tensor: 4 (over y, core).
Axes of the slice: x: 2, y: 2, z: 4, core: 2. Of those that a mesh axis runs over, the one named last changes fastest.
Arguments:
- tokens: bfloat16 [4096, 768], P(('dp', 'tensor')), may hold values from -6 to 6
- place: int32 [8, 512], P('dp'), may hold values from 0 to 511, each once within a row
- lengths: int32 [8, 3], P('dp'), may hold values from 1 to 320, 512 in all within a row
- expert_ids: int32 [2, 4096, 2], P(None, 'dp'), may hold values from 0 to 3, all different within a row
- gate_values: float32 [2, 4096, 2], P(None, 'dp'), may hold values from 0.25 to 1
- cotangent: bfloat16 [4096, 768], P(('dp', 'tensor')), may hold values from -6 to 6
- gain_attn: float32 [2, 768], P(None, 'dp'), may hold values from 0.5 to 1.5
- w_query: float32 [2, 768, 768], P(None, 'dp', 'tensor'), may hold values from -0.21875 to 0.21875
- w_key: float32 [2, 768, 768], P(None, 'dp', 'tensor'), may hold values from -0.21875 to 0.21875
- w_value: float32 [2, 768, 768], P(None, 'dp', 'tensor'), may hold values from -0.21875 to 0.21875
- w_out: float32 [2, 768, 768], P(None, 'tensor', 'dp'), may hold values from -0.75 to 0.75
- gain_ffn: float32 [2, 768], P(None, 'dp'), may hold values from 0.5 to 1.5
- exp_gate: float32 [2, 4, 768, 2048], P(None, None, 'dp', 'tensor'), may hold values from -0.21875 to 0.21875
- exp_up: float32 [2, 4, 768, 2048], P(None, None, 'dp', 'tensor'), may hold values from -0.21875 to 0.21875
- exp_down: float32 [2, 4, 2048, 768], P(None, None, 'tensor', 'dp'), may hold values from -0.1875 to 0.1875
- dense_gate: float32 [2, 768, 2048], P(None, 'dp', 'tensor'), may hold values from -0.21875 to 0.21875
- dense_up: float32 [2, 768, 2048], P(None, 'dp', 'tensor'), may hold values from -0.21875 to 0.21875
- dense_down: float32 [2, 2048, 768], P(None, 'tensor', 'dp'), may hold values from -0.125 to 0.125
Outputs:
- mixed: bfloat16 [4096, 768], P(('dp', 'tensor'))
- input_grad: float32 [4096, 768], P(('dp', 'tensor'))
- grad_gain_attn: float32 [2, 768], P(None, 'dp')
- grad_query: float32 [2, 768, 768], P(None, 'dp', 'tensor')
- grad_key: float32 [2, 768, 768], P(None, 'dp', 'tensor')
- grad_value: float32 [2, 768, 768], P(None, 'dp', 'tensor')
- grad_out: float32 [2, 768, 768], P(None, 'tensor', 'dp')
- grad_gain_ffn: float32 [2, 768], P(None, 'dp')
- grad_exp_gate: float32 [2, 4, 768, 2048], P(None, None, 'dp', 'tensor')
- grad_exp_up: float32 [2, 4, 768, 2048], P(None, None, 'dp', 'tensor')
- grad_exp_down: float32 [2, 4, 2048, 768], P(None, None, 'tensor', 'dp')
- grad_dense_gate: float32 [2, 768, 2048], P(None, 'dp', 'tensor')
- grad_dense_up: float32 [2, 768, 2048], P(None, 'dp', 'tensor')
- grad_dense_down: float32 [2, 2048, 768], P(None, 'tensor', 'dp')
The draws below stay inside these ranges and needn't reach their ends.
Inputs may be any that keep to these rules, and one draw needn't show every extreme that they name: `place`: each row is a permutation of 0 .. 511. `lengths`: each row sums to 512; its largest entry is exactly 320. `expert_ids`: a token's 2 experts differ; every expert is used by some token of each layer.
All inputs are finite; a program needn't handle non-finite values.
Results may differ from the reference program's by a relative error of at most 0.03.
Values may be sent and summed in bfloat16 or wider, within the bound.
A program may use at most 192 MiB of HBM per device.

```python
import math
import jax
import jax.numpy as jnp
import numpy as np
from jax import lax

D = 768
HEADS = 12
HD = 64
FF = 2048
FF_DENSE = 2048
EXPERTS = 4
TOP = 2
LAYERS = 2
DOCS = 3
TOK_DEV = 512
MAXLEN = 320
SHARDS = 8
TOKENS = 4096


def block_levels(own_key, extent, shards, low, high):
    loudness = 1.0
    for dim, parts in shards:
        heights = jax.random.uniform(jax.random.fold_in(jax.random.fold_in(own_key, 6), dim), (parts,), jnp.float32, low / len(shards), high / len(shards))
        loudness = loudness * jnp.repeat(jnp.exp(heights), extent[dim] // parts).reshape((-1,) + (1,) * (len(extent) - 1 - dim))
    return loudness


def choose_distinct(rng, rows, number_of, top, lift):
    sequence = jax.random.permutation(jax.random.fold_in(rng, 1), number_of)
    pull = sequence
    for power in range(3):
        pull = pull * pull // number_of
    pull = pull * lift // number_of
    lots = jax.random.randint(jax.random.fold_in(rng, 2), (rows, number_of), 0, 4096) + pull
    sure = jax.random.permutation(jax.random.fold_in(rng, 3), rows)[jnp.arange(number_of) % rows]
    lots = jnp.where(jnp.arange(rows)[:, None] == sure[None, :], 1 << 14, lots)
    priority = lots * number_of + jnp.arange(number_of)
    return lax.top_k(priority.astype(jnp.int32), top)[1].astype(jnp.int32)


def length_profile(count, total, most, slope):
    loads = [(1 << 20) // math.isqrt(rank ** slope) + 1 for rank in range(2, count + 1)]
    spare, given = total - most - (count - 1), [1] * (count - 1)
    while spare > 0:
        free = [i for i in range(count - 1) if given[i] < most]
        pool, remaining = sum([loads[i] for i in free]), spare
        for i in free:
            addition = min(most - given[i], max(1, remaining * loads[i] // pool), spare)
            given[i] = given[i] + addition
            spare = spare - addition
    return np.array([most] + given)


def ragged(own_key, count, total, bound, skew):
    if count == 2:
        one = jax.random.randint(own_key, (), max(1, total - bound), min(bound, total - 1) + 1)
        return jnp.stack([one, total - one])
    tallies = jnp.asarray(length_profile(count, total, bound, skew), jnp.int32)
    couples = (count - 1) // 2
    source_of, receiver = tallies[1:1 + 2 * couples:2], tallies[2:2 + 2 * couples:2]
    margin = jnp.minimum(source_of - 1, bound - receiver)
    moved = jax.random.randint(jax.random.fold_in(own_key, 1), (couples,), 0, 1 << 20) % (margin + 1)
    tallies = tallies.at[1:1 + 2 * couples:2].set(source_of - moved).at[2:2 + 2 * couples:2].set(receiver + moved)
    return tallies[jax.random.permutation(jax.random.fold_in(own_key, 2), count)]


def centred(rng, extent, spread, bound, pieces=(), kind=jnp.bfloat16):
    level = block_levels(rng, extent, pieces, -0.22, 0.18) if pieces else 1.0
    values = jax.random.normal(rng, extent, jnp.float32) * spread * level
    return jnp.minimum(jnp.maximum(values, -bound), bound).astype(kind)


def setup_inputs(seed: int = 0) -> dict:
    keys = jax.random.split(jax.random.key(seed), 19)
    tokens = centred(keys[0], (TOKENS, D), 1.0, 6.0, ((0, 32),))
    place = jax.vmap(lambda own: jax.random.permutation(own, TOK_DEV))(jax.random.split(keys[1], SHARDS)).reshape((SHARDS, TOK_DEV)).astype(jnp.int32)
    lengths = jax.vmap(lambda own: ragged(own, DOCS, TOK_DEV, MAXLEN, 2))(jax.random.split(keys[2], SHARDS)).reshape((SHARDS, DOCS)).astype(jnp.int32)
    expert_ids = choose_distinct(keys[3], LAYERS * TOKENS, EXPERTS, TOP, 4096).reshape((LAYERS, TOKENS, TOP))
    gate_values = jnp.clip(0.25 + 0.75 * jax.random.uniform(keys[4], (LAYERS, TOKENS, TOP), jnp.float32) ** block_levels(keys[4], (LAYERS, TOKENS, TOP), ((1, 8),), -0.2, 0.2), 0.25, 1.0)
    cotangent = centred(keys[5], (TOKENS, D), 1.0, 6.0, ((0, 32),))
    gain_attn = jnp.clip(1.0 + 0.1 * jax.random.normal(keys[6], (LAYERS, D), jnp.float32), 0.5, 1.5)
    w_query = centred(keys[7], (LAYERS, D, D), D ** -0.5, 0.21875, ((1, 8), (2, 4)), jnp.float32)
    w_key = centred(keys[8], (LAYERS, D, D), D ** -0.5, 0.21875, ((1, 8), (2, 4)), jnp.float32)
    w_value = centred(keys[9], (LAYERS, D, D), D ** -0.5, 0.21875, ((1, 8), (2, 4)), jnp.float32)
    w_out = centred(keys[10], (LAYERS, D, D), HD ** -0.5, 0.75, ((1, 4), (2, 8)), jnp.float32)
    gain_ffn = jnp.clip(1.0 + 0.1 * jax.random.normal(keys[11], (LAYERS, D), jnp.float32), 0.5, 1.5)
    exp_gate = centred(keys[12], (LAYERS, EXPERTS, D, FF), D ** -0.5, 0.21875, ((2, 8), (3, 4)), jnp.float32)
    exp_up = centred(keys[13], (LAYERS, EXPERTS, D, FF), D ** -0.5, 0.21875, ((2, 8), (3, 4)), jnp.float32)
    exp_down = centred(keys[14], (LAYERS, EXPERTS, FF, D), (FF // 2) ** -0.5, 0.1875, ((2, 4), (3, 8)), jnp.float32)
    dense_gate = centred(keys[15], (LAYERS, D, FF_DENSE), D ** -0.5, 0.21875, ((1, 8), (2, 4)), jnp.float32)
    dense_up = centred(keys[16], (LAYERS, D, FF_DENSE), D ** -0.5, 0.21875, ((1, 8), (2, 4)), jnp.float32)
    dense_down = centred(keys[17], (LAYERS, FF_DENSE, D), FF_DENSE ** -0.5, 0.125, ((1, 4), (2, 8)), jnp.float32)
    return {"tokens": tokens, "place": place, "lengths": lengths, "expert_ids": expert_ids, "gate_values": gate_values, "cotangent": cotangent, "gain_attn": gain_attn, "w_query": w_query, "w_key": w_key, "w_value": w_value, "w_out": w_out, "gain_ffn": gain_ffn, "exp_gate": exp_gate, "exp_up": exp_up, "exp_down": exp_down, "dense_gate": dense_gate, "dense_up": dense_up, "dense_down": dense_down}


EPSILON = 1e-06
MASKED_SCORE = -1e+30
HIGHEST = lax.Precision.HIGHEST

@jax.custom_vjp
def low(v):
    return lax.optimization_barrier(v.astype(jnp.bfloat16)).astype(jnp.float32)

@jax.custom_vjp
def low_back(v):
    return v

def low_keep(v):
    return (low(v), None)

def low_pass(kept, grad):
    return (grad,)

def back_keep(v):
    return (v, None)

def back_low(kept, grad):
    return (low(grad),)
low.defvjp(low_keep, low_pass)
low_back.defvjp(back_keep, back_low)

def layout(place_row, length_row):
    ends = jnp.cumsum(length_row, dtype=jnp.int32)
    after = place_row[:, None] >= ends[None, :]
    segment = lax.optimization_barrier(jnp.sum(after.astype(jnp.int32), axis=1, dtype=jnp.int32))
    begins = lax.optimization_barrier(jnp.sum(jnp.where(after, length_row[None, :], 0), axis=1, dtype=jnp.int32))
    return (segment, (place_row - begins).astype(jnp.int32))

def rope_tables(position, width):
    half_width = width // 2
    freqs = 10000.0 ** (-jnp.arange(half_width, dtype=jnp.float32) / half_width)
    angles = position.astype(jnp.float32)[:, None] * freqs[None, :]
    return (jnp.cos(angles)[:, None, :], jnp.sin(angles)[:, None, :])

def rotate(values, cosine, sine):
    half_width = values.shape[-1] // 2
    first_half = values[..., :half_width]
    second_half = values[..., half_width:]
    return jnp.concatenate([first_half * cosine - second_half * sine, first_half * sine + second_half * cosine], axis=-1)

def normed(values):
    return values * lax.rsqrt(lax.optimization_barrier(jnp.mean(values * values, axis=-1, keepdims=True)) + EPSILON)

def combine(id_rows, gate_rows, count):
    slots = (id_rows[:, :, None] == jnp.arange(count, dtype=jnp.int32)[None, None, :]).astype(jnp.float32)
    return lax.optimization_barrier(jnp.sum(slots * gate_rows[:, :, None], axis=1))

def layer_forward(x_in, weights, segment, position, cosine, sine, id_rows, gate_rows):
    gain_a, w_q, w_k, w_v, w_o, gain_f, e_gate, e_up, e_down, d_gate, d_up, d_down = weights
    tok_count = x_in.shape[0]
    a_in = low(normed(x_in) * gain_a)
    query = low_back(jnp.dot(a_in, w_q, precision=HIGHEST)).reshape(tok_count, HEADS, HD)
    key_raw = low_back(jnp.dot(a_in, w_k, precision=HIGHEST)).reshape(tok_count, HEADS, HD)
    value = low(low_back(jnp.dot(a_in, w_v, precision=HIGHEST))).reshape(tok_count, HEADS, HD)
    query_rot = low(rotate(query, cosine, sine))
    key_rot = low(rotate(key_raw, cosine, sine))
    scores = low_back(jnp.einsum('qhd,khd->hqk', query_rot, key_rot, precision=HIGHEST) * HD ** (-0.5))
    allowed = (segment[:, None] == segment[None, :]) & (position[None, :] <= position[:, None])
    scores = jnp.where(allowed[None], scores, MASKED_SCORE)
    top_score = lax.optimization_barrier(jnp.max(scores, axis=-1, keepdims=True))
    expo = jnp.exp(scores - top_score)
    probs = low(expo / lax.optimization_barrier(jnp.sum(expo, axis=-1, keepdims=True)))
    attended = low(low_back(jnp.einsum('hqk,khd->qhd', probs, value, precision=HIGHEST))).reshape(tok_count, HEADS * HD)
    resid = x_in + low_back(jnp.dot(attended, w_o, precision=HIGHEST))
    b_in = low(normed(resid) * gain_f)
    gate_d = low_back(jnp.dot(b_in, d_gate, precision=HIGHEST))
    up_d = low_back(jnp.dot(b_in, d_up, precision=HIGHEST))
    hidden_d = low(jax.nn.silu(gate_d) * up_d)
    mixing = combine(id_rows, gate_rows, EXPERTS)
    gate_e = low_back(jnp.einsum('td,edf->etf', b_in, e_gate, precision=HIGHEST))
    up_e = low_back(jnp.einsum('td,edf->etf', b_in, e_up, precision=HIGHEST))
    hidden_e = low(jnp.transpose(mixing)[:, :, None] * jax.nn.silu(gate_e) * up_e)
    branch = jnp.dot(hidden_d, d_down, precision=HIGHEST) + jnp.einsum('etf,efd->td', hidden_e, e_down, precision=HIGHEST)
    return resid + low_back(branch)

def reference(tokens, place, lengths, expert_ids, gate_values, cotangent, gain_attn, w_query, w_key, w_value, w_out, gain_ffn, exp_gate, exp_up, exp_down, dense_gate, dense_up, dense_down):
    masters = (gain_attn, w_query, w_key, w_value, w_out, gain_ffn, exp_gate, exp_up, exp_down, dense_gate, dense_up, dense_down)
    inputs = tokens.astype(jnp.float32).reshape(SHARDS, TOK_DEV, D)
    id_shards = jnp.transpose(expert_ids.reshape(LAYERS, SHARDS, TOK_DEV, TOP), (1, 0, 2, 3))
    gate_shards = jnp.transpose(gate_values.reshape(LAYERS, SHARDS, TOK_DEV, TOP), (1, 0, 2, 3))

    def forward(x_all, *master_list):
        rounded = [low(master) for master in master_list]

        def one_shard(carry, items):
            x_row, place_row, length_row, id_rows, gate_rows = items
            segment, position = layout(place_row, length_row)
            cosine, sine = rope_tables(position, HD)
            for layer_index in range(LAYERS):
                weights = [master[layer_index] for master in rounded]
                x_row = layer_forward(x_row, weights, segment, position, cosine, sine, id_rows[layer_index], gate_rows[layer_index])
            return (carry, x_row)
        unused, outputs = lax.scan(jax.checkpoint(one_shard), jnp.zeros((), jnp.float32), (x_all, place, lengths, id_shards, gate_shards))
        return outputs
    outputs, pullback = jax.vjp(forward, inputs, *masters)
    grads = pullback(cotangent.astype(jnp.float32).reshape(SHARDS, TOK_DEV, D))
    mixed = outputs.reshape(TOKENS, D).astype(jnp.bfloat16)
    input_grad = grads[0].reshape(TOKENS, D)
    return (mixed, input_grad, grads[1], grads[2], grads[3], grads[4], grads[5], grads[6], grads[7], grads[8], grads[9], grads[10], grads[11], grads[12])
```

```python
import functools

import jax
import jax.numpy as jnp
from jax import lax
from jax.experimental import pallas as pl
from jax.experimental.pallas import tpu as pltpu
from jax.sharding import PartitionSpec as P

HD = 64
EPSILON = 1e-06
MASKED_SCORE = -1e30
MESH = pl.DeviceIdType.MESH
ANY = pl.BlockSpec(memory_space=pl.ANY)
VMEM = pl.BlockSpec(memory_space=pltpu.VMEM)
F32 = jnp.float32
BF16 = jnp.bfloat16


def split_dp(dp):
    inner = 2 ** ((dp.bit_length() - 1) // 2)
    return dp // inner, inner


def place_of(inner):
    d = lax.axis_index("dp")
    return lax.div(d, inner), lax.rem(d, inner), lax.axis_index("tensor")


def across(t):
    return lax.rem(t + 2, 4), t + 1 - 2 * lax.rem(t, 2)


def meet(devices):
    barrier = pltpu.get_barrier_semaphore()
    for device in devices:
        pl.semaphore_signal(barrier, inc=1, device_id=device, device_id_type=MESH)
    pl.semaphore_wait(barrier, len(devices))


def send(source, target, send_sem, recv_sem, device):
    copy = pltpu.make_async_remote_copy(
        src_ref=source,
        dst_ref=target,
        send_sem=send_sem,
        recv_sem=recv_sem,
        device_id=device,
        device_id_type=MESH,
    )
    copy.start()
    return copy


def gather_kernel(outer, inner, own, out, zs, zr, ys, yr, cs, cr, ls):
    dz, dx, t = place_of(inner)
    d = lax.axis_index("dp")
    ty, tc = across(t)
    zdev = [(lax.rem(dz + k, outer) * inner + dx, t) for k in range(1, outer)]
    meet(zdev + [(d, ty), (d, tc)])
    mine = pltpu.make_async_copy(own, out.at[dz, t], ls)
    mine.start()
    zc = [
        send(own, out.at[dz, t], zs.at[k], zr.at[k], dev) for k, dev in enumerate(zdev)
    ]
    yc = [send(own, out.at[dz, t], ys.at[0], yr.at[0], (d, ty))]
    cc = [send(own, out.at[dz, t], cs.at[0], cr.at[0], (d, tc))]

    def second(k, source):
        yc[k].wait_recv()
        block = out.at[source, ty]
        at = outer + k
        cc.append(send(block, block, cs.at[at], cr.at[at], (d, tc)))

    before = dz
    for k in range(1, outer):
        source = lax.rem(dz - k + outer, outer)
        zc[k - 1].wait_recv()
        block = out.at[source, t]
        yc.append(send(block, block, ys.at[k], yr.at[k], (d, ty)))
        cc.append(send(block, block, cs.at[k], cr.at[k], (d, tc)))
        second(k - 1, before)
        before = source
    second(outer - 1, before)
    for copy in cc:
        copy.wait_recv()
    for copy in zc + yc + cc:
        copy.wait_send()
    mine.wait()


def gather(own, outer, inner, ident):
    dma = pltpu.SemaphoreType.DMA
    return pl.pallas_call(
        functools.partial(gather_kernel, outer, inner),
        out_shape=jax.ShapeDtypeStruct((outer, 4) + own.shape, own.dtype),
        in_specs=[VMEM],
        out_specs=ANY,
        scratch_shapes=[
            dma((max(outer - 1, 1),)),
            dma((max(outer - 1, 1),)),
            dma((outer,)),
            dma((outer,)),
            dma((2 * outer,)),
            dma((2 * outer,)),
            dma,
        ],
        compiler_params=pltpu.CompilerParams(collective_id=ident, has_side_effects=True),
        name="gather",
    )(own)


def scatter_kernel(
    outer, inner, part, out, from_c, sum_c, from_y, sum_y, from_z, cs, cr, ys, yr, zs, zr
):
    dz, dx, t = place_of(inner)
    d = lax.axis_index("dp")
    ty, tc = across(t)
    y, c = lax.div(t, 2), lax.rem(t, 2)
    zdev = [(lax.rem(dz + k, outer) * inner + dx, t) for k in range(1, outer)]
    meet(zdev + [(d, ty), (d, tc)])
    order = list(range(1, outer)) + [0]
    where = [lax.rem(dz + k, outer) for k in range(outer)]
    cc, yc, zc = {}, {}, {}
    for k in order:
        cc[k] = send(
            part.at[where[k], :, 1 - c], from_c.at[k], cs.at[k], cr.at[k], (d, tc)
        )

    def finish(k):
        yc[k].wait_recv()
        total = sum_c[k, y].astype(F32) + from_y[k].astype(F32)
        if k == 0:
            return total
        sum_y[k] = total.astype(BF16)
        zc[k] = send(
            sum_y.at[k], from_z.at[k - 1], zs.at[k - 1], zr.at[k - 1], zdev[k - 1]
        )
        return None

    last = None
    for k in order:
        cc[k].wait_recv()
        sum_c[k] = (part[where[k], :, c].astype(F32) + from_c[k].astype(F32)).astype(BF16)
        yc[k] = send(sum_c.at[k, 1 - y], from_y.at[k], ys.at[k], yr.at[k], (d, ty))
        if last is not None:
            finish(last)
        last = k
    total = finish(last)
    for k in order[:-1]:
        zc[k].wait_recv()
        total = total + from_z[k - 1].astype(F32)
    out[...] = total
    for group in (cc, yc, zc):
        for k in group:
            group[k].wait_send()


def scatter(part, outer, inner, ident):
    dma = pltpu.SemaphoreType.DMA
    rows, width = part.shape[-2:]
    low = max(outer - 1, 1)
    return pl.pallas_call(
        functools.partial(scatter_kernel, outer, inner),
        out_shape=jax.ShapeDtypeStruct((rows, width), F32),
        in_specs=[VMEM],
        out_specs=VMEM,
        scratch_shapes=[
            pltpu.VMEM((outer, 2, rows, width), BF16),
            pltpu.VMEM((outer, 2, rows, width), BF16),
            pltpu.VMEM((outer, rows, width), BF16),
            pltpu.VMEM((outer, rows, width), BF16),
            pltpu.VMEM((low, rows, width), BF16),
            dma((outer,)),
            dma((outer,)),
            dma((outer,)),
            dma((outer,)),
            dma((low,)),
            dma((low,)),
        ],
        compiler_params=pltpu.CompilerParams(collective_id=ident, has_side_effects=True),
        name="scatter",
    )(part)


def fetch_kernel(outer, inner, count, *refs):
    owns, outs, holds = refs[:count], refs[count : 2 * count], refs[2 * count : 3 * count]
    zs, zr, xs, xr, ls = refs[3 * count :]
    dz, dx, t = place_of(inner)
    d = lax.axis_index("dp")
    zdev = [(lax.rem(dz + k, outer) * inner + dx, t) for k in range(1, outer)]
    xdev = [(dz * inner + lax.rem(dx + j, inner), t) for j in range(1, inner)]
    meet(zdev + xdev)
    zc, xc, into, back = {}, [], [], []
    for i in range(count):
        spread = owns[i].shape[0] == outer
        here = owns[i].at[dz if spread else 0]
        into.append(pltpu.make_async_copy(here, holds[i], ls.at[i]))
        into[i].start()
        for k in range(1, outer):
            there = owns[i].at[lax.rem(dz + k, outer) if spread else 0]
            at = i * outer + k
            zc[i, k] = send(there, outs[i].at[d], zs.at[at], zr.at[at], zdev[k - 1])
        for j in range(1, inner):
            at = i * outer * inner + j
            xc.append(send(here, outs[i].at[d], xs.at[at], xr.at[at], xdev[j - 1]))
    for i in range(count):
        into[i].wait()
        back.append(pltpu.make_async_copy(holds[i], outs[i].at[d], ls.at[i]))
        back[i].start()
        for k in range(1, outer):
            zc[i, k].wait_recv()
            block = outs[i].at[lax.rem(dz - k + outer, outer) * inner + dx]
            for j in range(1, inner):
                at = (i * outer + k) * inner + j
                xc.append(send(block, block, xs.at[at], xr.at[at], xdev[j - 1]))
    for copy in xc:
        copy.wait_recv()
        copy.wait_send()
    for key in zc:
        zc[key].wait_send()
    for copy in back:
        copy.wait()


def fetch(owns, outer, inner, ident):
    dma = pltpu.SemaphoreType.DMA
    count = len(owns)
    dp = outer * inner
    return pl.pallas_call(
        functools.partial(fetch_kernel, outer, inner, count),
        out_shape=[jax.ShapeDtypeStruct((dp,) + own.shape[1:], own.dtype) for own in owns],
        in_specs=[ANY] * count,
        out_specs=[ANY] * count,
        scratch_shapes=[pltpu.VMEM(own.shape[1:], own.dtype) for own in owns]
        + [
            dma((count * outer,)),
            dma((count * outer,)),
            dma((count * dp,)),
            dma((count * dp,)),
            dma((count,)),
        ],
        compiler_params=pltpu.CompilerParams(collective_id=ident, has_side_effects=True),
        name="fetch",
    )(*owns)


def push_kernel(outer, inner, count, *refs):
    parts, outs = refs[:count], refs[count : 2 * count]
    froms, sums = refs[2 * count : 3 * count], refs[3 * count : 4 * count]
    xs, xr, zs, zr = refs[4 * count :]
    dz, dx, t = place_of(inner)
    zdev = [(lax.rem(dz + k, outer) * inner + dx, t) for k in range(1, outer)]
    xdev = [(dz * inner + lax.rem(dx + j, inner), t) for j in range(1, inner)]
    meet(zdev + xdev)
    order = list(range(1, outer)) + [0]
    xc, zc = {}, {}
    for i in range(count):
        for k in order:
            for j in range(1, inner):
                slot = lax.rem(dz + k, outer) * inner + lax.rem(dx + j, inner)
                at = (i * outer + k) * inner + j
                xc[i, k, j] = send(
                    parts[i].at[slot],
                    froms[i].at[j - 1, k],
                    xs.at[at],
                    xr.at[at],
                    xdev[j - 1],
                )
    for i in range(count):
        for k in order:
            slot = lax.rem(dz + k, outer) * inner + dx
            total = parts[i][slot].astype(F32)
            for j in range(1, inner):
                xc[i, k, j].wait_recv()
                total = total + froms[i][j - 1, k].astype(F32)
            total = total.astype(parts[i].dtype)
            if k:
                sums[i][k - 1] = total
                at = i * outer + k
                zc[i, k] = send(
                    sums[i].at[k - 1], outs[i].at[dz], zs.at[at], zr.at[at], zdev[k - 1]
                )
            else:
                outs[i][dz] = total
    for key in zc:
        zc[key].wait_recv()
        zc[key].wait_send()
    for key in xc:
        xc[key].wait_send()


def push(parts, outer, inner, ident):
    dma = pltpu.SemaphoreType.DMA
    count = len(parts)
    dp = outer * inner
    return pl.pallas_call(
        functools.partial(push_kernel, outer, inner, count),
        out_shape=[jax.ShapeDtypeStruct((outer,) + p.shape[1:], p.dtype) for p in parts],
        in_specs=[VMEM] * count,
        out_specs=[VMEM] * count,
        scratch_shapes=[pltpu.VMEM((inner - 1, outer) + p.shape[1:], p.dtype) for p in parts]
        + [pltpu.VMEM((outer - 1,) + p.shape[1:], p.dtype) for p in parts]
        + [
            dma((count * dp,)),
            dma((count * dp,)),
            dma((count * outer,)),
            dma((count * outer,)),
        ],
        compiler_params=pltpu.CompilerParams(collective_id=ident, has_side_effects=True),
        name="push",
    )(*parts)


def layout(place_row, length_row):
    ends = jnp.cumsum(length_row, dtype=jnp.int32)
    after = place_row[:, None] >= ends[None, :]
    segment = jnp.sum(after.astype(jnp.int32), axis=1, dtype=jnp.int32)
    begins = jnp.sum(jnp.where(after, length_row[None, :], 0), axis=1, dtype=jnp.int32)
    return (segment, place_row - begins)


def rope_tables(position, width):
    half_width = width // 2
    freqs = 10000.0 ** (-jnp.arange(half_width, dtype=F32) / half_width)
    angles = position.astype(F32)[:, None] * freqs[None, :]
    return (jnp.cos(angles)[:, None, :], jnp.sin(angles)[:, None, :])


def rotate(values, cosine, sine):
    half_width = values.shape[-1] // 2
    first_half = values[..., :half_width]
    second_half = values[..., half_width:]
    return jnp.concatenate(
        [first_half * cosine - second_half * sine, first_half * sine + second_half * cosine],
        axis=-1,
    )


def normed(values):
    inverse = lax.rsqrt(jnp.mean(values * values, axis=-1, keepdims=True) + EPSILON)
    return (values * inverse, inverse)


def norm_back(grad_normed, gain_row, unit_rows, inverse):
    scaled = grad_normed * gain_row
    return inverse * (scaled - unit_rows * jnp.mean(scaled * unit_rows, axis=-1, keepdims=True))


def silu_parts(values):
    sigma = jax.nn.sigmoid(values)
    return (values * sigma, sigma * (1.0 + values * (1.0 - sigma)))


def dot(left, right):
    return jnp.dot(left, right, preferred_element_type=F32)


def dot_nt(left, right):
    return lax.dot_general(left, right, (((1,), (1,)), ((), ())), preferred_element_type=F32)


def dot_tn(left, right):
    return lax.dot_general(left, right, (((0,), (0,)), ((), ())), preferred_element_type=F32)


def attention_scores(query_rot, key_rot, allowed):
    scores = jnp.einsum("qhd,khd->hqk", query_rot, key_rot, preferred_element_type=F32)
    return jnp.where(allowed[None], scores * HD ** (-0.5), MASKED_SCORE)


def make_body(dp):
    outer, inner = split_dp(dp)

    def attn_forward(x_rows, gain, w_attn, allowed, cosine, sine):
        heads_width = w_attn.shape[1] // 4
        unit, inverse = normed(x_rows)
        a_in = gather((unit * gain).astype(BF16), 1, dp, 0).reshape(-1, x_rows.shape[1])
        count = a_in.shape[0]
        raw = dot(a_in, w_attn[:, : 3 * heads_width])
        query = raw[:, :heads_width].reshape(count, -1, HD)
        key_raw = raw[:, heads_width : 2 * heads_width].reshape(count, -1, HD)
        value = raw[:, 2 * heads_width :].astype(BF16).reshape(count, -1, HD)
        query_rot = rotate(query, cosine, sine).astype(BF16)
        key_rot = rotate(key_raw, cosine, sine).astype(BF16)
        scores = attention_scores(query_rot, key_rot, allowed)
        top_score = jnp.max(scores, axis=-1, keepdims=True)
        expo = jnp.exp(scores - top_score)
        total = jnp.sum(expo, axis=-1, keepdims=True)
        probs = (expo / total).astype(BF16)
        log_total = top_score + jnp.log(total)
        attended = (
            jnp.einsum("hqk,khd->qhd", probs, value, preferred_element_type=F32)
            .astype(BF16)
            .reshape(count, heads_width)
        )
        part = dot_nt(attended, w_attn[:, 3 * heads_width :]).astype(BF16)
        resid = x_rows + scatter(part.reshape((1, 2, 2) + x_rows.shape), 1, dp, 1)
        return resid, (unit, inverse, a_in, query_rot, key_rot, value, log_total, attended)

    def ffn_forward(resid, gain, w_ffn, mixing):
        third = w_ffn.shape[1] // 3
        unit, inverse = normed(resid)
        b_in = gather((unit * gain).astype(BF16), outer, inner, 2).reshape(-1, resid.shape[1])
        both = dot(b_in, w_ffn[:, : 2 * third])
        gate, up = both[:, :third], both[:, third:]
        hidden = (mixing * jax.nn.silu(gate) * up).astype(BF16)
        part = dot_nt(hidden, w_ffn[:, 2 * third :]).astype(BF16)
        output = resid + scatter(part.reshape((outer, 2, 2) + resid.shape), outer, inner, 3)
        return output, (unit, inverse, b_in, both.astype(BF16), hidden)

    def ffn_backward(grad_y, kept, gain, w_ffn, mixing):
        unit, inverse, b_in, both, hidden = kept
        third = w_ffn.shape[1] // 3
        width = grad_y.shape[1]
        grad_branch = gather(grad_y.astype(BF16), outer, inner, 2).reshape(-1, width)
        grad_down = dot_tn(grad_branch, hidden).astype(BF16)
        gate, up = both[:, :third].astype(F32), both[:, third:].astype(F32)
        grad_hidden = dot(grad_branch, w_ffn[:, 2 * third :]) * mixing
        act, slope = silu_parts(gate)
        grad_both = jnp.concatenate(
            [(grad_hidden * up * slope).astype(BF16), (grad_hidden * act).astype(BF16)], axis=1
        )
        part = dot_nt(grad_both, w_ffn[:, : 2 * third]).astype(BF16)
        grad_b = scatter(part.reshape((outer, 2, 2) + grad_y.shape), outer, inner, 3)
        grad_in = dot_tn(b_in, grad_both).astype(BF16)
        part_gain = jnp.sum(grad_b * unit, axis=0)
        grad_resid = grad_y + norm_back(grad_b, gain, unit, inverse)
        return grad_resid, part_gain, grad_in, grad_down

    def attn_backward(grad_resid, kept, gain, w_attn, allowed, cosine, sine):
        unit, inverse, a_in, query_rot, key_rot, value, log_total, attended = kept
        heads_width = w_attn.shape[1] // 4
        width = grad_resid.shape[1]
        grad_attn = gather(grad_resid.astype(BF16), 1, dp, 0).reshape(-1, width)
        count = grad_attn.shape[0]
        grad_out = dot_tn(grad_attn, attended).astype(BF16)
        grad_attended = (
            dot(grad_attn, w_attn[:, 3 * heads_width :]).astype(BF16).reshape(count, -1, HD)
        )
        scores = attention_scores(query_rot, key_rot, allowed)
        probs_full = jnp.exp(scores - log_total)
        probs = probs_full.astype(BF16)
        grad_value = (
            jnp.einsum("hqk,qhd->khd", probs, grad_attended, preferred_element_type=F32)
            .astype(BF16)
            .reshape(count, heads_width)
        )
        grad_probs = jnp.einsum("qhd,khd->hqk", grad_attended, value, preferred_element_type=F32)
        grad_scores = (
            probs_full * (grad_probs - jnp.sum(grad_probs * probs_full, axis=-1, keepdims=True))
        ).astype(BF16)
        grad_qrot = jnp.einsum(
            "hqk,khd->qhd", grad_scores, key_rot, preferred_element_type=F32
        ) * HD ** (-0.5)
        grad_krot = jnp.einsum(
            "hqk,qhd->khd", grad_scores, query_rot, preferred_element_type=F32
        ) * HD ** (-0.5)
        grad_query = rotate(grad_qrot, cosine, -sine).astype(BF16).reshape(count, heads_width)
        grad_key = rotate(grad_krot, cosine, -sine).astype(BF16).reshape(count, heads_width)
        grad_raw = jnp.concatenate([grad_query, grad_key, grad_value], axis=1)
        part = dot_nt(grad_raw, w_attn[:, : 3 * heads_width]).astype(BF16)
        grad_a = scatter(part.reshape((1, 2, 2) + grad_resid.shape), 1, dp, 1)
        grad_raw_w = dot_tn(a_in, grad_raw).astype(BF16)
        part_gain = jnp.sum(grad_a * unit, axis=0)
        grad_x = grad_resid + norm_back(grad_a, gain, unit, inverse)
        return grad_x, part_gain, jnp.concatenate([grad_raw_w, grad_out], axis=1)

    def body(
        tokens,
        place,
        lengths,
        expert_ids,
        gate_values,
        cotangent,
        gain_attn,
        w_query,
        w_key,
        w_value,
        w_out,
        gain_ffn,
        exp_gate,
        exp_up,
        exp_down,
        dense_gate,
        dense_up,
        dense_down,
    ):
        layers, experts, rows, full = exp_gate.shape
        width = tokens.shape[1]
        slim = full // outer
        count = place.shape[1]
        segment, position = layout(place[0], lengths[0])
        allowed = (segment[:, None] == segment[None, :]) & (
            position[None, :] <= position[:, None]
        )
        cosine, sine = rope_tables(position, HD)

        slots = expert_ids[:, None] == jnp.arange(experts, dtype=jnp.int32)[None, :, None, None]
        mix_own = jnp.sum(jnp.where(slots, gate_values[:, None], 0.0), axis=-1)
        gains_own = jnp.pad(
            jnp.concatenate([gain_attn, gain_ffn], axis=0).astype(BF16).astype(F32),
            ((0, 8 - 2 * layers), (0, count - rows)),
        )
        small_own = jnp.concatenate([mix_own.reshape(-1, count), gains_own], axis=0)

        attn_own, ffn_own = [], []
        for level in range(layers):
            attn_own.append(
                jnp.concatenate(
                    [w_query[level], w_key[level], w_value[level], jnp.transpose(w_out[level])],
                    axis=1,
                ).astype(BF16)[None]
            )
            mats = (
                [exp_gate[level, e] for e in range(experts)]
                + [dense_gate[level]]
                + [exp_up[level, e] for e in range(experts)]
                + [dense_up[level]]
                + [jnp.transpose(exp_down[level, e]) for e in range(experts)]
                + [jnp.transpose(dense_down[level])]
            )
            mats = [m.astype(BF16) for m in mats]
            ffn_own.append(
                jnp.stack(
                    [
                        jnp.concatenate([m[:, k * slim : (k + 1) * slim] for m in mats], axis=1)
                        for k in range(outer)
                    ]
                )
            )
        first = fetch([small_own[None], attn_own[0], ffn_own[0]], outer, inner, 4)
        small_all = first[0]
        fetched = [first[1:]]
        for level in range(1, layers):
            fetched.append(fetch([attn_own[level], ffn_own[level]], outer, inner, 5))
        w_attn = [pair[0].reshape(width, -1) for pair in fetched]
        w_ffn = [pair[1].reshape(width, -1) for pair in fetched]

        gains = jnp.transpose(small_all[:, layers * experts :, :rows], (1, 0, 2)).reshape(8, width)
        dx = lax.rem(lax.axis_index("dp"), inner)
        mix_all = lax.dynamic_index_in_dim(
            small_all[:, : layers * experts].reshape(outer, inner, layers, experts, count),
            dx,
            axis=1,
            keepdims=False,
        )
        mixing = []
        for level in range(layers):
            mix_rows = jnp.transpose(mix_all[:, level], (0, 2, 1)).reshape(outer * count, experts)
            mixing.append(
                jnp.concatenate(
                    [
                        jnp.broadcast_to(mix_rows[:, e : e + 1], (outer * count, slim))
                        for e in range(experts)
                    ]
                    + [jnp.ones((outer * count, slim), F32)],
                    axis=1,
                )
            )

        state = tokens.astype(F32)
        kept_attn, kept_ffn = [], []
        for level in range(layers):
            state, kept = attn_forward(
                state, gains[level][None], w_attn[level], allowed, cosine, sine
            )
            kept_attn.append(kept)
            state, kept = ffn_forward(
                state, gains[layers + level][None], w_ffn[level], mixing[level]
            )
            kept_ffn.append(kept)
        mixed = state.astype(BF16)

        grad = cotangent.astype(F32)
        part_gains = [None] * (2 * layers)
        pushed = [None] * layers
        for level in reversed(range(layers)):
            grad, part_gains[layers + level], grad_in, grad_down = ffn_backward(
                grad, kept_ffn[level], gains[layers + level][None], w_ffn[level], mixing[level]
            )
            grad, part_gains[level], grad_attn = attn_backward(
                grad,
                kept_attn[level],
                gains[level][None],
                w_attn[level],
                allowed,
                cosine,
                sine,
            )
            parts = [
                grad_in.reshape(dp, rows, -1),
                grad_down.reshape(dp, rows, -1),
                grad_attn.reshape(dp, rows, -1),
            ]
            if level == 0:
                stacked = jnp.pad(jnp.stack(part_gains), ((0, 8 - 2 * layers), (0, 0)))
                parts.append(jnp.transpose(stacked.reshape(8, dp, rows), (1, 0, 2)))
                pushed[level] = push(parts, outer, inner, 6)
            else:
                pushed[level] = push(parts, outer, inner, 7)

        gain_part = jnp.sum(pushed[0][3], axis=0)
        gain_sum = jnp.sum(
            gather(jnp.pad(gain_part, ((0, 0), (0, 128 - rows))), 1, dp, 8)[0], axis=0
        )
        grad_gain_attn = gain_sum[:layers, :rows]
        grad_gain_ffn = gain_sum[layers : 2 * layers, :rows]

        kinds = experts + 1
        ups, downs, attns = [], [], []
        for level in range(layers):
            in_part, down_part, attn_part = pushed[level][:3]
            ups.append(
                jnp.concatenate(
                    [
                        jnp.stack(
                            [
                                in_part[k][:, m * slim : (m + 1) * slim]
                                for m in range(2 * kinds)
                            ]
                        )
                        for k in range(outer)
                    ],
                    axis=2,
                )
            )
            downs.append(
                jnp.concatenate(
                    [
                        jnp.stack(
                            [
                                jnp.transpose(down_part[k][:, m * slim : (m + 1) * slim])
                                for m in range(kinds)
                            ]
                        )
                        for k in range(outer)
                    ],
                    axis=1,
                )
            )
            attns.append(jnp.sum(attn_part.astype(F32), axis=0))
        up = jnp.stack(ups).astype(F32)
        down = jnp.stack(downs).astype(F32)
        attn = jnp.stack(attns)
        quarter = attn.shape[-1] // 4
        return (
            mixed,
            grad,
            grad_gain_attn,
            attn[:, :, :quarter],
            attn[:, :, quarter : 2 * quarter],
            attn[:, :, 2 * quarter : 3 * quarter],
            jnp.swapaxes(attn[:, :, 3 * quarter :], 1, 2),
            grad_gain_ffn,
            up[:, :experts],
            up[:, kinds : kinds + experts],
            down[:, :experts],
            up[:, experts],
            up[:, kinds + experts],
            down[:, experts],
        )

    return body


def solution(mesh):
    return jax.shard_map(
        make_body(mesh.shape["dp"]),
        mesh=mesh,
        in_specs=(
            P(("dp", "tensor"), None),
            P("dp", None),
            P("dp", None),
            P(None, "dp", None),
            P(None, "dp", None),
            P(("dp", "tensor"), None),
            P(None, "dp"),
            P(None, "dp", "tensor"),
            P(None, "dp", "tensor"),
            P(None, "dp", "tensor"),
            P(None, "tensor", "dp"),
            P(None, "dp"),
            P(None, None, "dp", "tensor"),
            P(None, None, "dp", "tensor"),
            P(None, None, "tensor", "dp"),
            P(None, "dp", "tensor"),
            P(None, "dp", "tensor"),
            P(None, "tensor", "dp"),
        ),
        out_specs=(
            P(("dp", "tensor"), None),
            P(("dp", "tensor"), None),
            P(None, "dp"),
            P(None, "dp", "tensor"),
            P(None, "dp", "tensor"),
            P(None, "dp", "tensor"),
            P(None, "tensor", "dp"),
            P(None, "dp"),
            P(None, None, "dp", "tensor"),
            P(None, None, "dp", "tensor"),
            P(None, None, "tensor", "dp"),
            P(None, "dp", "tensor"),
            P(None, "dp", "tensor"),
            P(None, "tensor", "dp"),
        ),
        check_vma=False,
    )
```

```python
import functools

import jax
import jax.numpy as jnp
from jax import lax
from jax.experimental import pallas as pl
from jax.experimental.pallas import tpu as pltpu
from jax.sharding import PartitionSpec as P

HD = 64
EPSILON = 1e-06
MASKED_SCORE = -1e30
MESH = pl.DeviceIdType.MESH
ANY = pl.BlockSpec(memory_space=pl.ANY)
VMEM = pl.BlockSpec(memory_space=pltpu.VMEM)
F32 = jnp.float32
BF16 = jnp.bfloat16


def split_dp(dp):
    inner = 2 ** ((dp.bit_length() - 1) // 2)
    return dp // inner, inner


def place_of(inner):
    d = lax.axis_index("dp")
    return lax.div(d, inner), lax.rem(d, inner), lax.axis_index("tensor")


def across(t):
    return lax.rem(t + 2, 4), t + 1 - 2 * lax.rem(t, 2)


def meet(devices):
    barrier = pltpu.get_barrier_semaphore()
    for device in devices:
        pl.semaphore_signal(barrier, inc=1, device_id=device, device_id_type=MESH)
    pl.semaphore_wait(barrier, len(devices))


def send(source, target, send_sem, recv_sem, device):
    copy = pltpu.make_async_remote_copy(
        src_ref=source,
        dst_ref=target,
        send_sem=send_sem,
        recv_sem=recv_sem,
        device_id=device,
        device_id_type=MESH,
    )
    copy.start()
    return copy


def gather_kernel(dp, own, out, *sems):
    take = Gather(1, dp, out, sems)
    out[0, take.t] = own[...]
    meet(take.friends())
    take.start()
    take.complete(0)
    take.finish()


def gather(own, dp, ident):
    return pl.pallas_call(
        functools.partial(gather_kernel, dp),
        out_shape=jax.ShapeDtypeStruct((1, 4) + own.shape, own.dtype),
        in_specs=[VMEM],
        out_specs=VMEM,
        scratch_shapes=gather_sems(1),
        compiler_params=pltpu.CompilerParams(collective_id=ident, has_side_effects=True),
        name="gather",
    )(own)


def fetch_kernel(outer, inner, count, *refs):
    cut = Cut(refs)
    extra = Fetch(outer, inner, cut(count), cut(count), cut(count), cut(5))
    meet(extra.zdev[1:] + extra.xdev)
    extra.start()
    extra.settle()
    for turn in extra.turns():
        turn()
    extra.finish()


def fetch(owns, outer, inner, ident):
    count = len(owns)
    return pl.pallas_call(
        functools.partial(fetch_kernel, outer, inner, count),
        out_shape=fetch_outs(owns, outer * inner),
        in_specs=[ANY] * count,
        out_specs=[ANY] * count,
        scratch_shapes=fetch_scratch(owns, outer, inner),
        compiler_params=pltpu.CompilerParams(collective_id=ident, has_side_effects=True),
        name="fetch",
    )(*owns)


def push_kernel(outer, inner, count, *refs):
    cut = Cut(refs)
    extra = Push(outer, inner, cut(count), cut(count), cut(3 * count), cut(6))
    meet(extra.zdev[:-1] + extra.xdev)
    extra.start()
    for turn in extra.turns():
        turn()
    extra.finish()


def push(parts, outer, inner, ident):
    count = len(parts)
    return pl.pallas_call(
        functools.partial(push_kernel, outer, inner, count),
        out_shape=push_outs(parts, outer),
        in_specs=[ANY] * count,
        out_specs=[ANY] * count,
        scratch_shapes=push_scratch(parts, outer, inner),
        compiler_params=pltpu.CompilerParams(collective_id=ident, has_side_effects=True),
        name="push",
    )(*parts)


def nearest(index, size, step):
    table = [sorted(range(size), key=lambda other: (abs(other - at), other)) for at in range(size)]
    found = 0
    for at in range(size):
        found = found + jnp.where(index == at, table[at][step], 0)
    return found


class Gather:
    def __init__(self, outer, inner, table, sems):
        self.outer, self.table = outer, table
        self.zs, self.zr, self.ys, self.yr, self.cs, self.cr = sems
        self.dz, self.dx, self.t = place_of(inner)
        self.d = lax.axis_index("dp")
        ty, tc = across(self.t)
        self.ty = ty
        self.pair, self.core = (self.d, ty), (self.d, tc)
        self.source = [nearest(self.dz, outer, step) for step in range(outer)]
        self.zdev = [(source * inner + self.dx, self.t) for source in self.source]
        self.zc, self.yc, self.cc, self.dc = [None], [], [], []

    def friends(self):
        return self.zdev[1:] + [self.pair, self.core]

    def start(self):
        own = self.table.at[self.dz, self.t]
        for step in range(1, self.outer):
            away = lax.rem(self.source[step] - self.dz + self.outer, self.outer)
            self.zc.append(send(own, own, self.zs.at[away], self.zr.at[away], self.zdev[step]))
        self.forward(0)

    def arrive(self, step):
        block = self.table.at[self.source[step], self.t]
        away = lax.rem(self.dz - self.source[step] + self.outer, self.outer)
        pltpu.make_async_remote_copy(
            src_ref=block,
            dst_ref=block,
            send_sem=self.zs.at[away],
            recv_sem=self.zr.at[away],
            device_id=self.zdev[step],
            device_id_type=MESH,
        ).wait_recv()
        self.forward(step)

    def forward(self, step):
        source = self.source[step]
        away = lax.rem(source - self.dz + self.outer, self.outer)
        block = self.table.at[source, self.t]
        self.yc.append(send(block, block, self.ys.at[step], self.yr.at[step], self.pair))
        self.cc.append(send(block, block, self.cs.at[step], self.cr.at[step], self.core))

    def complete(self, step):
        self.yc[step].wait_recv()
        at = self.outer + step
        block = self.table.at[self.source[step], self.ty]
        self.dc.append(send(block, block, self.cs.at[at], self.cr.at[at], self.core))
        self.cc[step].wait_recv()
        self.dc[step].wait_recv()

    def finish(self):
        for copy in self.zc[1:] + self.yc + self.cc + self.dc:
            copy.wait_send()


class Scatter:
    def __init__(self, outer, inner, part, room, sems):
        self.outer, self.part = outer, part
        self.from_c, self.sum_c, self.from_y, self.sum_y, self.from_z = room
        self.cs, self.cr, self.ys, self.yr, self.zs, self.zr = sems
        dz, dx, t = place_of(inner)
        d = lax.axis_index("dp")
        ty, tc = across(t)
        self.dz, self.y, self.c = dz, lax.div(t, 2), lax.rem(t, 2)
        self.pair, self.core = (d, ty), (d, tc)
        self.source = [nearest(dz, outer, step) for step in range(outer)]
        self.zdev = [(source * inner + dx, t) for source in self.source]
        self.cc, self.yc, self.zc = {}, {}, {}

    def core_send(self, step):
        self.cc[step] = send(
            self.part.at[self.source[step], :, 1 - self.c],
            self.from_c.at[step],
            self.cs.at[step],
            self.cr.at[step],
            self.core,
        )

    def pair_send(self, step):
        self.cc[step].wait_recv()
        mine = self.part[self.source[step], :, self.c].astype(F32)
        self.sum_c[step] = (mine + self.from_c[step].astype(F32)).astype(BF16)
        self.yc[step] = send(
            self.sum_c.at[step, 1 - self.y],
            self.from_y.at[step],
            self.ys.at[step],
            self.yr.at[step],
            self.pair,
        )

    def outer_send(self, step):
        self.yc[step].wait_recv()
        total = self.sum_c[step, self.y].astype(F32) + self.from_y[step].astype(F32)
        if step == 0:
            return total
        self.sum_y[step - 1] = total.astype(BF16)
        away = lax.rem(self.source[step] - self.dz + self.outer, self.outer)
        self.zc[step] = send(
            self.sum_y.at[step - 1],
            self.from_z.at[away - 1],
            self.zs.at[away - 1],
            self.zr.at[away - 1],
            self.zdev[step],
        )
        return None

    def total(self, total):
        for step in range(1, self.outer):
            away = lax.rem(self.dz - self.source[step] + self.outer, self.outer)
            block = self.from_z.at[away - 1]
            pltpu.make_async_remote_copy(
                src_ref=block,
                dst_ref=block,
                send_sem=self.zs.at[away - 1],
                recv_sem=self.zr.at[away - 1],
                device_id=self.zdev[step],
                device_id_type=MESH,
            ).wait_recv()
            total = total + self.from_z[away - 1].astype(F32)
        return total

    def finish(self):
        for group in (self.cc, self.yc, self.zc):
            for step in group:
                group[step].wait_send()


def gather_sems(outer):
    dma = pltpu.SemaphoreType.DMA
    return [dma((outer,)) for _ in range(4)] + [dma((2 * outer,)) for _ in range(2)]


def scatter_sems(outer):
    dma = pltpu.SemaphoreType.DMA
    return [dma((outer,)) for _ in range(6)]


def scatter_room(outer, rows, width):
    low = max(outer - 1, 1)
    return [
        pltpu.VMEM((outer, 2, rows, width), BF16),
        pltpu.VMEM((outer, 2, rows, width), BF16),
        pltpu.VMEM((outer, rows, width), BF16),
        pltpu.VMEM((low, rows, width), BF16),
        pltpu.VMEM((low, rows, width), BF16),
    ]


def pipeline(outer, take, give, compute, fill):
    fill = iter(fill)

    def filler(count):
        for _ in range(count):
            work = next(fill, None)
            if work is not None:
                work()

    take.start()
    filler(1)
    take.arrive(1)
    take.complete(0)
    compute(0)
    give.core_send(0)
    give.pair_send(0)
    for step in range(1, outer):
        if step == 1:
            take.complete(1)
        if step + 1 < outer:
            take.arrive(step + 1)
        if step > 1:
            give.pair_send(step - 1)
            take.complete(step)
        compute(step)
        give.core_send(step)
        if step == 1:
            filler(1)
        if step > 2:
            give.outer_send(step - 2)
    filler(1)
    give.pair_send(outer - 1)
    filler(2)
    if outer > 2:
        give.outer_send(outer - 2)
    filler(2)
    give.outer_send(outer - 1)
    filler(100)
    return give.outer_send(0)


class Fetch:
    def __init__(self, outer, inner, owns, outs, holds, sems):
        self.outer, self.inner, self.owns, self.outs, self.holds = outer, inner, owns, outs, holds
        self.zs, self.zr, self.xs, self.xr, self.ls = sems
        self.dz, dx, t = place_of(inner)
        self.dx, self.d = dx, lax.axis_index("dp")
        self.source = [nearest(self.dz, outer, step) for step in range(outer)]
        self.zdev = [(source * inner + dx, t) for source in self.source]
        self.xdev = [(self.dz * inner + lax.rem(dx + j, inner), t) for j in range(1, inner)]
        self.zc, self.xc, self.into, self.back = [], [], [], []

    def own(self, i, where):
        return self.owns[i].at[where if self.owns[i].shape[0] == self.outer else 0]

    def copy(self, i, step):
        away = lax.rem(self.source[step] - self.dz + self.outer, self.outer)
        at = i * self.outer + away
        return pltpu.make_async_remote_copy(
            src_ref=self.own(i, self.source[step]),
            dst_ref=self.outs[i].at[self.d],
            send_sem=self.zs.at[at],
            recv_sem=self.zr.at[at],
            device_id=self.zdev[step],
            device_id_type=MESH,
        )

    def start(self):
        for i in range(len(self.owns)):
            here = self.own(i, self.dz)
            self.into.append(pltpu.make_async_copy(here, self.holds[i], self.ls.at[i]))
            self.into[i].start()
            for step in range(1, self.outer):
                self.zc.append(self.copy(i, step))
                self.zc[-1].start()
            self.spread(i, 0, here, self.outs[i].at[self.d])

    def spread(self, i, step, block, target):
        for j in range(1, self.inner):
            at = (i * self.outer + step) * self.inner + j
            self.xc.append(
                send(block, target, self.xs.at[at], self.xr.at[at], self.xdev[j - 1])
            )

    def settle(self):
        for i, into in enumerate(self.into):
            into.wait()
            self.back.append(
                pltpu.make_async_copy(self.holds[i], self.outs[i].at[self.d], self.ls.at[i])
            )
            self.back[i].start()

    def turn(self, i, step):
        source = self.source[step]
        block = self.outs[i].at[source * self.inner + self.dx]
        away = lax.rem(self.dz - source + self.outer, self.outer)
        at = i * self.outer + away
        pltpu.make_async_remote_copy(
            src_ref=block,
            dst_ref=block,
            send_sem=self.zs.at[at],
            recv_sem=self.zr.at[at],
            device_id=self.zdev[step],
            device_id_type=MESH,
        ).wait_recv()
        self.spread(i, step, block, block)

    def turns(self):
        return [
            functools.partial(self.turn, i, step)
            for i in range(len(self.owns))
            for step in range(1, self.outer)
        ]

    def finish(self):
        for copy in self.xc:
            copy.wait_recv()
        for copy in self.xc + self.zc:
            copy.wait_send()
        for copy in self.back:
            copy.wait()


def fetch_outs(owns, dp):
    return [jax.ShapeDtypeStruct((dp,) + own.shape[1:], own.dtype) for own in owns]


def fetch_scratch(owns, outer, inner):
    dma = pltpu.SemaphoreType.DMA
    count = max(len(owns), 1)
    return [pltpu.VMEM(own.shape[1:], own.dtype) for own in owns] + [
        dma((count * outer,)),
        dma((count * outer,)),
        dma((count * outer * inner,)),
        dma((count * outer * inner,)),
        dma((count,)),
    ]


class Push:
    def __init__(self, outer, inner, parts, outs, room, sems):
        count = len(parts)
        self.outer, self.inner, self.parts, self.outs = outer, inner, parts, outs
        self.froms, self.mine, self.sums = room[:count], room[count : 2 * count], room[2 * count :]
        self.xs, self.xr, self.zs, self.zr, self.ls, self.ks = sems
        self.dz, dx, t = place_of(inner)
        self.dx = dx
        near = [nearest(self.dz, outer, step) for step in range(outer)]
        self.source = near[:0:-1] + near[:1]
        self.zdev = [(source * inner + dx, t) for source in self.source]
        self.xdev = [(self.dz * inner + lax.rem(dx + j, inner), t) for j in range(1, inner)]
        self.xc, self.zc, self.loads, self.keeps = {}, [], {}, []

    def start(self):
        for i in range(len(self.parts)):
            for step, source in enumerate(self.source):
                for j in range(1, self.inner):
                    slot = source * self.inner + lax.rem(self.dx + j, self.inner)
                    at = (i * self.outer + step) * self.inner + j
                    self.xc[i, step, j] = send(
                        self.parts[i].at[slot],
                        self.froms[i].at[j - 1, step],
                        self.xs.at[at],
                        self.xr.at[at],
                        self.xdev[j - 1],
                    )
                self.loads[i, step] = pltpu.make_async_copy(
                    self.parts[i].at[source * self.inner + self.dx],
                    self.mine[i].at[step],
                    self.ls.at[i * self.outer + step],
                )
                self.loads[i, step].start()

    def turn(self, i, step):
        self.loads[i, step].wait()
        total = self.mine[i][step].astype(F32)
        for j in range(1, self.inner):
            self.xc[i, step, j].wait_recv()
            total = total + self.froms[i][j - 1, step].astype(F32)
        self.sums[i][step] = total.astype(self.sums[i].dtype)
        target = self.outs[i].at[self.dz]
        if step < self.outer - 1:
            away = lax.rem(self.source[step] - self.dz + self.outer, self.outer)
            at = i * self.outer + away
            self.zc.append(
                send(self.sums[i].at[step], target, self.zs.at[at], self.zr.at[at], self.zdev[step])
            )
        else:
            self.keeps.append(
                pltpu.make_async_copy(self.sums[i].at[step], target, self.ks.at[i])
            )
            self.keeps[-1].start()

    def turns(self):
        return [
            functools.partial(self.turn, i, step)
            for i in range(len(self.parts))
            for step in range(self.outer)
        ]

    def finish(self):
        for copy in self.zc:
            copy.wait_recv()
            copy.wait_send()
        for key in self.xc:
            self.xc[key].wait_send()
        for copy in self.keeps:
            copy.wait()


def push_outs(parts, outer):
    return [jax.ShapeDtypeStruct((outer,) + part.shape[1:], part.dtype) for part in parts]


def push_scratch(parts, outer, inner):
    dma = pltpu.SemaphoreType.DMA
    count = max(len(parts), 1)
    across_x = [pltpu.VMEM((inner - 1, outer) + part.shape[1:], part.dtype) for part in parts]
    own = [pltpu.VMEM((outer,) + part.shape[1:], part.dtype) for part in parts]
    return (
        across_x
        + own
        + own
        + [
            dma((count * outer * inner,)),
            dma((count * outer * inner,)),
            dma((count * outer,)),
            dma((count * outer,)),
            dma((count * outer,)),
            dma((count,)),
        ]
    )


class Cut:
    def __init__(self, refs):
        self.refs, self.at = refs, 0

    def __call__(self, count):
        self.at += count
        return self.refs[self.at - count : self.at]


def ffn_forward_kernel(outer, inner, kinds, count, *refs):
    cut = Cut(refs)
    resid, gain, mix, w_in_any, w_down_any = cut(5)
    owns = cut(count)
    out, b_out, gu_out = cut(3)
    fetched = cut(count)
    w_in, w_down, b, gu, part = cut(5)
    room, take_sems, give_sems = cut(5), cut(6), cut(6)
    load_sem, keep_b, keep_gu = cut(3)
    extra = Fetch(outer, inner, owns, fetched, cut(count), cut(5)) if count else None
    rows, width = resid.shape
    third = w_down.shape[1]
    slim = third // kinds
    loads = [
        pltpu.make_async_copy(w_in_any, w_in, load_sem.at[0]),
        pltpu.make_async_copy(w_down_any, w_down, load_sem.at[1]),
    ]
    for load in loads:
        load.start()
    take = Gather(outer, inner, b, take_sems)
    give = Scatter(outer, inner, part, room, give_sems)
    x = resid[...]
    inverse = lax.rsqrt(jnp.mean(x * x, axis=-1, keepdims=True) + EPSILON)
    b[take.dz, take.t] = (x * inverse * gain[...]).astype(BF16)
    meet(take.friends() + (extra.xdev if count else []))
    keeps = []

    def compute(step):
        source = take.source[step]
        if step == 0:
            for load in loads:
                load.wait()

        @pl.loop(0, 2)
        def _(half):
            rows_in = b[source, pl.ds(2 * half, 2)].reshape(2 * rows, width)
            both = dot(rows_in, w_in[...])
            gu[source, half] = both.astype(BF16)
            gate, up = both[:, :third], both[:, third:]
            hidden = gate * jax.nn.sigmoid(gate) * up
            pieces = []
            for e in range(kinds):
                piece = hidden[:, e * slim : (e + 1) * slim]
                if e < kinds - 1:
                    piece = piece * mix[source, half, :, e : e + 1]
                pieces.append(piece.astype(BF16))
            hidden = jnp.concatenate(pieces, axis=1)
            sent = dot_nt(hidden, w_down[...])
            part[source, half] = sent.astype(BF16).reshape(2, rows, width)

        keeps.append(pltpu.make_async_copy(b.at[source], b_out.at[source], keep_b.at[step]))
        keeps.append(pltpu.make_async_copy(gu.at[source], gu_out.at[source], keep_gu.at[step]))
        keeps[-1].start()
        keeps[-2].start()

    fill = []
    if count:
        turns = extra.turns()

        def begin():
            extra.start()
            extra.settle()

        def rest():
            for turn in turns:
                turn()

        fill = [begin, rest]
    total = pipeline(outer, take, give, compute, fill)
    out[...] = resid[...] + give.total(total)
    take.finish()
    give.finish()
    if count:
        extra.finish()
    for keep in keeps:
        keep.wait()


def ffn_forward(resid, gain, mix, w_in, w_down, owns, outer, inner, ident):
    dma = pltpu.SemaphoreType.DMA
    rows, width = resid.shape
    third = w_down.shape[1]
    kinds = mix.shape[-1] + 1
    count = len(owns)
    return pl.pallas_call(
        functools.partial(ffn_forward_kernel, outer, inner, kinds, count),
        out_shape=[
            jax.ShapeDtypeStruct((rows, width), F32),
            jax.ShapeDtypeStruct((outer, 4, rows, width), BF16),
            jax.ShapeDtypeStruct((outer, 2, 2 * rows, 2 * third), BF16),
        ]
        + fetch_outs(owns, outer * inner),
        in_specs=[VMEM, VMEM, VMEM, ANY, ANY] + [ANY] * count,
        out_specs=[VMEM, ANY, ANY] + [ANY] * count,
        scratch_shapes=[
            pltpu.VMEM(w_in.shape, BF16),
            pltpu.VMEM(w_down.shape, BF16),
            pltpu.VMEM((outer, 4, rows, width), BF16),
            pltpu.VMEM((outer, 2, 2 * rows, 2 * third), BF16),
            pltpu.VMEM((outer, 2, 2, rows, width), BF16),
        ]
        + scatter_room(outer, rows, width)
        + gather_sems(outer)
        + scatter_sems(outer)
        + [dma((2,)), dma((outer,)), dma((outer,))]
        + (fetch_scratch(owns, outer, inner) if count else []),
        compiler_params=pltpu.CompilerParams(
            collective_id=ident, has_side_effects=True, vmem_limit_bytes=62 << 20
        ),
        name="ffn_forward",
    )(resid, gain, mix, w_in, w_down, *owns)


def ffn_backward_kernel(outer, inner, kinds, count, *refs):
    cut = Cut(refs)
    grad_y, resid, gain, mix, w_in_any, w_down_any, b_any, gu_any = cut(8)
    parts = cut(count)
    out, gain_out, grad_in, grad_down = cut(4)
    pushed = cut(count)
    w_in, w_down, b, gb, gu, dgu, hid, flip, part = cut(9)
    room, take_sems, give_sems = cut(5), cut(6), cut(6)
    load_sem, load_gu = cut(2)
    extra = Push(outer, inner, parts, pushed, cut(3 * count), cut(6)) if count else None
    rows, width = resid.shape
    tall = outer * 4 * rows
    third = w_down.shape[1]
    slim = third // kinds
    loads = [
        pltpu.make_async_copy(source, target, load_sem.at[i])
        for i, (source, target) in enumerate(
            ((b_any, b), (w_down_any, w_down), (w_in_any, w_in))
        )
    ]
    for load in loads:
        load.start()
    take = Gather(outer, inner, gb, take_sems)
    give = Scatter(outer, inner, part, room, give_sems)
    fills = [
        pltpu.make_async_copy(gu_any.at[source], gu.at[source], load_gu.at[step])
        for step, source in enumerate(take.source)
    ]
    for fill in fills:
        fill.start()
    gb[take.dz, take.t] = grad_y[...].astype(BF16)
    meet(take.friends() + (extra.xdev if count else []))

    def compute(step):
        source = take.source[step]
        if step == 0:
            loads[1].wait()
            loads[2].wait()
        fills[step].wait()

        @pl.loop(0, 2)
        def _(half):
            rows_in = gb[source, pl.ds(2 * half, 2)].reshape(2 * rows, width)
            grad_hidden = dot(rows_in, w_down[...])
            both = gu[source, half].astype(F32)
            gate, up = both[:, :third], both[:, third:]
            sigma = jax.nn.sigmoid(gate)
            act = gate * sigma
            slope = sigma * (1.0 + gate * (1.0 - sigma))
            hidden, grad_gate, grad_up = act * up, grad_hidden * up * slope, grad_hidden * act
            for e in range(kinds):
                here = slice(e * slim, (e + 1) * slim)
                there = slice(third + e * slim, third + (e + 1) * slim)
                scale = mix[source, half, :, e : e + 1] if e < kinds - 1 else 1.0
                hid[source, half, :, here] = (hidden[:, here] * scale).astype(BF16)
                dgu[source, half, :, here] = (grad_gate[:, here] * scale).astype(BF16)
                dgu[source, half, :, there] = (grad_up[:, here] * scale).astype(BF16)
            sent = dot_nt(dgu[source, half], w_in[...])
            part[source, half] = sent.astype(BF16).reshape(2, rows, width)

    def turned(table):
        @pl.loop(0, outer * 4)
        def _(at):
            block = table[lax.div(at, 4), lax.rem(at, 4)]
            flip[:, pl.ds(pl.multiple_of(at * rows, rows), rows)] = jnp.transpose(block)

    def weigh(target, source, low, high):
        values = source[...].reshape(tall, source.shape[-1])

        @pl.loop(0, width // 256)
        def _(at):
            here = pl.ds(pl.multiple_of(at * 256, 256), 256)
            target[here, low:high] = dot(flip[here, :], values[:, low:high]).astype(BF16)

    def begin():
        if count:
            extra.start()
        loads[0].wait()
        turned(b)

    def between():
        if count:
            for turn in extra.turns():
                turn()

    def pieces(total):
        return [(low, min(low + 256, total)) for low in range(0, total, 256)]

    fill = [begin, between]
    fill += [functools.partial(weigh, grad_in, dgu, *span) for span in pieces(2 * third)]
    fill += [functools.partial(turned, gb)]
    fill += [functools.partial(weigh, grad_down, hid, *span) for span in pieces(third)]
    total = pipeline(outer, take, give, compute, fill)
    grad_b = give.total(total)
    x = resid[...]
    inverse = lax.rsqrt(jnp.mean(x * x, axis=-1, keepdims=True) + EPSILON)
    unit = x * inverse
    gain_out[...] = jnp.sum(grad_b * unit, axis=0, keepdims=True)
    out[...] = grad_y[...] + norm_back(grad_b, gain[...], unit, inverse)
    take.finish()
    give.finish()
    if count:
        extra.finish()


def ffn_backward(grad_y, resid, gain, mix, w_in, w_down, b, both, parts, outer, inner, ident):
    dma = pltpu.SemaphoreType.DMA
    rows, width = resid.shape
    third = w_down.shape[1]
    kinds = mix.shape[-1] + 1
    count = len(parts)
    return pl.pallas_call(
        functools.partial(ffn_backward_kernel, outer, inner, kinds, count),
        out_shape=[
            jax.ShapeDtypeStruct((rows, width), F32),
            jax.ShapeDtypeStruct((1, width), F32),
            jax.ShapeDtypeStruct((width, 2 * third), BF16),
            jax.ShapeDtypeStruct((width, third), BF16),
        ]
        + push_outs(parts, outer),
        in_specs=[VMEM, VMEM, VMEM, VMEM, ANY, ANY, ANY, ANY] + [ANY] * count,
        out_specs=[VMEM, VMEM, VMEM, VMEM] + [ANY] * count,
        scratch_shapes=[
            pltpu.VMEM(w_in.shape, BF16),
            pltpu.VMEM(w_down.shape, BF16),
            pltpu.VMEM((outer, 4, rows, width), BF16),
            pltpu.VMEM((outer, 4, rows, width), BF16),
            pltpu.VMEM((outer, 2, 2 * rows, 2 * third), BF16),
            pltpu.VMEM((outer, 2, 2 * rows, 2 * third), BF16),
            pltpu.VMEM((outer, 2, 2 * rows, third), BF16),
            pltpu.VMEM((width, outer * 4 * rows), BF16),
            pltpu.VMEM((outer, 2, 2, rows, width), BF16),
        ]
        + scatter_room(outer, rows, width)
        + gather_sems(outer)
        + scatter_sems(outer)
        + [dma((3,)), dma((outer,))]
        + (push_scratch(parts, outer, inner) if count else []),
        compiler_params=pltpu.CompilerParams(
            collective_id=ident, has_side_effects=True, vmem_limit_bytes=63 << 20
        ),
        name="ffn_backward",
    )(grad_y, resid, gain, mix, w_in, w_down, b, both, *parts)


def swap_halves(values):
    width = values.shape[1]
    lane = lax.broadcasted_iota(jnp.int32, values.shape, 1)
    low = lax.rem(lane, HD) < HD // 2
    return jnp.where(
        low, pltpu.roll(values, width - HD // 2, 1), pltpu.roll(values, HD // 2, 1)
    )


def allowed_rows(marks, spot, top):
    del top
    return (spot >= marks[:, 1:2]) & (spot <= marks[:, 0:1])


def attn_forward_kernel(outer, inner, count, *refs):
    dp = outer * inner
    cut = Cut(refs)
    x_in, gain, weight, tables, marks, spot = cut(6)
    owns = cut(count)
    out, a_out, qk_out, v_out, lse_out, att_out = cut(6)
    fetched = cut(count)
    w, a, qk, v, att, part = cut(6)
    room, take_sems, give_sems = cut(5), cut(6), cut(6)
    load_sem, keep_sem = cut(2)
    extra = Fetch(outer, inner, owns, fetched, cut(count), cut(5))
    turns = extra.turns()
    rows, width = x_in.shape
    heads_width = w.shape[1] // 4
    heads = heads_width // HD
    load = pltpu.make_async_copy(weight, w, load_sem)
    load.start()
    take = Gather(1, dp, a, take_sems)
    give = Scatter(1, dp, part, room, give_sems)
    x = x_in[...]
    inverse = lax.rsqrt(jnp.mean(x * x, axis=-1, keepdims=True) + EPSILON)
    a[0, take.t] = (x * inverse * gain[...]).astype(BF16)
    meet(take.friends() + extra.zdev[1:] + extra.xdev)
    take.start()
    extra.start()
    load.wait()

    def project(block):
        both = dot(a[0, block], w[:, : 3 * heads_width])
        raw = both[:, : 2 * heads_width]
        times = 2 * heads_width // tables.shape[-1]
        cosine = jnp.concatenate([tables[0, block]] * times, axis=1)
        sine = jnp.concatenate([tables[1, block]] * times, axis=1)
        qk[block] = (raw * cosine + swap_halves(raw) * sine).astype(BF16)
        v[block] = both[:, 2 * heads_width :].astype(BF16)

    project(take.t)
    take.complete(0)
    for other in range(1, 4):
        project(lax.rem(take.t + other, 4))
    keeps = [pltpu.make_async_copy(a.at[0], a_out, keep_sem.at[0])]
    keeps.append(pltpu.make_async_copy(qk, qk_out, keep_sem.at[1]))
    keeps.append(pltpu.make_async_copy(v, v_out, keep_sem.at[2]))
    for keep in keeps:
        keep.start()

    def attend(block):
        keys = qk[...].reshape(4 * rows, 2 * heads_width)
        values = v[...].reshape(4 * rows, heads_width)
        allowed = allowed_rows(marks[block], spot[...], 0)
        pieces = []
        for head in range(heads):
            here = slice(head * HD, (head + 1) * HD)
            there = slice(heads_width + head * HD, heads_width + (head + 1) * HD)
            scores = dot_nt(qk[block, :, here], keys[:, there])
            scores = jnp.where(allowed, scores * HD ** (-0.5), MASKED_SCORE)
            top = jnp.max(scores, axis=-1, keepdims=True)
            expo = jnp.exp(scores - top)
            total = jnp.sum(expo, axis=-1, keepdims=True)
            probs = (expo / total).astype(BF16)
            lse_out[block, :, head : head + 1] = top + jnp.log(total)
            pieces.append(dot(probs, values[:, here]).astype(BF16))
        att[block] = jnp.concatenate(pieces, axis=1)
        sent = dot_nt(att[block], w[:, 3 * heads_width :]).astype(BF16)
        part[0, lax.div(block, 2), lax.rem(block, 2)] = sent

    y, c = give.y, give.c
    extra.settle()
    attend(2 * (1 - y) + 1 - c)
    attend(2 * y + 1 - c)
    give.core_send(0)
    turns[0]()
    attend(2 * (1 - y) + c)
    attend(2 * y + c)
    give.pair_send(0)
    for turn in turns[1:]:
        turn()
    keeps.append(pltpu.make_async_copy(att, att_out, keep_sem.at[3]))
    keeps[-1].start()
    out[...] = x_in[...] + give.outer_send(0)
    take.finish()
    give.finish()
    extra.finish()
    for keep in keeps:
        keep.wait()


def attn_forward(x, gain, weight, tables, marks, spot, owns, outer, inner, ident):
    count = len(owns)
    dma = pltpu.SemaphoreType.DMA
    rows, width = x.shape
    slim = weight.shape[1] // 4
    kept = [(4, rows, width), (4, rows, 2 * slim), (4, rows, slim)]
    return pl.pallas_call(
        functools.partial(attn_forward_kernel, outer, inner, count),
        out_shape=[jax.ShapeDtypeStruct((rows, width), F32)]
        + [jax.ShapeDtypeStruct(shape, BF16) for shape in kept]
        + [
            jax.ShapeDtypeStruct((4, rows, 8), F32),
            jax.ShapeDtypeStruct((4, rows, slim), BF16),
        ]
        + fetch_outs(owns, outer * inner),
        in_specs=[VMEM, VMEM, ANY, VMEM, VMEM, VMEM] + [ANY] * count,
        out_specs=[VMEM, ANY, ANY, ANY, VMEM, ANY] + [ANY] * count,
        scratch_shapes=[
            pltpu.VMEM(weight.shape, BF16),
            pltpu.VMEM((1, 4, rows, width), BF16),
            pltpu.VMEM(kept[1], BF16),
            pltpu.VMEM(kept[2], BF16),
            pltpu.VMEM(kept[2], BF16),
            pltpu.VMEM((1, 2, 2, rows, width), BF16),
        ]
        + scatter_room(1, rows, width)
        + gather_sems(1)
        + scatter_sems(1)
        + [dma, dma((4,))]
        + fetch_scratch(owns, outer, inner),
        compiler_params=pltpu.CompilerParams(collective_id=ident, has_side_effects=True),
        name="attn_forward",
    )(x, gain, weight, tables, marks, spot, *owns)


def attn_backward_kernel(outer, inner, count, *refs):
    dp = outer * inner
    cut = Cut(refs)
    grad_in, x_in, gain, weight, tables, marks, spot = cut(7)
    a_in, qk_in, v_in, lse, att_in = cut(5)
    parts = cut(count)
    out, gain_out, grad_w = cut(3)
    pushed = cut(count)
    w, a, qk, v, att, ga, g_att, raw, part = cut(9)
    room, take_sems, give_sems = cut(5), cut(6), cut(6)
    (load_sem,) = cut(1)
    extra = Push(outer, inner, parts, pushed, cut(3 * count), cut(6))
    turns = extra.turns()
    rows, width = x_in.shape
    tall = 4 * rows
    heads_width = w.shape[1] // 4
    heads = heads_width // HD
    loads = [
        pltpu.make_async_copy(source, target, load_sem.at[i])
        for i, (source, target) in enumerate(
            ((weight, w), (qk_in, qk), (v_in, v), (att_in, att), (a_in, a))
        )
    ]
    for load in loads:
        load.start()
    take = Gather(1, dp, ga, take_sems)
    give = Scatter(1, dp, part, room, give_sems)
    ga[0, take.t] = grad_in[...].astype(BF16)
    meet(take.friends() + extra.zdev[:-1] + extra.xdev)
    take.start()
    extra.start()
    for load in loads:
        load.wait()
    take.complete(0)
    turns[0]()
    grads = ga[...].reshape(tall, width)
    g_att[...] = dot(grads, w[:, 3 * heads_width :]).astype(BF16)
    all_qk = qk[...].reshape(tall, 2 * heads_width)
    all_v = v[...].reshape(tall, heads_width)
    all_marks = marks[...].reshape(tall, marks.shape[-1])
    all_lse = lse[...].reshape(tall, lse.shape[-1])
    allowed = allowed_rows(all_marks, spot[...], 0)
    q_grads, k_grads, v_grads = [], [], []
    for head in range(heads):
        here = slice(head * HD, (head + 1) * HD)
        there = slice(heads_width + head * HD, heads_width + (head + 1) * HD)
        query, key = all_qk[:, here], all_qk[:, there]
        scores = dot_nt(query, key)
        scores = jnp.where(allowed, scores * HD ** (-0.5), MASKED_SCORE)
        probs = jnp.exp(scores - all_lse[:, head : head + 1])
        grad_probs = dot_nt(g_att[:, here], all_v[:, here])
        inner = jnp.sum(grad_probs * probs, axis=-1, keepdims=True)
        grad_scores = (probs * (grad_probs - inner)).astype(BF16)
        v_grads.append(dot_tn(probs.astype(BF16), g_att[:, here]).astype(BF16))
        q_grads.append(dot(grad_scores, key))
        k_grads.append(dot_tn(grad_scores, query))
    rotated = jnp.concatenate(q_grads + k_grads, axis=1) * HD ** (-0.5)
    times = 2 * heads_width // tables.shape[-1]
    cosine = jnp.concatenate([tables[0].reshape(tall, -1)] * times, axis=1)
    sine = jnp.concatenate([tables[1].reshape(tall, -1)] * times, axis=1)
    raw[:, : 2 * heads_width] = (rotated * cosine - swap_halves(rotated) * sine).astype(BF16)
    raw[:, 2 * heads_width :] = jnp.concatenate(v_grads, axis=1)
    def back(block):
        at = pl.ds(pl.multiple_of(block * rows, rows), rows)
        sent = dot_nt(raw[at, :], w[:, : 3 * heads_width]).astype(BF16)
        part[0, lax.div(block, 2), lax.rem(block, 2)] = sent

    turns[1]()
    y, c = give.y, give.c
    back(2 * (1 - y) + 1 - c)
    back(2 * y + 1 - c)
    give.core_send(0)
    back(2 * (1 - y) + c)
    back(2 * y + c)
    give.pair_send(0)
    turns[2]()
    grad_w[:, : 3 * heads_width] = dot_tn(a[...].reshape(tall, width), raw[...]).astype(BF16)
    grad_w[:, 3 * heads_width :] = dot_tn(grads, att[...].reshape(tall, heads_width)).astype(
        BF16
    )
    grad_a = give.outer_send(0)
    x = x_in[...]
    inverse = lax.rsqrt(jnp.mean(x * x, axis=-1, keepdims=True) + EPSILON)
    unit = x * inverse
    gain_out[...] = jnp.sum(grad_a * unit, axis=0, keepdims=True)
    out[...] = grad_in[...] + norm_back(grad_a, gain[...], unit, inverse)
    for turn in turns[3:]:
        turn()
    take.finish()
    give.finish()
    extra.finish()


def attn_backward(grad, x, gain, weight, tables, marks, spot, kept, parts, outer, inner, ident):
    count = len(parts)
    dma = pltpu.SemaphoreType.DMA
    rows, width = x.shape
    slim = weight.shape[1] // 4
    return pl.pallas_call(
        functools.partial(attn_backward_kernel, outer, inner, count),
        out_shape=[
            jax.ShapeDtypeStruct((rows, width), F32),
            jax.ShapeDtypeStruct((1, width), F32),
            jax.ShapeDtypeStruct(weight.shape, BF16),
        ]
        + push_outs(parts, outer),
        in_specs=[VMEM, VMEM, VMEM, ANY, VMEM, VMEM, VMEM, ANY, ANY, ANY, VMEM, ANY]
        + [ANY] * count,
        out_specs=[VMEM, VMEM, VMEM] + [ANY] * count,
        scratch_shapes=[
            pltpu.VMEM(weight.shape, BF16),
            pltpu.VMEM((4, rows, width), BF16),
            pltpu.VMEM((4, rows, 2 * slim), BF16),
            pltpu.VMEM((4, rows, slim), BF16),
            pltpu.VMEM((4, rows, slim), BF16),
            pltpu.VMEM((1, 4, rows, width), BF16),
            pltpu.VMEM((4 * rows, slim), BF16),
            pltpu.VMEM((4 * rows, 3 * slim), BF16),
            pltpu.VMEM((1, 2, 2, rows, width), BF16),
        ]
        + scatter_room(1, rows, width)
        + gather_sems(1)
        + scatter_sems(1)
        + [dma((5,))]
        + push_scratch(parts, outer, inner),
        compiler_params=pltpu.CompilerParams(
            collective_id=ident, has_side_effects=True, vmem_limit_bytes=62 << 20
        ),
        name="attn_backward",
    )(grad, x, gain, weight, tables, marks, spot, *kept, *parts)


def layout(place_row, length_row):
    ends = jnp.cumsum(length_row, dtype=jnp.int32)
    after = place_row[:, None] >= ends[None, :]
    begins = jnp.sum(jnp.where(after, length_row[None, :], 0), axis=1, dtype=jnp.int32)
    return place_row - begins


def rope_tables(position):
    half_width = HD // 2
    freqs = 10000.0 ** (-jnp.arange(half_width, dtype=F32) / half_width)
    angles = position.astype(F32)[:, None] * freqs[None, :]
    cosine, sine = jnp.cos(angles), jnp.sin(angles)
    return jnp.stack(
        [
            jnp.concatenate([cosine] * 4, axis=1),
            jnp.concatenate([-sine, sine, -sine, sine], axis=1),
        ]
    )


def norm_back(grad_normed, gain_row, unit_rows, inverse):
    scaled = grad_normed * gain_row
    return inverse * (scaled - unit_rows * jnp.mean(scaled * unit_rows, axis=-1, keepdims=True))


def dot(left, right):
    return jnp.dot(left, right, preferred_element_type=F32)


def dot_nt(left, right):
    return lax.dot_general(left, right, (((1,), (1,)), ((), ())), preferred_element_type=F32)


def dot_tn(left, right):
    return lax.dot_general(left, right, (((0,), (0,)), ((), ())), preferred_element_type=F32)


def make_body(dp):
    outer, inner = split_dp(dp)

    def body(
        tokens,
        place,
        lengths,
        expert_ids,
        gate_values,
        cotangent,
        gain_attn,
        w_query,
        w_key,
        w_value,
        w_out,
        gain_ffn,
        exp_gate,
        exp_up,
        exp_down,
        dense_gate,
        dense_up,
        dense_down,
    ):
        layers, experts, rows, full = exp_gate.shape
        width = tokens.shape[1]
        slim = full // outer
        count = place.shape[1]
        position = layout(place[0], lengths[0])
        place_row = place[0].astype(F32)
        marks = jnp.stack([place_row, place_row - position.astype(F32)] * 4, axis=1)
        marks = marks.reshape(4, count // 4, 8)
        spot = place_row[None]
        tables = rope_tables(position).reshape(2, 4, count // 4, 128)

        slots = expert_ids[:, None] == jnp.arange(experts, dtype=jnp.int32)[None, :, None, None]
        mix_own = jnp.sum(jnp.where(slots, gate_values[:, None], 0.0), axis=-1)
        gains_own = jnp.pad(
            jnp.concatenate([gain_attn, gain_ffn], axis=0).astype(BF16).astype(F32),
            ((0, 8 - 2 * layers), (0, count - rows)),
        )
        small_own = jnp.concatenate([mix_own.reshape(-1, count), gains_own], axis=0)

        attn_own, ffn_own = [], []
        for level in range(layers):
            attn_own.append(
                jnp.concatenate(
                    [w_query[level], w_key[level], w_value[level], jnp.transpose(w_out[level])],
                    axis=1,
                ).astype(BF16)[None]
            )
            mats = (
                [exp_gate[level, e] for e in range(experts)]
                + [dense_gate[level]]
                + [exp_up[level, e] for e in range(experts)]
                + [dense_up[level]]
                + [jnp.transpose(exp_down[level, e]) for e in range(experts)]
                + [jnp.transpose(dense_down[level])]
            )
            mats = [m.astype(BF16) for m in mats]
            kinds = experts + 1
            ffn_own.append(
                [
                    jnp.stack(
                        [
                            jnp.concatenate(
                                [m[:, k * slim : (k + 1) * slim] for m in group], axis=1
                            )
                            for k in range(outer)
                        ]
                    )
                    for group in (mats[: 2 * kinds], mats[2 * kinds :])
                ]
            )
        small_all, first = fetch([small_own[None], attn_own[0]], outer, inner, 4)
        w_attn = [first.reshape(width, -1)]
        w_ffn = []

        gains = jnp.transpose(small_all[:, layers * experts :, :rows], (1, 0, 2)).reshape(8, width)
        dx = lax.rem(lax.axis_index("dp"), inner)
        mix_all = lax.dynamic_index_in_dim(
            small_all[:, : layers * experts].reshape(outer, inner, layers, experts, count),
            dx,
            axis=1,
            keepdims=False,
        )
        mixing = [
            jnp.transpose(mix_all[:, level], (0, 2, 1)).reshape(outer, 2, count // 2, experts)
            for level in range(layers)
        ]

        state = tokens.astype(F32)
        kept_attn, kept_ffn = [], []
        for level in range(layers):
            before = state
            state, *kept, w_in, w_down = attn_forward(
                before,
                gains[level][None],
                w_attn[level],
                tables,
                marks,
                spot,
                ffn_own[level],
                outer,
                inner,
                0,
            )
            kept_attn.append((before, kept))
            w_ffn.append((w_in.reshape(width, -1), w_down.reshape(width, -1)))
            resid = state
            more = [attn_own[level + 1]] if level + 1 < layers else []
            state, b_in, both, *fetched = ffn_forward(
                resid,
                gains[layers + level][None],
                mixing[level],
                *w_ffn[level],
                more,
                outer,
                inner,
                2 if more else 5,
            )
            w_attn += [block.reshape(width, -1) for block in fetched]
            kept_ffn.append((resid, b_in, both))
        mixed = state.astype(BF16)

        grad = cotangent.astype(F32)
        part_gains = [None] * (2 * layers)
        pushed_ffn, pushed_attn = [None] * layers, [None] * layers
        grad_attn = None
        for level in reversed(range(layers)):
            resid, b_in, both = kept_ffn[level]
            more = [] if grad_attn is None else [grad_attn.reshape(dp, rows, -1)]
            grad, part_gain, grad_in, grad_down, *moved = ffn_backward(
                grad,
                resid,
                gains[layers + level][None],
                mixing[level],
                *w_ffn[level],
                b_in,
                both,
                more,
                outer,
                inner,
                3 if more else 6,
            )
            part_gains[layers + level] = part_gain[0]
            if more:
                pushed_attn[level + 1] = moved[0]
            before, kept = kept_attn[level]
            grad, part_gain, grad_attn, *pushed_ffn[level] = attn_backward(
                grad,
                before,
                gains[level][None],
                w_attn[level],
                tables,
                marks,
                spot,
                kept,
                [grad_in.reshape(dp, rows, -1), grad_down.reshape(dp, rows, -1)],
                outer,
                inner,
                1,
            )
            part_gains[level] = part_gain[0]
        stacked = jnp.pad(jnp.stack(part_gains), ((0, 8 - 2 * layers), (0, 0)))
        stacked = jnp.transpose(stacked.reshape(8, dp, rows), (1, 0, 2))
        pushed_attn[0], gain_parts = push(
            [grad_attn.reshape(dp, rows, -1), stacked], outer, inner, 7
        )

        gain_part = jnp.sum(gain_parts, axis=0)
        gain_sum = jnp.sum(
            gather(jnp.pad(gain_part, ((0, 0), (0, 128 - rows))), dp, 8)[0], axis=0
        )
        grad_gain_attn = gain_sum[:layers, :rows]
        grad_gain_ffn = gain_sum[layers : 2 * layers, :rows]

        kinds = experts + 1
        ups, downs, attns = [], [], []
        for level in range(layers):
            in_part, down_part = pushed_ffn[level]
            attn_part = pushed_attn[level]
            ups.append(
                jnp.concatenate(
                    [
                        jnp.stack(
                            [
                                in_part[k][:, m * slim : (m + 1) * slim]
                                for m in range(2 * kinds)
                            ]
                        )
                        for k in range(outer)
                    ],
                    axis=2,
                )
            )
            downs.append(
                jnp.concatenate(
                    [
                        jnp.stack(
                            [
                                jnp.transpose(down_part[k][:, m * slim : (m + 1) * slim])
                                for m in range(kinds)
                            ]
                        )
                        for k in range(outer)
                    ],
                    axis=1,
                )
            )
            attns.append(jnp.sum(attn_part.astype(F32), axis=0))
        up = jnp.stack(ups).astype(F32)
        down = jnp.stack(downs).astype(F32)
        attn = jnp.stack(attns)
        quarter = attn.shape[-1] // 4
        return (
            mixed,
            grad,
            grad_gain_attn,
            attn[:, :, :quarter],
            attn[:, :, quarter : 2 * quarter],
            attn[:, :, 2 * quarter : 3 * quarter],
            jnp.swapaxes(attn[:, :, 3 * quarter :], 1, 2),
            grad_gain_ffn,
            up[:, :experts],
            up[:, kinds : kinds + experts],
            down[:, :experts],
            up[:, experts],
            up[:, kinds + experts],
            down[:, experts],
        )

    return body


def solution(mesh):
    return jax.shard_map(
        make_body(mesh.shape["dp"]),
        mesh=mesh,
        in_specs=(
            P(("dp", "tensor"), None),
            P("dp", None),
            P("dp", None),
            P(None, "dp", None),
            P(None, "dp", None),
            P(("dp", "tensor"), None),
            P(None, "dp"),
            P(None, "dp", "tensor"),
            P(None, "dp", "tensor"),
            P(None, "dp", "tensor"),
            P(None, "tensor", "dp"),
            P(None, "dp"),
            P(None, None, "dp", "tensor"),
            P(None, None, "dp", "tensor"),
            P(None, None, "tensor", "dp"),
            P(None, "dp", "tensor"),
            P(None, "dp", "tensor"),
            P(None, "tensor", "dp"),
        ),
        out_specs=(
            P(("dp", "tensor"), None),
            P(("dp", "tensor"), None),
            P(None, "dp"),
            P(None, "dp", "tensor"),
            P(None, "dp", "tensor"),
            P(None, "dp", "tensor"),
            P(None, "tensor", "dp"),
            P(None, "dp"),
            P(None, None, "dp", "tensor"),
            P(None, None, "dp", "tensor"),
            P(None, None, "tensor", "dp"),
            P(None, "dp", "tensor"),
            P(None, "dp", "tensor"),
            P(None, "tensor", "dp"),
        ),
        check_vma=False,
    )
```

```python
import functools

import jax
import jax.numpy as jnp
from jax import lax
from jax.experimental import pallas as pl
from jax.experimental.pallas import tpu as pltpu
from jax.sharding import PartitionSpec as P

HD = 64
EPSILON = 1e-06
MASKED_SCORE = -1e30
MESH = pl.DeviceIdType.MESH
ANY = pl.BlockSpec(memory_space=pl.ANY)
VMEM = pl.BlockSpec(memory_space=pltpu.VMEM)
F32 = jnp.float32
BF16 = jnp.bfloat16
PARTS = 2


def split_dp(dp):
    inner = 2 ** ((dp.bit_length() - 1) // 2)
    return dp // inner, inner


def place_of(inner):
    d = lax.axis_index("dp")
    return lax.div(d, inner), lax.rem(d, inner), lax.axis_index("tensor")


def across(t):
    return lax.rem(t + 2, 4), t + 1 - 2 * lax.rem(t, 2)


def meet(devices):
    barrier = pltpu.get_barrier_semaphore()
    for device in devices:
        pl.semaphore_signal(barrier, inc=1, device_id=device, device_id_type=MESH)
    pl.semaphore_wait(barrier, len(devices))


def send(source, target, send_sem, recv_sem, device):
    copy = pltpu.make_async_remote_copy(
        src_ref=source,
        dst_ref=target,
        send_sem=send_sem,
        recv_sem=recv_sem,
        device_id=device,
        device_id_type=MESH,
    )
    copy.start()
    return copy


def gather_kernel(dp, own, out, *sems):
    take = Gather(1, dp, out, sems)
    out[0, take.t] = own[...]
    meet(take.friends())
    take.start()
    take.complete(0)
    take.finish()


def gather(own, dp, ident):
    return pl.pallas_call(
        functools.partial(gather_kernel, dp),
        out_shape=jax.ShapeDtypeStruct((1, 4) + own.shape, own.dtype),
        in_specs=[VMEM],
        out_specs=VMEM,
        scratch_shapes=gather_sems(1),
        compiler_params=pltpu.CompilerParams(collective_id=ident, has_side_effects=True),
        name="gather",
    )(own)


def fetch_kernel(outer, inner, count, *refs):
    cut = Cut(refs)
    extra = Fetch(outer, inner, cut(count), cut(count), cut(count), cut(5))
    meet(extra.zdev[1:] + extra.xdev)
    extra.start()
    extra.settle()
    for turn in extra.turns():
        turn()
    extra.finish()


def fetch(owns, outer, inner, ident):
    count = len(owns)
    return pl.pallas_call(
        functools.partial(fetch_kernel, outer, inner, count),
        out_shape=fetch_outs(owns, outer * inner),
        in_specs=[ANY] * count,
        out_specs=[ANY] * count,
        scratch_shapes=fetch_scratch(owns, outer, inner),
        compiler_params=pltpu.CompilerParams(collective_id=ident, has_side_effects=True),
        name="fetch",
    )(*owns)


def push_kernel(outer, inner, count, *refs):
    cut = Cut(refs)
    extra = Push(outer, inner, cut(count), cut(count), cut(3 * count), cut(6))
    meet(extra.zdev[:-1] + extra.xdev)
    extra.start()
    for turn in extra.turns():
        turn()
    extra.finish()


def push(parts, outer, inner, ident):
    count = len(parts)
    return pl.pallas_call(
        functools.partial(push_kernel, outer, inner, count),
        out_shape=push_outs(parts, outer),
        in_specs=[ANY] * count,
        out_specs=[ANY] * count,
        scratch_shapes=push_scratch(parts, outer, inner),
        compiler_params=pltpu.CompilerParams(collective_id=ident, has_side_effects=True),
        name="push",
    )(*parts)


def nearest(index, size, step):
    table = [sorted(range(size), key=lambda other: (abs(other - at), other)) for at in range(size)]
    found = 0
    for at in range(size):
        found = found + jnp.where(index == at, table[at][step], 0)
    return found


class Gather:
    def __init__(self, outer, inner, table, sems, parts=1):
        self.outer, self.inner, self.table, self.parts = outer, inner, table, parts
        self.zs, self.zr, self.ys, self.yr, self.cs, self.cr = sems
        self.dz, self.dx, self.t = place_of(inner)
        self.d = lax.axis_index("dp")
        self.size = table.shape[2] // parts
        ty, tc = across(self.t)
        self.ty = ty
        self.pair, self.core = (self.d, ty), (self.d, tc)
        self.source = [nearest(self.dz, outer, step) for step in range(outer)]
        self.zdev = [(source * inner + self.dx, self.t) for source in self.source]
        self.steps = outer * parts
        self.yc, self.cc, self.dc = [], [], []

    def friends(self):
        return self.zdev[1:] + [self.pair, self.core]

    def rows(self, step):
        return pl.ds(step % self.parts * self.size, self.size)

    def origin(self, step):
        return self.source[step // self.parts]

    def outward(self, step, target, sent):
        at = self.origin(step) * self.parts + step % self.parts
        block = self.table.at[self.origin(step), self.t, self.rows(step)]
        target = jnp.minimum(jnp.maximum(target, 0), self.outer - 1)
        return pltpu.make_async_remote_copy(
            src_ref=block,
            dst_ref=block,
            send_sem=self.zs.at[at if sent is None else sent],
            recv_sem=self.zr.at[at],
            device_id=(target * self.inner + self.dx, self.t),
            device_id_type=MESH,
        )

    def passes(self, step):
        if self.outer == 1:
            return []
        if step < self.parts:
            last = self.steps + step
            return [
                (self.dz < self.outer - 1, self.outward(step, self.dz + 1, None)),
                (self.dz > 0, self.outward(step, self.dz - 1, last)),
            ]
        ahead = jnp.where(self.origin(step) < self.dz, self.dz + 1, self.dz - 1)
        inside = (ahead >= 0) & (ahead < self.outer)
        return [(inside, self.outward(step, ahead, None))]

    def start(self):
        for step in range(self.parts):
            for inside, copy in self.passes(step):
                pl.when(inside)(copy.start)
        for step in range(self.parts):
            self.forward(step)

    def arrive(self, step):
        self.outward(step, self.dz, None).wait_recv()
        for inside, copy in self.passes(step):
            pl.when(inside)(copy.start)
        self.forward(step)

    def forward(self, step):
        block = self.table.at[self.origin(step), self.t, self.rows(step)]
        self.yc.append(send(block, block, self.ys.at[step], self.yr.at[step], self.pair))
        self.cc.append(send(block, block, self.cs.at[step], self.cr.at[step], self.core))

    def complete(self, step):
        self.yc[step].wait_recv()
        at = self.steps + step
        block = self.table.at[self.origin(step), self.ty, self.rows(step)]
        self.dc.append(send(block, block, self.cs.at[at], self.cr.at[at], self.core))
        self.cc[step].wait_recv()
        self.dc[step].wait_recv()

    def finish(self):
        for step in range(self.steps):
            for inside, copy in self.passes(step):
                pl.when(inside)(copy.wait_send)
        for copy in self.yc + self.cc + self.dc:
            copy.wait_send()


class Scatter:
    def __init__(self, outer, inner, part, room, sems, parts=1):
        self.outer, self.part, self.parts = outer, part, parts
        self.from_c, self.sum_c, self.from_y, self.sum_y, self.from_z = room
        self.cs, self.cr, self.ys, self.yr, self.zs, self.zr = sems
        dz, dx, t = place_of(inner)
        d = lax.axis_index("dp")
        ty, tc = across(t)
        self.size = part.shape[3] // parts
        self.dz, self.y, self.c = dz, lax.div(t, 2), lax.rem(t, 2)
        self.pair, self.core = (d, ty), (d, tc)
        self.source = [nearest(dz, outer, step) for step in range(outer)]
        self.zdev = [(source * inner + dx, t) for source in self.source]
        self.steps = outer * parts
        self.cc, self.yc, self.zc = {}, {}, {}

    def rows(self, step):
        return pl.ds(step % self.parts * self.size, self.size)

    def core_send(self, step):
        source = self.source[step // self.parts]
        self.cc[step] = send(
            self.part.at[source, :, 1 - self.c, self.rows(step)],
            self.from_c.at[step],
            self.cs.at[step],
            self.cr.at[step],
            self.core,
        )

    def pair_send(self, step):
        source = self.source[step // self.parts]
        self.cc[step].wait_recv()
        mine = self.part[source, :, self.c, self.rows(step)].astype(F32)
        self.sum_c[step] = (mine + self.from_c[step].astype(F32)).astype(BF16)
        self.yc[step] = send(
            self.sum_c.at[step, 1 - self.y],
            self.from_y.at[step],
            self.ys.at[step],
            self.yr.at[step],
            self.pair,
        )

    def summed(self, step):
        self.yc[step].wait_recv()
        return self.sum_c[step, self.y].astype(F32) + self.from_y[step].astype(F32)

    def outward(self, step, source, away):
        at = (away - 1) * self.parts + step % self.parts
        return pltpu.make_async_remote_copy(
            src_ref=source,
            dst_ref=self.from_z.at[at],
            send_sem=self.zs.at[at],
            recv_sem=self.zr.at[at],
            device_id=self.zdev[step // self.parts],
            device_id_type=MESH,
        )

    def outer_send(self, step):
        self.sum_y[step] = self.summed(step).astype(BF16)
        away = lax.rem(self.source[step // self.parts] - self.dz + self.outer, self.outer)
        self.zc[step] = self.outward(step, self.sum_y.at[step], away)
        self.zc[step].start()

    def total(self):
        pieces = []
        for piece in range(self.parts):
            total = self.summed(piece)
            for step in range(self.parts + piece, self.steps, self.parts):
                away = lax.rem(self.dz - self.source[step // self.parts] + self.outer, self.outer)
                self.outward(step, self.sum_y.at[step], away).wait_recv()
                at = (away - 1) * self.parts + piece
                total = total + self.from_z[at].astype(F32)
            pieces.append(total)
        return pieces[0] if self.parts == 1 else jnp.concatenate(pieces, axis=0)

    def finish(self):
        for group in (self.cc, self.yc, self.zc):
            for step in group:
                group[step].wait_send()


def gather_sems(outer, parts=1):
    dma = pltpu.SemaphoreType.DMA
    steps = outer * parts
    return [dma((steps + parts,))] + [dma((steps,)) for _ in range(3)] + [dma((2 * steps,))] * 2


def scatter_sems(outer, parts=1):
    dma = pltpu.SemaphoreType.DMA
    return [dma((outer * parts,)) for _ in range(6)]


def scatter_room(outer, rows, width, parts=1):
    steps, size = outer * parts, rows // parts
    return [
        pltpu.VMEM((steps, 2, size, width), BF16),
        pltpu.VMEM((steps, 2, size, width), BF16),
        pltpu.VMEM((steps, size, width), BF16),
        pltpu.VMEM((steps, size, width), BF16),
        pltpu.VMEM((max(steps - parts, 1), size, width), BF16),
    ]


def pipeline(take, give, compute, begin, middle, late):
    steps, parts = take.steps, take.parts
    middle, late = list(middle), list(late)
    lag = parts + 1
    take.start()
    begin()
    for step in range(steps):
        if step + parts < steps:
            take.arrive(step + parts)
        take.complete(step)
        compute(step)
        give.core_send(step)
        if step:
            give.pair_send(step - 1)
        if step - lag >= parts:
            give.outer_send(step - lag)
        if step > steps // 2 and middle:
            middle.pop(0)()
    sent = max(parts, steps - lag)
    late = middle + late
    share = max(1, (len(late) + lag) // (lag + 1))
    give.pair_send(steps - 1)
    for step in range(sent, steps):
        for _ in range(share):
            if late:
                late.pop(0)()
        give.outer_send(step)
    for work in late:
        work()


class Fetch:
    def __init__(self, outer, inner, owns, outs, holds, sems):
        self.outer, self.inner, self.owns, self.outs, self.holds = outer, inner, owns, outs, holds
        self.zs, self.zr, self.xs, self.xr, self.ls = sems
        self.dz, dx, t = place_of(inner)
        self.dx, self.d = dx, lax.axis_index("dp")
        self.source = [nearest(self.dz, outer, step) for step in range(outer)]
        self.zdev = [(source * inner + dx, t) for source in self.source]
        self.xdev = [(self.dz * inner + lax.rem(dx + j, inner), t) for j in range(1, inner)]
        self.zc, self.xc, self.into, self.back = [], {}, [], []

    def own(self, i, where):
        return self.owns[i].at[where if self.owns[i].shape[0] == self.outer else 0]

    def copy(self, i, step):
        away = lax.rem(self.source[step] - self.dz + self.outer, self.outer)
        at = i * self.outer + away
        return pltpu.make_async_remote_copy(
            src_ref=self.own(i, self.source[step]),
            dst_ref=self.outs[i].at[self.d],
            send_sem=self.zs.at[at],
            recv_sem=self.zr.at[at],
            device_id=self.zdev[step],
            device_id_type=MESH,
        )

    def start(self):
        for i in range(len(self.owns)):
            here = self.own(i, self.dz)
            self.into.append(pltpu.make_async_copy(here, self.holds[i], self.ls.at[i]))
            self.into[i].start()
            for step in range(1, self.outer):
                self.zc.append(self.copy(i, step))
                self.zc[-1].start()
            self.spread(i, 0, here, self.outs[i].at[self.d])

    def spread(self, i, step, block, target):
        for j in range(1, self.inner):
            at = (i * self.outer + step) * self.inner + j
            self.xc[i, step, j] = send(
                block, target, self.xs.at[at], self.xr.at[at], self.xdev[j - 1]
            )

    def settle(self):
        for i, into in enumerate(self.into):
            into.wait()
            self.back.append(
                pltpu.make_async_copy(self.holds[i], self.outs[i].at[self.d], self.ls.at[i])
            )
            self.back[i].start()

    def turn(self, i, step):
        source = self.source[step]
        block = self.outs[i].at[source * self.inner + self.dx]
        away = lax.rem(self.dz - source + self.outer, self.outer)
        at = i * self.outer + away
        pltpu.make_async_remote_copy(
            src_ref=block,
            dst_ref=block,
            send_sem=self.zs.at[at],
            recv_sem=self.zr.at[at],
            device_id=self.zdev[step],
            device_id_type=MESH,
        ).wait_recv()
        self.spread(i, step, block, block)

    def turns(self, first=0, last=None):
        return [
            functools.partial(self.turn, i, step)
            for i in range(first, len(self.owns) if last is None else last)
            for step in range(1, self.outer)
        ]

    def land(self, i):
        for key in self.xc:
            if key[0] == i:
                self.xc[key].wait_recv()
        self.back[i].wait()

    def finish(self, first=0):
        for key in self.xc:
            if key[0] >= first:
                self.xc[key].wait_recv()
            self.xc[key].wait_send()
        for copy in self.zc:
            copy.wait_send()
        for copy in self.back[first:]:
            copy.wait()


def fetch_outs(owns, dp):
    return [jax.ShapeDtypeStruct((dp,) + own.shape[1:], own.dtype) for own in owns]


def fetch_scratch(owns, outer, inner):
    dma = pltpu.SemaphoreType.DMA
    count = max(len(owns), 1)
    return [pltpu.VMEM(own.shape[1:], own.dtype) for own in owns] + [
        dma((count * outer,)),
        dma((count * outer,)),
        dma((count * outer * inner,)),
        dma((count * outer * inner,)),
        dma((count,)),
    ]


class Push:
    def __init__(self, outer, inner, parts, outs, room, sems):
        count = len(parts)
        self.outer, self.inner, self.parts, self.outs = outer, inner, parts, outs
        self.froms, self.mine, self.sums = room[:count], room[count : 2 * count], room[2 * count :]
        self.xs, self.xr, self.zs, self.zr, self.ls, self.ks = sems
        self.dz, dx, t = place_of(inner)
        self.dx = dx
        near = [nearest(self.dz, outer, step) for step in range(outer)]
        self.source = near[:0:-1] + near[:1]
        self.zdev = [(source * inner + dx, t) for source in self.source]
        self.xdev = [(self.dz * inner + lax.rem(dx + j, inner), t) for j in range(1, inner)]
        self.xc, self.zc, self.loads, self.keeps = {}, [], {}, []

    def start(self, first=0, last=None):
        for i in range(first, len(self.parts) if last is None else last):
            for step, source in enumerate(self.source):
                for j in range(1, self.inner):
                    slot = source * self.inner + lax.rem(self.dx + j, self.inner)
                    at = (i * self.outer + step) * self.inner + j
                    self.xc[i, step, j] = send(
                        self.parts[i].at[slot],
                        self.froms[i].at[j - 1, step],
                        self.xs.at[at],
                        self.xr.at[at],
                        self.xdev[j - 1],
                    )
                self.loads[i, step] = pltpu.make_async_copy(
                    self.parts[i].at[source * self.inner + self.dx],
                    self.mine[i].at[step],
                    self.ls.at[i * self.outer + step],
                )
                self.loads[i, step].start()

    def turn(self, i, step):
        self.loads[i, step].wait()
        total = self.mine[i][step].astype(F32)
        for j in range(1, self.inner):
            self.xc[i, step, j].wait_recv()
            total = total + self.froms[i][j - 1, step].astype(F32)
        self.sums[i][step] = total.astype(self.sums[i].dtype)
        target = self.outs[i].at[self.dz]
        if step < self.outer - 1:
            away = lax.rem(self.source[step] - self.dz + self.outer, self.outer)
            at = i * self.outer + away
            self.zc.append(
                send(self.sums[i].at[step], target, self.zs.at[at], self.zr.at[at], self.zdev[step])
            )
        else:
            self.keeps.append(
                pltpu.make_async_copy(self.sums[i].at[step], target, self.ks.at[i])
            )
            self.keeps[-1].start()

    def turns(self):
        return [
            functools.partial(self.turn, i, step)
            for i in range(len(self.parts))
            for step in range(self.outer)
        ]

    def finish(self):
        for copy in self.zc:
            copy.wait_recv()
            copy.wait_send()
        for key in self.xc:
            self.xc[key].wait_send()
        for copy in self.keeps:
            copy.wait()


def push_outs(parts, outer):
    return [jax.ShapeDtypeStruct((outer,) + part.shape[1:], part.dtype) for part in parts]


def push_scratch(parts, outer, inner):
    dma = pltpu.SemaphoreType.DMA
    count = max(len(parts), 1)
    across_x = [pltpu.VMEM((inner - 1, outer) + part.shape[1:], part.dtype) for part in parts]
    own = [pltpu.VMEM((outer,) + part.shape[1:], part.dtype) for part in parts]
    return (
        across_x
        + own
        + own
        + [
            dma((count * outer * inner,)),
            dma((count * outer * inner,)),
            dma((count * outer,)),
            dma((count * outer,)),
            dma((count * outer,)),
            dma((count,)),
        ]
    )


class Cut:
    def __init__(self, refs):
        self.refs, self.at = refs, 0

    def __call__(self, count):
        self.at += count
        return self.refs[self.at - count : self.at]


def ffn_forward_kernel(outer, inner, kinds, count, *refs):
    cut = Cut(refs)
    resid, gain, mix, w_in_any, w_down_any = cut(5)
    owns = cut(count)
    out, b_out, gu_out = cut(3)
    fetched = cut(count)
    w_in, w_down, b, gu, part = cut(5)
    room, take_sems, give_sems = cut(5), cut(6), cut(6)
    load_sem, keep_b, keep_gu = cut(3)
    extra = Fetch(outer, inner, owns, fetched, cut(count), cut(5)) if count else None
    rows, width = resid.shape
    third = w_down.shape[1]
    slim = third // kinds
    loads = [
        pltpu.make_async_copy(w_in_any, w_in, load_sem.at[0]),
        pltpu.make_async_copy(w_down_any, w_down, load_sem.at[1]),
    ]
    for load in loads:
        load.start()
    take = Gather(outer, inner, b, take_sems, PARTS)
    give = Scatter(outer, inner, part, room, give_sems, PARTS)
    size = rows // PARTS
    x = resid[...]
    inverse = lax.rsqrt(jnp.mean(x * x, axis=-1, keepdims=True) + EPSILON)
    b[take.dz, take.t] = (x * inverse * gain[...]).astype(BF16)
    meet(take.friends() + (extra.xdev if count else []))
    keeps = []

    def compute(step):
        source, q = take.origin(step), step % PARTS
        here = take.rows(step)
        if step == 0:
            for load in loads:
                load.wait()
        rows_in = b[source, :, here].reshape(4 * size, width)
        scale = mix[source, :, here].reshape(4 * size, kinds - 1)
        both = dot(rows_in, w_in[...])
        gu[source, q] = both.astype(BF16)
        gate, up = both[:, :third], both[:, third:]
        hidden = gate * jax.nn.sigmoid(gate) * up
        pieces = []
        for e in range(kinds):
            piece = hidden[:, e * slim : (e + 1) * slim]
            if e < kinds - 1:
                piece = piece * scale[:, e : e + 1]
            pieces.append(piece.astype(BF16))
        hidden = jnp.concatenate(pieces, axis=1)
        sent = dot_nt(hidden, w_down[...]).astype(BF16)
        part[source, :, :, here] = sent.reshape(2, 2, size, width)
        if q == PARTS - 1:
            at = step // PARTS
            keeps.append(pltpu.make_async_copy(b.at[source], b_out.at[source], keep_b.at[at]))
            keeps.append(pltpu.make_async_copy(gu.at[source], gu_out.at[source], keep_gu.at[at]))
            keeps[-1].start()
            keeps[-2].start()

    def begin():
        if count:
            extra.start()
            extra.settle()

    pipeline(take, give, compute, begin, extra.turns() if count else [], [])
    out[...] = resid[...] + give.total()
    take.finish()
    give.finish()
    if count:
        extra.finish()
    for keep in keeps:
        keep.wait()


def ffn_forward(resid, gain, mix, w_in, w_down, owns, outer, inner, ident):
    dma = pltpu.SemaphoreType.DMA
    rows, width = resid.shape
    third = w_down.shape[1]
    kinds = mix.shape[-1] + 1
    count = len(owns)
    return pl.pallas_call(
        functools.partial(ffn_forward_kernel, outer, inner, kinds, count),
        out_shape=[
            jax.ShapeDtypeStruct((rows, width), F32),
            jax.ShapeDtypeStruct((outer, 4, rows, width), BF16),
            jax.ShapeDtypeStruct((outer, PARTS, 4 * rows // PARTS, 2 * third), BF16),
        ]
        + fetch_outs(owns, outer * inner),
        in_specs=[VMEM, VMEM, VMEM, ANY, ANY] + [ANY] * count,
        out_specs=[VMEM, ANY, ANY] + [ANY] * count,
        scratch_shapes=[
            pltpu.VMEM(w_in.shape, BF16),
            pltpu.VMEM(w_down.shape, BF16),
            pltpu.VMEM((outer, 4, rows, width), BF16),
            pltpu.VMEM((outer, PARTS, 4 * rows // PARTS, 2 * third), BF16),
            pltpu.VMEM((outer, 2, 2, rows, width), BF16),
        ]
        + scatter_room(outer, rows, width, PARTS)
        + gather_sems(outer, PARTS)
        + scatter_sems(outer, PARTS)
        + [dma((2,)), dma((outer,)), dma((outer,))]
        + (fetch_scratch(owns, outer, inner) if count else []),
        compiler_params=pltpu.CompilerParams(
            collective_id=ident, has_side_effects=True, vmem_limit_bytes=62 << 20
        ),
        name="ffn_forward",
    )(resid, gain, mix, w_in, w_down, *owns)


def ffn_backward_kernel(outer, inner, kinds, count, *refs):
    cut = Cut(refs)
    grad_y, resid, gain, mix, w_in_any, w_down_any, b_any, gu_any = cut(8)
    parts = cut(count)
    out, gain_out, grad_in, grad_down = cut(4)
    pushed = cut(count)
    w_in, w_down, b, gb, gu, dgu, hid, flip, part = cut(9)
    room, take_sems, give_sems = cut(5), cut(6), cut(6)
    load_sem, load_gu = cut(2)
    extra = Push(outer, inner, parts, pushed, cut(3 * count), cut(6)) if count else None
    rows, width = resid.shape
    tall = outer * 4 * rows
    third = w_down.shape[1]
    slim = third // kinds
    loads = [
        pltpu.make_async_copy(source, target, load_sem.at[i])
        for i, (source, target) in enumerate(
            ((b_any, b), (w_down_any, w_down), (w_in_any, w_in))
        )
    ]
    for load in loads:
        load.start()
    take = Gather(outer, inner, gb, take_sems, PARTS)
    give = Scatter(outer, inner, part, room, give_sems, PARTS)
    size = rows // PARTS
    fills = [
        pltpu.make_async_copy(gu_any.at[source], gu.at[source], load_gu.at[step])
        for step, source in enumerate(take.source)
    ]
    for fill in fills:
        fill.start()
    gb[take.dz, take.t] = grad_y[...].astype(BF16)
    meet(take.friends() + (extra.xdev if count else []))

    def compute(step):
        source, q = take.origin(step), step % PARTS
        here = take.rows(step)
        if step == 0:
            loads[1].wait()
            loads[2].wait()
        if q == 0:
            fills[step // PARTS].wait()
        rows_in = gb[source, :, here].reshape(4 * size, width)
        mixed = mix[source, :, here].reshape(4 * size, kinds - 1)
        grad_hidden = dot(rows_in, w_down[...])
        both = gu[source, q].astype(F32)
        gate, up = both[:, :third], both[:, third:]
        sigma = jax.nn.sigmoid(gate)
        act = gate * sigma
        slope = sigma * (1.0 + gate * (1.0 - sigma))
        hidden, grad_gate, grad_up = act * up, grad_hidden * up * slope, grad_hidden * act
        for e in range(kinds):
            cols = slice(e * slim, (e + 1) * slim)
            more = slice(third + e * slim, third + (e + 1) * slim)
            scale = mixed[:, e : e + 1] if e < kinds - 1 else 1.0
            hid[source, q, :, cols] = (hidden[:, cols] * scale).astype(BF16)
            dgu[source, q, :, cols] = (grad_gate[:, cols] * scale).astype(BF16)
            dgu[source, q, :, more] = (grad_up[:, cols] * scale).astype(BF16)
        sent = dot_nt(dgu[source, q], w_in[...]).astype(BF16)
        part[source, :, :, here] = sent.reshape(2, 2, size, width)

    def turned(table):
        @pl.loop(0, outer)
        def _(source):
            for q in range(PARTS):
                block = table[source, :, q * size : (q + 1) * size].reshape(4 * size, width)
                at = pl.multiple_of((source * PARTS + q) * 4 * size, 4 * size)
                flip[:, pl.ds(at, 4 * size)] = jnp.transpose(block)

    def weigh(target, source, low, high):
        values = source[...].reshape(tall, source.shape[-1])

        @pl.loop(0, width // 256)
        def _(at):
            here = pl.ds(pl.multiple_of(at * 256, 256), 256)
            target[here, low:high] = dot(flip[here, :], values[:, low:high]).astype(BF16)

    def begin():
        if count:
            extra.start()
        loads[0].wait()
        turned(b)

    def pieces(total):
        return [(low, min(low + 256, total)) for low in range(0, total, 256)]

    late = [functools.partial(weigh, grad_in, dgu, *span) for span in pieces(2 * third)]
    late += [functools.partial(turned, gb)]
    late += [functools.partial(weigh, grad_down, hid, *span) for span in pieces(third)]
    pipeline(take, give, compute, begin, extra.turns() if count else [], late)
    grad_b = give.total()
    x = resid[...]
    inverse = lax.rsqrt(jnp.mean(x * x, axis=-1, keepdims=True) + EPSILON)
    unit = x * inverse
    gain_out[...] = jnp.sum(grad_b * unit, axis=0, keepdims=True)
    out[...] = grad_y[...] + norm_back(grad_b, gain[...], unit, inverse)
    take.finish()
    give.finish()
    if count:
        extra.finish()


def ffn_backward(grad_y, resid, gain, mix, w_in, w_down, b, both, parts, outer, inner, ident):
    dma = pltpu.SemaphoreType.DMA
    rows, width = resid.shape
    third = w_down.shape[1]
    kinds = mix.shape[-1] + 1
    count = len(parts)
    return pl.pallas_call(
        functools.partial(ffn_backward_kernel, outer, inner, kinds, count),
        out_shape=[
            jax.ShapeDtypeStruct((rows, width), F32),
            jax.ShapeDtypeStruct((1, width), F32),
            jax.ShapeDtypeStruct((width, 2 * third), BF16),
            jax.ShapeDtypeStruct((width, third), BF16),
        ]
        + push_outs(parts, outer),
        in_specs=[VMEM, VMEM, VMEM, VMEM, ANY, ANY, ANY, ANY] + [ANY] * count,
        out_specs=[VMEM, VMEM, VMEM, VMEM] + [ANY] * count,
        scratch_shapes=[
            pltpu.VMEM(w_in.shape, BF16),
            pltpu.VMEM(w_down.shape, BF16),
            pltpu.VMEM((outer, 4, rows, width), BF16),
            pltpu.VMEM((outer, 4, rows, width), BF16),
            pltpu.VMEM((outer, PARTS, 4 * rows // PARTS, 2 * third), BF16),
            pltpu.VMEM((outer, PARTS, 4 * rows // PARTS, 2 * third), BF16),
            pltpu.VMEM((outer, PARTS, 4 * rows // PARTS, third), BF16),
            pltpu.VMEM((width, outer * 4 * rows), BF16),
            pltpu.VMEM((outer, 2, 2, rows, width), BF16),
        ]
        + scatter_room(outer, rows, width, PARTS)
        + gather_sems(outer, PARTS)
        + scatter_sems(outer, PARTS)
        + [dma((3,)), dma((outer,))]
        + (push_scratch(parts, outer, inner) if count else []),
        compiler_params=pltpu.CompilerParams(
            collective_id=ident, has_side_effects=True, vmem_limit_bytes=63 << 20
        ),
        name="ffn_backward",
    )(grad_y, resid, gain, mix, w_in, w_down, b, both, *parts)


def swap_halves(values):
    width = values.shape[1]
    lane = lax.broadcasted_iota(jnp.int32, values.shape, 1)
    low = lax.rem(lane, HD) < HD // 2
    return jnp.where(
        low, pltpu.roll(values, width - HD // 2, 1), pltpu.roll(values, HD // 2, 1)
    )


def allowed_rows(marks, spot, top):
    del top
    return (spot >= marks[:, 1:2]) & (spot <= marks[:, 0:1])


def attn_forward_kernel(outer, inner, count, lead, *refs):
    dp = outer * inner
    cut = Cut(refs)
    x_in, tables, marks, spot = cut(4)
    gain, weight = (None, None) if lead else cut(2)
    owns = cut(count)
    out, a_out, qk_out, v_out, lse_out, att_out = cut(6)
    fetched = cut(count)
    w, a, qk, v, att, part = cut(6)
    room, take_sems, give_sems = cut(5), cut(6), cut(6)
    load_sem, keep_sem = cut(2)
    extra = Fetch(outer, inner, owns, fetched, cut(count), cut(5))
    rows, width = x_in.shape
    heads_width = w.shape[1] // 4
    heads = heads_width // HD
    take = Gather(1, dp, a, take_sems)
    give = Scatter(1, dp, part, room, give_sems)
    x = x_in[...]
    inverse = lax.rsqrt(jnp.mean(x * x, axis=-1, keepdims=True) + EPSILON)
    friends = take.friends() + extra.zdev[1:] + extra.xdev
    if lead:
        (gains,) = cut(1)
        meet(friends)
        extra.start()
        extra.settle()
        for turn in extra.turns(0, 1):
            turn()
        extra.land(0)
        load = pltpu.make_async_copy(fetched[0], gains, load_sem.at[0])
        load.start()
        load.wait()
        a[0, take.t] = (x * inverse * jnp.sum(gains[...], axis=0)[:1]).astype(BF16)
        turns = extra.turns(1, 2)
        turns[0]()
        take.start()
        for turn in turns[1:]:
            turn()
        extra.land(1)
        slot = fetched[1].shape[1]
        loads = [
            pltpu.make_async_copy(
                fetched[1].at[at], w.at[pl.ds(at * slot, slot)], load_sem.at[at]
            )
            for at in range(dp)
        ]
        for load in loads:
            load.start()
        for load in loads:
            load.wait()
    else:
        load = pltpu.make_async_copy(weight, w, load_sem.at[0])
        load.start()
        a[0, take.t] = (x * inverse * gain[...]).astype(BF16)
        meet(friends)
        take.start()
        extra.start()
        extra.settle()
        load.wait()
    done = 2 if lead else 0
    turns = extra.turns(done)

    def project(block):
        both = dot(a[0, block], w[:, : 3 * heads_width])
        raw = both[:, : 2 * heads_width]
        times = 2 * heads_width // tables.shape[-1]
        cosine = jnp.concatenate([tables[0, block]] * times, axis=1)
        sine = jnp.concatenate([tables[1, block]] * times, axis=1)
        qk[block] = (raw * cosine + swap_halves(raw) * sine).astype(BF16)
        v[block] = both[:, 2 * heads_width :].astype(BF16)

    project(take.t)
    take.complete(0)
    for other in range(1, 4):
        project(lax.rem(take.t + other, 4))
    keeps = [pltpu.make_async_copy(a.at[0], a_out, keep_sem.at[0])]
    keeps.append(pltpu.make_async_copy(qk, qk_out, keep_sem.at[1]))
    keeps.append(pltpu.make_async_copy(v, v_out, keep_sem.at[2]))
    for keep in keeps:
        keep.start()

    def attend(block):
        keys = qk[...].reshape(4 * rows, 2 * heads_width)
        values = v[...].reshape(4 * rows, heads_width)
        allowed = allowed_rows(marks[block], spot[...], 0)
        pieces = []
        for head in range(heads):
            here = slice(head * HD, (head + 1) * HD)
            there = slice(heads_width + head * HD, heads_width + (head + 1) * HD)
            scores = dot_nt(qk[block, :, here], keys[:, there])
            scores = jnp.where(allowed, scores * HD ** (-0.5), MASKED_SCORE)
            top = jnp.max(scores, axis=-1, keepdims=True)
            expo = jnp.exp(scores - top)
            total = jnp.sum(expo, axis=-1, keepdims=True)
            probs = (expo / total).astype(BF16)
            lse_out[block, :, head : head + 1] = top + jnp.log(total)
            pieces.append(dot(probs, values[:, here]).astype(BF16))
        att[block] = jnp.concatenate(pieces, axis=1)
        sent = dot_nt(att[block], w[:, 3 * heads_width :]).astype(BF16)
        part[0, lax.div(block, 2), lax.rem(block, 2)] = sent

    y, c = give.y, give.c
    attend(2 * (1 - y) + 1 - c)
    attend(2 * y + 1 - c)
    give.core_send(0)
    turns[0]()
    attend(2 * (1 - y) + c)
    attend(2 * y + c)
    give.pair_send(0)
    for turn in turns[1:]:
        turn()
    keeps.append(pltpu.make_async_copy(att, att_out, keep_sem.at[3]))
    keeps[-1].start()
    out[...] = x_in[...] + give.total()
    take.finish()
    give.finish()
    extra.finish(done)
    for keep in keeps:
        keep.wait()


def attn_forward(x, gain, weight, tables, marks, spot, owns, outer, inner, ident):
    count = len(owns)
    dma = pltpu.SemaphoreType.DMA
    rows, width = x.shape
    lead = weight is None
    shape = (width, owns[1].shape[-1]) if lead else weight.shape
    slim = shape[1] // 4
    extras = [] if lead else [gain, weight]
    kept = [(4, rows, width), (4, rows, 2 * slim), (4, rows, slim)]
    return pl.pallas_call(
        functools.partial(attn_forward_kernel, outer, inner, count, lead),
        out_shape=[jax.ShapeDtypeStruct((rows, width), F32)]
        + [jax.ShapeDtypeStruct(shape, BF16) for shape in kept]
        + [
            jax.ShapeDtypeStruct((4, rows, 8), F32),
            jax.ShapeDtypeStruct((4, rows, slim), BF16),
        ]
        + fetch_outs(owns, outer * inner),
        in_specs=[VMEM] * 4 + ([] if lead else [VMEM, ANY]) + [ANY] * count,
        out_specs=[VMEM, ANY, ANY, ANY, VMEM, ANY] + [ANY] * count,
        scratch_shapes=[
            pltpu.VMEM(shape, BF16),
            pltpu.VMEM((1, 4, rows, width), BF16),
            pltpu.VMEM(kept[1], BF16),
            pltpu.VMEM(kept[2], BF16),
            pltpu.VMEM(kept[2], BF16),
            pltpu.VMEM((1, 2, 2, rows, width), BF16),
        ]
        + scatter_room(1, rows, width)
        + gather_sems(1)
        + scatter_sems(1)
        + [dma((outer * inner,)), dma((4,))]
        + fetch_scratch(owns, outer, inner)
        + ([pltpu.VMEM((outer * inner,) + owns[0].shape[1:], F32)] if lead else []),
        compiler_params=pltpu.CompilerParams(collective_id=ident, has_side_effects=True),
        name="attn_forward",
    )(x, tables, marks, spot, *extras, *owns)


def attn_backward_kernel(outer, inner, count, last, *refs):
    dp = outer * inner
    cut = Cut(refs)
    grad_in, x_in, gain, weight, tables, marks, spot = cut(7)
    a_in, qk_in, v_in, lse, att_in = cut(5)
    (others,) = cut(1) if last else (None,)
    parts = cut(count)
    out, gain_out = cut(2)
    (grad_w,) = (None,) if last else cut(1)
    total = count + 1 if last else count
    pushed = cut(total)
    w, a, qk, v, att, ga, g_att, raw, part = cut(9)
    room, take_sems, give_sems = cut(5), cut(6), cut(6)
    (load_sem,) = cut(1)
    room_x, sems_x = cut(3 * total), cut(6)
    if last:
        held, from_t, from_d, ts, tr, ds, dr = cut(7)
        parts = tuple(parts) + (held,)
    extra = Push(outer, inner, parts, pushed, room_x, sems_x)
    turns = extra.turns()
    friends = []
    rows, width = x_in.shape
    tall = 4 * rows
    heads_width = w.shape[1] // 4
    heads = heads_width // HD
    loads = [
        pltpu.make_async_copy(source, target, load_sem.at[i])
        for i, (source, target) in enumerate(
            ((weight, w), (qk_in, qk), (v_in, v), (att_in, att), (a_in, a))
        )
    ]
    for load in loads:
        load.start()
    take = Gather(1, dp, ga, take_sems)
    give = Scatter(1, dp, part, room, give_sems)
    ga[0, take.t] = grad_in[...].astype(BF16)
    if last:
        team = [(take.d, lax.rem(take.t + k, 4)) for k in range(1, 4)]
        peers = [(lax.rem(take.d + k, dp), take.t) for k in range(1, dp)]
        friends = team + peers
    else:
        friends = take.friends() + extra.zdev[:-1] + extra.xdev
    meet(friends)
    take.start()
    extra.start(0, count)
    for load in loads:
        load.wait()
    take.complete(0)
    turns[0]()
    grads = ga[...].reshape(tall, width)
    g_att[...] = dot(grads, w[:, 3 * heads_width :]).astype(BF16)
    all_qk = qk[...].reshape(tall, 2 * heads_width)
    all_v = v[...].reshape(tall, heads_width)
    all_marks = marks[...].reshape(tall, marks.shape[-1])
    all_lse = lse[...].reshape(tall, lse.shape[-1])
    allowed = allowed_rows(all_marks, spot[...], 0)
    q_grads, k_grads, v_grads = [], [], []
    for head in range(heads):
        here = slice(head * HD, (head + 1) * HD)
        there = slice(heads_width + head * HD, heads_width + (head + 1) * HD)
        query, key = all_qk[:, here], all_qk[:, there]
        scores = dot_nt(query, key)
        scores = jnp.where(allowed, scores * HD ** (-0.5), MASKED_SCORE)
        probs = jnp.exp(scores - all_lse[:, head : head + 1])
        grad_probs = dot_nt(g_att[:, here], all_v[:, here])
        inner = jnp.sum(grad_probs * probs, axis=-1, keepdims=True)
        grad_scores = (probs * (grad_probs - inner)).astype(BF16)
        v_grads.append(dot_tn(probs.astype(BF16), g_att[:, here]).astype(BF16))
        q_grads.append(dot(grad_scores, key))
        k_grads.append(dot_tn(grad_scores, query))
    rotated = jnp.concatenate(q_grads + k_grads, axis=1) * HD ** (-0.5)
    times = 2 * heads_width // tables.shape[-1]
    cosine = jnp.concatenate([tables[0].reshape(tall, -1)] * times, axis=1)
    sine = jnp.concatenate([tables[1].reshape(tall, -1)] * times, axis=1)
    raw[:, : 2 * heads_width] = (rotated * cosine - swap_halves(rotated) * sine).astype(BF16)
    raw[:, 2 * heads_width :] = jnp.concatenate(v_grads, axis=1)
    def back(block):
        at = pl.ds(pl.multiple_of(block * rows, rows), rows)
        sent = dot_nt(raw[at, :], w[:, : 3 * heads_width]).astype(BF16)
        part[0, lax.div(block, 2), lax.rem(block, 2)] = sent

    turns[1]()
    y, c = give.y, give.c
    back(2 * (1 - y) + 1 - c)
    back(2 * y + 1 - c)
    give.core_send(0)
    back(2 * (1 - y) + c)
    back(2 * y + c)
    give.pair_send(0)
    turns[2]()
    grad_raw = dot_tn(a[...].reshape(tall, width), raw[...]).astype(BF16)
    grad_out = dot_tn(grads, att[...].reshape(tall, heads_width)).astype(BF16)
    if last:
        held[:, :, : 3 * heads_width] = grad_raw.reshape(dp, width // dp, -1)
        held[:, :, 3 * heads_width :] = grad_out.reshape(dp, width // dp, -1)
    else:
        grad_w[:, : 3 * heads_width] = grad_raw
        grad_w[:, 3 * heads_width :] = grad_out
    grad_a = give.total()
    x = x_in[...]
    inverse = lax.rsqrt(jnp.mean(x * x, axis=-1, keepdims=True) + EPSILON)
    unit = x * inverse
    part_gain = jnp.sum(grad_a * unit, axis=0, keepdims=True)
    if last:
        row = lax.broadcasted_iota(jnp.int32, others.shape, 0)
        from_t[take.t] = others[...] + jnp.where(row == 0, part_gain, 0.0)
    else:
        gain_out[...] = part_gain
    out[...] = grad_in[...] + norm_back(grad_a, gain[...], unit, inverse)
    if last:
        extra.start(count, total)
        mine = from_t.at[take.t]
        copies = [
            send(mine, mine, ts.at[k], tr.at[k], device) for k, device in enumerate(team)
        ]
        for copy in copies:
            copy.wait_recv()
        from_d[take.d] = jnp.sum(from_t[...], axis=0)
        turns[3]()
        mine = from_d.at[take.d]
        more = [send(mine, mine, ds.at[k], dr.at[k], device) for k, device in enumerate(peers)]
        for turn in turns[4:]:
            turn()
        for copy in more:
            copy.wait_recv()
        gain_out[...] = jnp.sum(from_d[...], axis=0)
        for copy in copies + more:
            copy.wait_send()
    else:
        for turn in turns[3:]:
            turn()
    take.finish()
    give.finish()
    extra.finish()


def attn_backward(
    grad, x, gain, weight, tables, marks, spot, kept, others, parts, outer, inner, ident
):
    count = len(parts)
    dma = pltpu.SemaphoreType.DMA
    rows, width = x.shape
    slim = weight.shape[1] // 4
    dp = outer * inner
    last = others is not None
    whole = jax.ShapeDtypeStruct((dp, width // dp, 4 * slim), BF16)
    moved = list(parts) + ([whole] if last else [])
    wide = (8, width) if last else (1, width)
    return pl.pallas_call(
        functools.partial(attn_backward_kernel, outer, inner, count, last),
        out_shape=[
            jax.ShapeDtypeStruct((rows, width), F32),
            jax.ShapeDtypeStruct(wide, F32),
        ]
        + ([] if last else [jax.ShapeDtypeStruct(weight.shape, BF16)])
        + push_outs(moved, outer),
        in_specs=[VMEM, VMEM, VMEM, ANY, VMEM, VMEM, VMEM, ANY, ANY, ANY, VMEM, ANY]
        + ([VMEM] if last else [])
        + [ANY] * count,
        out_specs=[VMEM, VMEM] + ([] if last else [VMEM]) + [ANY] * len(moved),
        scratch_shapes=[
            pltpu.VMEM(weight.shape, BF16),
            pltpu.VMEM((4, rows, width), BF16),
            pltpu.VMEM((4, rows, 2 * slim), BF16),
            pltpu.VMEM((4, rows, slim), BF16),
            pltpu.VMEM((4, rows, slim), BF16),
            pltpu.VMEM((1, 4, rows, width), BF16),
            pltpu.VMEM((4 * rows, slim), BF16),
            pltpu.VMEM((4 * rows, 3 * slim), BF16),
            pltpu.VMEM((1, 2, 2, rows, width), BF16),
        ]
        + scatter_room(1, rows, width)
        + gather_sems(1)
        + scatter_sems(1)
        + [dma((5,))]
        + push_scratch(moved, outer, inner)
        + (
            [
                pltpu.VMEM(whole.shape, BF16),
                pltpu.VMEM((4, 8, width), F32),
                pltpu.VMEM((dp, 8, width), F32),
                dma((3,)),
                dma((3,)),
                dma((dp,)),
                dma((dp,)),
            ]
            if last
            else []
        ),
        compiler_params=pltpu.CompilerParams(
            collective_id=ident, has_side_effects=True, vmem_limit_bytes=62 << 20
        ),
        name="attn_backward",
    )(grad, x, gain, weight, tables, marks, spot, *kept, *([others] if last else []), *parts)


def layout(place_row, length_row):
    ends = jnp.cumsum(length_row, dtype=jnp.int32)
    after = place_row[:, None] >= ends[None, :]
    begins = jnp.sum(jnp.where(after, length_row[None, :], 0), axis=1, dtype=jnp.int32)
    return place_row - begins


def rope_tables(position):
    half_width = HD // 2
    freqs = 10000.0 ** (-jnp.arange(half_width, dtype=F32) / half_width)
    angles = position.astype(F32)[:, None] * freqs[None, :]
    cosine, sine = jnp.cos(angles), jnp.sin(angles)
    return jnp.stack(
        [
            jnp.concatenate([cosine] * 4, axis=1),
            jnp.concatenate([-sine, sine, -sine, sine], axis=1),
        ]
    )


def norm_back(grad_normed, gain_row, unit_rows, inverse):
    scaled = grad_normed * gain_row
    return inverse * (scaled - unit_rows * jnp.mean(scaled * unit_rows, axis=-1, keepdims=True))


def dot(left, right):
    return jnp.dot(left, right, preferred_element_type=F32)


def dot_nt(left, right):
    return lax.dot_general(left, right, (((1,), (1,)), ((), ())), preferred_element_type=F32)


def dot_tn(left, right):
    return lax.dot_general(left, right, (((0,), (0,)), ((), ())), preferred_element_type=F32)


def make_body(dp):
    outer, inner = split_dp(dp)

    def body(
        tokens,
        place,
        lengths,
        expert_ids,
        gate_values,
        cotangent,
        gain_attn,
        w_query,
        w_key,
        w_value,
        w_out,
        gain_ffn,
        exp_gate,
        exp_up,
        exp_down,
        dense_gate,
        dense_up,
        dense_down,
    ):
        layers, experts, rows, full = exp_gate.shape
        width = tokens.shape[1]
        slim = full // outer
        count = place.shape[1]
        position = layout(place[0], lengths[0])
        place_row = place[0].astype(F32)
        marks = jnp.stack([place_row, place_row - position.astype(F32)] * 4, axis=1)
        marks = marks.reshape(4, count // 4, 8)
        spot = place_row[None]
        tables = rope_tables(position).reshape(2, 4, count // 4, 128)

        slots = expert_ids[:, None] == jnp.arange(experts, dtype=jnp.int32)[None, :, None, None]
        mix_own = jnp.sum(jnp.where(slots, gate_values[:, None], 0.0), axis=-1)
        mix_own = mix_own.reshape(1, layers * experts, count)
        dx = lax.rem(lax.axis_index("dp"), inner)
        gains_own = jnp.concatenate([gain_attn, gain_ffn], axis=0).astype(BF16).astype(F32)
        spots = jnp.arange(dp, dtype=jnp.int32) == lax.axis_index("dp")
        gains_own = jnp.where(spots[None, :, None], gains_own[:, None], 0.0)
        gains_own = jnp.pad(gains_own.reshape(2 * layers, width), ((0, 8 - 2 * layers), (0, 0)))

        attn_own, ffn_own = [], []
        for level in range(layers):
            attn_own.append(
                jnp.concatenate(
                    [w_query[level], w_key[level], w_value[level], jnp.transpose(w_out[level])],
                    axis=1,
                ).astype(BF16)[None]
            )
            mats = (
                [exp_gate[level, e] for e in range(experts)]
                + [dense_gate[level]]
                + [exp_up[level, e] for e in range(experts)]
                + [dense_up[level]]
                + [jnp.transpose(exp_down[level, e]) for e in range(experts)]
                + [jnp.transpose(dense_down[level])]
            )
            mats = [m.astype(BF16) for m in mats]
            kinds = experts + 1
            ffn_own.append(
                [
                    jnp.stack(
                        [
                            jnp.concatenate(
                                [m[:, k * slim : (k + 1) * slim] for m in group], axis=1
                            )
                            for k in range(outer)
                        ]
                    )
                    for group in (mats[: 2 * kinds], mats[2 * kinds :])
                ]
            )
        merged = rows % 16 == 0
        state = tokens.astype(F32)
        lead = [gains_own[None], attn_own[0], mix_own]
        if merged:
            state_in = state
            state, *kept, gains_all, first, mix_all, w_in, w_down = attn_forward(
                state_in, None, None, tables, marks, spot, lead + ffn_own[0], outer, inner, 0
            )
        else:
            gains_all, first, mix_all = fetch(lead, outer, inner, 8)
        gains = jnp.sum(gains_all, axis=0)
        w_attn = [first.reshape(width, -1)]
        w_ffn = []
        mix_all = lax.dynamic_index_in_dim(
            mix_all.reshape(outer, inner, layers, experts, count), dx, axis=1, keepdims=False
        )
        mixing = [
            jnp.transpose(mix_all[:, level], (0, 2, 1)).reshape(outer, 4, count // 4, experts)
            for level in range(layers)
        ]

        kept_attn, kept_ffn = [], []
        for level in range(layers):
            if level == 0 and merged:
                before = state_in
            else:
                before = state
                inside = ffn_own[level] if level == 0 else ffn_own[level][:1]
                state, *kept = attn_forward(
                    before,
                    gains[level][None],
                    w_attn[level],
                    tables,
                    marks,
                    spot,
                    inside,
                    outer,
                    inner,
                    1 if level else 11,
                )
                if level:
                    w_in = kept.pop()
                else:
                    w_down, w_in = kept.pop(), kept.pop()
            kept_attn.append((before, kept))
            w_ffn.append((w_in.reshape(width, -1), w_down.reshape(width, -1)))
            resid = state
            more = [attn_own[level + 1], ffn_own[level + 1][1]] if level + 1 < layers else []
            state, b_in, both, *fetched = ffn_forward(
                resid,
                gains[layers + level][None],
                mixing[level],
                *w_ffn[level],
                more,
                outer,
                inner,
                2 if more else 3,
            )
            if more:
                w_attn.append(fetched[0].reshape(width, -1))
                w_down = fetched[1]
            kept_ffn.append((resid, b_in, both))
        mixed = state.astype(BF16)

        grad = cotangent.astype(F32)
        part_gains = [None] * (2 * layers)
        pushed_in, pushed_down = [None] * layers, [None] * layers
        pushed_attn = [None] * layers
        waiting = []
        for level in reversed(range(layers)):
            resid, b_in, both = kept_ffn[level]
            grad, part_gain, grad_in, grad_down, *moved = ffn_backward(
                grad,
                resid,
                gains[layers + level][None],
                mixing[level],
                *w_ffn[level],
                b_in,
                both,
                waiting,
                outer,
                inner,
                4 if waiting else 5,
            )
            part_gains[layers + level] = part_gain[0]
            if waiting:
                pushed_attn[level + 1], pushed_down[level + 1] = moved
            before, kept = kept_attn[level]
            inside = [grad_in.reshape(dp, rows, -1), grad_down.reshape(dp, rows, -1)]
            others = None
            if level == 0 and merged:
                part_gains[0] = jnp.zeros((width,), F32)
                others = jnp.pad(jnp.stack(part_gains), ((0, 8 - 2 * layers), (0, 0)))
            grad, part_gain, *moved = attn_backward(
                grad,
                before,
                gains[level][None],
                w_attn[level],
                tables,
                marks,
                spot,
                kept,
                others,
                inside[:1] if level else inside,
                outer,
                inner,
                6 if level else 7,
            )
            if level == 0 and merged:
                pushed_in[0], pushed_down[0], pushed_attn[0] = moved
                gain_sum = lax.dynamic_slice_in_dim(
                    part_gain, lax.axis_index("dp") * rows, rows, axis=1
                )
                continue
            part_gains[level] = part_gain[0]
            waiting = [moved[0].reshape(dp, rows, -1), inside[1]]
            pushed_in[level] = moved[1]
            if level == 0:
                pushed_down[0] = moved[2]
        if not merged:
            stacked = jnp.pad(jnp.stack(part_gains), ((0, 8 - 2 * layers), (0, 0)))
            stacked = jnp.transpose(stacked.reshape(8, dp, rows), (1, 0, 2))
            pushed_attn[0], gain_parts = push([waiting[0], stacked], outer, inner, 9)
            gain_part = jnp.sum(gain_parts, axis=0)
            gain_sum = jnp.sum(
                gather(jnp.pad(gain_part, ((0, 0), (0, 128 - rows))), dp, 10)[0], axis=0
            )
        grad_gain_attn = gain_sum[:layers, :rows]
        grad_gain_ffn = gain_sum[layers : 2 * layers, :rows]

        kinds = experts + 1
        ups, downs, attns = [], [], []
        for level in range(layers):
            in_part, down_part = pushed_in[level], pushed_down[level]
            attn_part = pushed_attn[level]
            ups.append(
                jnp.concatenate(
                    [
                        jnp.stack(
                            [
                                in_part[k][:, m * slim : (m + 1) * slim]
                                for m in range(2 * kinds)
                            ]
                        )
                        for k in range(outer)
                    ],
                    axis=2,
                )
            )
            downs.append(
                jnp.concatenate(
                    [
                        jnp.stack(
                            [
                                jnp.transpose(down_part[k][:, m * slim : (m + 1) * slim])
                                for m in range(kinds)
                            ]
                        )
                        for k in range(outer)
                    ],
                    axis=1,
                )
            )
            attns.append(jnp.sum(attn_part.astype(F32), axis=0))
        up = jnp.stack(ups).astype(F32)
        down = jnp.stack(downs).astype(F32)
        attn = jnp.stack(attns)
        quarter = attn.shape[-1] // 4
        return (
            mixed,
            grad,
            grad_gain_attn,
            attn[:, :, :quarter],
            attn[:, :, quarter : 2 * quarter],
            attn[:, :, 2 * quarter : 3 * quarter],
            jnp.swapaxes(attn[:, :, 3 * quarter :], 1, 2),
            grad_gain_ffn,
            up[:, :experts],
            up[:, kinds : kinds + experts],
            down[:, :experts],
            up[:, experts],
            up[:, kinds + experts],
            down[:, experts],
        )

    return body


def solution(mesh):
    return jax.shard_map(
        make_body(mesh.shape["dp"]),
        mesh=mesh,
        in_specs=(
            P(("dp", "tensor"), None),
            P("dp", None),
            P("dp", None),
            P(None, "dp", None),
            P(None, "dp", None),
            P(("dp", "tensor"), None),
            P(None, "dp"),
            P(None, "dp", "tensor"),
            P(None, "dp", "tensor"),
            P(None, "dp", "tensor"),
            P(None, "tensor", "dp"),
            P(None, "dp"),
            P(None, None, "dp", "tensor"),
            P(None, None, "dp", "tensor"),
            P(None, None, "tensor", "dp"),
            P(None, "dp", "tensor"),
            P(None, "dp", "tensor"),
            P(None, "tensor", "dp"),
        ),
        out_specs=(
            P(("dp", "tensor"), None),
            P(("dp", "tensor"), None),
            P(None, "dp"),
            P(None, "dp", "tensor"),
            P(None, "dp", "tensor"),
            P(None, "dp", "tensor"),
            P(None, "tensor", "dp"),
            P(None, "dp"),
            P(None, None, "dp", "tensor"),
            P(None, None, "dp", "tensor"),
            P(None, None, "tensor", "dp"),
            P(None, "dp", "tensor"),
            P(None, "dp", "tensor"),
            P(None, "tensor", "dp"),
        ),
        check_vma=False,
    )
```

```python
import functools

import jax
import jax.numpy as jnp
import numpy as np
from jax import lax
from jax.experimental import pallas as pl
from jax.experimental.pallas import tpu as pltpu
from jax.sharding import PartitionSpec as P

HD = 64
EPSILON = 1e-06
MASKED_SCORE = -1e30
MESH = pl.DeviceIdType.MESH
ANY = pl.BlockSpec(memory_space=pl.ANY)
VMEM = pl.BlockSpec(memory_space=pltpu.VMEM)
F32 = jnp.float32
BF16 = jnp.bfloat16
PARTS = 2
BOTH, OUTER, INNER = range(3)


def split_dp(dp):
    inner = 2 ** ((dp.bit_length() - 1) // 2)
    return dp // inner, inner


def place_of(inner):
    d = lax.axis_index("dp")
    return lax.div(d, inner), lax.rem(d, inner), lax.axis_index("tensor")


def across(t):
    return lax.rem(t + 2, 4), t + 1 - 2 * lax.rem(t, 2)


def meet(devices):
    barrier = pltpu.get_barrier_semaphore()
    for device in devices:
        pl.semaphore_signal(barrier, inc=1, device_id=device, device_id_type=MESH)
    pl.semaphore_wait(barrier, len(devices))


def send(source, target, send_sem, recv_sem, device):
    copy = pltpu.make_async_remote_copy(
        src_ref=source,
        dst_ref=target,
        send_sem=send_sem,
        recv_sem=recv_sem,
        device_id=device,
        device_id_type=MESH,
    )
    copy.start()
    return copy


def gather_kernel(dp, own, out, *sems):
    take = Gather(1, dp, out, sems)
    out[0, take.t] = own[...]
    meet(take.friends())
    take.start()
    take.complete(0)
    take.finish()


def gather(own, dp, ident):
    return pl.pallas_call(
        functools.partial(gather_kernel, dp),
        out_shape=jax.ShapeDtypeStruct((1, 4) + own.shape, own.dtype),
        in_specs=[VMEM],
        out_specs=VMEM,
        scratch_shapes=gather_sems(1),
        compiler_params=pltpu.CompilerParams(collective_id=ident, has_side_effects=True),
        name="gather",
    )(own)


def fetch_kernel(outer, inner, count, *refs):
    cut = Cut(refs)
    extra = Fetch(outer, inner, cut(count), cut(count), cut(count), cut(5), [BOTH] * count)
    meet(extra.zdev[1:] + extra.xdev)
    extra.start()
    extra.settle()
    for turn in extra.turns():
        turn()
    extra.finish()


def fetch(owns, outer, inner, ident):
    count = len(owns)
    return pl.pallas_call(
        functools.partial(fetch_kernel, outer, inner, count),
        out_shape=fetch_outs(owns, outer, inner, [BOTH] * count),
        in_specs=[ANY] * count,
        out_specs=[ANY] * count,
        scratch_shapes=fetch_scratch(owns, outer, inner, [BOTH] * count),
        compiler_params=pltpu.CompilerParams(collective_id=ident, has_side_effects=True),
        name="fetch",
    )(*owns)


def push_kernel(outer, inner, count, *refs):
    cut = Cut(refs)
    extra = Push(outer, inner, cut(count), cut(count), cut(3 * count), cut(6))
    meet(extra.zdev[:-1] + extra.xdev)
    extra.start()
    for turn in extra.turns():
        turn()
    extra.finish()


def push(parts, outer, inner, ident):
    count = len(parts)
    return pl.pallas_call(
        functools.partial(push_kernel, outer, inner, count),
        out_shape=push_outs(parts, outer),
        in_specs=[ANY] * count,
        out_specs=[ANY] * count,
        scratch_shapes=push_scratch(parts, outer, inner),
        compiler_params=pltpu.CompilerParams(collective_id=ident, has_side_effects=True),
        name="push",
    )(*parts)


def nearest(index, size, step):
    table = [sorted(range(size), key=lambda other: (abs(other - at), other)) for at in range(size)]
    found = 0
    for at in range(size):
        found = found + jnp.where(index == at, table[at][step], 0)
    return found


class Gather:
    def __init__(self, outer, inner, table, sems, parts=1):
        self.outer, self.inner, self.table, self.parts = outer, inner, table, parts
        self.zs, self.zr, self.ys, self.yr, self.cs, self.cr = sems
        self.dz, self.dx, self.t = place_of(inner)
        self.d = lax.axis_index("dp")
        self.size = table.shape[2] // parts
        ty, tc = across(self.t)
        self.ty = ty
        self.pair, self.core = (self.d, ty), (self.d, tc)
        self.source = [nearest(self.dz, outer, step) for step in range(outer)]
        self.zdev = [(source * inner + self.dx, self.t) for source in self.source]
        self.steps = outer * parts
        self.yc, self.cc, self.dc = [], [], []

    def friends(self):
        return self.zdev[1:] + [self.pair, self.core]

    def rows(self, step):
        return pl.ds(step % self.parts * self.size, self.size)

    def origin(self, step):
        return self.source[step // self.parts]

    def outward(self, step, target, sent):
        at = self.origin(step) * self.parts + step % self.parts
        block = self.table.at[self.origin(step), self.t, self.rows(step)]
        target = jnp.minimum(jnp.maximum(target, 0), self.outer - 1)
        return pltpu.make_async_remote_copy(
            src_ref=block,
            dst_ref=block,
            send_sem=self.zs.at[at if sent is None else sent],
            recv_sem=self.zr.at[at],
            device_id=(target * self.inner + self.dx, self.t),
            device_id_type=MESH,
        )

    def passes(self, step):
        if self.outer == 1:
            return []
        if step < self.parts:
            last = self.steps + step
            return [
                (self.dz < self.outer - 1, self.outward(step, self.dz + 1, None)),
                (self.dz > 0, self.outward(step, self.dz - 1, last)),
            ]
        ahead = jnp.where(self.origin(step) < self.dz, self.dz + 1, self.dz - 1)
        inside = (ahead >= 0) & (ahead < self.outer)
        return [(inside, self.outward(step, ahead, None))]

    def start(self):
        for step in range(self.parts):
            for inside, copy in self.passes(step):
                pl.when(inside)(copy.start)
        for step in range(self.parts):
            self.forward(step)

    def arrive(self, step):
        self.outward(step, self.dz, None).wait_recv()
        for inside, copy in self.passes(step):
            pl.when(inside)(copy.start)
        self.forward(step)

    def forward(self, step):
        block = self.table.at[self.origin(step), self.t, self.rows(step)]
        self.yc.append(send(block, block, self.ys.at[step], self.yr.at[step], self.pair))
        self.cc.append(send(block, block, self.cs.at[step], self.cr.at[step], self.core))

    def complete(self, step):
        self.yc[step].wait_recv()
        at = self.steps + step
        block = self.table.at[self.origin(step), self.ty, self.rows(step)]
        self.dc.append(send(block, block, self.cs.at[at], self.cr.at[at], self.core))
        self.cc[step].wait_recv()
        self.dc[step].wait_recv()

    def finish(self):
        for step in range(self.steps):
            for inside, copy in self.passes(step):
                pl.when(inside)(copy.wait_send)
        for copy in self.yc + self.cc + self.dc:
            copy.wait_send()


class Scatter:
    def __init__(self, outer, inner, part, room, sems, parts=1):
        self.outer, self.part, self.parts = outer, part, parts
        self.from_c, self.sum_c, self.from_y, self.sum_y, self.from_z = room
        self.cs, self.cr, self.ys, self.yr, self.zs, self.zr = sems
        dz, dx, t = place_of(inner)
        d = lax.axis_index("dp")
        ty, tc = across(t)
        self.size = part.shape[3] // parts
        self.dz, self.y, self.c = dz, lax.div(t, 2), lax.rem(t, 2)
        self.pair, self.core = (d, ty), (d, tc)
        self.source = [nearest(dz, outer, step) for step in range(outer)]
        self.zdev = [(source * inner + dx, t) for source in self.source]
        self.steps = outer * parts
        self.cc, self.yc, self.zc = {}, {}, {}

    def rows(self, step):
        return pl.ds(step % self.parts * self.size, self.size)

    def core_send(self, step):
        source = self.source[step // self.parts]
        self.cc[step] = send(
            self.part.at[source, :, 1 - self.c, self.rows(step)],
            self.from_c.at[step],
            self.cs.at[step],
            self.cr.at[step],
            self.core,
        )

    def pair_send(self, step):
        source = self.source[step // self.parts]
        self.cc[step].wait_recv()
        mine = self.part[source, :, self.c, self.rows(step)].astype(F32)
        self.sum_c[step] = (mine + self.from_c[step].astype(F32)).astype(BF16)
        self.yc[step] = send(
            self.sum_c.at[step, 1 - self.y],
            self.from_y.at[step],
            self.ys.at[step],
            self.yr.at[step],
            self.pair,
        )

    def summed(self, step):
        self.yc[step].wait_recv()
        return self.sum_c[step, self.y].astype(F32) + self.from_y[step].astype(F32)

    def outward(self, step, source, away):
        at = (away - 1) * self.parts + step % self.parts
        return pltpu.make_async_remote_copy(
            src_ref=source,
            dst_ref=self.from_z.at[at],
            send_sem=self.zs.at[at],
            recv_sem=self.zr.at[at],
            device_id=self.zdev[step // self.parts],
            device_id_type=MESH,
        )

    def outer_send(self, step):
        self.sum_y[step] = self.summed(step).astype(BF16)
        away = lax.rem(self.source[step // self.parts] - self.dz + self.outer, self.outer)
        self.zc[step] = self.outward(step, self.sum_y.at[step], away)
        self.zc[step].start()

    def total(self):
        pieces = []
        for piece in range(self.parts):
            total = self.summed(piece)
            for step in range(self.parts + piece, self.steps, self.parts):
                away = lax.rem(self.dz - self.source[step // self.parts] + self.outer, self.outer)
                self.outward(step, self.sum_y.at[step], away).wait_recv()
                at = (away - 1) * self.parts + piece
                total = total + self.from_z[at].astype(F32)
            pieces.append(total)
        return pieces[0] if self.parts == 1 else jnp.concatenate(pieces, axis=0)

    def finish(self):
        for group in (self.cc, self.yc, self.zc):
            for step in group:
                group[step].wait_send()


def gather_sems(outer, parts=1):
    dma = pltpu.SemaphoreType.DMA
    steps = outer * parts
    return [dma((steps + parts,))] + [dma((steps,)) for _ in range(3)] + [dma((2 * steps,))] * 2


def scatter_sems(outer, parts=1):
    dma = pltpu.SemaphoreType.DMA
    return [dma((outer * parts,)) for _ in range(6)]


def scatter_room(outer, rows, width, parts=1):
    steps, size = outer * parts, rows // parts
    return [
        pltpu.VMEM((steps, 2, size, width), BF16),
        pltpu.VMEM((steps, 2, size, width), BF16),
        pltpu.VMEM((steps, size, width), BF16),
        pltpu.VMEM((steps, size, width), BF16),
        pltpu.VMEM((max(steps - parts, 1), size, width), BF16),
    ]


def pipeline(take, give, compute, begin, after, middle, late):
    steps, parts = take.steps, take.parts
    middle, late = list(middle), list(late)
    lag = parts + 1
    take.start()
    begin()
    for step in range(steps):
        if step + parts < steps:
            take.arrive(step + parts)
        if step + parts == steps - 1:
            after()
        take.complete(step)
        compute(step)
        give.core_send(step)
        if step:
            give.pair_send(step - 1)
        if step - lag >= parts:
            give.outer_send(step - lag)
        if step + parts >= steps and middle:
            middle.pop(0)()
    sent = max(parts, steps - lag)
    late = middle + late
    share = max(1, (len(late) + lag) // (lag + 1))
    give.pair_send(steps - 1)
    for step in range(sent, steps):
        for _ in range(share):
            if late:
                late.pop(0)()
        give.outer_send(step)
    for work in late:
        work()


class Fetch:
    def __init__(self, outer, inner, owns, outs, holds, sems, modes):
        self.outer, self.inner, self.owns, self.outs, self.holds = outer, inner, owns, outs, holds
        self.zs, self.zr, self.xs, self.xr, self.ls = sems
        self.modes = modes
        self.dz, dx, t = place_of(inner)
        self.dx, self.d = dx, lax.axis_index("dp")
        self.source = [nearest(self.dz, outer, step) for step in range(outer)]
        self.zdev = [(source * inner + dx, t) for source in self.source]
        self.xdev = [(self.dz * inner + lax.rem(dx + j, inner), t) for j in range(1, inner)]
        self.zc, self.xc, self.into, self.back = [], {}, {}, {}

    def own(self, i, where):
        return self.owns[i].at[where if self.owns[i].shape[0] == self.outer else 0]

    def slot(self, i, source):
        if self.modes[i] == OUTER:
            return self.outs[i].at[source]
        return self.outs[i].at[source * self.inner + self.dx]

    def copy(self, i, step, source, target):
        away = lax.rem(source + self.outer, self.outer)
        at = i * self.outer + away
        return pltpu.make_async_remote_copy(
            src_ref=target[0],
            dst_ref=target[1],
            send_sem=self.zs.at[at],
            recv_sem=self.zr.at[at],
            device_id=self.zdev[step],
            device_id_type=MESH,
        )

    def start(self, first=0, last=None, aside=True):
        for i in range(first, len(self.owns) if last is None else last):
            inner = self.modes[i] == INNER
            here = self.owns[i] if inner else self.own(i, self.dz)
            at = i * (self.outer + 1)
            self.into[i] = pltpu.make_async_copy(here, self.holds[i], self.ls.at[at])
            self.into[i].start()
            if inner:
                for step, source in enumerate(self.source):
                    self.spread(i, step, self.owns[i].at[source], self.slot(i, source))
                continue
            for step in range(1, self.outer):
                source = self.source[step]
                refs = (self.own(i, source), self.slot(i, self.dz))
                self.zc.append(self.copy(i, step, source - self.dz, refs))
                self.zc[-1].start()
            if aside:
                self.aside(i)

    def aside(self, i):
        if self.modes[i] == BOTH:
            self.spread(i, 0, self.own(i, self.dz), self.slot(i, self.dz))

    def spread(self, i, step, block, target):
        for j in range(1, self.inner):
            at = (i * self.outer + step) * self.inner + j
            self.xc[i, step, j] = send(
                block, target, self.xs.at[at], self.xr.at[at], self.xdev[j - 1]
            )

    def settle(self):
        for i, into in self.into.items():
            into.wait()
            at = i * (self.outer + 1)
            if self.modes[i] == INNER:
                pairs = [
                    (self.holds[i].at[source], self.slot(i, source)) for source in self.source
                ]
            else:
                pairs = [(self.holds[i], self.slot(i, self.dz))]
            self.back[i] = [
                pltpu.make_async_copy(*pair, self.ls.at[at + 1 + k])
                for k, pair in enumerate(pairs)
            ]
            for copy in self.back[i]:
                copy.start()

    def turn(self, i, step):
        source = self.source[step]
        block = self.slot(i, source)
        self.copy(i, step, self.dz - source, (block, block)).wait_recv()
        if self.modes[i] == BOTH:
            self.spread(i, step, block, block)

    def turns(self, first=0, last=None):
        return [
            functools.partial(self.turn, i, step)
            for i in range(first, len(self.owns) if last is None else last)
            for step in range(1, self.outer)
            if self.modes[i] != INNER
        ]

    def land(self, i):
        for key in self.xc:
            if key[0] == i:
                self.xc[key].wait_recv()
        for copy in self.back[i]:
            copy.wait()

    def finish(self, first=0):
        for key in self.xc:
            if key[0] >= first:
                self.xc[key].wait_recv()
            self.xc[key].wait_send()
        for copy in self.zc:
            copy.wait_send()
        for i in self.back:
            if i >= first:
                for copy in self.back[i]:
                    copy.wait()


def fetch_outs(owns, outer, inner, modes):
    return [
        jax.ShapeDtypeStruct(
            (outer if mode == OUTER else outer * inner,) + own.shape[1:], own.dtype
        )
        for own, mode in zip(owns, modes)
    ]


def fetch_scratch(owns, outer, inner, modes):
    dma = pltpu.SemaphoreType.DMA
    count = max(len(owns), 1)
    return [
        pltpu.VMEM(own.shape if mode == INNER else own.shape[1:], own.dtype)
        for own, mode in zip(owns, modes)
    ] + [
        dma((count * outer,)),
        dma((count * outer,)),
        dma((count * outer * inner,)),
        dma((count * outer * inner,)),
        dma((count * (outer + 1),)),
    ]


class Push:
    def __init__(self, outer, inner, parts, outs, room, sems):
        count = len(parts)
        self.outer, self.inner, self.parts, self.outs = outer, inner, parts, outs
        self.froms, self.mine, self.sums = room[:count], room[count : 2 * count], room[2 * count :]
        self.xs, self.xr, self.zs, self.zr, self.ls, self.ks = sems
        self.dz, dx, t = place_of(inner)
        self.dx = dx
        near = [nearest(self.dz, outer, step) for step in range(outer)]
        self.source = near[:0:-1] + near[:1]
        self.zdev = [(source * inner + dx, t) for source in self.source]
        self.xdev = [(self.dz * inner + lax.rem(dx + j, inner), t) for j in range(1, inner)]
        self.xc, self.zc, self.loads, self.keeps = {}, [], {}, []

    def start(self, first=0, last=None):
        for i in range(first, len(self.parts) if last is None else last):
            for step, source in enumerate(self.source):
                for j in range(1, self.inner):
                    slot = source * self.inner + lax.rem(self.dx + j, self.inner)
                    at = (i * self.outer + step) * self.inner + j
                    self.xc[i, step, j] = send(
                        self.parts[i].at[slot],
                        self.froms[i].at[j - 1, step],
                        self.xs.at[at],
                        self.xr.at[at],
                        self.xdev[j - 1],
                    )
                self.loads[i, step] = pltpu.make_async_copy(
                    self.parts[i].at[source * self.inner + self.dx],
                    self.mine[i].at[step],
                    self.ls.at[i * self.outer + step],
                )
                self.loads[i, step].start()

    def turn(self, i, step):
        self.loads[i, step].wait()
        total = self.mine[i][step].astype(F32)
        for j in range(1, self.inner):
            self.xc[i, step, j].wait_recv()
            total = total + self.froms[i][j - 1, step].astype(F32)
        self.sums[i][step] = total.astype(self.sums[i].dtype)
        target = self.outs[i].at[self.dz]
        if step < self.outer - 1:
            away = lax.rem(self.source[step] - self.dz + self.outer, self.outer)
            at = i * self.outer + away
            self.zc.append(
                send(self.sums[i].at[step], target, self.zs.at[at], self.zr.at[at], self.zdev[step])
            )
        else:
            self.keeps.append(
                pltpu.make_async_copy(self.sums[i].at[step], target, self.ks.at[i])
            )
            self.keeps[-1].start()

    def turns(self):
        return [
            functools.partial(self.turn, i, step)
            for i in range(len(self.parts))
            for step in range(self.outer)
        ]

    def finish(self):
        for copy in self.zc:
            copy.wait_recv()
            copy.wait_send()
        for key in self.xc:
            self.xc[key].wait_send()
        for copy in self.keeps:
            copy.wait()


def push_outs(parts, outer):
    return [jax.ShapeDtypeStruct((outer,) + part.shape[1:], part.dtype) for part in parts]


def push_scratch(parts, outer, inner):
    dma = pltpu.SemaphoreType.DMA
    count = max(len(parts), 1)
    across_x = [pltpu.VMEM((inner - 1, outer) + part.shape[1:], part.dtype) for part in parts]
    own = [pltpu.VMEM((outer,) + part.shape[1:], part.dtype) for part in parts]
    return (
        across_x
        + own
        + own
        + [
            dma((count * outer * inner,)),
            dma((count * outer * inner,)),
            dma((count * outer,)),
            dma((count * outer,)),
            dma((count * outer,)),
            dma((count,)),
        ]
    )


class Cut:
    def __init__(self, refs):
        self.refs, self.at = refs, 0

    def __call__(self, count):
        self.at += count
        return self.refs[self.at - count : self.at]


class Mixer:
    def __init__(self, outer, inner, table, lines, mix, sems):
        self.lines, self.mix = lines, mix
        dx = lax.rem(lax.axis_index("dp"), inner)
        self.loads = [
            pltpu.make_async_copy(table.at[at * inner + dx], lines.at[at], sems.at[at])
            for at in range(outer)
        ]
        for load in self.loads:
            load.start()

    def turn(self):
        for at, load in enumerate(self.loads):
            load.wait()
            self.mix[at] = jnp.transpose(self.lines[at]).reshape(self.mix.shape[1:])


def ffn_forward_kernel(outer, inner, kinds, modes, level, row, *refs):
    count = len(modes)
    cut = Cut(refs)
    resid, gain, mix_any, w_in_any, w_down_any = cut(5)
    owns = cut(count)
    out, b_out, gu_out = cut(3)
    fetched = cut(count)
    w_in, w_down, b, gu, part, mix_rows, mix = cut(7)
    room, take_sems, give_sems = cut(5), cut(6), cut(6)
    load_sem, keep_b, keep_gu, load_mix = cut(4)
    extra = Fetch(outer, inner, owns, fetched, cut(count), cut(5), modes) if count else None
    rows, width = resid.shape
    third = w_down.shape[1]
    slim = third // kinds
    loads = [
        pltpu.make_async_copy(w_in_any, w_in, load_sem.at[0]),
        pltpu.make_async_copy(w_down_any, w_down, load_sem.at[1]),
    ]
    for load in loads:
        load.start()
    take = Gather(outer, inner, b, take_sems, PARTS)
    give = Scatter(outer, inner, part, room, give_sems, PARTS)
    size = rows // PARTS
    mixer = Mixer(outer, inner, mix_any, mix_rows, mix, load_mix)
    x = resid[...]
    inverse = lax.rsqrt(jnp.mean(x * x, axis=-1, keepdims=True) + EPSILON)
    b[take.dz, take.t] = (x * inverse * gain[row : row + 1]).astype(BF16)
    meet(take.friends() + (extra.xdev if count else []))
    keeps = []

    def compute(step):
        source, q = take.origin(step), step % PARTS
        here = take.rows(step)
        if step == 0:
            for load in loads:
                load.wait()
        rows_in = b[source, :, here].reshape(4 * size, width)
        scale = mix[source, :, here].reshape(4 * size, mix.shape[-1])
        both = dot(rows_in, w_in[...])
        gu[source, q] = both.astype(BF16)
        gate, up = both[:, :third], both[:, third:]
        hidden = gate * jax.nn.sigmoid(gate) * up
        pieces = []
        for e in range(kinds):
            piece = hidden[:, e * slim : (e + 1) * slim]
            if e < kinds - 1:
                at = level * (kinds - 1) + e
                piece = piece * scale[:, at : at + 1]
            pieces.append(piece.astype(BF16))
        hidden = jnp.concatenate(pieces, axis=1)
        sent = dot_nt(hidden, w_down[...]).astype(BF16)
        part[source, :, :, here] = sent.reshape(2, 2, size, width)
        if q == PARTS - 1:
            at = step // PARTS
            keeps.append(pltpu.make_async_copy(b.at[source], b_out.at[source], keep_b.at[at]))
            keeps.append(pltpu.make_async_copy(gu.at[source], gu_out.at[source], keep_gu.at[at]))
            keeps[-1].start()
            keeps[-2].start()

    def after():
        if count:
            extra.start()
            extra.settle()

    pipeline(take, give, compute, mixer.turn, after, extra.turns() if count else [], [])
    out[...] = resid[...] + give.total()
    take.finish()
    give.finish()
    if count:
        extra.finish()
    for keep in keeps:
        keep.wait()


def ffn_forward(
    resid, gain, level, row, kinds, mix, w_in, w_down, owns, modes, outer, inner, ident
):
    dma = pltpu.SemaphoreType.DMA
    rows, width = resid.shape
    third = w_down.shape[1]
    count = len(owns)
    return pl.pallas_call(
        functools.partial(ffn_forward_kernel, outer, inner, kinds, modes, level, row),
        out_shape=[
            jax.ShapeDtypeStruct((rows, width), F32),
            jax.ShapeDtypeStruct((outer, 4, rows, width), BF16),
            jax.ShapeDtypeStruct((outer, PARTS, 4 * rows // PARTS, 2 * third), BF16),
        ]
        + fetch_outs(owns, outer, inner, modes),
        in_specs=[VMEM, VMEM, ANY, ANY, ANY] + [ANY] * count,
        out_specs=[VMEM, ANY, ANY] + [ANY] * count,
        scratch_shapes=[
            pltpu.VMEM(w_in.shape, BF16),
            pltpu.VMEM(w_down.shape, BF16),
            pltpu.VMEM((outer, 4, rows, width), BF16),
            pltpu.VMEM((outer, PARTS, 4 * rows // PARTS, 2 * third), BF16),
            pltpu.VMEM((outer, 2, 2, rows, width), BF16),
            pltpu.VMEM((outer,) + mix.shape[1:], F32),
            pltpu.VMEM((outer, 4, rows, mix.shape[1]), F32),
        ]
        + scatter_room(outer, rows, width, PARTS)
        + gather_sems(outer, PARTS)
        + scatter_sems(outer, PARTS)
        + [dma((2,)), dma((outer,)), dma((outer,)), dma((outer,))]
        + (fetch_scratch(owns, outer, inner, modes) if count else []),
        compiler_params=pltpu.CompilerParams(
            collective_id=ident, has_side_effects=True, vmem_limit_bytes=62 << 20
        ),
        name="ffn_forward",
    )(resid, gain, mix, w_in, w_down, *owns)


def ffn_backward_kernel(outer, inner, kinds, count, level, row, *refs):
    cut = Cut(refs)
    grad_y, resid, gain, mix_any, w_in_any, w_down_any, b_any, gu_any = cut(8)
    parts = cut(count)
    out, gain_out, grad_in, grad_down = cut(4)
    pushed = cut(count)
    w_in, w_down, b, gb, gu, dgu, hid, flip, part, mix_rows, mix = cut(11)
    room, take_sems, give_sems = cut(5), cut(6), cut(6)
    load_sem, load_gu, load_mix = cut(3)
    extra = Push(outer, inner, parts, pushed, cut(3 * count), cut(6)) if count else None
    rows, width = resid.shape
    tall = outer * 4 * rows
    third = w_down.shape[1]
    slim = third // kinds
    loads = [
        pltpu.make_async_copy(source, target, load_sem.at[i])
        for i, (source, target) in enumerate(
            ((b_any, b), (w_down_any, w_down), (w_in_any, w_in))
        )
    ]
    for load in loads:
        load.start()
    take = Gather(outer, inner, gb, take_sems, PARTS)
    give = Scatter(outer, inner, part, room, give_sems, PARTS)
    size = rows // PARTS
    mixer = Mixer(outer, inner, mix_any, mix_rows, mix, load_mix)
    fills = [
        pltpu.make_async_copy(gu_any.at[source], gu.at[source], load_gu.at[step])
        for step, source in enumerate(take.source)
    ]
    for fill in fills:
        fill.start()
    gb[take.dz, take.t] = grad_y[...].astype(BF16)
    meet(take.friends() + (extra.xdev if count else []))

    def compute(step):
        source, q = take.origin(step), step % PARTS
        here = take.rows(step)
        if step == 0:
            loads[1].wait()
            loads[2].wait()
        if q == 0:
            fills[step // PARTS].wait()
        rows_in = gb[source, :, here].reshape(4 * size, width)
        mixed = mix[source, :, here].reshape(4 * size, mix.shape[-1])
        grad_hidden = dot(rows_in, w_down[...])
        both = gu[source, q].astype(F32)
        gate, up = both[:, :third], both[:, third:]
        sigma = jax.nn.sigmoid(gate)
        act = gate * sigma
        slope = sigma * (1.0 + gate * (1.0 - sigma))
        hidden, grad_gate, grad_up = act * up, grad_hidden * up * slope, grad_hidden * act
        for e in range(kinds):
            cols = slice(e * slim, (e + 1) * slim)
            more = slice(third + e * slim, third + (e + 1) * slim)
            at = level * (kinds - 1) + e
            scale = mixed[:, at : at + 1] if e < kinds - 1 else 1.0
            hid[source, q, :, cols] = (hidden[:, cols] * scale).astype(BF16)
            dgu[source, q, :, cols] = (grad_gate[:, cols] * scale).astype(BF16)
            dgu[source, q, :, more] = (grad_up[:, cols] * scale).astype(BF16)
        sent = dot_nt(dgu[source, q], w_in[...]).astype(BF16)
        part[source, :, :, here] = sent.reshape(2, 2, size, width)

    def turned(table):
        @pl.loop(0, outer)
        def _(source):
            for q in range(PARTS):
                block = table[source, :, q * size : (q + 1) * size].reshape(4 * size, width)
                at = pl.multiple_of((source * PARTS + q) * 4 * size, 4 * size)
                flip[:, pl.ds(at, 4 * size)] = jnp.transpose(block)

    def weigh(target, source, low, high):
        values = source[...].reshape(tall, source.shape[-1])

        @pl.loop(0, width // 256)
        def _(at):
            here = pl.ds(pl.multiple_of(at * 256, 256), 256)
            target[here, low:high] = dot(flip[here, :], values[:, low:high]).astype(BF16)

    def begin():
        if count:
            extra.start()
        mixer.turn()
        loads[0].wait()
        turned(b)

    def pieces(total):
        return [(low, min(low + 256, total)) for low in range(0, total, 256)]

    late = [functools.partial(weigh, grad_in, dgu, *span) for span in pieces(2 * third)]
    late += [functools.partial(turned, gb)]
    late += [functools.partial(weigh, grad_down, hid, *span) for span in pieces(third)]
    pipeline(take, give, compute, begin, lambda: None, extra.turns() if count else [], late)
    grad_b = give.total()
    x = resid[...]
    inverse = lax.rsqrt(jnp.mean(x * x, axis=-1, keepdims=True) + EPSILON)
    unit = x * inverse
    gain_out[...] = jnp.sum(grad_b * unit, axis=0, keepdims=True)
    out[...] = grad_y[...].astype(F32) + norm_back(grad_b, gain[row : row + 1], unit, inverse)
    take.finish()
    give.finish()
    if count:
        extra.finish()


def ffn_backward(
    grad_y, resid, gain, level, row, kinds, mix, w_in, w_down, b, both, parts, outer, inner, ident
):
    dma = pltpu.SemaphoreType.DMA
    rows, width = resid.shape
    third = w_down.shape[1]
    count = len(parts)
    return pl.pallas_call(
        functools.partial(ffn_backward_kernel, outer, inner, kinds, count, level, row),
        out_shape=[
            jax.ShapeDtypeStruct((rows, width), F32),
            jax.ShapeDtypeStruct((1, width), F32),
            jax.ShapeDtypeStruct((width, 2 * third), BF16),
            jax.ShapeDtypeStruct((width, third), BF16),
        ]
        + push_outs(parts, outer),
        in_specs=[VMEM, VMEM, VMEM, ANY, ANY, ANY, ANY, ANY] + [ANY] * count,
        out_specs=[VMEM, VMEM, VMEM, VMEM] + [ANY] * count,
        scratch_shapes=[
            pltpu.VMEM(w_in.shape, BF16),
            pltpu.VMEM(w_down.shape, BF16),
            pltpu.VMEM((outer, 4, rows, width), BF16),
            pltpu.VMEM((outer, 4, rows, width), BF16),
            pltpu.VMEM((outer, PARTS, 4 * rows // PARTS, 2 * third), BF16),
            pltpu.VMEM((outer, PARTS, 4 * rows // PARTS, 2 * third), BF16),
            pltpu.VMEM((outer, PARTS, 4 * rows // PARTS, third), BF16),
            pltpu.VMEM((width, outer * 4 * rows), BF16),
            pltpu.VMEM((outer, 2, 2, rows, width), BF16),
            pltpu.VMEM((outer,) + mix.shape[1:], F32),
            pltpu.VMEM((outer, 4, rows, mix.shape[1]), F32),
        ]
        + scatter_room(outer, rows, width, PARTS)
        + gather_sems(outer, PARTS)
        + scatter_sems(outer, PARTS)
        + [dma((3,)), dma((outer,)), dma((outer,))]
        + (push_scratch(parts, outer, inner) if count else []),
        compiler_params=pltpu.CompilerParams(
            collective_id=ident, has_side_effects=True, vmem_limit_bytes=63 << 20
        ),
        name="ffn_backward",
    )(grad_y, resid, gain, mix, w_in, w_down, b, both, *parts)


def swap_halves(values):
    width = values.shape[1]
    lane = lax.broadcasted_iota(jnp.int32, values.shape, 1)
    low = lax.rem(lane, HD) < HD // 2
    return jnp.where(
        low, pltpu.roll(values, width - HD // 2, 1), pltpu.roll(values, HD // 2, 1)
    )


def allowed_rows(marks, spot, top):
    del top
    return (spot >= marks[:, 1:2]) & (spot <= marks[:, 0:1])


def attn_forward_kernel(outer, inner, modes, lead, row, *refs):
    count = len(modes)
    dp = outer * inner
    cut = Cut(refs)
    x_in, tables, marks, spot = cut(4)
    gain, weight = (None, None) if lead else cut(2)
    owns = cut(count)
    out, a_out, qk_out, v_out, lse_out, att_out = cut(6)
    gain_out = cut(1)[0] if lead else None
    fetched = cut(count)
    w, a, qk, v, att, part = cut(6)
    room, take_sems, give_sems = cut(5), cut(6), cut(6)
    load_sem, keep_sem = cut(2)
    extra = Fetch(outer, inner, owns, fetched, cut(count), cut(5), modes)
    rows, width = x_in.shape
    heads_width = w.shape[1] // 4
    heads = heads_width // HD
    take = Gather(1, dp, a, take_sems)
    give = Scatter(1, dp, part, room, give_sems)
    x = x_in[...].astype(F32)
    inverse = lax.rsqrt(jnp.mean(x * x, axis=-1, keepdims=True) + EPSILON)
    friends = take.friends() + extra.zdev[1:] + extra.xdev
    if lead:
        (gains,) = cut(1)
        meet(friends)
        extra.start(0, 2)
        extra.start(2, None, False)
        extra.settle()
        for turn in extra.turns(0, 1):
            turn()
        extra.land(0)
        load = pltpu.make_async_copy(fetched[0], gains, load_sem.at[0])
        load.start()
        load.wait()
        gain_out[...] = jnp.sum(gains[...], axis=0)
        a[0, take.t] = (x * inverse * gain_out[row : row + 1]).astype(BF16)
        turns = extra.turns(1, 2)
        turns[0]()
        take.start()
        for turn in turns[1:]:
            turn()
        for i in range(2, count):
            extra.aside(i)
        extra.land(1)
        slot = fetched[1].shape[1]
        loads = [
            pltpu.make_async_copy(
                fetched[1].at[at], w.at[pl.ds(at * slot, slot)], load_sem.at[at]
            )
            for at in range(dp)
        ]
        for load in loads:
            load.start()
        for load in loads:
            load.wait()
    else:
        load = pltpu.make_async_copy(weight, w, load_sem.at[0])
        load.start()
        a[0, take.t] = (x * inverse * gain[row : row + 1]).astype(BF16)
        meet(friends)
        take.start()
        extra.start()
        extra.settle()
        load.wait()
    done = 2 if lead else 0
    turns = extra.turns(done)

    def project(block):
        both = dot(a[0, block], w[:, : 3 * heads_width])
        raw = both[:, : 2 * heads_width]
        times = 2 * heads_width // tables.shape[-1]
        cosine = jnp.concatenate([tables[0, block]] * times, axis=1)
        sine = jnp.concatenate([tables[1, block]] * times, axis=1)
        qk[block] = (raw * cosine + swap_halves(raw) * sine).astype(BF16)
        v[block] = both[:, 2 * heads_width :].astype(BF16)

    project(take.t)
    take.complete(0)
    for other in range(1, 4):
        project(lax.rem(take.t + other, 4))
    keeps = [pltpu.make_async_copy(a.at[0], a_out, keep_sem.at[0])]
    keeps.append(pltpu.make_async_copy(qk, qk_out, keep_sem.at[1]))
    keeps.append(pltpu.make_async_copy(v, v_out, keep_sem.at[2]))
    for keep in keeps:
        keep.start()

    def attend(block):
        keys = qk[...].reshape(4 * rows, 2 * heads_width)
        values = v[...].reshape(4 * rows, heads_width)
        allowed = allowed_rows(marks[block], spot[...], 0)
        pieces = []
        for head in range(heads):
            here = slice(head * HD, (head + 1) * HD)
            there = slice(heads_width + head * HD, heads_width + (head + 1) * HD)
            scores = dot_nt(qk[block, :, here], keys[:, there])
            scores = jnp.where(allowed, scores * HD ** (-0.5), MASKED_SCORE)
            top = jnp.max(scores, axis=-1, keepdims=True)
            expo = jnp.exp(scores - top)
            total = jnp.sum(expo, axis=-1, keepdims=True)
            probs = (expo / total).astype(BF16)
            lse_out[block, :, head : head + 1] = top + jnp.log(total)
            pieces.append(dot(probs, values[:, here]).astype(BF16))
        att[block] = jnp.concatenate(pieces, axis=1)
        sent = dot_nt(att[block], w[:, 3 * heads_width :]).astype(BF16)
        part[0, lax.div(block, 2), lax.rem(block, 2)] = sent

    y, c = give.y, give.c
    attend(2 * (1 - y) + 1 - c)
    attend(2 * y + 1 - c)
    give.core_send(0)
    turns[0]()
    attend(2 * (1 - y) + c)
    attend(2 * y + c)
    give.pair_send(0)
    for turn in turns[1:]:
        turn()
    keeps.append(pltpu.make_async_copy(att, att_out, keep_sem.at[3]))
    keeps[-1].start()
    out[...] = x_in[...].astype(F32) + give.total()
    take.finish()
    give.finish()
    extra.finish(done)
    for keep in keeps:
        keep.wait()


def attn_forward(
    x, gain, row, weight, tables, marks, spot, owns, modes, outer, inner, ident
):
    count = len(owns)
    dma = pltpu.SemaphoreType.DMA
    rows, width = x.shape
    lead = weight is None
    shape = (width, owns[1].shape[-1]) if lead else weight.shape
    slim = shape[1] // 4
    extras = [] if lead else [gain, weight]
    kept = [(4, rows, width), (4, rows, 2 * slim), (4, rows, slim)]
    return pl.pallas_call(
        functools.partial(attn_forward_kernel, outer, inner, modes, lead, row),
        out_shape=[jax.ShapeDtypeStruct((rows, width), F32)]
        + [jax.ShapeDtypeStruct(shape, BF16) for shape in kept]
        + [
            jax.ShapeDtypeStruct((4, rows, 8), F32),
            jax.ShapeDtypeStruct((4, rows, slim), BF16),
        ]
        + ([jax.ShapeDtypeStruct((8, width), F32)] if lead else [])
        + fetch_outs(owns, outer, inner, modes),
        in_specs=[VMEM] * 4 + ([] if lead else [VMEM, ANY]) + [ANY] * count,
        out_specs=[VMEM, ANY, ANY, ANY, VMEM, ANY] + [VMEM] * lead + [ANY] * count,
        scratch_shapes=[
            pltpu.VMEM(shape, BF16),
            pltpu.VMEM((1, 4, rows, width), BF16),
            pltpu.VMEM(kept[1], BF16),
            pltpu.VMEM(kept[2], BF16),
            pltpu.VMEM(kept[2], BF16),
            pltpu.VMEM((1, 2, 2, rows, width), BF16),
        ]
        + scatter_room(1, rows, width)
        + gather_sems(1)
        + scatter_sems(1)
        + [dma((outer * inner,)), dma((4,))]
        + fetch_scratch(owns, outer, inner, modes)
        + ([pltpu.VMEM((outer * inner,) + owns[0].shape[1:], F32)] if lead else []),
        compiler_params=pltpu.CompilerParams(collective_id=ident, has_side_effects=True),
        name="attn_forward",
    )(x, tables, marks, spot, *extras, *owns)


def attn_backward_kernel(outer, inner, count, last, row, *refs):
    dp = outer * inner
    cut = Cut(refs)
    grad_in, x_in, gain, weight, tables, marks, spot = cut(7)
    a_in, qk_in, v_in, lse, att_in = cut(5)
    others = cut(last)
    parts = cut(count)
    out, gain_out = cut(2)
    (grad_w,) = (None,) if last else cut(1)
    total = count + 1 if last else count
    pushed = cut(total)
    w, a, qk, v, att, ga, g_att, raw, part = cut(9)
    room, take_sems, give_sems = cut(5), cut(6), cut(6)
    (load_sem,) = cut(1)
    room_x, sems_x = cut(3 * total), cut(6)
    if last:
        held, from_t, from_d, ts, tr, ds, dr = cut(7)
        parts = tuple(parts) + (held,)
    extra = Push(outer, inner, parts, pushed, room_x, sems_x)
    turns = extra.turns()
    friends = []
    rows, width = x_in.shape
    tall = 4 * rows
    heads_width = w.shape[1] // 4
    heads = heads_width // HD
    loads = [
        pltpu.make_async_copy(source, target, load_sem.at[i])
        for i, (source, target) in enumerate(
            ((weight, w), (qk_in, qk), (v_in, v), (att_in, att), (a_in, a))
        )
    ]
    for load in loads:
        load.start()
    take = Gather(1, dp, ga, take_sems)
    give = Scatter(1, dp, part, room, give_sems)
    ga[0, take.t] = grad_in[...].astype(BF16)
    if last:
        team = [(take.d, lax.rem(take.t + k, 4)) for k in range(1, 4)]
        peers = [(lax.rem(take.d + k, dp), take.t) for k in range(1, dp)]
        friends = team + peers
    else:
        friends = take.friends() + extra.zdev[:-1] + extra.xdev
    meet(friends)
    take.start()
    extra.start(0, count)
    for load in loads:
        load.wait()
    take.complete(0)
    turns[0]()
    grads = ga[...].reshape(tall, width)
    g_att[...] = dot(grads, w[:, 3 * heads_width :]).astype(BF16)
    all_qk = qk[...].reshape(tall, 2 * heads_width)
    all_v = v[...].reshape(tall, heads_width)
    all_marks = marks[...].reshape(tall, marks.shape[-1])
    all_lse = lse[...].reshape(tall, lse.shape[-1])
    allowed = allowed_rows(all_marks, spot[...], 0)
    q_grads, k_grads, v_grads = [], [], []
    for head in range(heads):
        here = slice(head * HD, (head + 1) * HD)
        there = slice(heads_width + head * HD, heads_width + (head + 1) * HD)
        query, key = all_qk[:, here], all_qk[:, there]
        scores = dot_nt(query, key)
        scores = jnp.where(allowed, scores * HD ** (-0.5), MASKED_SCORE)
        probs = jnp.exp(scores - all_lse[:, head : head + 1])
        grad_probs = dot_nt(g_att[:, here], all_v[:, here])
        inner = jnp.sum(grad_probs * probs, axis=-1, keepdims=True)
        grad_scores = (probs * (grad_probs - inner)).astype(BF16)
        v_grads.append(dot_tn(probs.astype(BF16), g_att[:, here]).astype(BF16))
        q_grads.append(dot(grad_scores, key))
        k_grads.append(dot_tn(grad_scores, query))
    rotated = jnp.concatenate(q_grads + k_grads, axis=1) * HD ** (-0.5)
    times = 2 * heads_width // tables.shape[-1]
    cosine = jnp.concatenate([tables[0].reshape(tall, -1)] * times, axis=1)
    sine = jnp.concatenate([tables[1].reshape(tall, -1)] * times, axis=1)
    raw[:, : 2 * heads_width] = (rotated * cosine - swap_halves(rotated) * sine).astype(BF16)
    raw[:, 2 * heads_width :] = jnp.concatenate(v_grads, axis=1)
    def back(block):
        at = pl.ds(pl.multiple_of(block * rows, rows), rows)
        sent = dot_nt(raw[at, :], w[:, : 3 * heads_width]).astype(BF16)
        part[0, lax.div(block, 2), lax.rem(block, 2)] = sent

    turns[1]()
    y, c = give.y, give.c
    back(2 * (1 - y) + 1 - c)
    back(2 * y + 1 - c)
    give.core_send(0)
    back(2 * (1 - y) + c)
    back(2 * y + c)
    give.pair_send(0)
    turns[2]()
    grad_raw = dot_tn(a[...].reshape(tall, width), raw[...]).astype(BF16)
    grad_out = dot_tn(grads, att[...].reshape(tall, heads_width)).astype(BF16)
    if last:
        held[:, :, : 3 * heads_width] = grad_raw.reshape(dp, width // dp, -1)
        held[:, :, 3 * heads_width :] = grad_out.reshape(dp, width // dp, -1)
    else:
        grad_w[:, : 3 * heads_width] = grad_raw
        grad_w[:, 3 * heads_width :] = grad_out
    grad_a = give.total()
    x = x_in[...].astype(F32)
    inverse = lax.rsqrt(jnp.mean(x * x, axis=-1, keepdims=True) + EPSILON)
    unit = x * inverse
    part_gain = jnp.sum(grad_a * unit, axis=0, keepdims=True)
    if last:
        from_t[take.t] = jnp.zeros(from_t.shape[1:], F32)
        from_t[take.t, row : row + 1] = part_gain
        for at, other in zip([at for at in range(last + 1) if at != row], others):
            from_t[take.t, at : at + 1] = other[...]
    else:
        gain_out[...] = part_gain
    out[...] = grad_in[...] + norm_back(grad_a, gain[row : row + 1], unit, inverse)
    if last:
        extra.start(count, total)
        mine = from_t.at[take.t]
        copies = [
            send(mine, mine, ts.at[k], tr.at[k], device) for k, device in enumerate(team)
        ]
        for copy in copies:
            copy.wait_recv()
        from_d[take.d] = jnp.sum(from_t[...], axis=0)
        turns[3]()
        mine = from_d.at[take.d]
        more = [send(mine, mine, ds.at[k], dr.at[k], device) for k, device in enumerate(peers)]
        for turn in turns[4:]:
            turn()
        for copy in more:
            copy.wait_recv()
        gain_out[...] = jnp.sum(from_d[...], axis=0)
        for copy in copies + more:
            copy.wait_send()
    else:
        for turn in turns[3:]:
            turn()
    take.finish()
    give.finish()
    extra.finish()


def attn_backward(
    grad, x, gain, row, weight, tables, marks, spot, kept, others, parts, outer, inner, ident
):
    count = len(parts)
    dma = pltpu.SemaphoreType.DMA
    rows, width = x.shape
    slim = weight.shape[1] // 4
    dp = outer * inner
    last = len(others)
    whole = jax.ShapeDtypeStruct((dp, width // dp, 4 * slim), BF16)
    moved = list(parts) + ([whole] if last else [])
    wide = (8, width) if last else (1, width)
    return pl.pallas_call(
        functools.partial(attn_backward_kernel, outer, inner, count, last, row),
        out_shape=[
            jax.ShapeDtypeStruct((rows, width), F32),
            jax.ShapeDtypeStruct(wide, F32),
        ]
        + ([] if last else [jax.ShapeDtypeStruct(weight.shape, BF16)])
        + push_outs(moved, outer),
        in_specs=[VMEM, VMEM, VMEM, ANY, VMEM, VMEM, VMEM, ANY, ANY, ANY, VMEM, ANY]
        + [VMEM] * last
        + [ANY] * count,
        out_specs=[VMEM, VMEM] + ([] if last else [VMEM]) + [ANY] * len(moved),
        scratch_shapes=[
            pltpu.VMEM(weight.shape, BF16),
            pltpu.VMEM((4, rows, width), BF16),
            pltpu.VMEM((4, rows, 2 * slim), BF16),
            pltpu.VMEM((4, rows, slim), BF16),
            pltpu.VMEM((4, rows, slim), BF16),
            pltpu.VMEM((1, 4, rows, width), BF16),
            pltpu.VMEM((4 * rows, slim), BF16),
            pltpu.VMEM((4 * rows, 3 * slim), BF16),
            pltpu.VMEM((1, 2, 2, rows, width), BF16),
        ]
        + scatter_room(1, rows, width)
        + gather_sems(1)
        + scatter_sems(1)
        + [dma((5,))]
        + push_scratch(moved, outer, inner)
        + (
            [
                pltpu.VMEM(whole.shape, BF16),
                pltpu.VMEM((4, 8, width), F32),
                pltpu.VMEM((dp, 8, width), F32),
                dma((3,)),
                dma((3,)),
                dma((dp,)),
                dma((dp,)),
            ]
            if last
            else []
        ),
        compiler_params=pltpu.CompilerParams(
            collective_id=ident, has_side_effects=True, vmem_limit_bytes=62 << 20
        ),
        name="attn_backward",
    )(grad, x, gain, weight, tables, marks, spot, *kept, *others, *parts)


def pack_kernel(outer, dp, *refs):
    cut = Cut(refs)
    place, lengths, freqs, ids, gates, gain_attn, gain_ffn = cut(7)
    attn_any, ffn_any = cut(4), cut(6)
    tables, marks, spot, gains, mix = cut(5)
    layers, rows = gain_attn.shape
    attn_out, in_out, down_out = cut(layers), cut(layers), cut(layers)
    attn_in, ffn_in = cut(4), cut(6)
    attn_held, in_held, down_held = cut(layers), cut(layers), cut(layers)
    load_attn, load_ffn, keep = cut(3)
    loads_attn = [
        pltpu.make_async_copy(source, target, load_attn.at[i])
        for i, (source, target) in enumerate(zip(attn_any, attn_in))
    ]
    loads_ffn = [
        [
            pltpu.make_async_copy(source.at[level], target.at[level], load_ffn.at[level, i])
            for i, (source, target) in enumerate(zip(ffn_any, ffn_in))
        ]
        for level in range(layers)
    ]
    for load in sum(loads_ffn, loads_attn):
        load.start()
    count = place.shape[1]
    where = place[...]
    begins, end = jnp.zeros_like(where), 0
    for doc in range(lengths.shape[1]):
        end = end + lengths[0, doc]
        begins = begins + jnp.where(where >= end, lengths[0, doc], 0)
    spot[...] = where.astype(F32)
    lines = jnp.concatenate([where.astype(F32), begins.astype(F32)] * 4, axis=0)
    marks[...] = jnp.transpose(lines).reshape(4, count // 4, 8)
    angles = (where - begins).astype(F32) * freqs[...]
    cosine, sine = jnp.cos(angles), jnp.sin(angles)
    tables[0] = jnp.transpose(jnp.concatenate([cosine] * 4, axis=0)).reshape(4, count // 4, 128)
    tables[1] = jnp.transpose(jnp.concatenate([-sine, sine, -sine, sine], axis=0)).reshape(
        4, count // 4, 128
    )
    experts = mix.shape[0] // layers
    for level in range(layers):
        for e in range(experts):
            row = jnp.zeros((1, count), F32)
            for slot in range(ids.shape[1]):
                here = slice(slot, slot + 1)
                row = row + jnp.where(ids[level, here] == e, gates[level, here], 0.0)
            at = level * experts + e
            mix[at : at + 1] = row
    d = lax.axis_index("dp")
    gains[...] = jnp.zeros_like(gains)
    lane = lax.broadcasted_iota(jnp.int32, (layers, gains.shape[1]), 1)
    inside = (lane >= d * rows) & (lane < (d + 1) * rows)
    for i, gain in enumerate((gain_attn, gain_ffn)):
        wide = jnp.concatenate([gain[...].astype(BF16).astype(F32)] * dp, axis=1)
        gains[i * layers : (i + 1) * layers] = jnp.where(inside, wide, 0.0)
    keeps = []

    def leave(held, target):
        keeps.append(pltpu.make_async_copy(held, target, keep.at[len(keeps)]))
        keeps[-1].start()

    for load in loads_attn:
        load.wait()
    quarter = attn_in[0].shape[2]
    for level in range(layers):
        for i in range(4):
            values = attn_in[i][level]
            values = jnp.transpose(values) if i == 3 else values
            attn_held[level][0, :, i * quarter : (i + 1) * quarter] = values.astype(BF16)
        leave(attn_held[level], attn_out[level])
    for level in range(layers):
        for load in loads_ffn[level]:
            load.wait()
        slim = ffn_in[1].shape[2] // outer
        for group, (held, target) in enumerate(
            ((in_held, in_out), (in_held, in_out), (down_held, down_out))
        ):
            base = (experts + 1) * slim if group == 1 else 0
            for e in range(experts + 1):
                for k in range(outer):
                    cols = slice(k * slim, (k + 1) * slim)
                    if e < experts:
                        values = ffn_in[2 * group][level, e, :, cols]
                    else:
                        values = ffn_in[2 * group + 1][level, :, cols]
                    held[level][k, :, base + e * slim : base + (e + 1) * slim] = values.astype(
                        BF16
                    )
            if group:
                leave(held[level], target[level])
    for copy in keeps:
        copy.wait()


def pack(place, lengths, ids, gates, gain_attn, gain_ffn, attn, ffn, outer, dp):
    dma = pltpu.SemaphoreType.DMA
    layers, rows = gain_attn.shape
    count = place.shape[1]
    width = dp * rows
    experts = ffn[0].shape[1]
    slim = ffn[1].shape[2] // outer
    freqs = (10000.0 ** (-np.arange(HD // 2) / (HD // 2))).astype(np.float32)[:, None]
    blocks = (
        [(1, rows, 4 * attn[0].shape[2])] * layers
        + [(outer, rows, 2 * (experts + 1) * slim)] * layers
        + [(outer, rows, (experts + 1) * slim)] * layers
    )
    return pl.pallas_call(
        functools.partial(pack_kernel, outer, dp),
        out_shape=[
            jax.ShapeDtypeStruct((2, 4, count // 4, 128), F32),
            jax.ShapeDtypeStruct((4, count // 4, 8), F32),
            jax.ShapeDtypeStruct((1, count), F32),
            jax.ShapeDtypeStruct((8, width), F32),
            jax.ShapeDtypeStruct((layers * experts, count), F32),
        ]
        + [jax.ShapeDtypeStruct(block, BF16) for block in blocks],
        in_specs=[VMEM, pl.BlockSpec(memory_space=pltpu.SMEM)] + [VMEM] * 5 + [ANY] * 10,
        out_specs=[VMEM] * 5 + [ANY] * len(blocks),
        scratch_shapes=[pltpu.VMEM(m.shape, F32) for m in attn + ffn]
        + [pltpu.VMEM(block, BF16) for block in blocks]
        + [dma((4,)), dma((layers, 6)), dma((len(blocks),))],
        compiler_params=pltpu.CompilerParams(vmem_limit_bytes=62 << 20),
        name="pack",
    )(place, lengths, jnp.asarray(freqs), ids, gates, gain_attn, gain_ffn, *attn, *ffn)


def unpack_kernel(outer, layers, experts, *refs):
    cut = Cut(refs)
    in_any, down_any, attn_any = cut(layers), cut(layers), cut(layers)
    attn_out, ffn_out = cut(4), cut(6)
    in_v, down_v, attn_v = cut(layers), cut(layers), cut(layers)
    attn_held, ffn_held = cut(4), cut(6)
    load_sem, keep_attn, keep_ffn = cut(3)
    loads = [
        [
            pltpu.make_async_copy(source[level], target[level], load_sem.at[level, i])
            for i, (source, target) in enumerate(
                ((in_any, in_v), (down_any, down_v), (attn_any, attn_v))
            )
        ]
        for level in range(layers)
    ]
    for level in reversed(range(layers)):
        for load in loads[level]:
            load.start()
    keeps = []

    def leave(held, target, sem):
        keeps.append(pltpu.make_async_copy(held, target, sem))
        keeps[-1].start()

    slim = ffn_held[1].shape[2] // outer
    quarter = attn_held[0].shape[2]
    for level in reversed(range(layers)):
        for load in loads[level]:
            load.wait()
        for group, source in enumerate((in_v, in_v, down_v)):
            base = (experts + 1) * slim if group == 1 else 0
            for e in range(experts + 1):
                for k in range(outer):
                    cols = slice(k * slim, (k + 1) * slim)
                    values = source[level][k, :, base + e * slim : base + (e + 1) * slim]
                    if e < experts:
                        ffn_held[2 * group][level, e, :, cols] = values.astype(F32)
                    else:
                        ffn_held[2 * group + 1][level, :, cols] = values.astype(F32)
            for i in (2 * group, 2 * group + 1):
                leave(ffn_held[i].at[level], ffn_out[i].at[level], keep_ffn.at[level, i])
        total = jnp.sum(attn_v[level][...].astype(F32), axis=0)
        for i in range(4):
            values = total[:, i * quarter : (i + 1) * quarter]
            attn_held[i][level] = jnp.transpose(values) if i == 3 else values
            leave(attn_held[i].at[level], attn_out[i].at[level], keep_attn.at[level, i])
    for copy in keeps:
        copy.wait()


def unpack(pushed_in, pushed_down, pushed_attn, experts):
    dma = pltpu.SemaphoreType.DMA
    layers = len(pushed_in)
    outer, rows, third = pushed_down[0].shape
    full = outer * third // (experts + 1)
    quarter = pushed_attn[0].shape[2] // 4
    many, one = (layers, experts, rows, full), (layers, rows, full)
    shapes = [(layers, rows, quarter)] * 3 + [(layers, quarter, rows)] + [many, one] * 3
    moved = pushed_in + pushed_down + pushed_attn
    return pl.pallas_call(
        functools.partial(unpack_kernel, outer, layers, experts),
        out_shape=[jax.ShapeDtypeStruct(shape, F32) for shape in shapes],
        in_specs=[ANY] * len(moved),
        out_specs=[ANY] * 10,
        scratch_shapes=[pltpu.VMEM(part.shape, BF16) for part in moved]
        + [pltpu.VMEM(shape, F32) for shape in shapes]
        + [dma((layers, 3)), dma((layers, 4)), dma((layers, 6))],
        compiler_params=pltpu.CompilerParams(vmem_limit_bytes=62 << 20),
        name="unpack",
    )(*moved)


def layout(place_row, length_row):
    ends = jnp.cumsum(length_row, dtype=jnp.int32)
    after = place_row[:, None] >= ends[None, :]
    begins = jnp.sum(jnp.where(after, length_row[None, :], 0), axis=1, dtype=jnp.int32)
    return place_row - begins


def rope_tables(position):
    half_width = HD // 2
    freqs = 10000.0 ** (-jnp.arange(half_width, dtype=F32) / half_width)
    angles = position.astype(F32)[:, None] * freqs[None, :]
    cosine, sine = jnp.cos(angles), jnp.sin(angles)
    return jnp.stack(
        [
            jnp.concatenate([cosine] * 4, axis=1),
            jnp.concatenate([-sine, sine, -sine, sine], axis=1),
        ]
    )


def norm_back(grad_normed, gain_row, unit_rows, inverse):
    scaled = grad_normed * gain_row
    return inverse * (scaled - unit_rows * jnp.mean(scaled * unit_rows, axis=-1, keepdims=True))


def dot(left, right):
    return jnp.dot(left, right, preferred_element_type=F32)


def dot_nt(left, right):
    return lax.dot_general(left, right, (((1,), (1,)), ((), ())), preferred_element_type=F32)


def dot_tn(left, right):
    return lax.dot_general(left, right, (((0,), (0,)), ((), ())), preferred_element_type=F32)


def make_body(dp):
    outer, inner = split_dp(dp)

    def body(
        tokens,
        place,
        lengths,
        expert_ids,
        gate_values,
        cotangent,
        gain_attn,
        w_query,
        w_key,
        w_value,
        w_out,
        gain_ffn,
        exp_gate,
        exp_up,
        exp_down,
        dense_gate,
        dense_up,
        dense_down,
    ):
        layers, experts, rows, full = exp_gate.shape
        width = tokens.shape[1]
        slim = full // outer
        count = place.shape[1]
        kinds = experts + 1
        merged = rows % 16 == 0
        ids, gates = jnp.swapaxes(expert_ids, 1, 2), jnp.swapaxes(gate_values, 1, 2)
        downs = [jnp.swapaxes(exp_down, 2, 3), jnp.swapaxes(dense_down, 1, 2)]
        ffn = [exp_gate, dense_gate, exp_up, dense_up] + downs
        if merged:
            attn = [w_query, w_key, w_value, w_out]
            tables, marks, spot, gains_own, mix_own, *blocks = pack(
                place, lengths, ids, gates, gain_attn, gain_ffn, attn, ffn, outer, dp
            )
            attn_own = blocks[:layers]
            ffn_own = list(zip(blocks[layers : 2 * layers], blocks[2 * layers :]))
        else:
            position = layout(place[0], lengths[0])
            place_row = place[0].astype(F32)
            marks = jnp.stack([place_row, place_row - position.astype(F32)] * 4, axis=1)
            marks = marks.reshape(4, count // 4, 8)
            spot = place_row[None]
            tables = rope_tables(position).reshape(2, 4, count // 4, 128)
            slots = ids[:, None] == jnp.arange(experts, dtype=jnp.int32)[None, :, None, None]
            mix_own = jnp.sum(jnp.where(slots, gates[:, None], 0.0), axis=2)
            mix_own = mix_own.reshape(layers * experts, count)
            gains_own = jnp.concatenate([gain_attn, gain_ffn], axis=0).astype(BF16).astype(F32)
            spots = jnp.arange(dp, dtype=jnp.int32) == lax.axis_index("dp")
            gains_own = jnp.where(spots[None, :, None], gains_own[:, None], 0.0)
            gains_own = jnp.pad(
                gains_own.reshape(2 * layers, width), ((0, 8 - 2 * layers), (0, 0))
            )
            attn_own, ffn_own = [], []
            for level in range(layers):
                mats = [w_query[level], w_key[level], w_value[level], jnp.transpose(w_out[level])]
                attn_own.append(jnp.concatenate(mats, axis=1).astype(BF16)[None])
                mats = []
                for many, one in ((0, 1), (2, 3), (4, 5)):
                    mats += [ffn[many][level, e] for e in range(experts)] + [ffn[one][level]]
                mats = [m.astype(BF16) for m in mats]
                ffn_own.append(
                    [
                        jnp.stack(
                            [
                                jnp.concatenate(
                                    [m[:, k * slim : (k + 1) * slim] for m in group], axis=1
                                )
                                for k in range(outer)
                            ]
                        )
                        for group in (mats[: 2 * kinds], mats[2 * kinds :])
                    ]
                )
        state = tokens
        lead = [gains_own[None], attn_own[0], mix_own[None]]
        if merged:
            state_in = state
            ahead = [ffn_own[1][1]] if layers > 1 else []
            state, *kept = attn_forward(
                state_in,
                None,
                0,
                None,
                tables,
                marks,
                spot,
                lead + list(ffn_own[0]) + ahead,
                [BOTH] * 5 + [OUTER] * len(ahead),
                outer,
                inner,
                0,
            )
            part_down = kept.pop() if ahead else None
            gains, _, first, mix_all, w_in, w_down = kept[-6:]
            kept = kept[:-6]
        else:
            gains_all, first, mix_all = fetch(lead, outer, inner, 8)
            part_down = None
            gains = jnp.sum(gains_all, axis=0)
        w_attn = [first.reshape(width, -1)]
        w_ffn = []
        kept_attn, kept_ffn = [], []
        for level in range(layers):
            if level == 0 and merged:
                before = state_in
            else:
                before = state
                inside = list(ffn_own[level][: 1 if level else 2])
                state, *kept = attn_forward(
                    before,
                    gains,
                    level,
                    w_attn[level],
                    tables,
                    marks,
                    spot,
                    inside,
                    [BOTH] * len(inside),
                    outer,
                    inner,
                    1 if level else 11,
                )
                if level:
                    w_in = kept.pop()
                else:
                    w_down, w_in = kept.pop(), kept.pop()
            kept_attn.append((before, kept))
            w_ffn.append((w_in.reshape(width, -1), w_down.reshape(width, -1)))
            resid = state
            more, modes = [], []
            if level + 1 < layers:
                half = part_down is not None and level == 0
                more = [attn_own[level + 1], part_down if half else ffn_own[level + 1][1]]
                modes = [BOTH, INNER if half else BOTH]
            state, b_in, both, *fetched = ffn_forward(
                resid,
                gains,
                level,
                layers + level,
                kinds,
                mix_all,
                *w_ffn[level],
                more,
                modes,
                outer,
                inner,
                (2 if level == 0 else 12) if more else 3,
            )
            if more:
                w_attn.append(fetched[0].reshape(width, -1))
                w_down = fetched[1]
            kept_ffn.append((resid, b_in, both))
        mixed = state.astype(BF16)

        grad = cotangent
        part_gains = [None] * (2 * layers)
        pushed_in, pushed_down = [None] * layers, [None] * layers
        pushed_attn = [None] * layers
        waiting = []
        for level in reversed(range(layers)):
            resid, b_in, both = kept_ffn[level]
            grad, part_gain, grad_in, grad_down, *moved = ffn_backward(
                grad,
                resid,
                gains,
                level,
                layers + level,
                kinds,
                mix_all,
                *w_ffn[level],
                b_in,
                both,
                waiting,
                outer,
                inner,
                4 if waiting else 5,
            )
            part_gains[layers + level] = part_gain
            if waiting:
                (pushed_attn[level + 1],) = moved
            before, kept = kept_attn[level]
            inside = [grad_in.reshape(dp, rows, -1), grad_down.reshape(dp, rows, -1)]
            others = part_gains[1:] if level == 0 and merged else []
            grad, part_gain, *moved = attn_backward(
                grad,
                before,
                gains,
                level,
                w_attn[level],
                tables,
                marks,
                spot,
                kept,
                others,
                inside,
                outer,
                inner,
                6 if level else 7,
            )
            if level == 0 and merged:
                pushed_in[0], pushed_down[0], pushed_attn[0] = moved
                gain_sum = lax.dynamic_slice_in_dim(
                    part_gain, lax.axis_index("dp") * rows, rows, axis=1
                )
                continue
            part_gains[level] = part_gain
            waiting = [moved[0].reshape(dp, rows, -1)]
            pushed_in[level], pushed_down[level] = moved[1:]
        if not merged:
            stacked = jnp.concatenate(part_gains, axis=0)
            stacked = jnp.pad(stacked, ((0, 8 - 2 * layers), (0, 0)))
            stacked = jnp.transpose(stacked.reshape(8, dp, rows), (1, 0, 2))
            pushed_attn[0], gain_parts = push([waiting[0], stacked], outer, inner, 9)
            gain_part = jnp.sum(gain_parts, axis=0)
            gain_sum = jnp.sum(
                gather(jnp.pad(gain_part, ((0, 0), (0, 128 - rows))), dp, 10)[0], axis=0
            )
        grad_gain_attn = gain_sum[:layers, :rows]
        grad_gain_ffn = gain_sum[layers : 2 * layers, :rows]

        if merged:
            query, key, value, out, gate, gate_d, up, up_d, down, down_d = unpack(
                pushed_in, pushed_down, pushed_attn, experts
            )
        else:
            ups, downs, attns = [], [], []
            for level in range(layers):
                parts = pushed_in[level].reshape(outer, rows, 2 * kinds, slim)
                ups.append(jnp.transpose(parts, (2, 1, 0, 3)).reshape(2 * kinds, rows, full))
                parts = pushed_down[level].reshape(outer, rows, kinds, slim)
                downs.append(jnp.transpose(parts, (2, 1, 0, 3)).reshape(kinds, rows, full))
                attns.append(jnp.sum(pushed_attn[level].astype(F32), axis=0))
            ups, downs = jnp.stack(ups).astype(F32), jnp.stack(downs).astype(F32)
            gate, gate_d = ups[:, :experts], ups[:, experts]
            up, up_d = ups[:, kinds : kinds + experts], ups[:, kinds + experts]
            down, down_d = downs[:, :experts], downs[:, experts]
            query, key, value, out = jnp.split(jnp.stack(attns), 4, axis=2)
            out = jnp.swapaxes(out, 1, 2)
        return (
            mixed,
            grad,
            grad_gain_attn,
            query,
            key,
            value,
            out,
            grad_gain_ffn,
            gate,
            up,
            jnp.swapaxes(down, 2, 3),
            gate_d,
            up_d,
            jnp.swapaxes(down_d, 1, 2),
        )

    return body


def solution(mesh):
    return jax.shard_map(
        make_body(mesh.shape["dp"]),
        mesh=mesh,
        in_specs=(
            P(("dp", "tensor"), None),
            P("dp", None),
            P("dp", None),
            P(None, "dp", None),
            P(None, "dp", None),
            P(("dp", "tensor"), None),
            P(None, "dp"),
            P(None, "dp", "tensor"),
            P(None, "dp", "tensor"),
            P(None, "dp", "tensor"),
            P(None, "tensor", "dp"),
            P(None, "dp"),
            P(None, None, "dp", "tensor"),
            P(None, None, "dp", "tensor"),
            P(None, None, "tensor", "dp"),
            P(None, "dp", "tensor"),
            P(None, "dp", "tensor"),
            P(None, "tensor", "dp"),
        ),
        out_specs=(
            P(("dp", "tensor"), None),
            P(("dp", "tensor"), None),
            P(None, "dp"),
            P(None, "dp", "tensor"),
            P(None, "dp", "tensor"),
            P(None, "dp", "tensor"),
            P(None, "tensor", "dp"),
            P(None, "dp"),
            P(None, None, "dp", "tensor"),
            P(None, None, "dp", "tensor"),
            P(None, None, "tensor", "dp"),
            P(None, "dp", "tensor"),
            P(None, "dp", "tensor"),
            P(None, "tensor", "dp"),
        ),
        check_vma=False,
    )
```

```python
import functools

import jax
import jax.numpy as jnp
import numpy as np
from jax import lax
from jax.experimental import pallas as pl
from jax.experimental.pallas import tpu as pltpu
from jax.sharding import PartitionSpec as P

HD = 64
EPSILON = 1e-06
MASKED_SCORE = -1e30
MESH = pl.DeviceIdType.MESH
ANY = pl.BlockSpec(memory_space=pl.ANY)
VMEM = pl.BlockSpec(memory_space=pltpu.VMEM)
F32 = jnp.float32
BF16 = jnp.bfloat16
PARTS = 2
BOTH, OUTER, INNER = range(3)


def split_dp(dp):
    inner = 2 ** ((dp.bit_length() - 1) // 2)
    return dp // inner, inner


def place_of(inner):
    d = lax.axis_index("dp")
    return lax.div(d, inner), lax.rem(d, inner), lax.axis_index("tensor")


def across(t):
    return lax.rem(t + 2, 4), t + 1 - 2 * lax.rem(t, 2)


def meet(devices):
    barrier = pltpu.get_barrier_semaphore()
    for device in devices:
        pl.semaphore_signal(barrier, inc=1, device_id=device, device_id_type=MESH)
    pl.semaphore_wait(barrier, len(devices))


def send(source, target, send_sem, recv_sem, device):
    copy = pltpu.make_async_remote_copy(
        src_ref=source,
        dst_ref=target,
        send_sem=send_sem,
        recv_sem=recv_sem,
        device_id=device,
        device_id_type=MESH,
    )
    copy.start()
    return copy


def gather_kernel(dp, own, out, *sems):
    take = Gather(1, dp, out, sems)
    out[0, take.t] = own[...]
    meet(take.friends())
    take.start()
    take.complete(0)
    take.finish()


def gather(own, dp, ident):
    return pl.pallas_call(
        functools.partial(gather_kernel, dp),
        out_shape=jax.ShapeDtypeStruct((1, 4) + own.shape, own.dtype),
        in_specs=[VMEM],
        out_specs=VMEM,
        scratch_shapes=gather_sems(1),
        compiler_params=pltpu.CompilerParams(collective_id=ident, has_side_effects=True),
        name="gather",
    )(own)


def fetch_kernel(outer, inner, count, *refs):
    cut = Cut(refs)
    extra = Fetch(outer, inner, cut(count), cut(count), cut(count), cut(5), [BOTH] * count)
    meet(extra.zdev[1:] + extra.xdev)
    extra.start()
    extra.settle()
    for turn in extra.turns():
        turn()
    extra.finish()


def fetch(owns, outer, inner, ident):
    count = len(owns)
    return pl.pallas_call(
        functools.partial(fetch_kernel, outer, inner, count),
        out_shape=fetch_outs(owns, outer, inner, [BOTH] * count),
        in_specs=[ANY] * count,
        out_specs=[ANY] * count,
        scratch_shapes=fetch_scratch(owns, outer, inner, [BOTH] * count),
        compiler_params=pltpu.CompilerParams(collective_id=ident, has_side_effects=True),
        name="fetch",
    )(*owns)


def push_kernel(outer, inner, count, *refs):
    cut = Cut(refs)
    extra = Push(outer, inner, cut(count), cut(count), cut(3 * count), cut(6))
    meet(extra.zdev[:-1] + extra.xdev)
    extra.start()
    for turn in extra.turns():
        turn()
    extra.finish()


def push(parts, outer, inner, ident):
    count = len(parts)
    return pl.pallas_call(
        functools.partial(push_kernel, outer, inner, count),
        out_shape=push_outs(parts, outer),
        in_specs=[ANY] * count,
        out_specs=[ANY] * count,
        scratch_shapes=push_scratch(parts, outer, inner),
        compiler_params=pltpu.CompilerParams(collective_id=ident, has_side_effects=True),
        name="push",
    )(*parts)


def nearest(index, size, step):
    table = [sorted(range(size), key=lambda other: (abs(other - at), other)) for at in range(size)]
    found = 0
    for at in range(size):
        found = found + jnp.where(index == at, table[at][step], 0)
    return found


class Gather:
    def __init__(self, outer, inner, table, sems, parts=1):
        self.outer, self.inner, self.table, self.parts = outer, inner, table, parts
        self.zs, self.zr, self.ys, self.yr, self.cs, self.cr = sems
        self.dz, self.dx, self.t = place_of(inner)
        self.d = lax.axis_index("dp")
        self.size = table.shape[2] // parts
        ty, tc = across(self.t)
        self.ty = ty
        self.pair, self.core = (self.d, ty), (self.d, tc)
        self.source = [nearest(self.dz, outer, step) for step in range(outer)]
        self.zdev = [(source * inner + self.dx, self.t) for source in self.source]
        self.steps = outer * parts
        self.yc, self.cc, self.dc = [], [], []

    def friends(self):
        return self.zdev[1:] + [self.pair, self.core]

    def rows(self, step):
        return pl.ds(step % self.parts * self.size, self.size)

    def origin(self, step):
        return self.source[step // self.parts]

    def outward(self, step, target, sent):
        at = self.origin(step) * self.parts + step % self.parts
        block = self.table.at[self.origin(step), self.t, self.rows(step)]
        target = jnp.minimum(jnp.maximum(target, 0), self.outer - 1)
        return pltpu.make_async_remote_copy(
            src_ref=block,
            dst_ref=block,
            send_sem=self.zs.at[at if sent is None else sent],
            recv_sem=self.zr.at[at],
            device_id=(target * self.inner + self.dx, self.t),
            device_id_type=MESH,
        )

    def passes(self, step):
        if self.outer == 1:
            return []
        if step < self.parts:
            last = self.steps + step
            return [
                (self.dz < self.outer - 1, self.outward(step, self.dz + 1, None)),
                (self.dz > 0, self.outward(step, self.dz - 1, last)),
            ]
        ahead = jnp.where(self.origin(step) < self.dz, self.dz + 1, self.dz - 1)
        inside = (ahead >= 0) & (ahead < self.outer)
        return [(inside, self.outward(step, ahead, None))]

    def start(self):
        for step in range(self.parts):
            for inside, copy in self.passes(step):
                pl.when(inside)(copy.start)
        for step in range(self.parts):
            self.forward(step)

    def hop(self, step):
        ((inside, copy),) = self.passes(step)

        @pl.when(inside)
        def _():
            copy.wait_recv()
            copy.start()

    def arrive(self, step):
        ((inside, copy),) = self.passes(step)
        pl.when(jnp.logical_not(inside))(copy.wait_recv)
        self.forward(step)

    def forward(self, step):
        block = self.table.at[self.origin(step), self.t, self.rows(step)]
        self.yc.append(send(block, block, self.ys.at[step], self.yr.at[step], self.pair))
        self.cc.append(send(block, block, self.cs.at[step], self.cr.at[step], self.core))

    def complete(self, step):
        self.yc[step].wait_recv()
        at = self.steps + step
        block = self.table.at[self.origin(step), self.ty, self.rows(step)]
        self.dc.append(send(block, block, self.cs.at[at], self.cr.at[at], self.core))
        self.cc[step].wait_recv()
        self.dc[step].wait_recv()

    def finish(self):
        for step in range(self.steps):
            for inside, copy in self.passes(step):
                pl.when(inside)(copy.wait_send)
        for copy in self.yc + self.cc + self.dc:
            copy.wait_send()


class Scatter:
    def __init__(self, outer, inner, part, room, sems, parts=1):
        self.outer, self.part, self.parts = outer, part, parts
        self.from_c, self.from_y, self.from_z = room
        self.cs, self.cr, self.ys, self.yr, self.zs, self.zr = sems
        dz, dx, t = place_of(inner)
        d = lax.axis_index("dp")
        ty, tc = across(t)
        self.size = part.shape[3] // parts
        self.dz, self.y, self.c = dz, lax.div(t, 2), lax.rem(t, 2)
        self.pair, self.core = (d, ty), (d, tc)
        self.source = [nearest(dz, outer, step) for step in range(outer)]
        self.zdev = [(source * inner + dx, t) for source in self.source]
        self.steps = outer * parts
        self.cc, self.yc, self.zc = {}, {}, {}

    def rows(self, step):
        return pl.ds(step % self.parts * self.size, self.size)

    def core_send(self, step):
        source = self.source[step // self.parts]
        self.cc[step] = send(
            self.part.at[source, :, 1 - self.c, self.rows(step)],
            self.from_c.at[step],
            self.cs.at[step],
            self.cr.at[step],
            self.core,
        )

    def pair_send(self, step):
        source = self.source[step // self.parts]
        self.cc[step].wait_recv()
        mine = self.part[source, :, self.c, self.rows(step)].astype(F32)
        self.from_c[step] = (mine + self.from_c[step].astype(F32)).astype(BF16)
        self.yc[step] = send(
            self.from_c.at[step, 1 - self.y],
            self.from_y.at[step],
            self.ys.at[step],
            self.yr.at[step],
            self.pair,
        )

    def summed(self, step):
        self.yc[step].wait_recv()
        return self.from_c[step, self.y].astype(F32) + self.from_y[step].astype(F32)

    def outward(self, step, source, away):
        at = (away - 1) * self.parts + step % self.parts
        return pltpu.make_async_remote_copy(
            src_ref=source,
            dst_ref=self.from_z.at[at],
            send_sem=self.zs.at[at],
            recv_sem=self.zr.at[at],
            device_id=self.zdev[step // self.parts],
            device_id_type=MESH,
        )

    def outer_send(self, step):
        self.from_y[step] = self.summed(step).astype(BF16)
        away = lax.rem(self.source[step // self.parts] - self.dz + self.outer, self.outer)
        self.zc[step] = self.outward(step, self.from_y.at[step], away)
        self.zc[step].start()

    def total(self):
        pieces = []
        for piece in range(self.parts):
            total = self.summed(piece)
            for step in range(self.parts + piece, self.steps, self.parts):
                away = lax.rem(self.dz - self.source[step // self.parts] + self.outer, self.outer)
                self.outward(step, self.from_y.at[step], away).wait_recv()
                at = (away - 1) * self.parts + piece
                total = total + self.from_z[at].astype(F32)
            pieces.append(total)
        return pieces[0] if self.parts == 1 else jnp.concatenate(pieces, axis=0)

    def finish(self):
        for group in (self.cc, self.yc, self.zc):
            for step in group:
                group[step].wait_send()


def gather_sems(outer, parts=1):
    dma = pltpu.SemaphoreType.DMA
    steps = outer * parts
    return [dma((steps + parts,))] + [dma((steps,)) for _ in range(3)] + [dma((2 * steps,))] * 2


def scatter_sems(outer, parts=1):
    dma = pltpu.SemaphoreType.DMA
    return [dma((outer * parts,)) for _ in range(6)]


def scatter_room(outer, rows, width, parts=1):
    steps, size = outer * parts, rows // parts
    return [
        pltpu.VMEM((steps, 2, size, width), BF16),
        pltpu.VMEM((steps, size, width), BF16),
        pltpu.VMEM((max(steps - parts, 1), size, width), BF16),
    ]


def pipeline(take, give, compute, begin, after, post, middle, since, late):
    steps, parts = take.steps, take.parts
    middle, late = list(middle), list(late)
    lag = parts + 1
    take.start()
    begin()
    hops = list(range(parts, steps))
    for _ in range(min(2 * parts, len(hops))):
        take.hop(hops.pop(0))
    for step in range(steps):
        if step + parts < steps:
            take.arrive(step + parts)
        take.complete(step)
        compute(step)
        give.core_send(step)
        for _ in range(min(parts, len(hops))):
            take.hop(hops.pop(0))
        if step:
            give.pair_send(step - 1)
        if step - lag >= parts:
            give.outer_send(step - lag)
        if step == 1:
            after()
        if step >= since and middle:
            middle.pop(0)()
        post(step)
    sent = max(parts, steps - lag)
    late = middle + late
    give.pair_send(steps - 1)
    for step in range(sent, steps):
        if late:
            late.pop(0)()
        give.outer_send(step)
    for work in late:
        work()


def pieces_of(arrays, halves=True):
    items = []
    for i, array in enumerate(arrays):
        wide = array.shape[-1]
        count = 2 if halves and wide % 256 == 0 and wide > 1024 else 1
        size = wide // count
        items += [(i, slice(at * size, (at + 1) * size)) for at in range(count)]
    return items


class Fetch:
    def __init__(self, outer, inner, owns, outs, holds, sems, modes):
        self.outer, self.inner, self.owns, self.outs, self.holds = outer, inner, owns, outs, holds
        self.zs, self.zr, self.xs, self.xr, self.ls = sems
        self.modes, self.items = modes, pieces_of(owns)
        self.dz, dx, t = place_of(inner)
        self.dx, self.d = dx, lax.axis_index("dp")
        self.source = [nearest(self.dz, outer, step) for step in range(outer)]
        self.zdev = [(source * inner + dx, t) for source in self.source]
        self.xdev = [(self.dz * inner + lax.rem(dx + j, inner), t) for j in range(1, inner)]
        self.zc, self.xc, self.into, self.back = [], {}, {}, {}

    def own(self, item, where):
        i, cols = self.items[item]
        return self.owns[i].at[where if self.owns[i].shape[0] == self.outer else 0, :, cols]

    def slot(self, item, source):
        i, cols = self.items[item]
        if self.modes[i] != OUTER:
            source = source * self.inner + self.dx
        return self.outs[i].at[source, :, cols]

    def mode(self, item):
        return self.modes[self.items[item][0]]

    def chosen(self, first, last):
        last = len(self.owns) if last is None else last
        return [item for item, (i, _) in enumerate(self.items) if first <= i < last]

    def copy(self, item, step, away, refs):
        at = item * self.outer + lax.rem(away + self.outer, self.outer)
        return pltpu.make_async_remote_copy(
            src_ref=refs[0],
            dst_ref=refs[1],
            send_sem=self.zs.at[at],
            recv_sem=self.zr.at[at],
            device_id=self.zdev[step],
            device_id_type=MESH,
        )

    def start(self, first=0, last=None, aside=True):
        for item in self.chosen(first, last):
            i, cols = self.items[item]
            if self.mode(item) == INNER:
                for step, source in enumerate(self.source):
                    here = self.owns[i].at[source, :, cols]
                    self.spread(item, step, here, self.slot(item, source))
                continue
            for step in range(1, self.outer):
                source = self.source[step]
                refs = (self.own(item, source), self.slot(item, self.dz))
                self.zc.append(self.copy(item, step, source - self.dz, refs))
                self.zc[-1].start()
            if aside:
                self.aside(item)
        for i in range(first, len(self.owns) if last is None else last):
            where = self.dz if self.owns[i].shape[0] == self.outer else 0
            here = self.owns[i] if self.modes[i] == INNER else self.owns[i].at[where]
            at = i * (self.outer + 1)
            self.into[i] = pltpu.make_async_copy(here, self.holds[i], self.ls.at[at])
            self.into[i].start()

    def aside(self, item):
        if self.mode(item) == BOTH:
            self.spread(item, 0, self.own(item, self.dz), self.slot(item, self.dz))

    def spread(self, item, step, block, target):
        for j in range(1, self.inner):
            at = (item * self.outer + step) * self.inner + j
            self.xc[item, step, j] = send(
                block, target, self.xs.at[at], self.xr.at[at], self.xdev[j - 1]
            )

    def settle(self):
        for i, into in self.into.items():
            into.wait()
            at = i * (self.outer + 1)
            target = self.outs[i]
            if self.modes[i] == INNER:
                pairs = [
                    (self.holds[i].at[source], target.at[source * self.inner + self.dx])
                    for source in self.source
                ]
            else:
                here = self.dz if self.modes[i] == OUTER else self.d
                pairs = [(self.holds[i], target.at[here])]
            self.back[i] = [
                pltpu.make_async_copy(*pair, self.ls.at[at + 1 + k])
                for k, pair in enumerate(pairs)
            ]
            for copy in self.back[i]:
                copy.start()

    def turn(self, item, step):
        source = self.source[step]
        block = self.slot(item, source)
        self.copy(item, step, self.dz - source, (block, block)).wait_recv()
        if self.mode(item) == BOTH:
            self.spread(item, step, block, block)

    def turns(self, first=0, last=None):
        return [
            functools.partial(self.turn, item, step)
            for item in self.chosen(first, last)
            for step in range(1, self.outer)
            if self.mode(item) != INNER
        ]

    def land(self, i):
        for key in self.xc:
            if self.items[key[0]][0] == i:
                self.xc[key].wait_recv()
        for copy in self.back[i]:
            copy.wait()

    def finish(self, first=0):
        for key in self.xc:
            if self.items[key[0]][0] >= first:
                self.xc[key].wait_recv()
            self.xc[key].wait_send()
        for copy in self.zc:
            copy.wait_send()
        for i in self.back:
            if i >= first:
                for copy in self.back[i]:
                    copy.wait()


def fetch_outs(owns, outer, inner, modes):
    return [
        jax.ShapeDtypeStruct(
            (outer if mode == OUTER else outer * inner,) + own.shape[1:], own.dtype
        )
        for own, mode in zip(owns, modes)
    ]


def fetch_scratch(owns, outer, inner, modes):
    dma = pltpu.SemaphoreType.DMA
    count = max(len(pieces_of(owns)), 1)
    return [
        pltpu.VMEM(own.shape if mode == INNER else own.shape[1:], own.dtype)
        for own, mode in zip(owns, modes)
    ] + [
        dma((count * outer,)),
        dma((count * outer,)),
        dma((count * outer * inner,)),
        dma((count * outer * inner,)),
        dma((max(len(owns), 1) * (outer + 1),)),
    ]


class Push:
    def __init__(self, outer, inner, parts, outs, room, sems, halves=True):
        count = len(parts)
        self.outer, self.inner, self.parts, self.outs = outer, inner, parts, outs
        self.items = pieces_of(parts, halves)
        self.froms, self.mine, self.sums = room[:count], room[count : 2 * count], room[2 * count :]
        self.xs, self.xr, self.zs, self.zr, self.ls, self.ks = sems
        self.dz, dx, t = place_of(inner)
        self.dx = dx
        near = [nearest(self.dz, outer, step) for step in range(outer)]
        self.source = near[:0:-1] + near[:1]
        self.zdev = [(source * inner + dx, t) for source in self.source]
        self.xdev = [(self.dz * inner + lax.rem(dx + j, inner), t) for j in range(1, inner)]
        self.xc, self.zc, self.loads, self.keeps = {}, [], {}, []

    def start(self, first=0, last=None):
        last = len(self.parts) if last is None else last
        for item, (i, cols) in enumerate(self.items):
            if not first <= i < last:
                continue
            for step, source in enumerate(self.source):
                for j in range(1, self.inner):
                    slot = source * self.inner + lax.rem(self.dx + j, self.inner)
                    at = (item * self.outer + step) * self.inner + j
                    self.xc[item, step, j] = send(
                        self.parts[i].at[slot, :, cols],
                        self.froms[i].at[j - 1, step, :, cols],
                        self.xs.at[at],
                        self.xr.at[at],
                        self.xdev[j - 1],
                    )
                self.loads[item, step] = pltpu.make_async_copy(
                    self.parts[i].at[source * self.inner + self.dx, :, cols],
                    self.mine[i].at[step, :, cols],
                    self.ls.at[item * self.outer + step],
                )
                self.loads[item, step].start()

    def turn(self, item, step):
        i, cols = self.items[item]
        self.loads[item, step].wait()
        total = self.mine[i][step, :, cols].astype(F32)
        for j in range(1, self.inner):
            self.xc[item, step, j].wait_recv()
            total = total + self.froms[i][j - 1, step, :, cols].astype(F32)
        self.sums[i][step, :, cols] = total.astype(self.sums[i].dtype)
        source = self.sums[i].at[step, :, cols]
        target = self.outs[i].at[self.dz, :, cols]
        if step < self.outer - 1:
            away = lax.rem(self.source[step] - self.dz + self.outer, self.outer)
            at = item * self.outer + away
            self.zc.append(send(source, target, self.zs.at[at], self.zr.at[at], self.zdev[step]))
        else:
            self.keeps.append(pltpu.make_async_copy(source, target, self.ks.at[item]))
            self.keeps[-1].start()

    def turns(self):
        return [
            functools.partial(self.turn, item, step)
            for item in range(len(self.items))
            for step in range(self.outer)
        ]

    def finish(self):
        for copy in self.zc:
            copy.wait_recv()
            copy.wait_send()
        for key in self.xc:
            self.xc[key].wait_send()
        for copy in self.keeps:
            copy.wait()


def push_outs(parts, outer):
    return [jax.ShapeDtypeStruct((outer,) + part.shape[1:], part.dtype) for part in parts]


def push_scratch(parts, outer, inner):
    dma = pltpu.SemaphoreType.DMA
    count = max(len(pieces_of(parts)), 1)
    across_x = [pltpu.VMEM((inner - 1, outer) + part.shape[1:], part.dtype) for part in parts]
    own = [pltpu.VMEM((outer,) + part.shape[1:], part.dtype) for part in parts]
    return (
        across_x
        + own
        + own
        + [
            dma((count * outer * inner,)),
            dma((count * outer * inner,)),
            dma((count * outer,)),
            dma((count * outer,)),
            dma((count * outer,)),
            dma((count,)),
        ]
    )


class Cut:
    def __init__(self, refs):
        self.refs, self.at = refs, 0

    def __call__(self, count):
        self.at += count
        return self.refs[self.at - count : self.at]


class Mixer:
    def __init__(self, outer, inner, table, lines, mix, sems):
        self.lines, self.mix = lines, mix
        dx = lax.rem(lax.axis_index("dp"), inner)
        self.loads = [
            pltpu.make_async_copy(table.at[at * inner + dx], lines.at[at], sems.at[at])
            for at in range(outer)
        ]
        for load in self.loads:
            load.start()

    def turn(self):
        for at, load in enumerate(self.loads):
            load.wait()
            self.mix[at] = jnp.transpose(self.lines[at]).reshape(self.mix.shape[1:])


def ffn_forward_kernel(outer, inner, kinds, modes, level, row, *refs):
    count = len(modes)
    cut = Cut(refs)
    resid, gain, mix_any, w_in_any, w_down_any = cut(5)
    owns = cut(count)
    out, b_out, gu_out = cut(3)
    fetched = cut(count)
    w_in, w_down, b, gu, hid, part, mix_rows, mix = cut(8)
    room, take_sems, give_sems = cut(3), cut(6), cut(6)
    load_sem, keep_b, keep_gu, load_mix = cut(4)
    extra = Fetch(outer, inner, owns, fetched, cut(count), cut(5), modes) if count else None
    rows, width = resid.shape
    third = w_down.shape[1]
    slim = third // kinds
    loads = [
        pltpu.make_async_copy(w_in_any, w_in, load_sem.at[0]),
        pltpu.make_async_copy(w_down_any, w_down, load_sem.at[1]),
    ]
    for load in loads:
        load.start()
    take = Gather(outer, inner, b, take_sems, PARTS)
    give = Scatter(outer, inner, part, room, give_sems, PARTS)
    size = rows // PARTS
    mixer = Mixer(outer, inner, mix_any, mix_rows, mix, load_mix)
    x = resid[...]
    inverse = lax.rsqrt(jnp.mean(x * x, axis=-1, keepdims=True) + EPSILON)
    b[take.dz, take.t] = (x * inverse * gain[row : row + 1]).astype(BF16)
    meet(take.friends() + (extra.xdev if count else []))
    keeps = []

    def compute(step):
        source, q = take.origin(step), step % PARTS
        here = take.rows(step)
        if step == 0:
            for load in loads:
                load.wait()
        rows_in = b[source, :, here].reshape(4 * size, width)

        scale = mix[source, :, here].reshape(4 * size, mix.shape[-1])
        both = dot(rows_in, w_in[...])
        gu[source, q] = both.astype(BF16)
        gate, up = both[:, :third], both[:, third:]
        hidden = gate * jax.nn.sigmoid(gate) * up
        for e in range(kinds):
            piece = hidden[:, e * slim : (e + 1) * slim]
            if e < kinds - 1:
                col = level * (kinds - 1) + e
                piece = piece * scale[:, col : col + 1]
            hid[:, e * slim : (e + 1) * slim] = piece.astype(BF16)

        @pl.loop(0, width // 256)
        def _(at):
            cols = pl.ds(pl.multiple_of(at * 256, 256), 256)
            sent = dot_nt(hid[...], w_down[cols]).astype(BF16)
            part[source, :, :, here, cols] = sent.reshape(2, 2, size, 256)

        if q == PARTS - 1:
            at = step // PARTS
            keeps.append(pltpu.make_async_copy(b.at[source], b_out.at[source], keep_b.at[at]))
            keeps.append(pltpu.make_async_copy(gu.at[source], gu_out.at[source], keep_gu.at[at]))
            keeps[-1].start()
            keeps[-2].start()

    def after():
        if count:
            extra.start()
            extra.settle()

    turns = extra.turns() if count else []
    half = take.steps // 2
    pipeline(take, give, compute, mixer.turn, after, lambda step: None, turns, half, [])
    out[...] = resid[...] + give.total()
    take.finish()
    give.finish()
    if count:
        extra.finish()
    for keep in keeps:
        keep.wait()


def ffn_forward(
    resid, gain, level, row, kinds, mix, w_in, w_down, owns, modes, outer, inner, ident
):
    dma = pltpu.SemaphoreType.DMA
    rows, width = resid.shape
    third = w_down.shape[1]
    count = len(owns)
    return pl.pallas_call(
        functools.partial(ffn_forward_kernel, outer, inner, kinds, modes, level, row),
        out_shape=[
            jax.ShapeDtypeStruct((rows, width), F32),
            jax.ShapeDtypeStruct((outer, 4, rows, width), BF16),
            jax.ShapeDtypeStruct((outer, PARTS, 4 * rows // PARTS, 2 * third), BF16),
        ]
        + fetch_outs(owns, outer, inner, modes),
        in_specs=[VMEM, VMEM, ANY, ANY, ANY] + [ANY] * count,
        out_specs=[VMEM, ANY, ANY] + [ANY] * count,
        scratch_shapes=[
            pltpu.VMEM(w_in.shape, BF16),
            pltpu.VMEM(w_down.shape, BF16),
            pltpu.VMEM((outer, 4, rows, width), BF16),
            pltpu.VMEM((outer, PARTS, 4 * rows // PARTS, 2 * third), BF16),
            pltpu.VMEM((4 * rows // PARTS, third), BF16),
            pltpu.VMEM((outer, 2, 2, rows, width), BF16),
            pltpu.VMEM((outer,) + mix.shape[1:], F32),
            pltpu.VMEM((outer, 4, rows, mix.shape[1]), F32),
        ]
        + scatter_room(outer, rows, width, PARTS)
        + gather_sems(outer, PARTS)
        + scatter_sems(outer, PARTS)
        + [dma((2,)), dma((outer,)), dma((outer,)), dma((outer,))]
        + (fetch_scratch(owns, outer, inner, modes) if count else []),
        compiler_params=pltpu.CompilerParams(
            collective_id=ident, has_side_effects=True, vmem_limit_bytes=62 << 20
        ),
        name="ffn_forward",
    )(resid, gain, mix, w_in, w_down, *owns)


def ffn_backward_kernel(outer, inner, kinds, count, level, row, *refs):
    cut = Cut(refs)
    grad_y, resid, gain, mix_any, w_in_any, w_down_any, b_any, gu_any = cut(8)
    parts = cut(count)
    out, gain_out, grad_in, grad_down = cut(4)
    pushed = cut(count)
    w_in, w_down, b, gb, gu, dgu, hid, flip_b, flip_gb, part, mix_rows, mix = cut(12)
    room, take_sems, give_sems = cut(3), cut(6), cut(6)
    load_sem, load_gu, load_mix = cut(3)
    extra = Push(outer, inner, parts, pushed, cut(3 * count), cut(6)) if count else None
    rows, width = resid.shape
    tall = outer * 4 * rows
    third = w_down.shape[1]
    slim = third // kinds
    loads = [
        pltpu.make_async_copy(source, target, load_sem.at[i])
        for i, (source, target) in enumerate(
            ((b_any, b), (w_down_any, w_down), (w_in_any, w_in))
        )
    ]
    for load in loads:
        load.start()
    take = Gather(outer, inner, gb, take_sems, PARTS)
    give = Scatter(outer, inner, part, room, give_sems, PARTS)
    size = rows // PARTS
    mixer = Mixer(outer, inner, mix_any, mix_rows, mix, load_mix)
    fills = [
        pltpu.make_async_copy(gu_any.at[source], gu.at[source], load_gu.at[step])
        for step, source in enumerate(take.source)
    ]
    for fill in fills:
        fill.start()
    gb[take.dz, take.t] = grad_y[...].astype(BF16)
    meet(take.friends() + (extra.xdev if count else []))

    def compute(step):
        source, q = take.origin(step), step % PARTS
        here = take.rows(step)
        if step == 0:
            loads[1].wait()
            loads[2].wait()
        if q == 0:
            fills[step // PARTS].wait()
        rows_in = gb[source, :, here].reshape(4 * size, width)
        mixed = mix[source, :, here].reshape(4 * size, mix.shape[-1])
        grad_hidden = dot(rows_in, w_down[...])
        both = gu[source, q].astype(F32)
        gate, up = both[:, :third], both[:, third:]
        sigma = jax.nn.sigmoid(gate)
        act = gate * sigma
        slope = sigma * (1.0 + gate * (1.0 - sigma))
        hidden, grad_gate, grad_up = act * up, grad_hidden * up * slope, grad_hidden * act
        for e in range(kinds):
            cols = slice(e * slim, (e + 1) * slim)
            more = slice(third + e * slim, third + (e + 1) * slim)
            at = level * (kinds - 1) + e
            scale = mixed[:, at : at + 1] if e < kinds - 1 else 1.0
            hid[source, q, :, cols] = (hidden[:, cols] * scale).astype(BF16)
            dgu[source, q, :, cols] = (grad_gate[:, cols] * scale).astype(BF16)
            dgu[source, q, :, more] = (grad_up[:, cols] * scale).astype(BF16)

        @pl.loop(0, width // 256)
        def _(at):
            cols = pl.ds(pl.multiple_of(at * 256, 256), 256)
            sent = dot_nt(dgu[source, q], w_in[cols]).astype(BF16)
            part[source, :, :, here, cols] = sent.reshape(2, 2, size, 256)

    def post(step):
        source, q = take.origin(step), step % PARTS
        if step == 0:
            loads[0].wait()
        at = pl.multiple_of((source * PARTS + q) * 4 * size, 4 * size)
        for table, flip in ((b, flip_b), (gb, flip_gb)):
            block = table[source, :, take.rows(step)].reshape(4 * size, width)
            flip[:, pl.ds(at, 4 * size)] = jnp.transpose(block)

    def weigh(target, flip, source, low, high):
        values = source[...].reshape(tall, source.shape[-1])

        @pl.loop(0, width // 256)
        def _(at):
            here = pl.ds(pl.multiple_of(at * 256, 256), 256)
            target[here, low:high] = dot(flip[here, :], values[:, low:high]).astype(BF16)

    def begin():
        if count:
            extra.start()
        mixer.turn()

    def pieces(total):
        return [(low, min(low + 256, total)) for low in range(0, total, 256)]

    late = [functools.partial(weigh, grad_in, flip_b, dgu, *span) for span in pieces(2 * third)]
    late += [functools.partial(weigh, grad_down, flip_gb, hid, *span) for span in pieces(third)]
    turns = extra.turns() if count else []
    pipeline(take, give, compute, begin, lambda: None, post, turns, 2, late)
    grad_b = give.total()
    x = resid[...]
    inverse = lax.rsqrt(jnp.mean(x * x, axis=-1, keepdims=True) + EPSILON)
    unit = x * inverse
    gain_out[...] = jnp.sum(grad_b * unit, axis=0, keepdims=True)
    out[...] = grad_y[...].astype(F32) + norm_back(grad_b, gain[row : row + 1], unit, inverse)
    take.finish()
    give.finish()
    if count:
        extra.finish()


def ffn_backward(
    grad_y, resid, gain, level, row, kinds, mix, w_in, w_down, b, both, parts, outer, inner, ident
):
    dma = pltpu.SemaphoreType.DMA
    rows, width = resid.shape
    third = w_down.shape[1]
    count = len(parts)
    return pl.pallas_call(
        functools.partial(ffn_backward_kernel, outer, inner, kinds, count, level, row),
        out_shape=[
            jax.ShapeDtypeStruct((rows, width), F32),
            jax.ShapeDtypeStruct((1, width), F32),
            jax.ShapeDtypeStruct((width, 2 * third), BF16),
            jax.ShapeDtypeStruct((width, third), BF16),
        ]
        + push_outs(parts, outer),
        in_specs=[VMEM, VMEM, VMEM, ANY, ANY, ANY, ANY, ANY] + [ANY] * count,
        out_specs=[VMEM, VMEM, VMEM, VMEM] + [ANY] * count,
        scratch_shapes=[
            pltpu.VMEM(w_in.shape, BF16),
            pltpu.VMEM(w_down.shape, BF16),
            pltpu.VMEM((outer, 4, rows, width), BF16),
            pltpu.VMEM((outer, 4, rows, width), BF16),
            pltpu.VMEM((outer, PARTS, 4 * rows // PARTS, 2 * third), BF16),
            pltpu.VMEM((outer, PARTS, 4 * rows // PARTS, 2 * third), BF16),
            pltpu.VMEM((outer, PARTS, 4 * rows // PARTS, third), BF16),
            pltpu.VMEM((width, outer * 4 * rows), BF16),
            pltpu.VMEM((width, outer * 4 * rows), BF16),
            pltpu.VMEM((outer, 2, 2, rows, width), BF16),
            pltpu.VMEM((outer,) + mix.shape[1:], F32),
            pltpu.VMEM((outer, 4, rows, mix.shape[1]), F32),
        ]
        + scatter_room(outer, rows, width, PARTS)
        + gather_sems(outer, PARTS)
        + scatter_sems(outer, PARTS)
        + [dma((3,)), dma((outer,)), dma((outer,))]
        + (push_scratch(parts, outer, inner) if count else []),
        compiler_params=pltpu.CompilerParams(
            collective_id=ident, has_side_effects=True, vmem_limit_bytes=63 << 20
        ),
        name="ffn_backward",
    )(grad_y, resid, gain, mix, w_in, w_down, b, both, *parts)


def swap_halves(values):
    width = values.shape[1]
    lane = lax.broadcasted_iota(jnp.int32, values.shape, 1)
    low = lax.rem(lane, HD) < HD // 2
    return jnp.where(
        low, pltpu.roll(values, width - HD // 2, 1), pltpu.roll(values, HD // 2, 1)
    )


def allowed_rows(marks, spot, top):
    del top
    return (spot >= marks[:, 1:2]) & (spot <= marks[:, 0:1])


def attn_forward_kernel(outer, inner, modes, lead, row, *refs):
    count = len(modes)
    dp = outer * inner
    cut = Cut(refs)
    x_in, tables, marks, spot = cut(4)
    gain, weight = (None, None) if lead else cut(2)
    owns = cut(count)
    out, a_out, qk_out, v_out, lse_out, att_out = cut(6)
    gain_out = cut(1)[0] if lead else None
    fetched = cut(count)
    w, a, qk, v, att, part = cut(6)
    room, take_sems, give_sems = cut(3), cut(6), cut(6)
    load_sem, keep_sem = cut(2)
    extra = Fetch(outer, inner, owns, fetched, cut(count), cut(5), modes)
    rows, width = x_in.shape
    heads_width = w.shape[1] // 4
    heads = heads_width // HD
    take = Gather(1, dp, a, take_sems)
    give = Scatter(1, dp, part, room, give_sems)
    x = x_in[...].astype(F32)
    inverse = lax.rsqrt(jnp.mean(x * x, axis=-1, keepdims=True) + EPSILON)
    friends = take.friends() + extra.zdev[1:] + extra.xdev
    if lead:
        (gains,) = cut(1)
        meet(friends)
        extra.start(0, 2)
        extra.start(2, None, False)
        extra.settle()
        for turn in extra.turns(0, 1):
            turn()
        extra.land(0)
        load = pltpu.make_async_copy(fetched[0], gains, load_sem.at[0])
        load.start()
        load.wait()
        gain_out[...] = jnp.sum(gains[...], axis=0)
        a[0, take.t] = (x * inverse * gain_out[row : row + 1]).astype(BF16)
        turns = extra.turns(1, 2)
        turns[0]()
        take.start()
        for turn in turns[1:]:
            turn()
        for item in extra.chosen(2, None):
            extra.aside(item)
        extra.land(1)
        slot = fetched[1].shape[1]
        loads = [
            pltpu.make_async_copy(
                fetched[1].at[at], w.at[pl.ds(at * slot, slot)], load_sem.at[at]
            )
            for at in range(dp)
        ]
        for load in loads:
            load.start()
        for load in loads:
            load.wait()
    else:
        load = pltpu.make_async_copy(weight, w, load_sem.at[0])
        load.start()
        a[0, take.t] = (x * inverse * gain[row : row + 1]).astype(BF16)
        meet(friends)
        take.start()
        extra.start()
        extra.settle()
        load.wait()
    done = 2 if lead else 0
    turns = extra.turns(done)

    def project(block):
        both = dot(a[0, block], w[:, : 3 * heads_width])
        raw = both[:, : 2 * heads_width]
        times = 2 * heads_width // tables.shape[-1]
        cosine = jnp.concatenate([tables[0, block]] * times, axis=1)
        sine = jnp.concatenate([tables[1, block]] * times, axis=1)
        qk[block] = (raw * cosine + swap_halves(raw) * sine).astype(BF16)
        v[block] = both[:, 2 * heads_width :].astype(BF16)

    project(take.t)
    take.complete(0)
    for other in range(1, 4):
        project(lax.rem(take.t + other, 4))
    keeps = [pltpu.make_async_copy(a.at[0], a_out, keep_sem.at[0])]
    keeps.append(pltpu.make_async_copy(qk, qk_out, keep_sem.at[1]))
    keeps.append(pltpu.make_async_copy(v, v_out, keep_sem.at[2]))
    for keep in keeps:
        keep.start()

    def attend(block):
        keys = qk[...].reshape(4 * rows, 2 * heads_width)
        values = v[...].reshape(4 * rows, heads_width)
        allowed = allowed_rows(marks[block], spot[...], 0)
        pieces = []
        for head in range(heads):
            here = slice(head * HD, (head + 1) * HD)
            there = slice(heads_width + head * HD, heads_width + (head + 1) * HD)
            scores = dot_nt(qk[block, :, here], keys[:, there])
            scores = jnp.where(allowed, scores * HD ** (-0.5), MASKED_SCORE)
            top = jnp.max(scores, axis=-1, keepdims=True)
            expo = jnp.exp(scores - top)
            total = jnp.sum(expo, axis=-1, keepdims=True)
            probs = (expo / total).astype(BF16)
            lse_out[block, :, head : head + 1] = top + jnp.log(total)
            pieces.append(dot(probs, values[:, here]).astype(BF16))
        att[block] = jnp.concatenate(pieces, axis=1)
        sent = dot_nt(att[block], w[:, 3 * heads_width :]).astype(BF16)
        part[0, lax.div(block, 2), lax.rem(block, 2)] = sent

    y, c = give.y, give.c
    attend(2 * (1 - y) + 1 - c)
    attend(2 * y + 1 - c)
    give.core_send(0)
    turns[0]()
    attend(2 * (1 - y) + c)
    attend(2 * y + c)
    give.pair_send(0)
    for turn in turns[1:]:
        turn()
    keeps.append(pltpu.make_async_copy(att, att_out, keep_sem.at[3]))
    keeps[-1].start()
    out[...] = x_in[...].astype(F32) + give.total()
    take.finish()
    give.finish()
    extra.finish(done)
    for keep in keeps:
        keep.wait()


def attn_forward(
    x, gain, row, weight, tables, marks, spot, owns, modes, outer, inner, ident
):
    count = len(owns)
    dma = pltpu.SemaphoreType.DMA
    rows, width = x.shape
    lead = weight is None
    shape = (width, owns[1].shape[-1]) if lead else weight.shape
    slim = shape[1] // 4
    extras = [] if lead else [gain, weight]
    kept = [(4, rows, width), (4, rows, 2 * slim), (4, rows, slim)]
    return pl.pallas_call(
        functools.partial(attn_forward_kernel, outer, inner, modes, lead, row),
        out_shape=[jax.ShapeDtypeStruct((rows, width), F32)]
        + [jax.ShapeDtypeStruct(shape, BF16) for shape in kept]
        + [
            jax.ShapeDtypeStruct((4, rows, 8), F32),
            jax.ShapeDtypeStruct((4, rows, slim), BF16),
        ]
        + ([jax.ShapeDtypeStruct((8, width), F32)] if lead else [])
        + fetch_outs(owns, outer, inner, modes),
        in_specs=[VMEM] * 4 + ([] if lead else [VMEM, ANY]) + [ANY] * count,
        out_specs=[VMEM, ANY, ANY, ANY, VMEM, ANY] + [VMEM] * lead + [ANY] * count,
        scratch_shapes=[
            pltpu.VMEM(shape, BF16),
            pltpu.VMEM((1, 4, rows, width), BF16),
            pltpu.VMEM(kept[1], BF16),
            pltpu.VMEM(kept[2], BF16),
            pltpu.VMEM(kept[2], BF16),
            pltpu.VMEM((1, 2, 2, rows, width), BF16),
        ]
        + scatter_room(1, rows, width)
        + gather_sems(1)
        + scatter_sems(1)
        + [dma((outer * inner,)), dma((4,))]
        + fetch_scratch(owns, outer, inner, modes)
        + ([pltpu.VMEM((outer * inner,) + owns[0].shape[1:], F32)] if lead else []),
        compiler_params=pltpu.CompilerParams(collective_id=ident, has_side_effects=True),
        name="attn_forward",
    )(x, tables, marks, spot, *extras, *owns)


def attn_backward_kernel(outer, inner, count, last, row, *refs):
    dp = outer * inner
    cut = Cut(refs)
    grad_in, x_in, gain, weight, tables, marks, spot = cut(7)
    a_in, qk_in, v_in, lse, att_in = cut(5)
    others = cut(last)
    parts = cut(count)
    out, gain_out = cut(2)
    (grad_w,) = (None,) if last else cut(1)
    total = count + 1 if last else count
    pushed = cut(total)
    w, a, qk, v, att, ga, g_att, raw, part = cut(9)
    room, take_sems, give_sems = cut(3), cut(6), cut(6)
    (load_sem,) = cut(1)
    room_x, sems_x = cut(3 * total), cut(6)
    if last:
        held, from_t, from_d, ts, tr, ds, dr = cut(7)
        parts = tuple(parts) + (held,)
    extra = Push(outer, inner, parts, pushed, room_x, sems_x, not last)
    turns = extra.turns()
    friends = []
    rows, width = x_in.shape
    tall = 4 * rows
    heads_width = w.shape[1] // 4
    heads = heads_width // HD
    loads = [
        pltpu.make_async_copy(source, target, load_sem.at[i])
        for i, (source, target) in enumerate(
            ((weight, w), (qk_in, qk), (v_in, v), (att_in, att), (a_in, a))
        )
    ]
    for load in loads:
        load.start()
    take = Gather(1, dp, ga, take_sems)
    give = Scatter(1, dp, part, room, give_sems)
    ga[0, take.t] = grad_in[...].astype(BF16)
    if last:
        team = [(take.d, lax.rem(take.t + k, 4)) for k in range(1, 4)]
        peers = [(lax.rem(take.d + k, dp), take.t) for k in range(1, dp)]
        friends = team + peers
    else:
        friends = take.friends() + extra.zdev[:-1] + extra.xdev
    meet(friends)
    take.start()
    extra.start(0, count)
    for load in loads:
        load.wait()
    take.complete(0)
    turns[0]()
    grads = ga[...].reshape(tall, width)
    g_att[...] = dot(grads, w[:, 3 * heads_width :]).astype(BF16)
    all_qk = qk[...].reshape(tall, 2 * heads_width)
    all_v = v[...].reshape(tall, heads_width)
    all_marks = marks[...].reshape(tall, marks.shape[-1])
    all_lse = lse[...].reshape(tall, lse.shape[-1])
    allowed = allowed_rows(all_marks, spot[...], 0)
    q_grads, k_grads, v_grads = [], [], []
    for head in range(heads):
        here = slice(head * HD, (head + 1) * HD)
        there = slice(heads_width + head * HD, heads_width + (head + 1) * HD)
        query, key = all_qk[:, here], all_qk[:, there]
        scores = dot_nt(query, key)
        scores = jnp.where(allowed, scores * HD ** (-0.5), MASKED_SCORE)
        probs = jnp.exp(scores - all_lse[:, head : head + 1])
        grad_probs = dot_nt(g_att[:, here], all_v[:, here])
        inner = jnp.sum(grad_probs * probs, axis=-1, keepdims=True)
        grad_scores = (probs * (grad_probs - inner)).astype(BF16)
        v_grads.append(dot_tn(probs.astype(BF16), g_att[:, here]).astype(BF16))
        q_grads.append(dot(grad_scores, key))
        k_grads.append(dot_tn(grad_scores, query))
    rotated = jnp.concatenate(q_grads + k_grads, axis=1) * HD ** (-0.5)
    times = 2 * heads_width // tables.shape[-1]
    cosine = jnp.concatenate([tables[0].reshape(tall, -1)] * times, axis=1)
    sine = jnp.concatenate([tables[1].reshape(tall, -1)] * times, axis=1)
    raw[:, : 2 * heads_width] = (rotated * cosine - swap_halves(rotated) * sine).astype(BF16)
    raw[:, 2 * heads_width :] = jnp.concatenate(v_grads, axis=1)
    def back(block):
        at = pl.ds(pl.multiple_of(block * rows, rows), rows)
        sent = dot_nt(raw[at, :], w[:, : 3 * heads_width]).astype(BF16)
        part[0, lax.div(block, 2), lax.rem(block, 2)] = sent

    turns[1]()
    y, c = give.y, give.c
    back(2 * (1 - y) + 1 - c)
    back(2 * y + 1 - c)
    give.core_send(0)
    back(2 * (1 - y) + c)
    back(2 * y + c)
    give.pair_send(0)
    turns[2]()
    grad_raw = dot_tn(a[...].reshape(tall, width), raw[...]).astype(BF16)
    grad_out = dot_tn(grads, att[...].reshape(tall, heads_width)).astype(BF16)
    if last:
        held[:, :, : 3 * heads_width] = grad_raw.reshape(dp, width // dp, -1)
        held[:, :, 3 * heads_width :] = grad_out.reshape(dp, width // dp, -1)
    else:
        grad_w[:, : 3 * heads_width] = grad_raw
        grad_w[:, 3 * heads_width :] = grad_out
    grad_a = give.total()
    x = x_in[...].astype(F32)
    inverse = lax.rsqrt(jnp.mean(x * x, axis=-1, keepdims=True) + EPSILON)
    unit = x * inverse
    part_gain = jnp.sum(grad_a * unit, axis=0, keepdims=True)
    if last:
        from_t[take.t] = jnp.zeros(from_t.shape[1:], F32)
        from_t[take.t, row : row + 1] = part_gain
        for at, other in zip([at for at in range(last + 1) if at != row], others):
            from_t[take.t, at : at + 1] = other[...]
    else:
        gain_out[...] = part_gain
    out[...] = grad_in[...] + norm_back(grad_a, gain[row : row + 1], unit, inverse)
    if last:
        extra.start(count, total)
        mine = from_t.at[take.t]
        copies = [
            send(mine, mine, ts.at[k], tr.at[k], device) for k, device in enumerate(team)
        ]
        for copy in copies:
            copy.wait_recv()
        from_d[take.d] = jnp.sum(from_t[...], axis=0)
        turns[3]()
        mine = from_d.at[take.d]
        more = [send(mine, mine, ds.at[k], dr.at[k], device) for k, device in enumerate(peers)]
        for turn in turns[4:]:
            turn()
        for copy in more:
            copy.wait_recv()
        gain_out[...] = jnp.sum(from_d[...], axis=0)
        for copy in copies + more:
            copy.wait_send()
    else:
        for turn in turns[3:]:
            turn()
    take.finish()
    give.finish()
    extra.finish()


def attn_backward(
    grad, x, gain, row, weight, tables, marks, spot, kept, others, parts, outer, inner, ident
):
    count = len(parts)
    dma = pltpu.SemaphoreType.DMA
    rows, width = x.shape
    slim = weight.shape[1] // 4
    dp = outer * inner
    last = len(others)
    whole = jax.ShapeDtypeStruct((dp, width // dp, 4 * slim), BF16)
    moved = list(parts) + ([whole] if last else [])
    wide = (8, width) if last else (1, width)
    return pl.pallas_call(
        functools.partial(attn_backward_kernel, outer, inner, count, last, row),
        out_shape=[
            jax.ShapeDtypeStruct((rows, width), F32),
            jax.ShapeDtypeStruct(wide, F32),
        ]
        + ([] if last else [jax.ShapeDtypeStruct(weight.shape, BF16)])
        + push_outs(moved, outer),
        in_specs=[VMEM, VMEM, VMEM, ANY, VMEM, VMEM, VMEM, ANY, ANY, ANY, VMEM, ANY]
        + [VMEM] * last
        + [ANY] * count,
        out_specs=[VMEM, VMEM] + ([] if last else [VMEM]) + [ANY] * len(moved),
        scratch_shapes=[
            pltpu.VMEM(weight.shape, BF16),
            pltpu.VMEM((4, rows, width), BF16),
            pltpu.VMEM((4, rows, 2 * slim), BF16),
            pltpu.VMEM((4, rows, slim), BF16),
            pltpu.VMEM((4, rows, slim), BF16),
            pltpu.VMEM((1, 4, rows, width), BF16),
            pltpu.VMEM((4 * rows, slim), BF16),
            pltpu.VMEM((4 * rows, 3 * slim), BF16),
            pltpu.VMEM((1, 2, 2, rows, width), BF16),
        ]
        + scatter_room(1, rows, width)
        + gather_sems(1)
        + scatter_sems(1)
        + [dma((5,))]
        + push_scratch(moved, outer, inner)
        + (
            [
                pltpu.VMEM(whole.shape, BF16),
                pltpu.VMEM((4, 8, width), F32),
                pltpu.VMEM((dp, 8, width), F32),
                dma((3,)),
                dma((3,)),
                dma((dp,)),
                dma((dp,)),
            ]
            if last
            else []
        ),
        compiler_params=pltpu.CompilerParams(
            collective_id=ident, has_side_effects=True, vmem_limit_bytes=62 << 20
        ),
        name="attn_backward",
    )(grad, x, gain, weight, tables, marks, spot, *kept, *others, *parts)


def pack_kernel(outer, dp, *refs):
    cut = Cut(refs)
    place, lengths, freqs, ids, gates, gain_attn, gain_ffn = cut(7)
    attn_any, ffn_any = cut(4), cut(6)
    tables, marks, spot, gains, mix = cut(5)
    layers, rows = gain_attn.shape
    attn_out, in_out, down_out = cut(layers), cut(layers), cut(layers)
    attn_in, ffn_in = cut(4), cut(6)
    attn_held, in_held, down_held = cut(layers), cut(layers), cut(layers)
    load_attn, load_ffn, keep = cut(3)
    loads_attn = [
        pltpu.make_async_copy(source, target, load_attn.at[i])
        for i, (source, target) in enumerate(zip(attn_any, attn_in))
    ]
    loads_ffn = [
        [
            pltpu.make_async_copy(source.at[level], target.at[level], load_ffn.at[level, i])
            for i, (source, target) in enumerate(zip(ffn_any, ffn_in))
        ]
        for level in range(layers)
    ]
    for load in sum(loads_ffn, loads_attn):
        load.start()
    count = place.shape[1]
    where = place[...]
    begins, end = jnp.zeros_like(where), 0
    for doc in range(lengths.shape[1]):
        end = end + lengths[0, doc]
        begins = begins + jnp.where(where >= end, lengths[0, doc], 0)
    spot[...] = where.astype(F32)
    lines = jnp.concatenate([where.astype(F32), begins.astype(F32)] * 4, axis=0)
    marks[...] = jnp.transpose(lines).reshape(4, count // 4, 8)
    angles = (where - begins).astype(F32) * freqs[...]
    cosine, sine = jnp.cos(angles), jnp.sin(angles)
    tables[0] = jnp.transpose(jnp.concatenate([cosine] * 4, axis=0)).reshape(4, count // 4, 128)
    tables[1] = jnp.transpose(jnp.concatenate([-sine, sine, -sine, sine], axis=0)).reshape(
        4, count // 4, 128
    )
    experts = mix.shape[0] // layers
    for level in range(layers):
        for e in range(experts):
            row = jnp.zeros((1, count), F32)
            for slot in range(ids.shape[1]):
                here = slice(slot, slot + 1)
                row = row + jnp.where(ids[level, here] == e, gates[level, here], 0.0)
            at = level * experts + e
            mix[at : at + 1] = row
    d = lax.axis_index("dp")
    gains[...] = jnp.zeros_like(gains)
    lane = lax.broadcasted_iota(jnp.int32, (layers, gains.shape[1]), 1)
    inside = (lane >= d * rows) & (lane < (d + 1) * rows)
    for i, gain in enumerate((gain_attn, gain_ffn)):
        wide = jnp.concatenate([gain[...].astype(BF16).astype(F32)] * dp, axis=1)
        gains[i * layers : (i + 1) * layers] = jnp.where(inside, wide, 0.0)
    keeps = []

    def leave(held, target):
        keeps.append(pltpu.make_async_copy(held, target, keep.at[len(keeps)]))
        keeps[-1].start()

    for load in loads_attn:
        load.wait()
    quarter = attn_in[0].shape[2]
    for level in range(layers):
        for i in range(4):
            values = attn_in[i][level]
            values = jnp.transpose(values) if i == 3 else values
            attn_held[level][0, :, i * quarter : (i + 1) * quarter] = values.astype(BF16)
        leave(attn_held[level], attn_out[level])
    for level in range(layers):
        for load in loads_ffn[level]:
            load.wait()
        slim = ffn_in[1].shape[2] // outer
        for group, (held, target) in enumerate(
            ((in_held, in_out), (in_held, in_out), (down_held, down_out))
        ):
            base = (experts + 1) * slim if group == 1 else 0
            for e in range(experts + 1):
                for k in range(outer):
                    cols = slice(k * slim, (k + 1) * slim)
                    if e < experts:
                        values = ffn_in[2 * group][level, e, :, cols]
                    else:
                        values = ffn_in[2 * group + 1][level, :, cols]
                    held[level][k, :, base + e * slim : base + (e + 1) * slim] = values.astype(
                        BF16
                    )
            if group:
                leave(held[level], target[level])
    for copy in keeps:
        copy.wait()


def pack(place, lengths, ids, gates, gain_attn, gain_ffn, attn, ffn, outer, dp):
    dma = pltpu.SemaphoreType.DMA
    layers, rows = gain_attn.shape
    count = place.shape[1]
    width = dp * rows
    experts = ffn[0].shape[1]
    slim = ffn[1].shape[2] // outer
    freqs = (10000.0 ** (-np.arange(HD // 2) / (HD // 2))).astype(np.float32)[:, None]
    blocks = (
        [(1, rows, 4 * attn[0].shape[2])] * layers
        + [(outer, rows, 2 * (experts + 1) * slim)] * layers
        + [(outer, rows, (experts + 1) * slim)] * layers
    )
    return pl.pallas_call(
        functools.partial(pack_kernel, outer, dp),
        out_shape=[
            jax.ShapeDtypeStruct((2, 4, count // 4, 128), F32),
            jax.ShapeDtypeStruct((4, count // 4, 8), F32),
            jax.ShapeDtypeStruct((1, count), F32),
            jax.ShapeDtypeStruct((8, width), F32),
            jax.ShapeDtypeStruct((layers * experts, count), F32),
        ]
        + [jax.ShapeDtypeStruct(block, BF16) for block in blocks],
        in_specs=[VMEM, pl.BlockSpec(memory_space=pltpu.SMEM)] + [VMEM] * 5 + [ANY] * 10,
        out_specs=[VMEM] * 5 + [ANY] * len(blocks),
        scratch_shapes=[pltpu.VMEM(m.shape, F32) for m in attn + ffn]
        + [pltpu.VMEM(block, BF16) for block in blocks]
        + [dma((4,)), dma((layers, 6)), dma((len(blocks),))],
        compiler_params=pltpu.CompilerParams(vmem_limit_bytes=62 << 20),
        name="pack",
    )(place, lengths, jnp.asarray(freqs), ids, gates, gain_attn, gain_ffn, *attn, *ffn)


def unpack_kernel(outer, layers, experts, *refs):
    cut = Cut(refs)
    in_any, down_any, attn_any = cut(layers), cut(layers), cut(layers)
    attn_out, ffn_out = cut(4), cut(6)
    in_v, down_v, attn_v = cut(layers), cut(layers), cut(layers)
    attn_held, ffn_held = cut(4), cut(6)
    load_sem, keep_attn, keep_ffn = cut(3)
    loads = [
        [
            pltpu.make_async_copy(source[level], target[level], load_sem.at[level, i])
            for i, (source, target) in enumerate(
                ((in_any, in_v), (down_any, down_v), (attn_any, attn_v))
            )
        ]
        for level in range(layers)
    ]
    for level in reversed(range(layers)):
        for load in loads[level]:
            load.start()
    keeps = []

    def leave(held, target, sem):
        keeps.append(pltpu.make_async_copy(held, target, sem))
        keeps[-1].start()

    slim = ffn_held[1].shape[2] // outer
    quarter = attn_held[0].shape[2]
    for level in reversed(range(layers)):
        for load in loads[level]:
            load.wait()
        for group, source in enumerate((in_v, in_v, down_v)):
            base = (experts + 1) * slim if group == 1 else 0
            for e in range(experts + 1):
                for k in range(outer):
                    cols = slice(k * slim, (k + 1) * slim)
                    values = source[level][k, :, base + e * slim : base + (e + 1) * slim]
                    if e < experts:
                        ffn_held[2 * group][level, e, :, cols] = values.astype(F32)
                    else:
                        ffn_held[2 * group + 1][level, :, cols] = values.astype(F32)
            for i in (2 * group, 2 * group + 1):
                leave(ffn_held[i].at[level], ffn_out[i].at[level], keep_ffn.at[level, i])
        total = jnp.sum(attn_v[level][...].astype(F32), axis=0)
        for i in range(4):
            values = total[:, i * quarter : (i + 1) * quarter]
            attn_held[i][level] = jnp.transpose(values) if i == 3 else values
            leave(attn_held[i].at[level], attn_out[i].at[level], keep_attn.at[level, i])
    for copy in keeps:
        copy.wait()


def unpack(pushed_in, pushed_down, pushed_attn, experts):
    dma = pltpu.SemaphoreType.DMA
    layers = len(pushed_in)
    outer, rows, third = pushed_down[0].shape
    full = outer * third // (experts + 1)
    quarter = pushed_attn[0].shape[2] // 4
    many, one = (layers, experts, rows, full), (layers, rows, full)
    shapes = [(layers, rows, quarter)] * 3 + [(layers, quarter, rows)] + [many, one] * 3
    moved = pushed_in + pushed_down + pushed_attn
    return pl.pallas_call(
        functools.partial(unpack_kernel, outer, layers, experts),
        out_shape=[jax.ShapeDtypeStruct(shape, F32) for shape in shapes],
        in_specs=[ANY] * len(moved),
        out_specs=[ANY] * 10,
        scratch_shapes=[pltpu.VMEM(part.shape, BF16) for part in moved]
        + [pltpu.VMEM(shape, F32) for shape in shapes]
        + [dma((layers, 3)), dma((layers, 4)), dma((layers, 6))],
        compiler_params=pltpu.CompilerParams(vmem_limit_bytes=62 << 20),
        name="unpack",
    )(*moved)


def layout(place_row, length_row):
    ends = jnp.cumsum(length_row, dtype=jnp.int32)
    after = place_row[:, None] >= ends[None, :]
    begins = jnp.sum(jnp.where(after, length_row[None, :], 0), axis=1, dtype=jnp.int32)
    return place_row - begins


def rope_tables(position):
    half_width = HD // 2
    freqs = 10000.0 ** (-jnp.arange(half_width, dtype=F32) / half_width)
    angles = position.astype(F32)[:, None] * freqs[None, :]
    cosine, sine = jnp.cos(angles), jnp.sin(angles)
    return jnp.stack(
        [
            jnp.concatenate([cosine] * 4, axis=1),
            jnp.concatenate([-sine, sine, -sine, sine], axis=1),
        ]
    )


def norm_back(grad_normed, gain_row, unit_rows, inverse):
    scaled = grad_normed * gain_row
    return inverse * (scaled - unit_rows * jnp.mean(scaled * unit_rows, axis=-1, keepdims=True))


def dot(left, right):
    return jnp.dot(left, right, preferred_element_type=F32)


def dot_nt(left, right):
    return lax.dot_general(left, right, (((1,), (1,)), ((), ())), preferred_element_type=F32)


def dot_tn(left, right):
    return lax.dot_general(left, right, (((0,), (0,)), ((), ())), preferred_element_type=F32)


def make_body(dp):
    outer, inner = split_dp(dp)

    def body(
        tokens,
        place,
        lengths,
        expert_ids,
        gate_values,
        cotangent,
        gain_attn,
        w_query,
        w_key,
        w_value,
        w_out,
        gain_ffn,
        exp_gate,
        exp_up,
        exp_down,
        dense_gate,
        dense_up,
        dense_down,
    ):
        layers, experts, rows, full = exp_gate.shape
        width = tokens.shape[1]
        slim = full // outer
        count = place.shape[1]
        kinds = experts + 1
        merged = rows % 16 == 0
        ids, gates = jnp.swapaxes(expert_ids, 1, 2), jnp.swapaxes(gate_values, 1, 2)
        downs = [jnp.swapaxes(exp_down, 2, 3), jnp.swapaxes(dense_down, 1, 2)]
        ffn = [exp_gate, dense_gate, exp_up, dense_up] + downs
        if merged:
            attn = [w_query, w_key, w_value, w_out]
            tables, marks, spot, gains_own, mix_own, *blocks = pack(
                place, lengths, ids, gates, gain_attn, gain_ffn, attn, ffn, outer, dp
            )
            attn_own = blocks[:layers]
            ffn_own = list(zip(blocks[layers : 2 * layers], blocks[2 * layers :]))
        else:
            position = layout(place[0], lengths[0])
            place_row = place[0].astype(F32)
            marks = jnp.stack([place_row, place_row - position.astype(F32)] * 4, axis=1)
            marks = marks.reshape(4, count // 4, 8)
            spot = place_row[None]
            tables = rope_tables(position).reshape(2, 4, count // 4, 128)
            slots = ids[:, None] == jnp.arange(experts, dtype=jnp.int32)[None, :, None, None]
            mix_own = jnp.sum(jnp.where(slots, gates[:, None], 0.0), axis=2)
            mix_own = mix_own.reshape(layers * experts, count)
            gains_own = jnp.concatenate([gain_attn, gain_ffn], axis=0).astype(BF16).astype(F32)
            spots = jnp.arange(dp, dtype=jnp.int32) == lax.axis_index("dp")
            gains_own = jnp.where(spots[None, :, None], gains_own[:, None], 0.0)
            gains_own = jnp.pad(
                gains_own.reshape(2 * layers, width), ((0, 8 - 2 * layers), (0, 0))
            )
            attn_own, ffn_own = [], []
            for level in range(layers):
                mats = [w_query[level], w_key[level], w_value[level], jnp.transpose(w_out[level])]
                attn_own.append(jnp.concatenate(mats, axis=1).astype(BF16)[None])
                mats = []
                for many, one in ((0, 1), (2, 3), (4, 5)):
                    mats += [ffn[many][level, e] for e in range(experts)] + [ffn[one][level]]
                mats = [m.astype(BF16) for m in mats]
                ffn_own.append(
                    [
                        jnp.stack(
                            [
                                jnp.concatenate(
                                    [m[:, k * slim : (k + 1) * slim] for m in group], axis=1
                                )
                                for k in range(outer)
                            ]
                        )
                        for group in (mats[: 2 * kinds], mats[2 * kinds :])
                    ]
                )
        state = tokens
        lead = [gains_own[None], attn_own[0], mix_own[None]]
        if merged:
            state_in = state
            ahead = [ffn_own[1][1]] if layers > 1 else []
            state, *kept = attn_forward(
                state_in,
                None,
                0,
                None,
                tables,
                marks,
                spot,
                lead + list(ffn_own[0]) + ahead,
                [BOTH] * 5 + [OUTER] * len(ahead),
                outer,
                inner,
                0,
            )
            part_down = kept.pop() if ahead else None
            gains, _, first, mix_all, w_in, w_down = kept[-6:]
            kept = kept[:-6]
        else:
            gains_all, first, mix_all = fetch(lead, outer, inner, 8)
            part_down = None
            gains = jnp.sum(gains_all, axis=0)
        w_attn = [first.reshape(width, -1)]
        w_ffn = []
        kept_attn, kept_ffn = [], []
        for level in range(layers):
            if level == 0 and merged:
                before = state_in
            else:
                before = state
                inside = list(ffn_own[level][: 1 if level else 2])
                state, *kept = attn_forward(
                    before,
                    gains,
                    level,
                    w_attn[level],
                    tables,
                    marks,
                    spot,
                    inside,
                    [BOTH] * len(inside),
                    outer,
                    inner,
                    1 if level else 11,
                )
                if level:
                    w_in = kept.pop()
                else:
                    w_down, w_in = kept.pop(), kept.pop()
            kept_attn.append((before, kept))
            w_ffn.append((w_in.reshape(width, -1), w_down.reshape(width, -1)))
            resid = state
            more, modes = [], []
            if level + 1 < layers:
                half = part_down is not None and level == 0
                more = [attn_own[level + 1], part_down if half else ffn_own[level + 1][1]]
                modes = [BOTH, INNER if half else BOTH]
            state, b_in, both, *fetched = ffn_forward(
                resid,
                gains,
                level,
                layers + level,
                kinds,
                mix_all,
                *w_ffn[level],
                more,
                modes,
                outer,
                inner,
                (2 if level == 0 else 12) if more else 3,
            )
            if more:
                w_attn.append(fetched[0].reshape(width, -1))
                w_down = fetched[1]
            kept_ffn.append((resid, b_in, both))
        mixed = state.astype(BF16)

        grad = cotangent
        part_gains = [None] * (2 * layers)
        pushed_in, pushed_down = [None] * layers, [None] * layers
        pushed_attn = [None] * layers
        waiting = []
        for level in reversed(range(layers)):
            resid, b_in, both = kept_ffn[level]
            grad, part_gain, grad_in, grad_down, *moved = ffn_backward(
                grad,
                resid,
                gains,
                level,
                layers + level,
                kinds,
                mix_all,
                *w_ffn[level],
                b_in,
                both,
                waiting,
                outer,
                inner,
                4 if waiting else 5,
            )
            part_gains[layers + level] = part_gain
            if waiting:
                (pushed_attn[level + 1],) = moved
            before, kept = kept_attn[level]
            inside = [grad_in.reshape(dp, rows, -1), grad_down.reshape(dp, rows, -1)]
            others = part_gains[1:] if level == 0 and merged else []
            grad, part_gain, *moved = attn_backward(
                grad,
                before,
                gains,
                level,
                w_attn[level],
                tables,
                marks,
                spot,
                kept,
                others,
                inside,
                outer,
                inner,
                6 if level else 7,
            )
            if level == 0 and merged:
                pushed_in[0], pushed_down[0], pushed_attn[0] = moved
                gain_sum = lax.dynamic_slice_in_dim(
                    part_gain, lax.axis_index("dp") * rows, rows, axis=1
                )
                continue
            part_gains[level] = part_gain
            waiting = [moved[0].reshape(dp, rows, -1)]
            pushed_in[level], pushed_down[level] = moved[1:]
        if not merged:
            stacked = jnp.concatenate(part_gains, axis=0)
            stacked = jnp.pad(stacked, ((0, 8 - 2 * layers), (0, 0)))
            stacked = jnp.transpose(stacked.reshape(8, dp, rows), (1, 0, 2))
            pushed_attn[0], gain_parts = push([waiting[0], stacked], outer, inner, 9)
            gain_part = jnp.sum(gain_parts, axis=0)
            gain_sum = jnp.sum(
                gather(jnp.pad(gain_part, ((0, 0), (0, 128 - rows))), dp, 10)[0], axis=0
            )
        grad_gain_attn = gain_sum[:layers, :rows]
        grad_gain_ffn = gain_sum[layers : 2 * layers, :rows]

        if merged:
            query, key, value, out, gate, gate_d, up, up_d, down, down_d = unpack(
                pushed_in, pushed_down, pushed_attn, experts
            )
        else:
            ups, downs, attns = [], [], []
            for level in range(layers):
                parts = pushed_in[level].reshape(outer, rows, 2 * kinds, slim)
                ups.append(jnp.transpose(parts, (2, 1, 0, 3)).reshape(2 * kinds, rows, full))
                parts = pushed_down[level].reshape(outer, rows, kinds, slim)
                downs.append(jnp.transpose(parts, (2, 1, 0, 3)).reshape(kinds, rows, full))
                attns.append(jnp.sum(pushed_attn[level].astype(F32), axis=0))
            ups, downs = jnp.stack(ups).astype(F32), jnp.stack(downs).astype(F32)
            gate, gate_d = ups[:, :experts], ups[:, experts]
            up, up_d = ups[:, kinds : kinds + experts], ups[:, kinds + experts]
            down, down_d = downs[:, :experts], downs[:, experts]
            query, key, value, out = jnp.split(jnp.stack(attns), 4, axis=2)
            out = jnp.swapaxes(out, 1, 2)
        return (
            mixed,
            grad,
            grad_gain_attn,
            query,
            key,
            value,
            out,
            grad_gain_ffn,
            gate,
            up,
            jnp.swapaxes(down, 2, 3),
            gate_d,
            up_d,
            jnp.swapaxes(down_d, 1, 2),
        )

    return body


def solution(mesh):
    return jax.shard_map(
        make_body(mesh.shape["dp"]),
        mesh=mesh,
        in_specs=(
            P(("dp", "tensor"), None),
            P("dp", None),
            P("dp", None),
            P(None, "dp", None),
            P(None, "dp", None),
            P(("dp", "tensor"), None),
            P(None, "dp"),
            P(None, "dp", "tensor"),
            P(None, "dp", "tensor"),
            P(None, "dp", "tensor"),
            P(None, "tensor", "dp"),
            P(None, "dp"),
            P(None, None, "dp", "tensor"),
            P(None, None, "dp", "tensor"),
            P(None, None, "tensor", "dp"),
            P(None, "dp", "tensor"),
            P(None, "dp", "tensor"),
            P(None, "tensor", "dp"),
        ),
        out_specs=(
            P(("dp", "tensor"), None),
            P(("dp", "tensor"), None),
            P(None, "dp"),
            P(None, "dp", "tensor"),
            P(None, "dp", "tensor"),
            P(None, "dp", "tensor"),
            P(None, "tensor", "dp"),
            P(None, "dp"),
            P(None, None, "dp", "tensor"),
            P(None, None, "dp", "tensor"),
            P(None, None, "tensor", "dp"),
            P(None, "dp", "tensor"),
            P(None, "dp", "tensor"),
            P(None, "tensor", "dp"),
        ),
        check_vma=False,
    )
```

```python
import functools

import jax
import jax.numpy as jnp
import numpy as np
from jax import lax
from jax.experimental import pallas as pl
from jax.experimental.pallas import tpu as pltpu
from jax.sharding import PartitionSpec as P

HD = 64
EPSILON = 1e-06
MASKED_SCORE = -1e30
MESH = pl.DeviceIdType.MESH
ANY = pl.BlockSpec(memory_space=pl.ANY)
VMEM = pl.BlockSpec(memory_space=pltpu.VMEM)
F32 = jnp.float32
BF16 = jnp.bfloat16
PARTS = 2
BOTH, OUTER, INNER = range(3)


def split_dp(dp):
    inner = 2 ** ((dp.bit_length() - 1) // 2)
    return dp // inner, inner


def place_of(inner):
    d = lax.axis_index("dp")
    return lax.div(d, inner), lax.rem(d, inner), lax.axis_index("tensor")


def across(t):
    return lax.rem(t + 2, 4), t + 1 - 2 * lax.rem(t, 2)


def meet(devices):
    barrier = pltpu.get_barrier_semaphore()
    for device in devices:
        pl.semaphore_signal(barrier, inc=1, device_id=device, device_id_type=MESH)
    pl.semaphore_wait(barrier, len(devices))


def send(source, target, send_sem, recv_sem, device):
    copy = pltpu.make_async_remote_copy(
        src_ref=source,
        dst_ref=target,
        send_sem=send_sem,
        recv_sem=recv_sem,
        device_id=device,
        device_id_type=MESH,
    )
    copy.start()
    return copy


def gather_kernel(dp, own, out, *sems):
    take = Gather(1, dp, out, sems)
    out[0, take.t] = own[...]
    meet(take.friends())
    take.start()
    take.complete(0)
    take.finish()


def gather(own, dp, ident):
    return pl.pallas_call(
        functools.partial(gather_kernel, dp),
        out_shape=jax.ShapeDtypeStruct((1, 4) + own.shape, own.dtype),
        in_specs=[VMEM],
        out_specs=VMEM,
        scratch_shapes=gather_sems(1),
        compiler_params=pltpu.CompilerParams(collective_id=ident, has_side_effects=True),
        name="gather",
    )(own)


def fetch_kernel(outer, inner, count, *refs):
    cut = Cut(refs)
    extra = Fetch(outer, inner, cut(count), cut(count), cut(count), cut(5), [BOTH] * count)
    meet(extra.zdev[1:] + extra.xdev)
    extra.start()
    extra.settle()
    for turn in extra.turns():
        turn()
    extra.finish()


def fetch(owns, outer, inner, ident):
    count = len(owns)
    return pl.pallas_call(
        functools.partial(fetch_kernel, outer, inner, count),
        out_shape=fetch_outs(owns, outer, inner, [BOTH] * count),
        in_specs=[ANY] * count,
        out_specs=[ANY] * count,
        scratch_shapes=fetch_scratch(owns, outer, inner, [BOTH] * count),
        compiler_params=pltpu.CompilerParams(collective_id=ident, has_side_effects=True),
        name="fetch",
    )(*owns)


def push_kernel(outer, inner, count, *refs):
    cut = Cut(refs)
    extra = Push(outer, inner, cut(count), cut(count), cut(3 * count), cut(6))
    meet(extra.zdev[:-1] + extra.xdev)
    extra.start()
    for turn in extra.turns():
        turn()
    extra.finish()


def push(parts, outer, inner, ident):
    count = len(parts)
    return pl.pallas_call(
        functools.partial(push_kernel, outer, inner, count),
        out_shape=push_outs(parts, outer),
        in_specs=[ANY] * count,
        out_specs=[ANY] * count,
        scratch_shapes=push_scratch(parts, outer, inner),
        compiler_params=pltpu.CompilerParams(collective_id=ident, has_side_effects=True),
        name="push",
    )(*parts)


def nearest(index, size, step):
    table = [sorted(range(size), key=lambda other: (abs(other - at), other)) for at in range(size)]
    found = 0
    for at in range(size):
        found = found + jnp.where(index == at, table[at][step], 0)
    return found


class Gather:
    def __init__(self, outer, inner, table, sems, parts=1):
        self.outer, self.inner, self.table, self.parts = outer, inner, table, parts
        self.zs, self.zr, self.ys, self.yr, self.cs, self.cr = sems
        self.dz, self.dx, self.t = place_of(inner)
        self.d = lax.axis_index("dp")
        self.size = table.shape[2] // parts
        ty, tc = across(self.t)
        self.ty = ty
        self.pair, self.core = (self.d, ty), (self.d, tc)
        self.source = [nearest(self.dz, outer, step) for step in range(outer)]
        self.zdev = [(source * inner + self.dx, self.t) for source in self.source]
        self.steps = outer * parts
        self.yc, self.cc, self.dc = [], [], []

    def friends(self):
        return self.zdev[1:] + [self.pair, self.core]

    def rows(self, step):
        return pl.ds(step % self.parts * self.size, self.size)

    def origin(self, step):
        return self.source[step // self.parts]

    def outward(self, step, target, sent):
        at = self.origin(step) * self.parts + step % self.parts
        block = self.table.at[self.origin(step), self.t, self.rows(step)]
        target = jnp.minimum(jnp.maximum(target, 0), self.outer - 1)
        return pltpu.make_async_remote_copy(
            src_ref=block,
            dst_ref=block,
            send_sem=self.zs.at[at if sent is None else sent],
            recv_sem=self.zr.at[at],
            device_id=(target * self.inner + self.dx, self.t),
            device_id_type=MESH,
        )

    def passes(self, step):
        if self.outer == 1:
            return []
        if step < self.parts:
            last = self.steps + step
            return [
                (self.dz < self.outer - 1, self.outward(step, self.dz + 1, None)),
                (self.dz > 0, self.outward(step, self.dz - 1, last)),
            ]
        ahead = jnp.where(self.origin(step) < self.dz, self.dz + 1, self.dz - 1)
        inside = (ahead >= 0) & (ahead < self.outer)
        return [(inside, self.outward(step, ahead, None))]

    def start(self):
        for step in range(self.parts):
            for inside, copy in self.passes(step):
                pl.when(inside)(copy.start)
        for step in range(self.parts):
            self.forward(step)

    def hop(self, step):
        ((inside, copy),) = self.passes(step)

        @pl.when(inside)
        def _():
            copy.wait_recv()
            copy.start()

    def arrive(self, step):
        ((inside, copy),) = self.passes(step)
        pl.when(jnp.logical_not(inside))(copy.wait_recv)
        self.forward(step)

    def forward(self, step):
        block = self.table.at[self.origin(step), self.t, self.rows(step)]
        self.yc.append(send(block, block, self.ys.at[step], self.yr.at[step], self.pair))
        self.cc.append(send(block, block, self.cs.at[step], self.cr.at[step], self.core))

    def complete(self, step):
        self.yc[step].wait_recv()
        at = self.steps + step
        block = self.table.at[self.origin(step), self.ty, self.rows(step)]
        self.dc.append(send(block, block, self.cs.at[at], self.cr.at[at], self.core))
        self.cc[step].wait_recv()
        self.dc[step].wait_recv()

    def finish(self):
        for step in range(self.steps):
            for inside, copy in self.passes(step):
                pl.when(inside)(copy.wait_send)
        for copy in self.yc + self.cc + self.dc:
            copy.wait_send()


class Scatter:
    def __init__(self, outer, inner, part, room, sems, parts=1):
        self.outer, self.part, self.parts = outer, part, parts
        self.from_c, self.from_y, self.from_z = room
        self.cs, self.cr, self.ys, self.yr, self.zs, self.zr = sems
        dz, dx, t = place_of(inner)
        d = lax.axis_index("dp")
        ty, tc = across(t)
        self.size = part.shape[3] // parts
        self.dz, self.y, self.c = dz, lax.div(t, 2), lax.rem(t, 2)
        self.pair, self.core = (d, ty), (d, tc)
        self.source = [nearest(dz, outer, step) for step in range(outer)]
        self.zdev = [(source * inner + dx, t) for source in self.source]
        self.steps = outer * parts
        self.cc, self.yc, self.zc = {}, {}, {}

    def rows(self, step):
        return pl.ds(step % self.parts * self.size, self.size)

    def core_send(self, step):
        source = self.source[step // self.parts]
        self.cc[step] = send(
            self.part.at[source, :, 1 - self.c, self.rows(step)],
            self.from_c.at[step],
            self.cs.at[step],
            self.cr.at[step],
            self.core,
        )

    def pair_send(self, step):
        source = self.source[step // self.parts]
        self.cc[step].wait_recv()
        mine = self.part[source, :, self.c, self.rows(step)].astype(F32)
        self.from_c[step] = (mine + self.from_c[step].astype(F32)).astype(BF16)
        self.yc[step] = send(
            self.from_c.at[step, 1 - self.y],
            self.from_y.at[step],
            self.ys.at[step],
            self.yr.at[step],
            self.pair,
        )

    def summed(self, step):
        self.yc[step].wait_recv()
        return self.from_c[step, self.y].astype(F32) + self.from_y[step].astype(F32)

    def outward(self, step, source, away):
        at = (away - 1) * self.parts + step % self.parts
        return pltpu.make_async_remote_copy(
            src_ref=source,
            dst_ref=self.from_z.at[at],
            send_sem=self.zs.at[at],
            recv_sem=self.zr.at[at],
            device_id=self.zdev[step // self.parts],
            device_id_type=MESH,
        )

    def outer_send(self, step):
        self.from_y[step] = self.summed(step).astype(BF16)
        away = lax.rem(self.source[step // self.parts] - self.dz + self.outer, self.outer)
        self.zc[step] = self.outward(step, self.from_y.at[step], away)
        self.zc[step].start()

    def total(self):
        pieces = []
        for piece in range(self.parts):
            total = self.summed(piece)
            for step in range(self.parts + piece, self.steps, self.parts):
                away = lax.rem(self.dz - self.source[step // self.parts] + self.outer, self.outer)
                self.outward(step, self.from_y.at[step], away).wait_recv()
                at = (away - 1) * self.parts + piece
                total = total + self.from_z[at].astype(F32)
            pieces.append(total)
        return pieces[0] if self.parts == 1 else jnp.concatenate(pieces, axis=0)

    def finish(self):
        for group in (self.cc, self.yc, self.zc):
            for step in group:
                group[step].wait_send()


def gather_sems(outer, parts=1):
    dma = pltpu.SemaphoreType.DMA
    steps = outer * parts
    return [dma((steps + parts,))] + [dma((steps,)) for _ in range(3)] + [dma((2 * steps,))] * 2


def scatter_sems(outer, parts=1):
    dma = pltpu.SemaphoreType.DMA
    return [dma((outer * parts,)) for _ in range(6)]


def scatter_room(outer, rows, width, parts=1):
    steps, size = outer * parts, rows // parts
    return [
        pltpu.VMEM((steps, 2, size, width), BF16),
        pltpu.VMEM((steps, size, width), BF16),
        pltpu.VMEM((max(steps - parts, 1), size, width), BF16),
    ]


def pipeline(take, give, compute, begin, after, post, middle, since, late):
    steps, parts = take.steps, take.parts
    middle, late = list(middle), list(late)
    lag = parts + 1
    take.start()
    begin()
    hops = list(range(parts, steps))
    for _ in range(min(2 * parts, len(hops))):
        take.hop(hops.pop(0))
    for step in range(steps):
        if step + parts < steps:
            take.arrive(step + parts)
        take.complete(step)
        if step > parts:
            give.pair_send(step - 1)
        compute(step)
        give.core_send(step)
        for _ in range(min(parts, len(hops))):
            take.hop(hops.pop(0))
        if step - lag >= parts:
            give.outer_send(step - lag)
        if step == 1:
            after()
        if step >= since and middle:
            middle.pop(0)()
        post(step)
    sent = max(parts, steps - lag)
    late = middle + late
    give.pair_send(steps - 1)
    for step in range(parts):
        give.pair_send(step)
    for step in range(sent, steps):
        if late:
            late.pop(0)()
        give.outer_send(step)
    for work in late:
        work()


def pieces_of(arrays, halves=True):
    items = []
    for i, array in enumerate(arrays):
        wide = array.shape[-1]
        count = 2 if halves and wide % 256 == 0 and wide > 1024 else 1
        size = wide // count
        items += [(i, slice(at * size, (at + 1) * size)) for at in range(count)]
    return items


class Fetch:
    def __init__(self, outer, inner, owns, outs, holds, sems, modes):
        self.outer, self.inner, self.owns, self.outs, self.holds = outer, inner, owns, outs, holds
        self.zs, self.zr, self.xs, self.xr, self.ls = sems
        self.modes, self.items = modes, pieces_of(owns)
        self.dz, dx, t = place_of(inner)
        self.dx, self.d = dx, lax.axis_index("dp")
        self.source = [nearest(self.dz, outer, step) for step in range(outer)]
        self.zdev = [(source * inner + dx, t) for source in self.source]
        self.xdev = [(self.dz * inner + lax.rem(dx + j, inner), t) for j in range(1, inner)]
        self.zc, self.xc, self.into, self.back = [], {}, {}, {}

    def own(self, item, where):
        i, cols = self.items[item]
        return self.owns[i].at[where if self.owns[i].shape[0] == self.outer else 0, :, cols]

    def slot(self, item, source):
        i, cols = self.items[item]
        if self.modes[i] != OUTER:
            source = source * self.inner + self.dx
        return self.outs[i].at[source, :, cols]

    def mode(self, item):
        return self.modes[self.items[item][0]]

    def chosen(self, first, last):
        last = len(self.owns) if last is None else last
        return [item for item, (i, _) in enumerate(self.items) if first <= i < last]

    def copy(self, item, step, away, refs):
        at = item * self.outer + lax.rem(away + self.outer, self.outer)
        return pltpu.make_async_remote_copy(
            src_ref=refs[0],
            dst_ref=refs[1],
            send_sem=self.zs.at[at],
            recv_sem=self.zr.at[at],
            device_id=self.zdev[step],
            device_id_type=MESH,
        )

    def start(self, first=0, last=None, aside=True):
        for item in self.chosen(first, last):
            i, cols = self.items[item]
            if self.mode(item) == INNER:
                for step, source in enumerate(self.source):
                    here = self.owns[i].at[source, :, cols]
                    self.spread(item, step, here, self.slot(item, source))
                continue
            for step in range(1, self.outer):
                source = self.source[step]
                refs = (self.own(item, source), self.slot(item, self.dz))
                self.zc.append(self.copy(item, step, source - self.dz, refs))
                self.zc[-1].start()
            if aside:
                self.aside(item)
        for i in range(first, len(self.owns) if last is None else last):
            where = self.dz if self.owns[i].shape[0] == self.outer else 0
            here = self.owns[i] if self.modes[i] == INNER else self.owns[i].at[where]
            at = i * (self.outer + 1)
            self.into[i] = pltpu.make_async_copy(here, self.holds[i], self.ls.at[at])
            self.into[i].start()

    def aside(self, item):
        if self.mode(item) == BOTH:
            self.spread(item, 0, self.own(item, self.dz), self.slot(item, self.dz))

    def spread(self, item, step, block, target):
        for j in range(1, self.inner):
            at = (item * self.outer + step) * self.inner + j
            self.xc[item, step, j] = send(
                block, target, self.xs.at[at], self.xr.at[at], self.xdev[j - 1]
            )

    def settle(self):
        for i, into in self.into.items():
            into.wait()
            at = i * (self.outer + 1)
            target = self.outs[i]
            if self.modes[i] == INNER:
                pairs = [
                    (self.holds[i].at[source], target.at[source * self.inner + self.dx])
                    for source in self.source
                ]
            else:
                here = self.dz if self.modes[i] == OUTER else self.d
                pairs = [(self.holds[i], target.at[here])]
            self.back[i] = [
                pltpu.make_async_copy(*pair, self.ls.at[at + 1 + k])
                for k, pair in enumerate(pairs)
            ]
            for copy in self.back[i]:
                copy.start()

    def turn(self, item, step):
        source = self.source[step]
        block = self.slot(item, source)
        self.copy(item, step, self.dz - source, (block, block)).wait_recv()
        if self.mode(item) == BOTH:
            self.spread(item, step, block, block)

    def turns(self, first=0, last=None):
        return [
            functools.partial(self.turn, item, step)
            for item in self.chosen(first, last)
            for step in range(1, self.outer)
            if self.mode(item) != INNER
        ]

    def land(self, i):
        for key in self.xc:
            if self.items[key[0]][0] == i:
                self.xc[key].wait_recv()
        for copy in self.back[i]:
            copy.wait()

    def finish(self, first=0):
        for key in self.xc:
            if self.items[key[0]][0] >= first:
                self.xc[key].wait_recv()
            self.xc[key].wait_send()
        for copy in self.zc:
            copy.wait_send()
        for i in self.back:
            if i >= first:
                for copy in self.back[i]:
                    copy.wait()


def fetch_outs(owns, outer, inner, modes):
    return [
        jax.ShapeDtypeStruct(
            (outer if mode == OUTER else outer * inner,) + own.shape[1:], own.dtype
        )
        for own, mode in zip(owns, modes)
    ]


def fetch_scratch(owns, outer, inner, modes):
    dma = pltpu.SemaphoreType.DMA
    count = max(len(pieces_of(owns)), 1)
    return [
        pltpu.VMEM(own.shape if mode == INNER else own.shape[1:], own.dtype)
        for own, mode in zip(owns, modes)
    ] + [
        dma((count * outer,)),
        dma((count * outer,)),
        dma((count * outer * inner,)),
        dma((count * outer * inner,)),
        dma((max(len(owns), 1) * (outer + 1),)),
    ]


class Push:
    def __init__(self, outer, inner, parts, outs, room, sems, halves=True):
        count = len(parts)
        self.outer, self.inner, self.parts, self.outs = outer, inner, parts, outs
        self.items = pieces_of(parts, halves)
        self.froms, self.mine, self.sums = room[:count], room[count : 2 * count], room[2 * count :]
        self.xs, self.xr, self.zs, self.zr, self.ls, self.ks = sems
        self.dz, dx, t = place_of(inner)
        self.dx = dx
        near = [nearest(self.dz, outer, step) for step in range(outer)]
        self.source = near[:0:-1] + near[:1]
        self.zdev = [(source * inner + dx, t) for source in self.source]
        self.xdev = [(self.dz * inner + lax.rem(dx + j, inner), t) for j in range(1, inner)]
        self.xc, self.zc, self.loads, self.keeps = {}, [], {}, []

    def start(self, first=0, last=None):
        last = len(self.parts) if last is None else last
        chosen = [entry for entry in enumerate(self.items) if first <= entry[1][0] < last]
        for step, source in enumerate(self.source):
            for item, (i, cols) in chosen:
                for j in range(1, self.inner):
                    slot = source * self.inner + lax.rem(self.dx + j, self.inner)
                    at = (item * self.outer + step) * self.inner + j
                    self.xc[item, step, j] = send(
                        self.parts[i].at[slot, :, cols],
                        self.froms[i].at[j - 1, step, :, cols],
                        self.xs.at[at],
                        self.xr.at[at],
                        self.xdev[j - 1],
                    )
                self.loads[item, step] = pltpu.make_async_copy(
                    self.parts[i].at[source * self.inner + self.dx, :, cols],
                    self.mine[i].at[step, :, cols],
                    self.ls.at[item * self.outer + step],
                )
                self.loads[item, step].start()

    def turn(self, item, step):
        i, cols = self.items[item]
        self.loads[item, step].wait()
        total = self.mine[i][step, :, cols].astype(F32)
        for j in range(1, self.inner):
            self.xc[item, step, j].wait_recv()
            total = total + self.froms[i][j - 1, step, :, cols].astype(F32)
        self.sums[i][step, :, cols] = total.astype(self.sums[i].dtype)
        source = self.sums[i].at[step, :, cols]
        target = self.outs[i].at[self.dz, :, cols]
        if step < self.outer - 1:
            away = lax.rem(self.source[step] - self.dz + self.outer, self.outer)
            at = item * self.outer + away
            self.zc.append(send(source, target, self.zs.at[at], self.zr.at[at], self.zdev[step]))
        else:
            self.keeps.append(pltpu.make_async_copy(source, target, self.ks.at[item]))
            self.keeps[-1].start()

    def turns(self, first=0, last=None):
        last = len(self.parts) if last is None else last
        return [
            functools.partial(self.turn, item, step)
            for step in range(self.outer)
            for item, (i, _) in enumerate(self.items)
            if first <= i < last
        ]

    def finish(self):
        for copy in self.zc:
            copy.wait_recv()
            copy.wait_send()
        for key in self.xc:
            self.xc[key].wait_send()
        for copy in self.keeps:
            copy.wait()


def push_outs(parts, outer):
    return [jax.ShapeDtypeStruct((outer,) + part.shape[1:], part.dtype) for part in parts]


def push_scratch(parts, outer, inner):
    dma = pltpu.SemaphoreType.DMA
    count = max(len(pieces_of(parts)), 1)
    across_x = [pltpu.VMEM((inner - 1, outer) + part.shape[1:], part.dtype) for part in parts]
    own = [pltpu.VMEM((outer,) + part.shape[1:], part.dtype) for part in parts]
    return (
        across_x
        + own
        + own
        + [
            dma((count * outer * inner,)),
            dma((count * outer * inner,)),
            dma((count * outer,)),
            dma((count * outer,)),
            dma((count * outer,)),
            dma((count,)),
        ]
    )


class Cut:
    def __init__(self, refs):
        self.refs, self.at = refs, 0

    def __call__(self, count):
        self.at += count
        return self.refs[self.at - count : self.at]


class Mixer:
    def __init__(self, outer, inner, table, lines, mix, sems):
        self.lines, self.mix = lines, mix
        dx = lax.rem(lax.axis_index("dp"), inner)
        self.loads = [
            pltpu.make_async_copy(table.at[at * inner + dx], lines.at[at], sems.at[at])
            for at in range(outer)
        ]
        for load in self.loads:
            load.start()

    def turn(self):
        for at, load in enumerate(self.loads):
            load.wait()
            self.mix[at] = jnp.transpose(self.lines[at]).reshape(self.mix.shape[1:])


def ffn_forward_kernel(outer, inner, kinds, modes, level, row, *refs):
    count = len(modes)
    cut = Cut(refs)
    resid, gain, mix_any, w_in_any, w_down_any = cut(5)
    owns = cut(count)
    out, b_out, gu_out = cut(3)
    fetched = cut(count)
    w_in, w_down, b, gu, hid, part, mix_rows, mix = cut(8)
    room, take_sems, give_sems = cut(3), cut(6), cut(6)
    load_sem, keep_b, keep_gu, load_mix = cut(4)
    extra = Fetch(outer, inner, owns, fetched, cut(count), cut(5), modes) if count else None
    rows, width = resid.shape
    third = w_down.shape[1]
    slim = third // kinds
    loads = [
        pltpu.make_async_copy(w_in_any, w_in, load_sem.at[0]),
        pltpu.make_async_copy(w_down_any, w_down, load_sem.at[1]),
    ]
    for load in loads:
        load.start()
    take = Gather(outer, inner, b, take_sems, PARTS)
    give = Scatter(outer, inner, part, room, give_sems, PARTS)
    size = rows // PARTS
    mixer = Mixer(outer, inner, mix_any, mix_rows, mix, load_mix)
    x = resid[...]
    inverse = lax.rsqrt(jnp.mean(x * x, axis=-1, keepdims=True) + EPSILON)
    b[take.dz, take.t] = (x * inverse * gain[row : row + 1]).astype(BF16)
    meet(take.friends() + (extra.xdev if count else []))
    keeps = []

    def compute(step):
        source, q = take.origin(step), step % PARTS
        here = take.rows(step)
        if step == 0:
            for load in loads:
                load.wait()
        rows_in = b[source, :, here].reshape(4 * size, width)

        scale = mix[source, :, here].reshape(4 * size, mix.shape[-1])
        both = dot(rows_in, w_in[...])
        gu[source, q] = both.astype(BF16)
        gate, up = both[:, :third], both[:, third:]
        hidden = gate * jax.nn.sigmoid(gate) * up
        for e in range(kinds):
            piece = hidden[:, e * slim : (e + 1) * slim]
            if e < kinds - 1:
                col = level * (kinds - 1) + e
                piece = piece * scale[:, col : col + 1]
            hid[:, e * slim : (e + 1) * slim] = piece.astype(BF16)

        @pl.loop(0, width // 256)
        def _(at):
            cols = pl.ds(pl.multiple_of(at * 256, 256), 256)
            sent = dot_nt(hid[...], w_down[cols]).astype(BF16)
            part[source, :, :, here, cols] = sent.reshape(2, 2, size, 256)

        if q == PARTS - 1:
            at = step // PARTS
            keeps.append(pltpu.make_async_copy(b.at[source], b_out.at[source], keep_b.at[at]))
            keeps.append(pltpu.make_async_copy(gu.at[source], gu_out.at[source], keep_gu.at[at]))
            keeps[-1].start()
            keeps[-2].start()

    def after():
        if count:
            extra.start()
            extra.settle()

    turns = extra.turns() if count else []
    half = take.steps // 2
    pipeline(take, give, compute, mixer.turn, after, lambda step: None, turns, half, [])
    out[...] = resid[...] + give.total()
    take.finish()
    give.finish()
    if count:
        extra.finish()
    for keep in keeps:
        keep.wait()


def ffn_forward(
    resid, gain, level, row, kinds, mix, w_in, w_down, owns, modes, outer, inner, ident
):
    dma = pltpu.SemaphoreType.DMA
    rows, width = resid.shape
    third = w_down.shape[1]
    count = len(owns)
    return pl.pallas_call(
        functools.partial(ffn_forward_kernel, outer, inner, kinds, modes, level, row),
        out_shape=[
            jax.ShapeDtypeStruct((rows, width), F32),
            jax.ShapeDtypeStruct((outer, 4, rows, width), BF16),
            jax.ShapeDtypeStruct((outer, PARTS, 4 * rows // PARTS, 2 * third), BF16),
        ]
        + fetch_outs(owns, outer, inner, modes),
        in_specs=[VMEM, VMEM, ANY, ANY, ANY] + [ANY] * count,
        out_specs=[VMEM, ANY, ANY] + [ANY] * count,
        scratch_shapes=[
            pltpu.VMEM(w_in.shape, BF16),
            pltpu.VMEM(w_down.shape, BF16),
            pltpu.VMEM((outer, 4, rows, width), BF16),
            pltpu.VMEM((outer, PARTS, 4 * rows // PARTS, 2 * third), BF16),
            pltpu.VMEM((4 * rows // PARTS, third), BF16),
            pltpu.VMEM((outer, 2, 2, rows, width), BF16),
            pltpu.VMEM((outer,) + mix.shape[1:], F32),
            pltpu.VMEM((outer, 4, rows, mix.shape[1]), F32),
        ]
        + scatter_room(outer, rows, width, PARTS)
        + gather_sems(outer, PARTS)
        + scatter_sems(outer, PARTS)
        + [dma((2,)), dma((outer,)), dma((outer,)), dma((outer,))]
        + (fetch_scratch(owns, outer, inner, modes) if count else []),
        compiler_params=pltpu.CompilerParams(
            collective_id=ident, has_side_effects=True, vmem_limit_bytes=62 << 20
        ),
        name="ffn_forward",
    )(resid, gain, mix, w_in, w_down, *owns)


def ffn_backward_kernel(outer, inner, kinds, count, level, row, *refs):
    cut = Cut(refs)
    grad_y, resid, gain, mix_any, w_in_any, w_down_any, b_any, gu_any = cut(8)
    parts = cut(count)
    out, gain_out, grad_in, grad_down = cut(4)
    pushed = cut(count)
    w_in, w_down, b, gb, gu, dgu, hid, flip_b, flip_gb, part, mix_rows, mix = cut(12)
    room, take_sems, give_sems = cut(3), cut(6), cut(6)
    load_sem, load_gu, load_mix = cut(3)
    extra = Push(outer, inner, parts, pushed, cut(3 * count), cut(6)) if count else None
    rows, width = resid.shape
    tall = outer * 4 * rows
    third = w_down.shape[1]
    slim = third // kinds
    loads = [
        pltpu.make_async_copy(source, target, load_sem.at[i])
        for i, (source, target) in enumerate(
            ((b_any, b), (w_down_any, w_down), (w_in_any, w_in))
        )
    ]
    for load in loads:
        load.start()
    take = Gather(outer, inner, gb, take_sems, PARTS)
    give = Scatter(outer, inner, part, room, give_sems, PARTS)
    size = rows // PARTS
    mixer = Mixer(outer, inner, mix_any, mix_rows, mix, load_mix)
    fills = [
        pltpu.make_async_copy(gu_any.at[source], gu.at[source], load_gu.at[step])
        for step, source in enumerate(take.source)
    ]
    for fill in fills:
        fill.start()
    gb[take.dz, take.t] = grad_y[...].astype(BF16)
    meet(take.friends() + (extra.xdev if count else []))

    def compute(step):
        source, q = take.origin(step), step % PARTS
        here = take.rows(step)
        if step == 0:
            loads[1].wait()
            loads[2].wait()
        if q == 0:
            fills[step // PARTS].wait()
        rows_in = gb[source, :, here].reshape(4 * size, width)
        mixed = mix[source, :, here].reshape(4 * size, mix.shape[-1])
        grad_hidden = dot(rows_in, w_down[...])
        both = gu[source, q].astype(F32)
        gate, up = both[:, :third], both[:, third:]
        sigma = jax.nn.sigmoid(gate)
        act = gate * sigma
        slope = sigma * (1.0 + gate * (1.0 - sigma))
        hidden, grad_gate, grad_up = act * up, grad_hidden * up * slope, grad_hidden * act
        for e in range(kinds):
            cols = slice(e * slim, (e + 1) * slim)
            more = slice(third + e * slim, third + (e + 1) * slim)
            at = level * (kinds - 1) + e
            scale = mixed[:, at : at + 1] if e < kinds - 1 else 1.0
            hid[source, q, :, cols] = (hidden[:, cols] * scale).astype(BF16)
            dgu[source, q, :, cols] = (grad_gate[:, cols] * scale).astype(BF16)
            dgu[source, q, :, more] = (grad_up[:, cols] * scale).astype(BF16)

        @pl.loop(0, width // 256)
        def _(at):
            cols = pl.ds(pl.multiple_of(at * 256, 256), 256)
            sent = dot_nt(dgu[source, q], w_in[cols]).astype(BF16)
            part[source, :, :, here, cols] = sent.reshape(2, 2, size, 256)

    def post(step):
        source, q = take.origin(step), step % PARTS
        if step == 0:
            loads[0].wait()
        at = pl.multiple_of((source * PARTS + q) * 4 * size, 4 * size)
        for table, flip in ((b, flip_b), (gb, flip_gb)):
            block = table[source, :, take.rows(step)].reshape(4 * size, width)
            flip[:, pl.ds(at, 4 * size)] = jnp.transpose(block)

    def weigh(target, flip, source, low, high):
        values = source[...].reshape(tall, source.shape[-1])

        @pl.loop(0, width // 256)
        def _(at):
            here = pl.ds(pl.multiple_of(at * 256, 256), 256)
            target[here, low:high] = dot(flip[here, :], values[:, low:high]).astype(BF16)

    def begin():
        if count:
            extra.start()
        mixer.turn()

    def pieces(total):
        return [(low, min(low + 256, total)) for low in range(0, total, 256)]

    late = [functools.partial(weigh, grad_in, flip_b, dgu, *span) for span in pieces(2 * third)]
    late += [functools.partial(weigh, grad_down, flip_gb, hid, *span) for span in pieces(third)]
    turns = extra.turns() if count else []
    pipeline(take, give, compute, begin, lambda: None, post, turns, 2, late)
    grad_b = give.total()
    x = resid[...]
    inverse = lax.rsqrt(jnp.mean(x * x, axis=-1, keepdims=True) + EPSILON)
    unit = x * inverse
    gain_out[...] = jnp.sum(grad_b * unit, axis=0, keepdims=True)
    out[...] = grad_y[...].astype(F32) + norm_back(grad_b, gain[row : row + 1], unit, inverse)
    take.finish()
    give.finish()
    if count:
        extra.finish()


def ffn_backward(
    grad_y, resid, gain, level, row, kinds, mix, w_in, w_down, b, both, parts, outer, inner, ident
):
    dma = pltpu.SemaphoreType.DMA
    rows, width = resid.shape
    third = w_down.shape[1]
    count = len(parts)
    return pl.pallas_call(
        functools.partial(ffn_backward_kernel, outer, inner, kinds, count, level, row),
        out_shape=[
            jax.ShapeDtypeStruct((rows, width), F32),
            jax.ShapeDtypeStruct((1, width), F32),
            jax.ShapeDtypeStruct((width, 2 * third), BF16),
            jax.ShapeDtypeStruct((width, third), BF16),
        ]
        + push_outs(parts, outer),
        in_specs=[VMEM, VMEM, VMEM, ANY, ANY, ANY, ANY, ANY] + [ANY] * count,
        out_specs=[VMEM, VMEM, VMEM, VMEM] + [ANY] * count,
        scratch_shapes=[
            pltpu.VMEM(w_in.shape, BF16),
            pltpu.VMEM(w_down.shape, BF16),
            pltpu.VMEM((outer, 4, rows, width), BF16),
            pltpu.VMEM((outer, 4, rows, width), BF16),
            pltpu.VMEM((outer, PARTS, 4 * rows // PARTS, 2 * third), BF16),
            pltpu.VMEM((outer, PARTS, 4 * rows // PARTS, 2 * third), BF16),
            pltpu.VMEM((outer, PARTS, 4 * rows // PARTS, third), BF16),
            pltpu.VMEM((width, outer * 4 * rows), BF16),
            pltpu.VMEM((width, outer * 4 * rows), BF16),
            pltpu.VMEM((outer, 2, 2, rows, width), BF16),
            pltpu.VMEM((outer,) + mix.shape[1:], F32),
            pltpu.VMEM((outer, 4, rows, mix.shape[1]), F32),
        ]
        + scatter_room(outer, rows, width, PARTS)
        + gather_sems(outer, PARTS)
        + scatter_sems(outer, PARTS)
        + [dma((3,)), dma((outer,)), dma((outer,))]
        + (push_scratch(parts, outer, inner) if count else []),
        compiler_params=pltpu.CompilerParams(
            collective_id=ident, has_side_effects=True, vmem_limit_bytes=63 << 20
        ),
        name="ffn_backward",
    )(grad_y, resid, gain, mix, w_in, w_down, b, both, *parts)


def swap_halves(values):
    width = values.shape[1]
    lane = lax.broadcasted_iota(jnp.int32, values.shape, 1)
    low = lax.rem(lane, HD) < HD // 2
    return jnp.where(
        low, pltpu.roll(values, width - HD // 2, 1), pltpu.roll(values, HD // 2, 1)
    )


def allowed_rows(marks, spot, top):
    del top
    return (spot >= marks[:, 1:2]) & (spot <= marks[:, 0:1])


def attn_forward_kernel(outer, inner, modes, lead, row, *refs):
    count = len(modes)
    dp = outer * inner
    cut = Cut(refs)
    x_in, tables, marks, spot = cut(4)
    gain, weight = (None, None) if lead else cut(2)
    owns = cut(count)
    out, a_out, qk_out, v_out, lse_out, att_out = cut(6)
    gain_out = cut(1)[0] if lead else None
    fetched = cut(count)
    w, a, qk, v, att, part = cut(6)
    room, take_sems, give_sems = cut(3), cut(6), cut(6)
    load_sem, keep_sem = cut(2)
    extra = Fetch(outer, inner, owns, fetched, cut(count), cut(5), modes)
    rows, width = x_in.shape
    heads_width = w.shape[1] // 4
    heads = heads_width // HD
    take = Gather(1, dp, a, take_sems)
    give = Scatter(1, dp, part, room, give_sems)
    x = x_in[...].astype(F32)
    inverse = lax.rsqrt(jnp.mean(x * x, axis=-1, keepdims=True) + EPSILON)
    friends = take.friends() + extra.zdev[1:] + extra.xdev
    if lead:
        (gains,) = cut(1)
        meet(friends)
        extra.start(0, 2)
        extra.start(2, None, False)
        extra.settle()
        for turn in extra.turns(0, 1):
            turn()
        extra.land(0)
        load = pltpu.make_async_copy(fetched[0], gains, load_sem.at[0])
        load.start()
        load.wait()
        gain_out[...] = jnp.sum(gains[...], axis=0)
        a[0, take.t] = (x * inverse * gain_out[row : row + 1]).astype(BF16)
        turns = extra.turns(1, 2)
        turns[0]()
        take.start()
        for turn in turns[1:]:
            turn()
        for item in extra.chosen(2, None):
            extra.aside(item)
        early = extra.turns(3)
        early[0]()
        extra.land(1)
        slot = fetched[1].shape[1]
        loads = [
            pltpu.make_async_copy(
                fetched[1].at[at], w.at[pl.ds(at * slot, slot)], load_sem.at[at]
            )
            for at in range(dp)
        ]
        for load in loads:
            load.start()
        for load in loads:
            load.wait()
    else:
        load = pltpu.make_async_copy(weight, w, load_sem.at[0])
        load.start()
        a[0, take.t] = (x * inverse * gain[row : row + 1]).astype(BF16)
        meet(friends)
        take.start()
        extra.start()
        extra.settle()
        load.wait()
    done = 2 if lead else 0
    turns = extra.turns(2, 3) + extra.turns(3)[1:] if lead else extra.turns()

    def project(block):
        both = dot(a[0, block], w[:, : 3 * heads_width])
        raw = both[:, : 2 * heads_width]
        times = 2 * heads_width // tables.shape[-1]
        cosine = jnp.concatenate([tables[0, block]] * times, axis=1)
        sine = jnp.concatenate([tables[1, block]] * times, axis=1)
        qk[block] = (raw * cosine + swap_halves(raw) * sine).astype(BF16)
        v[block] = both[:, 2 * heads_width :].astype(BF16)

    project(take.t)
    take.complete(0)
    turns.pop(0)()

    @pl.loop(1, 4)
    def _(other):
        project(lax.rem(take.t + other, 4))

    keeps = [pltpu.make_async_copy(a.at[0], a_out, keep_sem.at[0])]
    keeps.append(pltpu.make_async_copy(qk, qk_out, keep_sem.at[1]))
    keeps.append(pltpu.make_async_copy(v, v_out, keep_sem.at[2]))
    for keep in keeps:
        keep.start()

    def attend(block):
        keys = qk[...].reshape(4 * rows, 2 * heads_width)
        values = v[...].reshape(4 * rows, heads_width)
        allowed = allowed_rows(marks[block], spot[...], 0)
        pieces = []
        for head in range(heads):
            here = slice(head * HD, (head + 1) * HD)
            there = slice(heads_width + head * HD, heads_width + (head + 1) * HD)
            scores = dot_nt(qk[block, :, here], keys[:, there])
            scores = jnp.where(allowed, scores * HD ** (-0.5), MASKED_SCORE)
            top = jnp.max(scores, axis=-1, keepdims=True)
            expo = jnp.exp(scores - top)
            total = jnp.sum(expo, axis=-1, keepdims=True)
            probs = (expo / total).astype(BF16)
            lse_out[block, :, head : head + 1] = top + jnp.log(total)
            pieces.append(dot(probs, values[:, here]).astype(BF16))
        att[block] = jnp.concatenate(pieces, axis=1)
        sent = dot_nt(att[block], w[:, 3 * heads_width :]).astype(BF16)
        part[0, lax.div(block, 2), lax.rem(block, 2)] = sent

    y, c = give.y, give.c

    @pl.loop(0, 2)
    def _(at):
        attend(2 * jnp.where(at == 0, 1 - y, y) + 1 - c)

    give.core_send(0)
    turns.pop(0)()

    @pl.loop(0, 2)
    def _(at):
        attend(2 * jnp.where(at == 0, 1 - y, y) + c)

    give.pair_send(0)
    for turn in turns:
        turn()
    keeps.append(pltpu.make_async_copy(att, att_out, keep_sem.at[3]))
    keeps[-1].start()
    out[...] = x_in[...].astype(F32) + give.total()
    take.finish()
    give.finish()
    extra.finish(done)
    for keep in keeps:
        keep.wait()


def attn_forward(
    x, gain, row, weight, tables, marks, spot, owns, modes, outer, inner, ident
):
    count = len(owns)
    dma = pltpu.SemaphoreType.DMA
    rows, width = x.shape
    lead = weight is None
    shape = (width, owns[1].shape[-1]) if lead else weight.shape
    slim = shape[1] // 4
    extras = [] if lead else [gain, weight]
    kept = [(4, rows, width), (4, rows, 2 * slim), (4, rows, slim)]
    return pl.pallas_call(
        functools.partial(attn_forward_kernel, outer, inner, modes, lead, row),
        out_shape=[jax.ShapeDtypeStruct((rows, width), F32)]
        + [jax.ShapeDtypeStruct(shape, BF16) for shape in kept]
        + [
            jax.ShapeDtypeStruct((4, rows, 8), F32),
            jax.ShapeDtypeStruct((4, rows, slim), BF16),
        ]
        + ([jax.ShapeDtypeStruct((8, width), F32)] if lead else [])
        + fetch_outs(owns, outer, inner, modes),
        in_specs=[VMEM] * 4 + ([] if lead else [VMEM, ANY]) + [ANY] * count,
        out_specs=[VMEM, ANY, ANY, ANY, VMEM, ANY] + [VMEM] * lead + [ANY] * count,
        scratch_shapes=[
            pltpu.VMEM(shape, BF16),
            pltpu.VMEM((1, 4, rows, width), BF16),
            pltpu.VMEM(kept[1], BF16),
            pltpu.VMEM(kept[2], BF16),
            pltpu.VMEM(kept[2], BF16),
            pltpu.VMEM((1, 2, 2, rows, width), BF16),
        ]
        + scatter_room(1, rows, width)
        + gather_sems(1)
        + scatter_sems(1)
        + [dma((outer * inner,)), dma((4,))]
        + fetch_scratch(owns, outer, inner, modes)
        + ([pltpu.VMEM((outer * inner,) + owns[0].shape[1:], F32)] if lead else []),
        compiler_params=pltpu.CompilerParams(collective_id=ident, has_side_effects=True),
        name="attn_forward",
    )(x, tables, marks, spot, *extras, *owns)


def attn_backward_kernel(outer, inner, count, last, row, *refs):
    dp = outer * inner
    cut = Cut(refs)
    grad_in, x_in, gain, weight, tables, marks, spot = cut(7)
    a_in, qk_in, v_in, lse, att_in = cut(5)
    others = cut(last)
    parts = cut(count)
    out, gain_out = cut(2)
    (grad_w,) = (None,) if last else cut(1)
    total = count + 1 if last else count
    pushed = cut(total)
    w, a, qk, v, att, ga, g_att, raw, part = cut(9)
    room, take_sems, give_sems = cut(3), cut(6), cut(6)
    (load_sem,) = cut(1)
    room_x, sems_x = cut(3 * total), cut(6)
    if last:
        held, from_t, from_d, ts, tr, ds, dr = cut(7)
        parts = tuple(parts) + (held,)
    extra = Push(outer, inner, parts, pushed, room_x, sems_x)
    turns = extra.turns(0, count) + extra.turns(count)
    friends = []
    rows, width = x_in.shape
    tall = 4 * rows
    heads_width = w.shape[1] // 4
    heads = heads_width // HD
    loads = [
        pltpu.make_async_copy(source, target, load_sem.at[i])
        for i, (source, target) in enumerate(
            ((weight, w), (qk_in, qk), (v_in, v), (att_in, att), (a_in, a))
        )
    ]
    for load in loads:
        load.start()
    take = Gather(1, dp, ga, take_sems)
    give = Scatter(1, dp, part, room, give_sems)
    ga[0, take.t] = grad_in[...].astype(BF16)
    if last:
        team = [(take.d, lax.rem(take.t + k, 4)) for k in range(1, 4)]
        peers = [(lax.rem(take.d + k, dp), take.t) for k in range(1, dp)]
        friends = team + peers
    else:
        friends = take.friends() + extra.zdev[:-1] + extra.xdev
    meet(friends)
    take.start()
    extra.start(0, count)
    for load in loads:
        load.wait()
    take.complete(0)
    turns = list(turns)

    def advance(count):
        for _ in range(min(count, len(turns) - spare)):
            turns.pop(0)()

    spare = 1 if last else 0
    advance(2)
    grads = ga[...].reshape(tall, width)
    g_att[...] = dot(grads, w[:, 3 * heads_width :]).astype(BF16)
    all_qk = qk[...].reshape(tall, 2 * heads_width)
    all_v = v[...].reshape(tall, heads_width)
    all_marks = marks[...].reshape(tall, marks.shape[-1])
    all_lse = lse[...].reshape(tall, lse.shape[-1])
    allowed = allowed_rows(all_marks, spot[...], 0)
    q_grads, k_grads, v_grads = [], [], []
    for head in range(heads):
        here = slice(head * HD, (head + 1) * HD)
        there = slice(heads_width + head * HD, heads_width + (head + 1) * HD)
        query, key = all_qk[:, here], all_qk[:, there]
        scores = dot_nt(query, key)
        scores = jnp.where(allowed, scores * HD ** (-0.5), MASKED_SCORE)
        probs = jnp.exp(scores - all_lse[:, head : head + 1])
        grad_probs = dot_nt(g_att[:, here], all_v[:, here])
        inner = jnp.sum(grad_probs * probs, axis=-1, keepdims=True)
        grad_scores = (probs * (grad_probs - inner)).astype(BF16)
        v_grads.append(dot_tn(probs.astype(BF16), g_att[:, here]).astype(BF16))
        q_grads.append(dot(grad_scores, key))
        k_grads.append(dot_tn(grad_scores, query))
    rotated = jnp.concatenate(q_grads + k_grads, axis=1) * HD ** (-0.5)
    times = 2 * heads_width // tables.shape[-1]
    cosine = jnp.concatenate([tables[0].reshape(tall, -1)] * times, axis=1)
    sine = jnp.concatenate([tables[1].reshape(tall, -1)] * times, axis=1)
    raw[:, : 2 * heads_width] = (rotated * cosine - swap_halves(rotated) * sine).astype(BF16)
    raw[:, 2 * heads_width :] = jnp.concatenate(v_grads, axis=1)
    def back(block):
        at = pl.ds(pl.multiple_of(block * rows, rows), rows)
        sent = dot_nt(raw[at, :], w[:, : 3 * heads_width]).astype(BF16)
        part[0, lax.div(block, 2), lax.rem(block, 2)] = sent

    advance(2)
    y, c = give.y, give.c
    back(2 * (1 - y) + 1 - c)
    back(2 * y + 1 - c)
    give.core_send(0)
    back(2 * (1 - y) + c)
    back(2 * y + c)
    give.pair_send(0)
    advance(2)
    grad_raw = dot_tn(a[...].reshape(tall, width), raw[...]).astype(BF16)
    grad_out = dot_tn(grads, att[...].reshape(tall, heads_width)).astype(BF16)
    if last:
        held[:, :, : 3 * heads_width] = grad_raw.reshape(dp, width // dp, -1)
        held[:, :, 3 * heads_width :] = grad_out.reshape(dp, width // dp, -1)
        extra.start(count, total)
    else:
        grad_w[:, : 3 * heads_width] = grad_raw
        grad_w[:, 3 * heads_width :] = grad_out
    advance(1)
    grad_a = give.total()
    x = x_in[...].astype(F32)
    inverse = lax.rsqrt(jnp.mean(x * x, axis=-1, keepdims=True) + EPSILON)
    unit = x * inverse
    part_gain = jnp.sum(grad_a * unit, axis=0, keepdims=True)
    if last:
        from_t[take.t] = jnp.zeros(from_t.shape[1:], F32)
        from_t[take.t, row : row + 1] = part_gain
        for at, other in zip([at for at in range(last + 1) if at != row], others):
            from_t[take.t, at : at + 1] = other[...]
    else:
        gain_out[...] = part_gain
    out[...] = grad_in[...] + norm_back(grad_a, gain[row : row + 1], unit, inverse)
    if last:
        mine = from_t.at[take.t]
        copies = [
            send(mine, mine, ts.at[k], tr.at[k], device) for k, device in enumerate(team)
        ]
        for copy in copies:
            copy.wait_recv()
        from_d[take.d] = jnp.sum(from_t[...], axis=0)
        advance(1)
        mine = from_d.at[take.d]
        more = [send(mine, mine, ds.at[k], dr.at[k], device) for k, device in enumerate(peers)]
        for turn in turns:
            turn()
        for copy in more:
            copy.wait_recv()
        gain_out[...] = jnp.sum(from_d[...], axis=0)
        for copy in copies + more:
            copy.wait_send()
    else:
        for turn in turns:
            turn()
    take.finish()
    give.finish()
    extra.finish()


def attn_backward(
    grad, x, gain, row, weight, tables, marks, spot, kept, others, parts, outer, inner, ident
):
    count = len(parts)
    dma = pltpu.SemaphoreType.DMA
    rows, width = x.shape
    slim = weight.shape[1] // 4
    dp = outer * inner
    last = len(others)
    whole = jax.ShapeDtypeStruct((dp, width // dp, 4 * slim), BF16)
    moved = list(parts) + ([whole] if last else [])
    wide = (8, width) if last else (1, width)
    return pl.pallas_call(
        functools.partial(attn_backward_kernel, outer, inner, count, last, row),
        out_shape=[
            jax.ShapeDtypeStruct((rows, width), F32),
            jax.ShapeDtypeStruct(wide, F32),
        ]
        + ([] if last else [jax.ShapeDtypeStruct(weight.shape, BF16)])
        + push_outs(moved, outer),
        in_specs=[VMEM, VMEM, VMEM, ANY, VMEM, VMEM, VMEM, ANY, ANY, ANY, VMEM, ANY]
        + [VMEM] * last
        + [ANY] * count,
        out_specs=[VMEM, VMEM] + ([] if last else [VMEM]) + [ANY] * len(moved),
        scratch_shapes=[
            pltpu.VMEM(weight.shape, BF16),
            pltpu.VMEM((4, rows, width), BF16),
            pltpu.VMEM((4, rows, 2 * slim), BF16),
            pltpu.VMEM((4, rows, slim), BF16),
            pltpu.VMEM((4, rows, slim), BF16),
            pltpu.VMEM((1, 4, rows, width), BF16),
            pltpu.VMEM((4 * rows, slim), BF16),
            pltpu.VMEM((4 * rows, 3 * slim), BF16),
            pltpu.VMEM((1, 2, 2, rows, width), BF16),
        ]
        + scatter_room(1, rows, width)
        + gather_sems(1)
        + scatter_sems(1)
        + [dma((5,))]
        + push_scratch(moved, outer, inner)
        + (
            [
                pltpu.VMEM(whole.shape, BF16),
                pltpu.VMEM((4, 8, width), F32),
                pltpu.VMEM((dp, 8, width), F32),
                dma((3,)),
                dma((3,)),
                dma((dp,)),
                dma((dp,)),
            ]
            if last
            else []
        ),
        compiler_params=pltpu.CompilerParams(
            collective_id=ident, has_side_effects=True, vmem_limit_bytes=62 << 20
        ),
        name="attn_backward",
    )(grad, x, gain, weight, tables, marks, spot, *kept, *others, *parts)


def pack_kernel(outer, dp, *refs):
    cut = Cut(refs)
    place, lengths, freqs, ids, gates, gain_attn, gain_ffn = cut(7)
    attn_any, ffn_any = cut(4), cut(6)
    tables, marks, spot, gains, mix = cut(5)
    layers, rows = gain_attn.shape
    attn_out, in_out, down_out = cut(layers), cut(layers), cut(layers)
    attn_in, ffn_in = cut(4), cut(6)
    attn_held, in_held, down_held = cut(layers), cut(layers), cut(layers)
    load_attn, load_ffn, keep = cut(3)
    loads_attn = [
        pltpu.make_async_copy(source, target, load_attn.at[i])
        for i, (source, target) in enumerate(zip(attn_any, attn_in))
    ]
    loads_ffn = [
        [
            pltpu.make_async_copy(source.at[level], target.at[level], load_ffn.at[level, i])
            for i, (source, target) in enumerate(zip(ffn_any, ffn_in))
        ]
        for level in range(layers)
    ]
    for load in sum(loads_ffn, loads_attn):
        load.start()
    count = place.shape[1]
    where = place[...]
    begins, end = jnp.zeros_like(where), 0
    for doc in range(lengths.shape[1]):
        end = end + lengths[0, doc]
        begins = begins + jnp.where(where >= end, lengths[0, doc], 0)
    spot[...] = where.astype(F32)
    lines = jnp.concatenate([where.astype(F32), begins.astype(F32)] * 4, axis=0)
    marks[...] = jnp.transpose(lines).reshape(4, count // 4, 8)
    angles = (where - begins).astype(F32) * freqs[...]
    cosine, sine = jnp.cos(angles), jnp.sin(angles)
    tables[0] = jnp.transpose(jnp.concatenate([cosine] * 4, axis=0)).reshape(4, count // 4, 128)
    tables[1] = jnp.transpose(jnp.concatenate([-sine, sine, -sine, sine], axis=0)).reshape(
        4, count // 4, 128
    )
    experts = mix.shape[0] // layers
    for level in range(layers):
        for e in range(experts):
            row = jnp.zeros((1, count), F32)
            for slot in range(ids.shape[1]):
                here = slice(slot, slot + 1)
                row = row + jnp.where(ids[level, here] == e, gates[level, here], 0.0)
            at = level * experts + e
            mix[at : at + 1] = row
    d = lax.axis_index("dp")
    gains[...] = jnp.zeros_like(gains)
    lane = lax.broadcasted_iota(jnp.int32, (layers, gains.shape[1]), 1)
    inside = (lane >= d * rows) & (lane < (d + 1) * rows)
    for i, gain in enumerate((gain_attn, gain_ffn)):
        wide = jnp.concatenate([gain[...].astype(BF16).astype(F32)] * dp, axis=1)
        gains[i * layers : (i + 1) * layers] = jnp.where(inside, wide, 0.0)
    keeps = []

    def leave(held, target):
        keeps.append(pltpu.make_async_copy(held, target, keep.at[len(keeps)]))
        keeps[-1].start()

    for load in loads_attn:
        load.wait()
    quarter = attn_in[0].shape[2]
    for level in range(layers):
        for i in range(4):
            values = attn_in[i][level]
            values = jnp.transpose(values) if i == 3 else values
            attn_held[level][0, :, i * quarter : (i + 1) * quarter] = values.astype(BF16)
        leave(attn_held[level], attn_out[level])
    for level in range(layers):
        for load in loads_ffn[level]:
            load.wait()
        slim = ffn_in[1].shape[2] // outer
        for group, (held, target) in enumerate(
            ((in_held, in_out), (in_held, in_out), (down_held, down_out))
        ):
            base = (experts + 1) * slim if group == 1 else 0
            for e in range(experts + 1):
                for k in range(outer):
                    cols = slice(k * slim, (k + 1) * slim)
                    if e < experts:
                        values = ffn_in[2 * group][level, e, :, cols]
                    else:
                        values = ffn_in[2 * group + 1][level, :, cols]
                    held[level][k, :, base + e * slim : base + (e + 1) * slim] = values.astype(
                        BF16
                    )
            if group:
                leave(held[level], target[level])
    for copy in keeps:
        copy.wait()


def pack(place, lengths, ids, gates, gain_attn, gain_ffn, attn, ffn, outer, dp):
    dma = pltpu.SemaphoreType.DMA
    layers, rows = gain_attn.shape
    count = place.shape[1]
    width = dp * rows
    experts = ffn[0].shape[1]
    slim = ffn[1].shape[2] // outer
    freqs = (10000.0 ** (-np.arange(HD // 2) / (HD // 2))).astype(np.float32)[:, None]
    blocks = (
        [(1, rows, 4 * attn[0].shape[2])] * layers
        + [(outer, rows, 2 * (experts + 1) * slim)] * layers
        + [(outer, rows, (experts + 1) * slim)] * layers
    )
    return pl.pallas_call(
        functools.partial(pack_kernel, outer, dp),
        out_shape=[
            jax.ShapeDtypeStruct((2, 4, count // 4, 128), F32),
            jax.ShapeDtypeStruct((4, count // 4, 8), F32),
            jax.ShapeDtypeStruct((1, count), F32),
            jax.ShapeDtypeStruct((8, width), F32),
            jax.ShapeDtypeStruct((layers * experts, count), F32),
        ]
        + [jax.ShapeDtypeStruct(block, BF16) for block in blocks],
        in_specs=[VMEM, pl.BlockSpec(memory_space=pltpu.SMEM)] + [VMEM] * 5 + [ANY] * 10,
        out_specs=[VMEM] * 5 + [ANY] * len(blocks),
        scratch_shapes=[pltpu.VMEM(m.shape, F32) for m in attn + ffn]
        + [pltpu.VMEM(block, BF16) for block in blocks]
        + [dma((4,)), dma((layers, 6)), dma((len(blocks),))],
        compiler_params=pltpu.CompilerParams(vmem_limit_bytes=62 << 20),
        name="pack",
    )(place, lengths, jnp.asarray(freqs), ids, gates, gain_attn, gain_ffn, *attn, *ffn)


def unpack_kernel(outer, layers, experts, *refs):
    cut = Cut(refs)
    in_any, down_any, attn_any = cut(layers), cut(layers), cut(layers)
    attn_out, ffn_out = cut(4), cut(6)
    in_v, down_v, attn_v = cut(layers), cut(layers), cut(layers)
    attn_held, ffn_held = cut(4), cut(6)
    load_sem, keep_attn, keep_ffn = cut(3)
    loads = [
        [
            pltpu.make_async_copy(source[level], target[level], load_sem.at[level, i])
            for i, (source, target) in enumerate(
                ((in_any, in_v), (down_any, down_v), (attn_any, attn_v))
            )
        ]
        for level in range(layers)
    ]
    for level in reversed(range(layers)):
        for load in loads[level]:
            load.start()
    keeps = []

    def leave(held, target, sem):
        keeps.append(pltpu.make_async_copy(held, target, sem))
        keeps[-1].start()

    slim = ffn_held[1].shape[2] // outer
    quarter = attn_held[0].shape[2]
    for level in reversed(range(layers)):
        for load in loads[level]:
            load.wait()
        for group, source in enumerate((in_v, in_v, down_v)):
            base = (experts + 1) * slim if group == 1 else 0
            for e in range(experts + 1):
                for k in range(outer):
                    cols = slice(k * slim, (k + 1) * slim)
                    values = source[level][k, :, base + e * slim : base + (e + 1) * slim]
                    if e < experts:
                        ffn_held[2 * group][level, e, :, cols] = values.astype(F32)
                    else:
                        ffn_held[2 * group + 1][level, :, cols] = values.astype(F32)
            for i in (2 * group, 2 * group + 1):
                leave(ffn_held[i].at[level], ffn_out[i].at[level], keep_ffn.at[level, i])
        total = jnp.sum(attn_v[level][...].astype(F32), axis=0)
        for i in range(4):
            values = total[:, i * quarter : (i + 1) * quarter]
            attn_held[i][level] = jnp.transpose(values) if i == 3 else values
            leave(attn_held[i].at[level], attn_out[i].at[level], keep_attn.at[level, i])
    for copy in keeps:
        copy.wait()


def unpack(pushed_in, pushed_down, pushed_attn, experts):
    dma = pltpu.SemaphoreType.DMA
    layers = len(pushed_in)
    outer, rows, third = pushed_down[0].shape
    full = outer * third // (experts + 1)
    quarter = pushed_attn[0].shape[2] // 4
    many, one = (layers, experts, rows, full), (layers, rows, full)
    shapes = [(layers, rows, quarter)] * 3 + [(layers, quarter, rows)] + [many, one] * 3
    moved = pushed_in + pushed_down + pushed_attn
    return pl.pallas_call(
        functools.partial(unpack_kernel, outer, layers, experts),
        out_shape=[jax.ShapeDtypeStruct(shape, F32) for shape in shapes],
        in_specs=[ANY] * len(moved),
        out_specs=[ANY] * 10,
        scratch_shapes=[pltpu.VMEM(part.shape, BF16) for part in moved]
        + [pltpu.VMEM(shape, F32) for shape in shapes]
        + [dma((layers, 3)), dma((layers, 4)), dma((layers, 6))],
        compiler_params=pltpu.CompilerParams(vmem_limit_bytes=62 << 20),
        name="unpack",
    )(*moved)


def layout(place_row, length_row):
    ends = jnp.cumsum(length_row, dtype=jnp.int32)
    after = place_row[:, None] >= ends[None, :]
    begins = jnp.sum(jnp.where(after, length_row[None, :], 0), axis=1, dtype=jnp.int32)
    return place_row - begins


def rope_tables(position):
    half_width = HD // 2
    freqs = 10000.0 ** (-jnp.arange(half_width, dtype=F32) / half_width)
    angles = position.astype(F32)[:, None] * freqs[None, :]
    cosine, sine = jnp.cos(angles), jnp.sin(angles)
    return jnp.stack(
        [
            jnp.concatenate([cosine] * 4, axis=1),
            jnp.concatenate([-sine, sine, -sine, sine], axis=1),
        ]
    )


def norm_back(grad_normed, gain_row, unit_rows, inverse):
    scaled = grad_normed * gain_row
    return inverse * (scaled - unit_rows * jnp.mean(scaled * unit_rows, axis=-1, keepdims=True))


def dot(left, right):
    return jnp.dot(left, right, preferred_element_type=F32)


def dot_nt(left, right):
    return lax.dot_general(left, right, (((1,), (1,)), ((), ())), preferred_element_type=F32)


def dot_tn(left, right):
    return lax.dot_general(left, right, (((0,), (0,)), ((), ())), preferred_element_type=F32)


def make_body(dp):
    outer, inner = split_dp(dp)

    def body(
        tokens,
        place,
        lengths,
        expert_ids,
        gate_values,
        cotangent,
        gain_attn,
        w_query,
        w_key,
        w_value,
        w_out,
        gain_ffn,
        exp_gate,
        exp_up,
        exp_down,
        dense_gate,
        dense_up,
        dense_down,
    ):
        layers, experts, rows, full = exp_gate.shape
        width = tokens.shape[1]
        slim = full // outer
        count = place.shape[1]
        kinds = experts + 1
        merged = rows % 16 == 0
        ids, gates = jnp.swapaxes(expert_ids, 1, 2), jnp.swapaxes(gate_values, 1, 2)
        downs = [jnp.swapaxes(exp_down, 2, 3), jnp.swapaxes(dense_down, 1, 2)]
        ffn = [exp_gate, dense_gate, exp_up, dense_up] + downs
        if merged:
            attn = [w_query, w_key, w_value, w_out]
            tables, marks, spot, gains_own, mix_own, *blocks = pack(
                place, lengths, ids, gates, gain_attn, gain_ffn, attn, ffn, outer, dp
            )
            attn_own = blocks[:layers]
            ffn_own = list(zip(blocks[layers : 2 * layers], blocks[2 * layers :]))
        else:
            position = layout(place[0], lengths[0])
            place_row = place[0].astype(F32)
            marks = jnp.stack([place_row, place_row - position.astype(F32)] * 4, axis=1)
            marks = marks.reshape(4, count // 4, 8)
            spot = place_row[None]
            tables = rope_tables(position).reshape(2, 4, count // 4, 128)
            slots = ids[:, None] == jnp.arange(experts, dtype=jnp.int32)[None, :, None, None]
            mix_own = jnp.sum(jnp.where(slots, gates[:, None], 0.0), axis=2)
            mix_own = mix_own.reshape(layers * experts, count)
            gains_own = jnp.concatenate([gain_attn, gain_ffn], axis=0).astype(BF16).astype(F32)
            spots = jnp.arange(dp, dtype=jnp.int32) == lax.axis_index("dp")
            gains_own = jnp.where(spots[None, :, None], gains_own[:, None], 0.0)
            gains_own = jnp.pad(
                gains_own.reshape(2 * layers, width), ((0, 8 - 2 * layers), (0, 0))
            )
            attn_own, ffn_own = [], []
            for level in range(layers):
                mats = [w_query[level], w_key[level], w_value[level], jnp.transpose(w_out[level])]
                attn_own.append(jnp.concatenate(mats, axis=1).astype(BF16)[None])
                mats = []
                for many, one in ((0, 1), (2, 3), (4, 5)):
                    mats += [ffn[many][level, e] for e in range(experts)] + [ffn[one][level]]
                mats = [m.astype(BF16) for m in mats]
                ffn_own.append(
                    [
                        jnp.stack(
                            [
                                jnp.concatenate(
                                    [m[:, k * slim : (k + 1) * slim] for m in group], axis=1
                                )
                                for k in range(outer)
                            ]
                        )
                        for group in (mats[: 2 * kinds], mats[2 * kinds :])
                    ]
                )
        state = tokens
        lead = [gains_own[None], attn_own[0], mix_own[None]]
        if merged:
            state_in = state
            ahead = [ffn_own[1][1]] if layers > 1 else []
            state, *kept = attn_forward(
                state_in,
                None,
                0,
                None,
                tables,
                marks,
                spot,
                lead + list(ffn_own[0]) + ahead,
                [BOTH] * 5 + [OUTER] * len(ahead),
                outer,
                inner,
                0,
            )
            part_down = kept.pop() if ahead else None
            gains, _, first, mix_all, w_in, w_down = kept[-6:]
            kept = kept[:-6]
        else:
            gains_all, first, mix_all = fetch(lead, outer, inner, 8)
            part_down = None
            gains = jnp.sum(gains_all, axis=0)
        w_attn = [first.reshape(width, -1)]
        w_ffn = []
        kept_attn, kept_ffn = [], []
        for level in range(layers):
            if level == 0 and merged:
                before = state_in
            else:
                before = state
                inside = list(ffn_own[level][: 1 if level else 2])
                state, *kept = attn_forward(
                    before,
                    gains,
                    level,
                    w_attn[level],
                    tables,
                    marks,
                    spot,
                    inside,
                    [BOTH] * len(inside),
                    outer,
                    inner,
                    1 if level else 11,
                )
                if level:
                    w_in = kept.pop()
                else:
                    w_down, w_in = kept.pop(), kept.pop()
            kept_attn.append((before, kept))
            w_ffn.append((w_in.reshape(width, -1), w_down.reshape(width, -1)))
            resid = state
            more, modes = [], []
            if level + 1 < layers:
                half = part_down is not None and level == 0
                more = [attn_own[level + 1], part_down if half else ffn_own[level + 1][1]]
                modes = [BOTH, INNER if half else BOTH]
            state, b_in, both, *fetched = ffn_forward(
                resid,
                gains,
                level,
                layers + level,
                kinds,
                mix_all,
                *w_ffn[level],
                more,
                modes,
                outer,
                inner,
                (2 if level == 0 else 12) if more else 3,
            )
            if more:
                w_attn.append(fetched[0].reshape(width, -1))
                w_down = fetched[1]
            kept_ffn.append((resid, b_in, both))
        mixed = state.astype(BF16)

        grad = cotangent
        part_gains = [None] * (2 * layers)
        pushed_in, pushed_down = [None] * layers, [None] * layers
        pushed_attn = [None] * layers
        waiting = []
        for level in reversed(range(layers)):
            resid, b_in, both = kept_ffn[level]
            grad, part_gain, grad_in, grad_down, *moved = ffn_backward(
                grad,
                resid,
                gains,
                level,
                layers + level,
                kinds,
                mix_all,
                *w_ffn[level],
                b_in,
                both,
                waiting,
                outer,
                inner,
                4 if waiting else 5,
            )
            part_gains[layers + level] = part_gain
            if waiting:
                (pushed_attn[level + 1],) = moved
            before, kept = kept_attn[level]
            inside = [grad_in.reshape(dp, rows, -1), grad_down.reshape(dp, rows, -1)]
            others = part_gains[1:] if level == 0 and merged else []
            grad, part_gain, *moved = attn_backward(
                grad,
                before,
                gains,
                level,
                w_attn[level],
                tables,
                marks,
                spot,
                kept,
                others,
                inside,
                outer,
                inner,
                6 if level else 7,
            )
            if level == 0 and merged:
                pushed_in[0], pushed_down[0], pushed_attn[0] = moved
                gain_sum = lax.dynamic_slice_in_dim(
                    part_gain, lax.axis_index("dp") * rows, rows, axis=1
                )
                continue
            part_gains[level] = part_gain
            waiting = [moved[0].reshape(dp, rows, -1)]
            pushed_in[level], pushed_down[level] = moved[1:]
        if not merged:
            stacked = jnp.concatenate(part_gains, axis=0)
            stacked = jnp.pad(stacked, ((0, 8 - 2 * layers), (0, 0)))
            stacked = jnp.transpose(stacked.reshape(8, dp, rows), (1, 0, 2))
            pushed_attn[0], gain_parts = push([waiting[0], stacked], outer, inner, 9)
            gain_part = jnp.sum(gain_parts, axis=0)
            gain_sum = jnp.sum(
                gather(jnp.pad(gain_part, ((0, 0), (0, 128 - rows))), dp, 10)[0], axis=0
            )
        grad_gain_attn = gain_sum[:layers, :rows]
        grad_gain_ffn = gain_sum[layers : 2 * layers, :rows]

        if merged:
            query, key, value, out, gate, gate_d, up, up_d, down, down_d = unpack(
                pushed_in, pushed_down, pushed_attn, experts
            )
        else:
            ups, downs, attns = [], [], []
            for level in range(layers):
                parts = pushed_in[level].reshape(outer, rows, 2 * kinds, slim)
                ups.append(jnp.transpose(parts, (2, 1, 0, 3)).reshape(2 * kinds, rows, full))
                parts = pushed_down[level].reshape(outer, rows, kinds, slim)
                downs.append(jnp.transpose(parts, (2, 1, 0, 3)).reshape(kinds, rows, full))
                attns.append(jnp.sum(pushed_attn[level].astype(F32), axis=0))
            ups, downs = jnp.stack(ups).astype(F32), jnp.stack(downs).astype(F32)
            gate, gate_d = ups[:, :experts], ups[:, experts]
            up, up_d = ups[:, kinds : kinds + experts], ups[:, kinds + experts]
            down, down_d = downs[:, :experts], downs[:, experts]
            query, key, value, out = jnp.split(jnp.stack(attns), 4, axis=2)
            out = jnp.swapaxes(out, 1, 2)
        return (
            mixed,
            grad,
            grad_gain_attn,
            query,
            key,
            value,
            out,
            grad_gain_ffn,
            gate,
            up,
            jnp.swapaxes(down, 2, 3),
            gate_d,
            up_d,
            jnp.swapaxes(down_d, 1, 2),
        )

    return body


def solution(mesh):
    return jax.shard_map(
        make_body(mesh.shape["dp"]),
        mesh=mesh,
        in_specs=(
            P(("dp", "tensor"), None),
            P("dp", None),
            P("dp", None),
            P(None, "dp", None),
            P(None, "dp", None),
            P(("dp", "tensor"), None),
            P(None, "dp"),
            P(None, "dp", "tensor"),
            P(None, "dp", "tensor"),
            P(None, "dp", "tensor"),
            P(None, "tensor", "dp"),
            P(None, "dp"),
            P(None, None, "dp", "tensor"),
            P(None, None, "dp", "tensor"),
            P(None, None, "tensor", "dp"),
            P(None, "dp", "tensor"),
            P(None, "dp", "tensor"),
            P(None, "tensor", "dp"),
        ),
        out_specs=(
            P(("dp", "tensor"), None),
            P(("dp", "tensor"), None),
            P(None, "dp"),
            P(None, "dp", "tensor"),
            P(None, "dp", "tensor"),
            P(None, "dp", "tensor"),
            P(None, "tensor", "dp"),
            P(None, "dp"),
            P(None, None, "dp", "tensor"),
            P(None, None, "dp", "tensor"),
            P(None, None, "tensor", "dp"),
            P(None, "dp", "tensor"),
            P(None, "dp", "tensor"),
            P(None, "tensor", "dp"),
        ),
        check_vma=False,
    )
```

```python
import functools

import jax
import jax.numpy as jnp
import numpy as np
from jax import lax
from jax.experimental import pallas as pl
from jax.experimental.pallas import tpu as pltpu
from jax.sharding import PartitionSpec as P

HD = 64
EPSILON = 1e-06
MASKED_SCORE = -1e30
MESH = pl.DeviceIdType.MESH
ANY = pl.BlockSpec(memory_space=pl.ANY)
VMEM = pl.BlockSpec(memory_space=pltpu.VMEM)
F32 = jnp.float32
BF16 = jnp.bfloat16
PARTS = 2
BOTH, OUTER, INNER = range(3)


def split_dp(dp):
    inner = 2 ** ((dp.bit_length() - 1) // 2)
    return dp // inner, inner


def place_of(inner):
    d = lax.axis_index("dp")
    return lax.div(d, inner), lax.rem(d, inner), lax.axis_index("tensor")


def across(t):
    return lax.rem(t + 2, 4), t + 1 - 2 * lax.rem(t, 2)


def meet(devices):
    barrier = pltpu.get_barrier_semaphore()
    for device in devices:
        pl.semaphore_signal(barrier, inc=1, device_id=device, device_id_type=MESH)
    pl.semaphore_wait(barrier, len(devices))


def send(source, target, send_sem, recv_sem, device):
    copy = pltpu.make_async_remote_copy(
        src_ref=source,
        dst_ref=target,
        send_sem=send_sem,
        recv_sem=recv_sem,
        device_id=device,
        device_id_type=MESH,
    )
    copy.start()
    return copy


def gather_kernel(dp, own, out, *sems):
    take = Gather(1, dp, out, sems)
    out[0, take.t] = own[...]
    meet(take.friends())
    take.start()
    take.complete(0)
    take.finish()


def gather(own, dp, ident):
    return pl.pallas_call(
        functools.partial(gather_kernel, dp),
        out_shape=jax.ShapeDtypeStruct((1, 4) + own.shape, own.dtype),
        in_specs=[VMEM],
        out_specs=VMEM,
        scratch_shapes=gather_sems(1),
        compiler_params=pltpu.CompilerParams(collective_id=ident, has_side_effects=True),
        name="gather",
    )(own)


def fetch_kernel(outer, inner, count, *refs):
    cut = Cut(refs)
    extra = Fetch(outer, inner, cut(count), cut(count), cut(count), cut(5), [BOTH] * count)
    meet(extra.zdev[1:] + extra.xdev)
    extra.start()
    extra.settle()
    for turn in extra.turns():
        turn()
    extra.finish()


def fetch(owns, outer, inner, ident):
    count = len(owns)
    return pl.pallas_call(
        functools.partial(fetch_kernel, outer, inner, count),
        out_shape=fetch_outs(owns, outer, inner, [BOTH] * count),
        in_specs=[ANY] * count,
        out_specs=[ANY] * count,
        scratch_shapes=fetch_scratch(owns, outer, inner, [BOTH] * count),
        compiler_params=pltpu.CompilerParams(collective_id=ident, has_side_effects=True),
        name="fetch",
    )(*owns)


def push_kernel(outer, inner, count, *refs):
    cut = Cut(refs)
    extra = Push(outer, inner, cut(count), cut(count), cut(3 * count), cut(6))
    meet(extra.zdev[:-1] + extra.xdev)
    extra.start()
    for turn in extra.turns():
        turn()
    extra.finish()


def push(parts, outer, inner, ident):
    count = len(parts)
    return pl.pallas_call(
        functools.partial(push_kernel, outer, inner, count),
        out_shape=push_outs(parts, outer),
        in_specs=[ANY] * count,
        out_specs=[ANY] * count,
        scratch_shapes=push_scratch(parts, outer, inner),
        compiler_params=pltpu.CompilerParams(collective_id=ident, has_side_effects=True),
        name="push",
    )(*parts)


def nearest(index, size, step):
    table = [sorted(range(size), key=lambda other: (abs(other - at), other)) for at in range(size)]
    found = 0
    for at in range(size):
        found = found + jnp.where(index == at, table[at][step], 0)
    return found


class Gather:
    def __init__(self, outer, inner, table, sems, parts=1):
        self.outer, self.inner, self.table, self.parts = outer, inner, table, parts
        self.zs, self.zr, self.ys, self.yr, self.cs, self.cr = sems
        self.dz, self.dx, self.t = place_of(inner)
        self.d = lax.axis_index("dp")
        self.size = table.shape[2] // parts
        ty, tc = across(self.t)
        self.ty = ty
        self.pair, self.core = (self.d, ty), (self.d, tc)
        self.source = [nearest(self.dz, outer, step) for step in range(outer)]
        self.zdev = [(source * inner + self.dx, self.t) for source in self.source]
        self.steps = outer * parts
        self.yc, self.cc, self.dc = [], [], []

    def friends(self):
        return self.zdev[1:] + [self.pair, self.core]

    def rows(self, step):
        return pl.ds(step % self.parts * self.size, self.size)

    def origin(self, step):
        return self.source[step // self.parts]

    def outward(self, step, target, sent):
        at = self.origin(step) * self.parts + step % self.parts
        block = self.table.at[self.origin(step), self.t, self.rows(step)]
        target = jnp.minimum(jnp.maximum(target, 0), self.outer - 1)
        return pltpu.make_async_remote_copy(
            src_ref=block,
            dst_ref=block,
            send_sem=self.zs.at[at if sent is None else sent],
            recv_sem=self.zr.at[at],
            device_id=(target * self.inner + self.dx, self.t),
            device_id_type=MESH,
        )

    def passes(self, step):
        if self.outer == 1:
            return []
        if step < self.parts:
            last = self.steps + step
            return [
                (self.dz < self.outer - 1, self.outward(step, self.dz + 1, None)),
                (self.dz > 0, self.outward(step, self.dz - 1, last)),
            ]
        ahead = jnp.where(self.origin(step) < self.dz, self.dz + 1, self.dz - 1)
        inside = (ahead >= 0) & (ahead < self.outer)
        return [(inside, self.outward(step, ahead, None))]

    def start(self):
        for step in range(self.parts):
            for inside, copy in self.passes(step):
                pl.when(inside)(copy.start)
        for step in range(self.parts):
            self.forward(step)

    def hop(self, step):
        ((inside, copy),) = self.passes(step)

        @pl.when(inside)
        def _():
            copy.wait_recv()
            copy.start()

    def arrive(self, step):
        ((inside, copy),) = self.passes(step)
        pl.when(jnp.logical_not(inside))(copy.wait_recv)
        self.forward(step)

    def forward(self, step):
        block = self.table.at[self.origin(step), self.t, self.rows(step)]
        self.yc.append(send(block, block, self.ys.at[step], self.yr.at[step], self.pair))
        self.cc.append(send(block, block, self.cs.at[step], self.cr.at[step], self.core))

    def complete(self, step):
        self.yc[step].wait_recv()
        at = self.steps + step
        block = self.table.at[self.origin(step), self.ty, self.rows(step)]
        self.dc.append(send(block, block, self.cs.at[at], self.cr.at[at], self.core))
        self.cc[step].wait_recv()
        self.dc[step].wait_recv()

    def finish(self):
        for step in range(self.steps):
            for inside, copy in self.passes(step):
                pl.when(inside)(copy.wait_send)
        for copy in self.yc + self.cc + self.dc:
            copy.wait_send()


class Scatter:
    def __init__(self, outer, inner, part, room, sems, parts=1):
        self.outer, self.part, self.parts = outer, part, parts
        self.from_c, self.from_y, self.from_z = room
        self.cs, self.cr, self.ys, self.yr, self.zs, self.zr = sems
        dz, dx, t = place_of(inner)
        d = lax.axis_index("dp")
        ty, tc = across(t)
        self.size = part.shape[3] // parts
        self.dz, self.y, self.c = dz, lax.div(t, 2), lax.rem(t, 2)
        self.pair, self.core = (d, ty), (d, tc)
        self.source = [nearest(dz, outer, step) for step in range(outer)]
        self.zdev = [(source * inner + dx, t) for source in self.source]
        self.steps = outer * parts
        self.cc, self.yc, self.zc = {}, {}, {}

    def rows(self, step):
        return pl.ds(step % self.parts * self.size, self.size)

    def core_send(self, step):
        source = self.source[step // self.parts]
        self.cc[step] = send(
            self.part.at[source, :, 1 - self.c, self.rows(step)],
            self.from_c.at[step],
            self.cs.at[step],
            self.cr.at[step],
            self.core,
        )

    def pair_send(self, step):
        source = self.source[step // self.parts]
        self.cc[step].wait_recv()
        mine = self.part[source, :, self.c, self.rows(step)].astype(F32)
        self.from_c[step] = (mine + self.from_c[step].astype(F32)).astype(BF16)
        self.yc[step] = send(
            self.from_c.at[step, 1 - self.y],
            self.from_y.at[step],
            self.ys.at[step],
            self.yr.at[step],
            self.pair,
        )

    def summed(self, step):
        self.yc[step].wait_recv()
        return self.from_c[step, self.y].astype(F32) + self.from_y[step].astype(F32)

    def outward(self, step, source, away):
        at = (away - 1) * self.parts + step % self.parts
        return pltpu.make_async_remote_copy(
            src_ref=source,
            dst_ref=self.from_z.at[at],
            send_sem=self.zs.at[at],
            recv_sem=self.zr.at[at],
            device_id=self.zdev[step // self.parts],
            device_id_type=MESH,
        )

    def outer_send(self, step):
        self.from_y[step] = self.summed(step).astype(BF16)
        away = lax.rem(self.source[step // self.parts] - self.dz + self.outer, self.outer)
        self.zc[step] = self.outward(step, self.from_y.at[step], away)
        self.zc[step].start()

    def total(self):
        pieces = []
        for piece in range(self.parts):
            total = self.summed(piece)
            for step in range(self.parts + piece, self.steps, self.parts):
                away = lax.rem(self.dz - self.source[step // self.parts] + self.outer, self.outer)
                self.outward(step, self.from_y.at[step], away).wait_recv()
                at = (away - 1) * self.parts + piece
                total = total + self.from_z[at].astype(F32)
            pieces.append(total)
        return pieces[0] if self.parts == 1 else jnp.concatenate(pieces, axis=0)

    def finish(self):
        for group in (self.cc, self.yc, self.zc):
            for step in group:
                group[step].wait_send()


def gather_sems(outer, parts=1):
    dma = pltpu.SemaphoreType.DMA
    steps = outer * parts
    return [dma((steps + parts,))] + [dma((steps,)) for _ in range(3)] + [dma((2 * steps,))] * 2


def scatter_sems(outer, parts=1):
    dma = pltpu.SemaphoreType.DMA
    return [dma((outer * parts,)) for _ in range(6)]


def scatter_room(outer, rows, width, parts=1):
    steps, size = outer * parts, rows // parts
    return [
        pltpu.VMEM((steps, 2, size, width), BF16),
        pltpu.VMEM((steps, size, width), BF16),
        pltpu.VMEM((max(steps - parts, 1), size, width), BF16),
    ]


def pipeline(take, give, compute, begin, after, post, middle, since, late):
    steps, parts = take.steps, take.parts
    middle, late = list(middle), list(late)
    lag = parts + 1
    take.start()
    begin()
    hops = list(range(parts, steps))
    for _ in range(min(2 * parts, len(hops))):
        take.hop(hops.pop(0))
    for step in range(steps):
        if step + parts < steps:
            take.arrive(step + parts)
        take.complete(step)
        if step > parts:
            give.pair_send(step - 1)
        compute(step)
        give.core_send(step)
        for _ in range(min(parts, len(hops))):
            take.hop(hops.pop(0))
        if step - lag >= parts:
            give.outer_send(step - lag)
        if step == 1:
            after()
        if step >= since and middle:
            middle.pop(0)()
        post(step)
    sent = max(parts, steps - lag)
    late = middle + late
    give.pair_send(steps - 1)
    for step in range(parts):
        give.pair_send(step)
    for step in range(sent, steps):
        if late:
            late.pop(0)()
        give.outer_send(step)
    for work in late:
        work()


def pieces_of(arrays, halves=True):
    items = []
    for i, array in enumerate(arrays):
        wide = array.shape[-1]
        count = 2 if halves and wide % 256 == 0 and wide > 1024 else 1
        size = wide // count
        items += [(i, slice(at * size, (at + 1) * size)) for at in range(count)]
    return items


class Fetch:
    def __init__(self, outer, inner, owns, outs, holds, sems, modes):
        self.outer, self.inner, self.owns, self.outs, self.holds = outer, inner, owns, outs, holds
        self.zs, self.zr, self.xs, self.xr, self.ls = sems
        self.modes, self.items = modes, pieces_of(owns)
        self.dz, dx, t = place_of(inner)
        self.dx, self.d = dx, lax.axis_index("dp")
        self.source = [nearest(self.dz, outer, step) for step in range(outer)]
        self.zdev = [(source * inner + dx, t) for source in self.source]
        self.xdev = [(self.dz * inner + lax.rem(dx + j, inner), t) for j in range(1, inner)]
        self.zc, self.xc, self.into, self.back = [], {}, {}, {}

    def own(self, item, where):
        i, cols = self.items[item]
        return self.owns[i].at[where if self.owns[i].shape[0] == self.outer else 0, :, cols]

    def slot(self, item, source):
        i, cols = self.items[item]
        if self.modes[i] != OUTER:
            source = source * self.inner + self.dx
        return self.outs[i].at[source, :, cols]

    def mode(self, item):
        return self.modes[self.items[item][0]]

    def chosen(self, first, last):
        last = len(self.owns) if last is None else last
        return [item for item, (i, _) in enumerate(self.items) if first <= i < last]

    def copy(self, item, step, away, refs):
        at = item * self.outer + lax.rem(away + self.outer, self.outer)
        return pltpu.make_async_remote_copy(
            src_ref=refs[0],
            dst_ref=refs[1],
            send_sem=self.zs.at[at],
            recv_sem=self.zr.at[at],
            device_id=self.zdev[step],
            device_id_type=MESH,
        )

    def start(self, first=0, last=None, aside=True):
        for item in self.chosen(first, last):
            i, cols = self.items[item]
            if self.mode(item) == INNER:
                for step, source in enumerate(self.source):
                    here = self.owns[i].at[source, :, cols]
                    self.spread(item, step, here, self.slot(item, source))
                continue
            for step in range(1, self.outer):
                source = self.source[step]
                refs = (self.own(item, source), self.slot(item, self.dz))
                self.zc.append(self.copy(item, step, source - self.dz, refs))
                self.zc[-1].start()
            if aside:
                self.aside(item)
        for i in range(first, len(self.owns) if last is None else last):
            where = self.dz if self.owns[i].shape[0] == self.outer else 0
            here = self.owns[i] if self.modes[i] == INNER else self.owns[i].at[where]
            at = i * (self.outer + 1)
            self.into[i] = pltpu.make_async_copy(here, self.holds[i], self.ls.at[at])
            self.into[i].start()

    def aside(self, item):
        if self.mode(item) == BOTH:
            self.spread(item, 0, self.own(item, self.dz), self.slot(item, self.dz))

    def spread(self, item, step, block, target):
        for j in range(1, self.inner):
            at = (item * self.outer + step) * self.inner + j
            self.xc[item, step, j] = send(
                block, target, self.xs.at[at], self.xr.at[at], self.xdev[j - 1]
            )

    def settle(self):
        for i, into in self.into.items():
            into.wait()
            at = i * (self.outer + 1)
            target = self.outs[i]
            if self.modes[i] == INNER:
                pairs = [
                    (self.holds[i].at[source], target.at[source * self.inner + self.dx])
                    for source in self.source
                ]
            else:
                here = self.dz if self.modes[i] == OUTER else self.d
                pairs = [(self.holds[i], target.at[here])]
            self.back[i] = [
                pltpu.make_async_copy(*pair, self.ls.at[at + 1 + k])
                for k, pair in enumerate(pairs)
            ]
            for copy in self.back[i]:
                copy.start()

    def turn(self, item, step):
        source = self.source[step]
        block = self.slot(item, source)
        self.copy(item, step, self.dz - source, (block, block)).wait_recv()
        if self.mode(item) == BOTH:
            self.spread(item, step, block, block)

    def turns(self, first=0, last=None):
        return [
            functools.partial(self.turn, item, step)
            for item in self.chosen(first, last)
            for step in range(1, self.outer)
            if self.mode(item) != INNER
        ]

    def land(self, i):
        for key in self.xc:
            if self.items[key[0]][0] == i:
                self.xc[key].wait_recv()
        for copy in self.back[i]:
            copy.wait()

    def finish(self, first=0):
        for key in self.xc:
            if self.items[key[0]][0] >= first:
                self.xc[key].wait_recv()
            self.xc[key].wait_send()
        for copy in self.zc:
            copy.wait_send()
        for i in self.back:
            if i >= first:
                for copy in self.back[i]:
                    copy.wait()


def fetch_outs(owns, outer, inner, modes):
    return [
        jax.ShapeDtypeStruct(
            (outer if mode == OUTER else outer * inner,) + own.shape[1:], own.dtype
        )
        for own, mode in zip(owns, modes)
    ]


def fetch_scratch(owns, outer, inner, modes):
    dma = pltpu.SemaphoreType.DMA
    count = max(len(pieces_of(owns)), 1)
    return [
        pltpu.VMEM(own.shape if mode == INNER else own.shape[1:], own.dtype)
        for own, mode in zip(owns, modes)
    ] + [
        dma((count * outer,)),
        dma((count * outer,)),
        dma((count * outer * inner,)),
        dma((count * outer * inner,)),
        dma((max(len(owns), 1) * (outer + 1),)),
    ]


class Push:
    def __init__(self, outer, inner, parts, outs, room, sems, halves=True):
        count = len(parts)
        self.outer, self.inner, self.parts, self.outs = outer, inner, parts, outs
        self.items = pieces_of(parts, halves)
        self.froms, self.mine, self.sums = room[:count], room[count : 2 * count], room[2 * count :]
        self.xs, self.xr, self.zs, self.zr, self.ls, self.ks = sems
        self.dz, dx, t = place_of(inner)
        self.dx = dx
        near = [nearest(self.dz, outer, step) for step in range(outer)]
        self.source = near[:0:-1] + near[:1]
        self.zdev = [(source * inner + dx, t) for source in self.source]
        self.xdev = [(self.dz * inner + lax.rem(dx + j, inner), t) for j in range(1, inner)]
        self.xc, self.zc, self.loads, self.keeps = {}, [], {}, []

    def start(self, first=0, last=None):
        last = len(self.parts) if last is None else last
        chosen = [entry for entry in enumerate(self.items) if first <= entry[1][0] < last]
        for step, source in enumerate(self.source):
            for item, (i, cols) in chosen:
                for j in range(1, self.inner):
                    slot = source * self.inner + lax.rem(self.dx + j, self.inner)
                    at = (item * self.outer + step) * self.inner + j
                    self.xc[item, step, j] = send(
                        self.parts[i].at[slot, :, cols],
                        self.froms[i].at[j - 1, step, :, cols],
                        self.xs.at[at],
                        self.xr.at[at],
                        self.xdev[j - 1],
                    )
                self.loads[item, step] = pltpu.make_async_copy(
                    self.parts[i].at[source * self.inner + self.dx, :, cols],
                    self.mine[i].at[step, :, cols],
                    self.ls.at[item * self.outer + step],
                )
                self.loads[item, step].start()

    def turn(self, item, step):
        i, cols = self.items[item]
        self.loads[item, step].wait()
        total = self.mine[i][step, :, cols].astype(F32)
        for j in range(1, self.inner):
            self.xc[item, step, j].wait_recv()
            total = total + self.froms[i][j - 1, step, :, cols].astype(F32)
        self.sums[i][step, :, cols] = total.astype(self.sums[i].dtype)
        source = self.sums[i].at[step, :, cols]
        target = self.outs[i].at[self.dz, :, cols]
        if step < self.outer - 1:
            away = lax.rem(self.source[step] - self.dz + self.outer, self.outer)
            at = item * self.outer + away
            self.zc.append(send(source, target, self.zs.at[at], self.zr.at[at], self.zdev[step]))
        else:
            self.keeps.append(pltpu.make_async_copy(source, target, self.ks.at[item]))
            self.keeps[-1].start()

    def turns(self, first=0, last=None):
        last = len(self.parts) if last is None else last
        return [
            functools.partial(self.turn, item, step)
            for step in range(self.outer)
            for item, (i, _) in enumerate(self.items)
            if first <= i < last
        ]

    def finish(self):
        for copy in self.zc:
            copy.wait_recv()
            copy.wait_send()
        for key in self.xc:
            self.xc[key].wait_send()
        for copy in self.keeps:
            copy.wait()


def push_outs(parts, outer):
    return [jax.ShapeDtypeStruct((outer,) + part.shape[1:], part.dtype) for part in parts]


def push_scratch(parts, outer, inner):
    dma = pltpu.SemaphoreType.DMA
    count = max(len(pieces_of(parts)), 1)
    across_x = [pltpu.VMEM((inner - 1, outer) + part.shape[1:], part.dtype) for part in parts]
    own = [pltpu.VMEM((outer,) + part.shape[1:], part.dtype) for part in parts]
    return (
        across_x
        + own
        + own
        + [
            dma((count * outer * inner,)),
            dma((count * outer * inner,)),
            dma((count * outer,)),
            dma((count * outer,)),
            dma((count * outer,)),
            dma((count,)),
        ]
    )


class Cut:
    def __init__(self, refs):
        self.refs, self.at = refs, 0

    def __call__(self, count):
        self.at += count
        return self.refs[self.at - count : self.at]


class Mixer:
    def __init__(self, outer, inner, table, lines, mix, sems):
        self.lines, self.mix = lines, mix
        dx = lax.rem(lax.axis_index("dp"), inner)
        self.loads = [
            pltpu.make_async_copy(table.at[at * inner + dx], lines.at[at], sems.at[at])
            for at in range(outer)
        ]
        for load in self.loads:
            load.start()

    def turn(self):
        for at, load in enumerate(self.loads):
            load.wait()
            self.mix[at] = jnp.transpose(self.lines[at]).reshape(self.mix.shape[1:])


def ffn_forward_kernel(outer, inner, kinds, modes, level, row, *refs):
    count = len(modes)
    cut = Cut(refs)
    resid, gain, mix_any, w_in_any, w_down_any = cut(5)
    owns = cut(count)
    out, b_out, gu_out = cut(3)
    fetched = cut(count)
    w_in, w_down, b, gu, hid, part, mix_rows, mix = cut(8)
    room, take_sems, give_sems = cut(3), cut(6), cut(6)
    load_sem, keep_b, keep_gu, load_mix = cut(4)
    extra = Fetch(outer, inner, owns, fetched, cut(count), cut(5), modes) if count else None
    rows, width = resid.shape
    third = w_down.shape[1]
    slim = third // kinds
    loads = [
        pltpu.make_async_copy(w_in_any, w_in, load_sem.at[0]),
        pltpu.make_async_copy(w_down_any, w_down, load_sem.at[1]),
    ]
    for load in loads:
        load.start()
    take = Gather(outer, inner, b, take_sems, PARTS)
    give = Scatter(outer, inner, part, room, give_sems, PARTS)
    size = rows // PARTS
    mixer = Mixer(outer, inner, mix_any, mix_rows, mix, load_mix)
    x = resid[...]
    inverse = lax.rsqrt(jnp.mean(x * x, axis=-1, keepdims=True) + EPSILON)
    b[take.dz, take.t] = (x * inverse * gain[row : row + 1]).astype(BF16)
    meet(take.friends() + (extra.xdev if count else []))
    keeps = []

    def compute(step):
        source, q = take.origin(step), step % PARTS
        here = take.rows(step)
        if step == 0:
            for load in loads:
                load.wait()
        rows_in = b[source, :, here].reshape(4 * size, width)

        scale = mix[source, :, here].reshape(4 * size, mix.shape[-1])
        both = dot(rows_in, w_in[...])
        gu[source, q] = both.astype(BF16)
        gate, up = both[:, :third], both[:, third:]
        hidden = gate * jax.nn.sigmoid(gate) * up
        for e in range(kinds):
            piece = hidden[:, e * slim : (e + 1) * slim]
            if e < kinds - 1:
                col = level * (kinds - 1) + e
                piece = piece * scale[:, col : col + 1]
            hid[:, e * slim : (e + 1) * slim] = piece.astype(BF16)

        sent = dot_nt(hid[...], w_down[...]).astype(BF16)
        part[source, :, :, here] = sent.reshape(2, 2, size, width)

        if q == PARTS - 1:
            at = step // PARTS
            keeps.append(pltpu.make_async_copy(b.at[source], b_out.at[source], keep_b.at[at]))
            keeps.append(pltpu.make_async_copy(gu.at[source], gu_out.at[source], keep_gu.at[at]))
            keeps[-1].start()
            keeps[-2].start()

    def after():
        if count:
            extra.start()
            extra.settle()

    turns = extra.turns() if count else []
    half = take.steps // 2
    pipeline(take, give, compute, mixer.turn, after, lambda step: None, turns, half, [])
    out[...] = resid[...] + give.total()
    take.finish()
    give.finish()
    if count:
        extra.finish()
    for keep in keeps:
        keep.wait()


def ffn_forward(
    resid, gain, level, row, kinds, mix, w_in, w_down, owns, modes, outer, inner, ident
):
    dma = pltpu.SemaphoreType.DMA
    rows, width = resid.shape
    third = w_down.shape[1]
    count = len(owns)
    return pl.pallas_call(
        functools.partial(ffn_forward_kernel, outer, inner, kinds, modes, level, row),
        out_shape=[
            jax.ShapeDtypeStruct((rows, width), F32),
            jax.ShapeDtypeStruct((outer, 4, rows, width), BF16),
            jax.ShapeDtypeStruct((outer, PARTS, 4 * rows // PARTS, 2 * third), BF16),
        ]
        + fetch_outs(owns, outer, inner, modes),
        in_specs=[VMEM, VMEM, ANY, ANY, ANY] + [ANY] * count,
        out_specs=[VMEM, ANY, ANY] + [ANY] * count,
        scratch_shapes=[
            pltpu.VMEM(w_in.shape, BF16),
            pltpu.VMEM(w_down.shape, BF16),
            pltpu.VMEM((outer, 4, rows, width), BF16),
            pltpu.VMEM((outer, PARTS, 4 * rows // PARTS, 2 * third), BF16),
            pltpu.VMEM((4 * rows // PARTS, third), BF16),
            pltpu.VMEM((outer, 2, 2, rows, width), BF16),
            pltpu.VMEM((outer,) + mix.shape[1:], F32),
            pltpu.VMEM((outer, 4, rows, mix.shape[1]), F32),
        ]
        + scatter_room(outer, rows, width, PARTS)
        + gather_sems(outer, PARTS)
        + scatter_sems(outer, PARTS)
        + [dma((2,)), dma((outer,)), dma((outer,)), dma((outer,))]
        + (fetch_scratch(owns, outer, inner, modes) if count else []),
        compiler_params=pltpu.CompilerParams(
            collective_id=ident, has_side_effects=True, vmem_limit_bytes=62 << 20
        ),
        name="ffn_forward",
    )(resid, gain, mix, w_in, w_down, *owns)


def ffn_backward_kernel(outer, inner, kinds, count, level, row, *refs):
    cut = Cut(refs)
    grad_y, resid, gain, mix_any, w_in_any, w_down_any, b_any, gu_any = cut(8)
    parts = cut(count)
    out, gain_out, grad_in, grad_down = cut(4)
    pushed = cut(count)
    w_in, w_down, b, gb, gu, dgu, hid, flip_b, flip_gb, part, mix_rows, mix = cut(12)
    room, take_sems, give_sems = cut(3), cut(6), cut(6)
    load_sem, load_gu, load_mix = cut(3)
    extra = Push(outer, inner, parts, pushed, cut(3 * count), cut(6)) if count else None
    rows, width = resid.shape
    tall = outer * 4 * rows
    third = w_down.shape[1]
    slim = third // kinds
    loads = [
        pltpu.make_async_copy(source, target, load_sem.at[i])
        for i, (source, target) in enumerate(
            ((b_any, b), (w_down_any, w_down), (w_in_any, w_in))
        )
    ]
    for load in loads:
        load.start()
    take = Gather(outer, inner, gb, take_sems, PARTS)
    give = Scatter(outer, inner, part, room, give_sems, PARTS)
    size = rows // PARTS
    mixer = Mixer(outer, inner, mix_any, mix_rows, mix, load_mix)
    fills = [
        pltpu.make_async_copy(gu_any.at[source], gu.at[source], load_gu.at[step])
        for step, source in enumerate(take.source)
    ]
    for fill in fills:
        fill.start()
    gb[take.dz, take.t] = grad_y[...].astype(BF16)
    meet(take.friends() + (extra.xdev if count else []))

    def compute(step):
        source, q = take.origin(step), step % PARTS
        here = take.rows(step)
        if step == 0:
            loads[1].wait()
            loads[2].wait()
        if q == 0:
            fills[step // PARTS].wait()
        rows_in = gb[source, :, here].reshape(4 * size, width)
        mixed = mix[source, :, here].reshape(4 * size, mix.shape[-1])
        grad_hidden = dot(rows_in, w_down[...])
        both = gu[source, q].astype(F32)
        gate, up = both[:, :third], both[:, third:]
        sigma = jax.nn.sigmoid(gate)
        act = gate * sigma
        slope = sigma * (1.0 + gate * (1.0 - sigma))
        hidden, grad_gate, grad_up = act * up, grad_hidden * up * slope, grad_hidden * act
        for e in range(kinds):
            cols = slice(e * slim, (e + 1) * slim)
            more = slice(third + e * slim, third + (e + 1) * slim)
            at = level * (kinds - 1) + e
            scale = mixed[:, at : at + 1] if e < kinds - 1 else 1.0
            hid[source, q, :, cols] = (hidden[:, cols] * scale).astype(BF16)
            dgu[source, q, :, cols] = (grad_gate[:, cols] * scale).astype(BF16)
            dgu[source, q, :, more] = (grad_up[:, cols] * scale).astype(BF16)
        sent = dot_nt(dgu[source, q], w_in[...]).astype(BF16)
        part[source, :, :, here] = sent.reshape(2, 2, size, width)

    def post(step):
        source, q = take.origin(step), step % PARTS
        if step == 0:
            loads[0].wait()
        at = pl.multiple_of((source * PARTS + q) * 4 * size, 4 * size)
        for table, flip in ((b, flip_b), (gb, flip_gb)):
            block = table[source, :, take.rows(step)].reshape(4 * size, width)
            flip[:, pl.ds(at, 4 * size)] = jnp.transpose(block)

    def weigh(target, flip, source, low, high):
        values = source[...].reshape(tall, source.shape[-1])

        @pl.loop(0, width // 256)
        def _(at):
            here = pl.ds(pl.multiple_of(at * 256, 256), 256)
            target[here, low:high] = dot(flip[here, :], values[:, low:high]).astype(BF16)

    def begin():
        if count:
            extra.start()
        mixer.turn()

    def pieces(total):
        return [(low, min(low + 256, total)) for low in range(0, total, 256)]

    late = [functools.partial(weigh, grad_in, flip_b, dgu, *span) for span in pieces(2 * third)]
    late += [functools.partial(weigh, grad_down, flip_gb, hid, *span) for span in pieces(third)]
    turns = extra.turns() if count else []
    pipeline(take, give, compute, begin, lambda: None, post, turns, 2, late)
    grad_b = give.total()
    x = resid[...]
    inverse = lax.rsqrt(jnp.mean(x * x, axis=-1, keepdims=True) + EPSILON)
    unit = x * inverse
    gain_out[...] = jnp.sum(grad_b * unit, axis=0, keepdims=True)
    out[...] = grad_y[...].astype(F32) + norm_back(grad_b, gain[row : row + 1], unit, inverse)
    take.finish()
    give.finish()
    if count:
        extra.finish()


def ffn_backward(
    grad_y, resid, gain, level, row, kinds, mix, w_in, w_down, b, both, parts, outer, inner, ident
):
    dma = pltpu.SemaphoreType.DMA
    rows, width = resid.shape
    third = w_down.shape[1]
    count = len(parts)
    return pl.pallas_call(
        functools.partial(ffn_backward_kernel, outer, inner, kinds, count, level, row),
        out_shape=[
            jax.ShapeDtypeStruct((rows, width), F32),
            jax.ShapeDtypeStruct((1, width), F32),
            jax.ShapeDtypeStruct((width, 2 * third), BF16),
            jax.ShapeDtypeStruct((width, third), BF16),
        ]
        + push_outs(parts, outer),
        in_specs=[VMEM, VMEM, VMEM, ANY, ANY, ANY, ANY, ANY] + [ANY] * count,
        out_specs=[VMEM, VMEM, VMEM, VMEM] + [ANY] * count,
        scratch_shapes=[
            pltpu.VMEM(w_in.shape, BF16),
            pltpu.VMEM(w_down.shape, BF16),
            pltpu.VMEM((outer, 4, rows, width), BF16),
            pltpu.VMEM((outer, 4, rows, width), BF16),
            pltpu.VMEM((outer, PARTS, 4 * rows // PARTS, 2 * third), BF16),
            pltpu.VMEM((outer, PARTS, 4 * rows // PARTS, 2 * third), BF16),
            pltpu.VMEM((outer, PARTS, 4 * rows // PARTS, third), BF16),
            pltpu.VMEM((width, outer * 4 * rows), BF16),
            pltpu.VMEM((width, outer * 4 * rows), BF16),
            pltpu.VMEM((outer, 2, 2, rows, width), BF16),
            pltpu.VMEM((outer,) + mix.shape[1:], F32),
            pltpu.VMEM((outer, 4, rows, mix.shape[1]), F32),
        ]
        + scatter_room(outer, rows, width, PARTS)
        + gather_sems(outer, PARTS)
        + scatter_sems(outer, PARTS)
        + [dma((3,)), dma((outer,)), dma((outer,))]
        + (push_scratch(parts, outer, inner) if count else []),
        compiler_params=pltpu.CompilerParams(
            collective_id=ident, has_side_effects=True, vmem_limit_bytes=63 << 20
        ),
        name="ffn_backward",
    )(grad_y, resid, gain, mix, w_in, w_down, b, both, *parts)


def swap_halves(values):
    width = values.shape[1]
    lane = lax.broadcasted_iota(jnp.int32, values.shape, 1)
    low = lax.rem(lane, HD) < HD // 2
    return jnp.where(
        low, pltpu.roll(values, width - HD // 2, 1), pltpu.roll(values, HD // 2, 1)
    )


def allowed_rows(marks, spot, top):
    del top
    return (spot >= marks[:, 1:2]) & (spot <= marks[:, 0:1])


def attn_forward_kernel(outer, inner, modes, lead, row, *refs):
    count = len(modes)
    dp = outer * inner
    cut = Cut(refs)
    x_in, tables, marks, spot = cut(4)
    gain, weight = (None, None) if lead else cut(2)
    owns = cut(count)
    out, a_out, qk_out, v_out, lse_out, att_out = cut(6)
    gain_out = cut(1)[0] if lead else None
    fetched = cut(count)
    w, a, qk, v, att, part = cut(6)
    room, take_sems, give_sems = cut(3), cut(6), cut(6)
    load_sem, keep_sem = cut(2)
    extra = Fetch(outer, inner, owns, fetched, cut(count), cut(5), modes)
    rows, width = x_in.shape
    heads_width = w.shape[1] // 4
    heads = heads_width // HD
    take = Gather(1, dp, a, take_sems)
    give = Scatter(1, dp, part, room, give_sems)
    x = x_in[...].astype(F32)
    inverse = lax.rsqrt(jnp.mean(x * x, axis=-1, keepdims=True) + EPSILON)
    friends = take.friends() + extra.zdev[1:] + extra.xdev
    if lead:
        (gains,) = cut(1)
        meet(friends)
        extra.start(0, 2)
        extra.start(2, None, False)
        extra.settle()
        for turn in extra.turns(0, 1):
            turn()
        extra.land(0)
        load = pltpu.make_async_copy(fetched[0], gains, load_sem.at[0])
        load.start()
        load.wait()
        gain_out[...] = jnp.sum(gains[...], axis=0)
        a[0, take.t] = (x * inverse * gain_out[row : row + 1]).astype(BF16)
        turns = extra.turns(1, 2)
        turns[0]()
        take.start()
        for turn in turns[1:]:
            turn()
        for item in extra.chosen(2, None):
            extra.aside(item)
        early = extra.turns(3)
        early[0]()
        extra.land(1)
        slot = fetched[1].shape[1]
        loads = [
            pltpu.make_async_copy(
                fetched[1].at[at], w.at[pl.ds(at * slot, slot)], load_sem.at[at]
            )
            for at in range(dp)
        ]
        for load in loads:
            load.start()
        for load in loads:
            load.wait()
    else:
        load = pltpu.make_async_copy(weight, w, load_sem.at[0])
        load.start()
        a[0, take.t] = (x * inverse * gain[row : row + 1]).astype(BF16)
        meet(friends)
        take.start()
        extra.start()
        extra.settle()
        load.wait()
    done = 2 if lead else 0
    turns = extra.turns(2, 3) + extra.turns(3)[1:] if lead else extra.turns()

    def project(block):
        both = dot(a[0, block], w[:, : 3 * heads_width])
        raw = both[:, : 2 * heads_width]
        times = 2 * heads_width // tables.shape[-1]
        cosine = jnp.concatenate([tables[0, block]] * times, axis=1)
        sine = jnp.concatenate([tables[1, block]] * times, axis=1)
        qk[block] = (raw * cosine + swap_halves(raw) * sine).astype(BF16)
        v[block] = both[:, 2 * heads_width :].astype(BF16)

    project(take.t)
    take.complete(0)
    turns.pop(0)()

    @pl.loop(1, 4)
    def _(other):
        project(lax.rem(take.t + other, 4))

    keeps = [pltpu.make_async_copy(a.at[0], a_out, keep_sem.at[0])]
    keeps.append(pltpu.make_async_copy(qk, qk_out, keep_sem.at[1]))
    keeps.append(pltpu.make_async_copy(v, v_out, keep_sem.at[2]))
    for keep in keeps:
        keep.start()

    def attend(block):
        keys = qk[...].reshape(4 * rows, 2 * heads_width)
        values = v[...].reshape(4 * rows, heads_width)
        allowed = allowed_rows(marks[block], spot[...], 0)
        pieces = []
        for head in range(heads):
            here = slice(head * HD, (head + 1) * HD)
            there = slice(heads_width + head * HD, heads_width + (head + 1) * HD)
            scores = dot_nt(qk[block, :, here], keys[:, there])
            scores = jnp.where(allowed, scores * HD ** (-0.5), MASKED_SCORE)
            top = jnp.max(scores, axis=-1, keepdims=True)
            expo = jnp.exp(scores - top)
            total = jnp.sum(expo, axis=-1, keepdims=True)
            probs = (expo / total).astype(BF16)
            lse_out[block, :, head : head + 1] = top + jnp.log(total)
            pieces.append(dot(probs, values[:, here]).astype(BF16))
        att[block] = jnp.concatenate(pieces, axis=1)
        sent = dot_nt(att[block], w[:, 3 * heads_width :]).astype(BF16)
        part[0, lax.div(block, 2), lax.rem(block, 2)] = sent

    y, c = give.y, give.c

    @pl.loop(0, 2)
    def _(at):
        attend(2 * jnp.where(at == 0, 1 - y, y) + 1 - c)

    give.core_send(0)
    turns.pop(0)()

    @pl.loop(0, 2)
    def _(at):
        attend(2 * jnp.where(at == 0, 1 - y, y) + c)

    give.pair_send(0)
    for turn in turns:
        turn()
    keeps.append(pltpu.make_async_copy(att, att_out, keep_sem.at[3]))
    keeps[-1].start()
    out[...] = x_in[...].astype(F32) + give.total()
    take.finish()
    give.finish()
    extra.finish(done)
    for keep in keeps:
        keep.wait()


def attn_forward(
    x, gain, row, weight, tables, marks, spot, owns, modes, outer, inner, ident
):
    count = len(owns)
    dma = pltpu.SemaphoreType.DMA
    rows, width = x.shape
    lead = weight is None
    shape = (width, owns[1].shape[-1]) if lead else weight.shape
    slim = shape[1] // 4
    extras = [] if lead else [gain, weight]
    kept = [(4, rows, width), (4, rows, 2 * slim), (4, rows, slim)]
    return pl.pallas_call(
        functools.partial(attn_forward_kernel, outer, inner, modes, lead, row),
        out_shape=[jax.ShapeDtypeStruct((rows, width), F32)]
        + [jax.ShapeDtypeStruct(shape, BF16) for shape in kept]
        + [
            jax.ShapeDtypeStruct((4, rows, 8), F32),
            jax.ShapeDtypeStruct((4, rows, slim), BF16),
        ]
        + ([jax.ShapeDtypeStruct((8, width), F32)] if lead else [])
        + fetch_outs(owns, outer, inner, modes),
        in_specs=[VMEM] * 4 + ([] if lead else [VMEM, ANY]) + [ANY] * count,
        out_specs=[VMEM, ANY, ANY, ANY, VMEM, ANY] + [VMEM] * lead + [ANY] * count,
        scratch_shapes=[
            pltpu.VMEM(shape, BF16),
            pltpu.VMEM((1, 4, rows, width), BF16),
            pltpu.VMEM(kept[1], BF16),
            pltpu.VMEM(kept[2], BF16),
            pltpu.VMEM(kept[2], BF16),
            pltpu.VMEM((1, 2, 2, rows, width), BF16),
        ]
        + scatter_room(1, rows, width)
        + gather_sems(1)
        + scatter_sems(1)
        + [dma((outer * inner,)), dma((4,))]
        + fetch_scratch(owns, outer, inner, modes)
        + ([pltpu.VMEM((outer * inner,) + owns[0].shape[1:], F32)] if lead else []),
        compiler_params=pltpu.CompilerParams(collective_id=ident, has_side_effects=True),
        name="attn_forward",
    )(x, tables, marks, spot, *extras, *owns)


def attn_backward_kernel(outer, inner, count, last, row, *refs):
    dp = outer * inner
    cut = Cut(refs)
    grad_in, x_in, gain, weight, tables, marks, spot = cut(7)
    a_in, qk_in, v_in, lse, att_in = cut(5)
    others = cut(last)
    parts = cut(count)
    out, gain_out = cut(2)
    (grad_w,) = (None,) if last else cut(1)
    total = count + 1 if last else count
    pushed = cut(total)
    w, a, qk, v, att, ga, g_att, raw, part = cut(9)
    room, take_sems, give_sems = cut(3), cut(6), cut(6)
    (load_sem,) = cut(1)
    room_x, sems_x = cut(3 * total), cut(6)
    if last:
        held, from_t, from_d, ts, tr, ds, dr = cut(7)
        parts = tuple(parts) + (held,)
    extra = Push(outer, inner, parts, pushed, room_x, sems_x)
    turns = extra.turns(0, count) + extra.turns(count)
    friends = []
    rows, width = x_in.shape
    tall = 4 * rows
    heads_width = w.shape[1] // 4
    heads = heads_width // HD
    loads = [
        pltpu.make_async_copy(source, target, load_sem.at[i])
        for i, (source, target) in enumerate(
            ((weight, w), (qk_in, qk), (v_in, v), (att_in, att), (a_in, a))
        )
    ]
    for load in loads:
        load.start()
    take = Gather(1, dp, ga, take_sems)
    give = Scatter(1, dp, part, room, give_sems)
    ga[0, take.t] = grad_in[...].astype(BF16)
    if last:
        team = [(take.d, lax.rem(take.t + k, 4)) for k in range(1, 4)]
        peers = [(lax.rem(take.d + k, dp), take.t) for k in range(1, dp)]
        friends = team + peers
    else:
        friends = take.friends() + extra.zdev[:-1] + extra.xdev
    meet(friends)
    take.start()
    extra.start(0, count)
    for load in loads:
        load.wait()
    take.complete(0)
    turns = list(turns)

    def advance(count):
        for _ in range(min(count, len(turns) - spare)):
            turns.pop(0)()

    spare = 1 if last else 0
    advance(2)
    grads = ga[...].reshape(tall, width)
    g_att[...] = dot(grads, w[:, 3 * heads_width :]).astype(BF16)
    all_qk = qk[...].reshape(tall, 2 * heads_width)
    all_v = v[...].reshape(tall, heads_width)
    all_marks = marks[...].reshape(tall, marks.shape[-1])
    all_lse = lse[...].reshape(tall, lse.shape[-1])
    allowed = allowed_rows(all_marks, spot[...], 0)
    q_grads, k_grads, v_grads = [], [], []
    for head in range(heads):
        here = slice(head * HD, (head + 1) * HD)
        there = slice(heads_width + head * HD, heads_width + (head + 1) * HD)
        query, key = all_qk[:, here], all_qk[:, there]
        scores = dot_nt(query, key)
        scores = jnp.where(allowed, scores * HD ** (-0.5), MASKED_SCORE)
        probs = jnp.exp(scores - all_lse[:, head : head + 1])
        grad_probs = dot_nt(g_att[:, here], all_v[:, here])
        inner = jnp.sum(grad_probs * probs, axis=-1, keepdims=True)
        grad_scores = (probs * (grad_probs - inner)).astype(BF16)
        v_grads.append(dot_tn(probs.astype(BF16), g_att[:, here]).astype(BF16))
        q_grads.append(dot(grad_scores, key))
        k_grads.append(dot_tn(grad_scores, query))
    rotated = jnp.concatenate(q_grads + k_grads, axis=1) * HD ** (-0.5)
    times = 2 * heads_width // tables.shape[-1]
    cosine = jnp.concatenate([tables[0].reshape(tall, -1)] * times, axis=1)
    sine = jnp.concatenate([tables[1].reshape(tall, -1)] * times, axis=1)
    raw[:, : 2 * heads_width] = (rotated * cosine - swap_halves(rotated) * sine).astype(BF16)
    raw[:, 2 * heads_width :] = jnp.concatenate(v_grads, axis=1)
    def back(block):
        at = pl.ds(pl.multiple_of(block * rows, rows), rows)
        sent = dot_nt(raw[at, :], w[:, : 3 * heads_width]).astype(BF16)
        part[0, lax.div(block, 2), lax.rem(block, 2)] = sent

    advance(2)
    y, c = give.y, give.c
    back(2 * (1 - y) + 1 - c)
    back(2 * y + 1 - c)
    give.core_send(0)
    back(2 * (1 - y) + c)
    back(2 * y + c)
    give.pair_send(0)
    advance(2)
    grad_raw = dot_tn(a[...].reshape(tall, width), raw[...]).astype(BF16)
    grad_out = dot_tn(grads, att[...].reshape(tall, heads_width)).astype(BF16)
    if last:
        held[:, :, : 3 * heads_width] = grad_raw.reshape(dp, width // dp, -1)
        held[:, :, 3 * heads_width :] = grad_out.reshape(dp, width // dp, -1)
        extra.start(count, total)
    else:
        grad_w[:, : 3 * heads_width] = grad_raw
        grad_w[:, 3 * heads_width :] = grad_out
    advance(1)
    grad_a = give.total()
    x = x_in[...].astype(F32)
    inverse = lax.rsqrt(jnp.mean(x * x, axis=-1, keepdims=True) + EPSILON)
    unit = x * inverse
    part_gain = jnp.sum(grad_a * unit, axis=0, keepdims=True)
    if last:
        from_t[take.t] = jnp.zeros(from_t.shape[1:], F32)
        from_t[take.t, row : row + 1] = part_gain
        for at, other in zip([at for at in range(last + 1) if at != row], others):
            from_t[take.t, at : at + 1] = other[...]
    else:
        gain_out[...] = part_gain
    out[...] = grad_in[...] + norm_back(grad_a, gain[row : row + 1], unit, inverse)
    if last:
        mine = from_t.at[take.t]
        copies = [
            send(mine, mine, ts.at[k], tr.at[k], device) for k, device in enumerate(team)
        ]
        for copy in copies:
            copy.wait_recv()
        from_d[take.d] = jnp.sum(from_t[...], axis=0)
        advance(1)
        mine = from_d.at[take.d]
        more = [send(mine, mine, ds.at[k], dr.at[k], device) for k, device in enumerate(peers)]
        for turn in turns:
            turn()
        for copy in more:
            copy.wait_recv()
        gain_out[...] = jnp.sum(from_d[...], axis=0)
        for copy in copies + more:
            copy.wait_send()
    else:
        for turn in turns:
            turn()
    take.finish()
    give.finish()
    extra.finish()


def attn_backward(
    grad, x, gain, row, weight, tables, marks, spot, kept, others, parts, outer, inner, ident
):
    count = len(parts)
    dma = pltpu.SemaphoreType.DMA
    rows, width = x.shape
    slim = weight.shape[1] // 4
    dp = outer * inner
    last = len(others)
    whole = jax.ShapeDtypeStruct((dp, width // dp, 4 * slim), BF16)
    moved = list(parts) + ([whole] if last else [])
    wide = (8, width) if last else (1, width)
    return pl.pallas_call(
        functools.partial(attn_backward_kernel, outer, inner, count, last, row),
        out_shape=[
            jax.ShapeDtypeStruct((rows, width), F32),
            jax.ShapeDtypeStruct(wide, F32),
        ]
        + ([] if last else [jax.ShapeDtypeStruct(weight.shape, BF16)])
        + push_outs(moved, outer),
        in_specs=[VMEM, VMEM, VMEM, ANY, VMEM, VMEM, VMEM, ANY, ANY, ANY, VMEM, ANY]
        + [VMEM] * last
        + [ANY] * count,
        out_specs=[VMEM, VMEM] + ([] if last else [VMEM]) + [ANY] * len(moved),
        scratch_shapes=[
            pltpu.VMEM(weight.shape, BF16),
            pltpu.VMEM((4, rows, width), BF16),
            pltpu.VMEM((4, rows, 2 * slim), BF16),
            pltpu.VMEM((4, rows, slim), BF16),
            pltpu.VMEM((4, rows, slim), BF16),
            pltpu.VMEM((1, 4, rows, width), BF16),
            pltpu.VMEM((4 * rows, slim), BF16),
            pltpu.VMEM((4 * rows, 3 * slim), BF16),
            pltpu.VMEM((1, 2, 2, rows, width), BF16),
        ]
        + scatter_room(1, rows, width)
        + gather_sems(1)
        + scatter_sems(1)
        + [dma((5,))]
        + push_scratch(moved, outer, inner)
        + (
            [
                pltpu.VMEM(whole.shape, BF16),
                pltpu.VMEM((4, 8, width), F32),
                pltpu.VMEM((dp, 8, width), F32),
                dma((3,)),
                dma((3,)),
                dma((dp,)),
                dma((dp,)),
            ]
            if last
            else []
        ),
        compiler_params=pltpu.CompilerParams(
            collective_id=ident, has_side_effects=True, vmem_limit_bytes=62 << 20
        ),
        name="attn_backward",
    )(grad, x, gain, weight, tables, marks, spot, *kept, *others, *parts)


def pack_kernel(outer, dp, *refs):
    cut = Cut(refs)
    place, lengths, freqs, ids, gates, gain_attn, gain_ffn = cut(7)
    attn_any, ffn_any = cut(4), cut(6)
    tables, marks, spot, gains, mix = cut(5)
    layers, rows = gain_attn.shape
    attn_out, in_out, down_out = cut(layers), cut(layers), cut(layers)
    attn_in, ffn_in = cut(4), cut(6)
    attn_held, in_held, down_held = cut(layers), cut(layers), cut(layers)
    load_attn, load_ffn, keep = cut(3)
    loads_attn = [
        pltpu.make_async_copy(source, target, load_attn.at[i])
        for i, (source, target) in enumerate(zip(attn_any, attn_in))
    ]
    loads_ffn = [
        [
            pltpu.make_async_copy(source.at[level], target.at[level], load_ffn.at[level, i])
            for i, (source, target) in enumerate(zip(ffn_any, ffn_in))
        ]
        for level in range(layers)
    ]
    for load in sum(loads_ffn, loads_attn):
        load.start()
    count = place.shape[1]
    where = place[...]
    begins, end = jnp.zeros_like(where), 0
    for doc in range(lengths.shape[1]):
        end = end + lengths[0, doc]
        begins = begins + jnp.where(where >= end, lengths[0, doc], 0)
    spot[...] = where.astype(F32)
    lines = jnp.concatenate([where.astype(F32), begins.astype(F32)] * 4, axis=0)
    marks[...] = jnp.transpose(lines).reshape(4, count // 4, 8)
    angles = (where - begins).astype(F32) * freqs[...]
    cosine, sine = jnp.cos(angles), jnp.sin(angles)
    tables[0] = jnp.transpose(jnp.concatenate([cosine] * 4, axis=0)).reshape(4, count // 4, 128)
    tables[1] = jnp.transpose(jnp.concatenate([-sine, sine, -sine, sine], axis=0)).reshape(
        4, count // 4, 128
    )
    experts = mix.shape[0] // layers
    for level in range(layers):
        for e in range(experts):
            row = jnp.zeros((1, count), F32)
            for slot in range(ids.shape[1]):
                here = slice(slot, slot + 1)
                row = row + jnp.where(ids[level, here] == e, gates[level, here], 0.0)
            at = level * experts + e
            mix[at : at + 1] = row
    d = lax.axis_index("dp")
    gains[...] = jnp.zeros_like(gains)
    lane = lax.broadcasted_iota(jnp.int32, (layers, gains.shape[1]), 1)
    inside = (lane >= d * rows) & (lane < (d + 1) * rows)
    for i, gain in enumerate((gain_attn, gain_ffn)):
        wide = jnp.concatenate([gain[...].astype(BF16).astype(F32)] * dp, axis=1)
        gains[i * layers : (i + 1) * layers] = jnp.where(inside, wide, 0.0)
    keeps = []

    def leave(held, target):
        keeps.append(pltpu.make_async_copy(held, target, keep.at[len(keeps)]))
        keeps[-1].start()

    for load in loads_attn:
        load.wait()
    quarter = attn_in[0].shape[2]
    for level in range(layers):
        for i in range(4):
            values = attn_in[i][level]
            values = jnp.transpose(values) if i == 3 else values
            attn_held[level][0, :, i * quarter : (i + 1) * quarter] = values.astype(BF16)
        leave(attn_held[level], attn_out[level])
    for level in range(layers):
        for load in loads_ffn[level]:
            load.wait()
        slim = ffn_in[1].shape[2] // outer
        for group, (held, target) in enumerate(
            ((in_held, in_out), (in_held, in_out), (down_held, down_out))
        ):
            base = (experts + 1) * slim if group == 1 else 0
            for e in range(experts + 1):
                for k in range(outer):
                    cols = slice(k * slim, (k + 1) * slim)
                    if e < experts:
                        values = ffn_in[2 * group][level, e, :, cols]
                    else:
                        values = ffn_in[2 * group + 1][level, :, cols]
                    held[level][k, :, base + e * slim : base + (e + 1) * slim] = values.astype(
                        BF16
                    )
            if group:
                leave(held[level], target[level])
    for copy in keeps:
        copy.wait()


def pack(place, lengths, ids, gates, gain_attn, gain_ffn, attn, ffn, outer, dp):
    dma = pltpu.SemaphoreType.DMA
    layers, rows = gain_attn.shape
    count = place.shape[1]
    width = dp * rows
    experts = ffn[0].shape[1]
    slim = ffn[1].shape[2] // outer
    freqs = (10000.0 ** (-np.arange(HD // 2) / (HD // 2))).astype(np.float32)[:, None]
    blocks = (
        [(1, rows, 4 * attn[0].shape[2])] * layers
        + [(outer, rows, 2 * (experts + 1) * slim)] * layers
        + [(outer, rows, (experts + 1) * slim)] * layers
    )
    return pl.pallas_call(
        functools.partial(pack_kernel, outer, dp),
        out_shape=[
            jax.ShapeDtypeStruct((2, 4, count // 4, 128), F32),
            jax.ShapeDtypeStruct((4, count // 4, 8), F32),
            jax.ShapeDtypeStruct((1, count), F32),
            jax.ShapeDtypeStruct((8, width), F32),
            jax.ShapeDtypeStruct((layers * experts, count), F32),
        ]
        + [jax.ShapeDtypeStruct(block, BF16) for block in blocks],
        in_specs=[VMEM, pl.BlockSpec(memory_space=pltpu.SMEM)] + [VMEM] * 5 + [ANY] * 10,
        out_specs=[VMEM] * 5 + [ANY] * len(blocks),
        scratch_shapes=[pltpu.VMEM(m.shape, F32) for m in attn + ffn]
        + [pltpu.VMEM(block, BF16) for block in blocks]
        + [dma((4,)), dma((layers, 6)), dma((len(blocks),))],
        compiler_params=pltpu.CompilerParams(vmem_limit_bytes=62 << 20),
        name="pack",
    )(place, lengths, jnp.asarray(freqs), ids, gates, gain_attn, gain_ffn, *attn, *ffn)


def unpack_kernel(outer, layers, experts, *refs):
    cut = Cut(refs)
    in_any, down_any, attn_any = cut(layers), cut(layers), cut(layers)
    attn_out, ffn_out = cut(4), cut(6)
    in_v, down_v, attn_v = cut(layers), cut(layers), cut(layers)
    attn_held, ffn_held = cut(4), cut(6)
    load_sem, keep_attn, keep_ffn = cut(3)
    loads = [
        [
            pltpu.make_async_copy(source[level], target[level], load_sem.at[level, i])
            for i, (source, target) in enumerate(
                ((in_any, in_v), (down_any, down_v), (attn_any, attn_v))
            )
        ]
        for level in range(layers)
    ]
    for level in reversed(range(layers)):
        for load in loads[level]:
            load.start()
    keeps = []

    def leave(held, target, sem):
        keeps.append(pltpu.make_async_copy(held, target, sem))
        keeps[-1].start()

    slim = ffn_held[1].shape[2] // outer
    quarter = attn_held[0].shape[2]
    for level in reversed(range(layers)):
        for load in loads[level]:
            load.wait()
        for group, source in enumerate((in_v, in_v, down_v)):
            base = (experts + 1) * slim if group == 1 else 0
            for e in range(experts + 1):
                for k in range(outer):
                    cols = slice(k * slim, (k + 1) * slim)
                    values = source[level][k, :, base + e * slim : base + (e + 1) * slim]
                    if e < experts:
                        ffn_held[2 * group][level, e, :, cols] = values.astype(F32)
                    else:
                        ffn_held[2 * group + 1][level, :, cols] = values.astype(F32)
            for i in (2 * group, 2 * group + 1):
                leave(ffn_held[i].at[level], ffn_out[i].at[level], keep_ffn.at[level, i])
        total = jnp.sum(attn_v[level][...].astype(F32), axis=0)
        for i in range(4):
            values = total[:, i * quarter : (i + 1) * quarter]
            attn_held[i][level] = jnp.transpose(values) if i == 3 else values
            leave(attn_held[i].at[level], attn_out[i].at[level], keep_attn.at[level, i])
    for copy in keeps:
        copy.wait()


def unpack(pushed_in, pushed_down, pushed_attn, experts):
    dma = pltpu.SemaphoreType.DMA
    layers = len(pushed_in)
    outer, rows, third = pushed_down[0].shape
    full = outer * third // (experts + 1)
    quarter = pushed_attn[0].shape[2] // 4
    many, one = (layers, experts, rows, full), (layers, rows, full)
    shapes = [(layers, rows, quarter)] * 3 + [(layers, quarter, rows)] + [many, one] * 3
    moved = pushed_in + pushed_down + pushed_attn
    return pl.pallas_call(
        functools.partial(unpack_kernel, outer, layers, experts),
        out_shape=[jax.ShapeDtypeStruct(shape, F32) for shape in shapes],
        in_specs=[ANY] * len(moved),
        out_specs=[ANY] * 10,
        scratch_shapes=[pltpu.VMEM(part.shape, BF16) for part in moved]
        + [pltpu.VMEM(shape, F32) for shape in shapes]
        + [dma((layers, 3)), dma((layers, 4)), dma((layers, 6))],
        compiler_params=pltpu.CompilerParams(vmem_limit_bytes=62 << 20),
        name="unpack",
    )(*moved)


def layout(place_row, length_row):
    ends = jnp.cumsum(length_row, dtype=jnp.int32)
    after = place_row[:, None] >= ends[None, :]
    begins = jnp.sum(jnp.where(after, length_row[None, :], 0), axis=1, dtype=jnp.int32)
    return place_row - begins


def rope_tables(position):
    half_width = HD // 2
    freqs = 10000.0 ** (-jnp.arange(half_width, dtype=F32) / half_width)
    angles = position.astype(F32)[:, None] * freqs[None, :]
    cosine, sine = jnp.cos(angles), jnp.sin(angles)
    return jnp.stack(
        [
            jnp.concatenate([cosine] * 4, axis=1),
            jnp.concatenate([-sine, sine, -sine, sine], axis=1),
        ]
    )


def norm_back(grad_normed, gain_row, unit_rows, inverse):
    scaled = grad_normed * gain_row
    return inverse * (scaled - unit_rows * jnp.mean(scaled * unit_rows, axis=-1, keepdims=True))


def dot(left, right):
    return jnp.dot(left, right, preferred_element_type=F32)


def dot_nt(left, right):
    return lax.dot_general(left, right, (((1,), (1,)), ((), ())), preferred_element_type=F32)


def dot_tn(left, right):
    return lax.dot_general(left, right, (((0,), (0,)), ((), ())), preferred_element_type=F32)


def make_body(dp):
    outer, inner = split_dp(dp)

    def body(
        tokens,
        place,
        lengths,
        expert_ids,
        gate_values,
        cotangent,
        gain_attn,
        w_query,
        w_key,
        w_value,
        w_out,
        gain_ffn,
        exp_gate,
        exp_up,
        exp_down,
        dense_gate,
        dense_up,
        dense_down,
    ):
        layers, experts, rows, full = exp_gate.shape
        width = tokens.shape[1]
        slim = full // outer
        count = place.shape[1]
        kinds = experts + 1
        merged = rows % 16 == 0
        ids, gates = jnp.swapaxes(expert_ids, 1, 2), jnp.swapaxes(gate_values, 1, 2)
        downs = [jnp.swapaxes(exp_down, 2, 3), jnp.swapaxes(dense_down, 1, 2)]
        ffn = [exp_gate, dense_gate, exp_up, dense_up] + downs
        if merged:
            attn = [w_query, w_key, w_value, w_out]
            tables, marks, spot, gains_own, mix_own, *blocks = pack(
                place, lengths, ids, gates, gain_attn, gain_ffn, attn, ffn, outer, dp
            )
            attn_own = blocks[:layers]
            ffn_own = list(zip(blocks[layers : 2 * layers], blocks[2 * layers :]))
        else:
            position = layout(place[0], lengths[0])
            place_row = place[0].astype(F32)
            marks = jnp.stack([place_row, place_row - position.astype(F32)] * 4, axis=1)
            marks = marks.reshape(4, count // 4, 8)
            spot = place_row[None]
            tables = rope_tables(position).reshape(2, 4, count // 4, 128)
            slots = ids[:, None] == jnp.arange(experts, dtype=jnp.int32)[None, :, None, None]
            mix_own = jnp.sum(jnp.where(slots, gates[:, None], 0.0), axis=2)
            mix_own = mix_own.reshape(layers * experts, count)
            gains_own = jnp.concatenate([gain_attn, gain_ffn], axis=0).astype(BF16).astype(F32)
            spots = jnp.arange(dp, dtype=jnp.int32) == lax.axis_index("dp")
            gains_own = jnp.where(spots[None, :, None], gains_own[:, None], 0.0)
            gains_own = jnp.pad(
                gains_own.reshape(2 * layers, width), ((0, 8 - 2 * layers), (0, 0))
            )
            attn_own, ffn_own = [], []
            for level in range(layers):
                mats = [w_query[level], w_key[level], w_value[level], jnp.transpose(w_out[level])]
                attn_own.append(jnp.concatenate(mats, axis=1).astype(BF16)[None])
                mats = []
                for many, one in ((0, 1), (2, 3), (4, 5)):
                    mats += [ffn[many][level, e] for e in range(experts)] + [ffn[one][level]]
                mats = [m.astype(BF16) for m in mats]
                ffn_own.append(
                    [
                        jnp.stack(
                            [
                                jnp.concatenate(
                                    [m[:, k * slim : (k + 1) * slim] for m in group], axis=1
                                )
                                for k in range(outer)
                            ]
                        )
                        for group in (mats[: 2 * kinds], mats[2 * kinds :])
                    ]
                )
        state = tokens
        lead = [gains_own[None], attn_own[0], mix_own[None]]
        if merged:
            state_in = state
            ahead = [ffn_own[1][1]] if layers > 1 else []
            state, *kept = attn_forward(
                state_in,
                None,
                0,
                None,
                tables,
                marks,
                spot,
                lead + list(ffn_own[0]) + ahead,
                [BOTH] * 5 + [OUTER] * len(ahead),
                outer,
                inner,
                0,
            )
            part_down = kept.pop() if ahead else None
            gains, _, first, mix_all, w_in, w_down = kept[-6:]
            kept = kept[:-6]
        else:
            gains_all, first, mix_all = fetch(lead, outer, inner, 8)
            part_down = None
            gains = jnp.sum(gains_all, axis=0)
        w_attn = [first.reshape(width, -1)]
        w_ffn = []
        kept_attn, kept_ffn = [], []
        for level in range(layers):
            if level == 0 and merged:
                before = state_in
            else:
                before = state
                inside = list(ffn_own[level][: 1 if level else 2])
                state, *kept = attn_forward(
                    before,
                    gains,
                    level,
                    w_attn[level],
                    tables,
                    marks,
                    spot,
                    inside,
                    [BOTH] * len(inside),
                    outer,
                    inner,
                    1 if level else 11,
                )
                if level:
                    w_in = kept.pop()
                else:
                    w_down, w_in = kept.pop(), kept.pop()
            kept_attn.append((before, kept))
            w_ffn.append((w_in.reshape(width, -1), w_down.reshape(width, -1)))
            resid = state
            more, modes = [], []
            if level + 1 < layers:
                half = part_down is not None and level == 0
                more = [attn_own[level + 1], part_down if half else ffn_own[level + 1][1]]
                modes = [BOTH, INNER if half else BOTH]
            state, b_in, both, *fetched = ffn_forward(
                resid,
                gains,
                level,
                layers + level,
                kinds,
                mix_all,
                *w_ffn[level],
                more,
                modes,
                outer,
                inner,
                (2 if level == 0 else 12) if more else 3,
            )
            if more:
                w_attn.append(fetched[0].reshape(width, -1))
                w_down = fetched[1]
            kept_ffn.append((resid, b_in, both))
        mixed = state.astype(BF16)

        grad = cotangent
        part_gains = [None] * (2 * layers)
        pushed_in, pushed_down = [None] * layers, [None] * layers
        pushed_attn = [None] * layers
        waiting = []
        for level in reversed(range(layers)):
            resid, b_in, both = kept_ffn[level]
            grad, part_gain, grad_in, grad_down, *moved = ffn_backward(
                grad,
                resid,
                gains,
                level,
                layers + level,
                kinds,
                mix_all,
                *w_ffn[level],
                b_in,
                both,
                waiting,
                outer,
                inner,
                4 if waiting else 5,
            )
            part_gains[layers + level] = part_gain
            if waiting:
                (pushed_attn[level + 1],) = moved
            before, kept = kept_attn[level]
            inside = [grad_in.reshape(dp, rows, -1), grad_down.reshape(dp, rows, -1)]
            others = part_gains[1:] if level == 0 and merged else []
            grad, part_gain, *moved = attn_backward(
                grad,
                before,
                gains,
                level,
                w_attn[level],
                tables,
                marks,
                spot,
                kept,
                others,
                inside,
                outer,
                inner,
                6 if level else 7,
            )
            if level == 0 and merged:
                pushed_in[0], pushed_down[0], pushed_attn[0] = moved
                gain_sum = lax.dynamic_slice_in_dim(
                    part_gain, lax.axis_index("dp") * rows, rows, axis=1
                )
                continue
            part_gains[level] = part_gain
            waiting = [moved[0].reshape(dp, rows, -1)]
            pushed_in[level], pushed_down[level] = moved[1:]
        if not merged:
            stacked = jnp.concatenate(part_gains, axis=0)
            stacked = jnp.pad(stacked, ((0, 8 - 2 * layers), (0, 0)))
            stacked = jnp.transpose(stacked.reshape(8, dp, rows), (1, 0, 2))
            pushed_attn[0], gain_parts = push([waiting[0], stacked], outer, inner, 9)
            gain_part = jnp.sum(gain_parts, axis=0)
            gain_sum = jnp.sum(
                gather(jnp.pad(gain_part, ((0, 0), (0, 128 - rows))), dp, 10)[0], axis=0
            )
        grad_gain_attn = gain_sum[:layers, :rows]
        grad_gain_ffn = gain_sum[layers : 2 * layers, :rows]

        if merged:
            query, key, value, out, gate, gate_d, up, up_d, down, down_d = unpack(
                pushed_in, pushed_down, pushed_attn, experts
            )
        else:
            ups, downs, attns = [], [], []
            for level in range(layers):
                parts = pushed_in[level].reshape(outer, rows, 2 * kinds, slim)
                ups.append(jnp.transpose(parts, (2, 1, 0, 3)).reshape(2 * kinds, rows, full))
                parts = pushed_down[level].reshape(outer, rows, kinds, slim)
                downs.append(jnp.transpose(parts, (2, 1, 0, 3)).reshape(kinds, rows, full))
                attns.append(jnp.sum(pushed_attn[level].astype(F32), axis=0))
            ups, downs = jnp.stack(ups).astype(F32), jnp.stack(downs).astype(F32)
            gate, gate_d = ups[:, :experts], ups[:, experts]
            up, up_d = ups[:, kinds : kinds + experts], ups[:, kinds + experts]
            down, down_d = downs[:, :experts], downs[:, experts]
            query, key, value, out = jnp.split(jnp.stack(attns), 4, axis=2)
            out = jnp.swapaxes(out, 1, 2)
        return (
            mixed,
            grad,
            grad_gain_attn,
            query,
            key,
            value,
            out,
            grad_gain_ffn,
            gate,
            up,
            jnp.swapaxes(down, 2, 3),
            gate_d,
            up_d,
            jnp.swapaxes(down_d, 1, 2),
        )

    return body


def solution(mesh):
    return jax.shard_map(
        make_body(mesh.shape["dp"]),
        mesh=mesh,
        in_specs=(
            P(("dp", "tensor"), None),
            P("dp", None),
            P("dp", None),
            P(None, "dp", None),
            P(None, "dp", None),
            P(("dp", "tensor"), None),
            P(None, "dp"),
            P(None, "dp", "tensor"),
            P(None, "dp", "tensor"),
            P(None, "dp", "tensor"),
            P(None, "tensor", "dp"),
            P(None, "dp"),
            P(None, None, "dp", "tensor"),
            P(None, None, "dp", "tensor"),
            P(None, None, "tensor", "dp"),
            P(None, "dp", "tensor"),
            P(None, "dp", "tensor"),
            P(None, "tensor", "dp"),
        ),
        out_specs=(
            P(("dp", "tensor"), None),
            P(("dp", "tensor"), None),
            P(None, "dp"),
            P(None, "dp", "tensor"),
            P(None, "dp", "tensor"),
            P(None, "dp", "tensor"),
            P(None, "tensor", "dp"),
            P(None, "dp"),
            P(None, None, "dp", "tensor"),
            P(None, None, "dp", "tensor"),
            P(None, None, "tensor", "dp"),
            P(None, "dp", "tensor"),
            P(None, "dp", "tensor"),
            P(None, "tensor", "dp"),
        ),
        check_vma=False,
    )
```
